32 devices in a mesh: rep: 2 (over y), gx: 4 (over z), gy: 4 (over x, core).
Axes of the slice: x: 2, y: 2, z: 4, core: 2. Of those that a mesh axis runs over, the one named last changes fastest.
Arguments:
- positions: float32 [3, 8, 4, 1024], P(None, ('rep', 'gx'), 'gy'), parts along dimension 1, may hold values from 0 to 256, as said below
- charges: float32 [8, 4, 1024], P(('rep', 'gx'), 'gy'), parts along dimension 0, may hold values from -2 to 2
- pair_lists: int32 [8, 4, 4, 4], P(('rep', 'gx'), 'gy'), parts along dimension 0, may hold values from 0 to 35, as said below
- slab_dest: int32 [8, 4, 8], P(('rep', 'gx'), 'gy'), parts along dimension 0, may hold values from 0 to 3, as said below
- atom_counts: int32 [8, 4], P(('rep', 'gx'), 'gy'), parts along dimension 0, may hold values from 512 to 1024, as said below
Outputs:
- short_forces: float32 [3, 8, 4, 1024], P(None, ('rep', 'gx'), 'gy'), parts along dimension 1
- long_forces: float32 [3, 8, 4, 1024], P(None, ('rep', 'gx'), 'gy'), parts along dimension 1
The draws below stay inside these ranges and needn't reach their ends.
There are 2 independent parts, one for each index of `rep`. The reference program is written for one: setup_inputs(seed, part) draws one part's arguments, and reference() takes and returns one part's arrays. A program takes and returns all parts, laid end to end along the dimension named above; each array names one. Nothing has to cross between parts.
Inputs may be any that keep to these rules, and one draw needn't show every extreme that they name: `positions`: the first coordinate lies in [0, 64), the second in [0, 64), and the third in the slab of the atom's block, [s * 32, (s + 1) * 32). `pair_lists`: each list names 4 different clusters of the neighbourhood, the cluster's own, 16 + c for cluster c, first; the others are clusters whose blocks' slabs lie nearest to those of the cluster's own blocks. `slab_dest`: the blocks of a cell name slabs in non-decreasing order; at most 4 blocks of one cell name one slab, and in every cell some slab is named by exactly 4. `atom_counts`: some cell holds 1024 atoms in every draw.
All inputs are finite; a program needn't handle non-finite values.
Results may differ from the reference program's by a relative error of at most 0.0003.
Values sent between devices are 32-bit elements; how exact they have to be, the bound alone decides.
A program may use at most 128 MiB of HBM per device.

```python
import jax
import jax.numpy as jnp
from jax import lax

GRID_X = 256
GRID_Y = 256
GRID_Z = 128
BLOCK = 128
JLIST = 4
CLUSTERS_DEV = 4
ATOMS_DEV = 1024
BLOCKS_DEV = 8
SLOTS = 4
XC = 64
YC = 64
ZC = 32
N_GX = 4
N_GY = 4


def slab_layout(key):
    devices = N_GX * N_GY
    tokens = N_GY * SLOTS
    token_slab = jnp.arange(tokens, dtype=jnp.int32) // SLOTS

    def one_cell(cell_key):
        keys = jax.random.split(cell_key, 3)
        favour = jax.random.randint(keys[0], (N_GY,), 0, 400)
        busiest = jax.random.randint(keys[1], (), 0, N_GY)
        noise = jax.random.randint(keys[2], (tokens,), 0, 1000)
        score = noise + favour[token_slab] + 100000 * (token_slab == busiest).astype(jnp.int32)
        score = score * 4096 + jnp.arange(tokens, dtype=jnp.int32)
        picked = lax.top_k(score, BLOCKS_DEV)[1]
        return jnp.sort(token_slab[picked])
    keys = jax.random.split(jax.random.fold_in(key, 11), devices)
    return jax.vmap(one_cell)(keys).reshape(N_GX, N_GY, BLOCKS_DEV).astype(jnp.int32)


def draw_slab_dest(key, part):
    return slab_layout(key)


def draw_positions(key, part):
    slabs = slab_layout(key)
    atom_slab = jnp.repeat(slabs, BLOCK, axis=2).astype(jnp.float32)
    keys = jax.random.split(jax.random.fold_in(key, 23), 3)
    shape = (N_GX, N_GY, ATOMS_DEV)
    across = jax.random.uniform(keys[0], shape, jnp.float32, 0.0, XC * 1.0)
    along = jax.random.uniform(keys[1], shape, jnp.float32, 0.0, YC * 1.0)
    height = (atom_slab + jax.random.uniform(keys[2], shape, jnp.float32, 0.02, 0.98)) * ZC
    return jnp.stack([across, along, height])


def draw_charges(key, part):
    shape = (N_GX, N_GY, ATOMS_DEV)
    charge_key = jax.random.fold_in(key, 37)
    return jnp.clip(0.5 * jax.random.normal(charge_key, shape, jnp.float32), -2.0, 2.0)


def draw_pair_lists(key, part):
    candidates = 9 * CLUSTERS_DEV
    per_cluster = BLOCKS_DEV // CLUSTERS_DEV
    slabs = slab_layout(key).reshape(N_GX, N_GY, CLUSTERS_DEV, per_cluster)
    lowest = slabs[:, :, :, 0]
    highest = slabs[:, :, :, per_cluster - 1]
    low_parts = []
    high_parts = []
    for step_x in (-1, 0, 1):
        for step_y in (-1, 0, 1):
            low_parts.append(jnp.roll(lowest, (-step_x, -step_y), axis=(0, 1)))
            high_parts.append(jnp.roll(highest, (-step_x, -step_y), axis=(0, 1)))
    near_low = jnp.stack(low_parts, axis=2).reshape(N_GX, N_GY, candidates)
    near_high = jnp.stack(high_parts, axis=2).reshape(N_GX, N_GY, candidates)
    above = near_low[:, :, None, :] - highest[:, :, :, None]
    below = lowest[:, :, :, None] - near_high[:, :, None, :]
    slab_gap = jnp.maximum(0, jnp.maximum(above, below))
    noise = jax.random.randint(jax.random.fold_in(key, 53), (N_GX, N_GY, CLUSTERS_DEV, candidates), 0, 4096)
    own_index = 4 * CLUSTERS_DEV + jnp.arange(CLUSTERS_DEV, dtype=jnp.int32)[:, None]
    choice_index = jnp.arange(candidates, dtype=jnp.int32)[None, :]
    score = ((256 - slab_gap) * 4096 + noise) * 512 + choice_index
    score = score + (choice_index == own_index).astype(jnp.int32) * (1 << 29)
    return lax.top_k(score, JLIST)[1].astype(jnp.int32)


def draw_atom_counts(key, part):
    keys = jax.random.split(jax.random.fold_in(key, 41), 2)
    counts = jax.random.randint(keys[0], (N_GX * N_GY,), ATOMS_DEV // 2, ATOMS_DEV + 1)
    fullest = jax.random.randint(keys[1], (), 0, N_GX * N_GY)
    counts = jnp.where(jnp.arange(N_GX * N_GY) == fullest, ATOMS_DEV, counts)
    return counts.reshape(N_GX, N_GY).astype(jnp.int32)


def setup_inputs(seed: int = 0, part: int = 0) -> dict:
    key_of = jax.random.split(jax.random.key(seed), 6)
    own_keys = jax.random.split(jax.random.fold_in(key_of[5], part), 6)
    positions = draw_positions(jax.random.fold_in(jax.random.fold_in(key_of[5], part), 71), part)
    charges = draw_charges(jax.random.fold_in(jax.random.fold_in(key_of[5], part), 71), part)
    pair_lists = draw_pair_lists(jax.random.fold_in(jax.random.fold_in(key_of[5], part), 71), part)
    slab_dest = draw_slab_dest(jax.random.fold_in(jax.random.fold_in(key_of[5], part), 71), part)
    atom_counts = draw_atom_counts(jax.random.fold_in(jax.random.fold_in(key_of[5], part), 71), part)
    return dict(positions=positions, charges=charges, pair_lists=pair_lists, slab_dest=slab_dest, atom_counts=atom_counts)


spacing = 0.16
ewald_split = 3.47
cutoff = 0.9
soft_core = 0.09
root_factor = 1.1283791670955126

def spline_weights(fraction):
    remain = 1.0 - fraction
    square = fraction * fraction
    cube_part = square * fraction
    values = jnp.stack([remain * remain * remain / 6.0, (3.0 * cube_part - 6.0 * square + 4.0) / 6.0, (-3.0 * cube_part + 3.0 * square + 3.0 * fraction + 1.0) / 6.0, cube_part / 6.0])
    slopes = jnp.stack([-0.5 * remain * remain, 0.5 * (3.0 * square - 4.0 * fraction), 0.5 * (-3.0 * square + 2.0 * fraction + 1.0), 0.5 * square])
    return (values, slopes)

def split_cells(coordinate, offset, cell_count):
    inside = coordinate - offset
    lowest = jnp.clip(jnp.floor(inside).astype(jnp.int32), 0, cell_count - 1)
    return (lowest, inside - lowest.astype(inside.dtype))

def influence(index_x, index_y, index_z):

    def signed(index, period):
        return jnp.where(index <= period // 2, index, index - period).astype(jnp.float32) / (period * spacing)

    def modulus(index, period):
        return ((2.0 + jnp.cos(index.astype(jnp.float32) * (2.0 * jnp.pi / period))) / 3.0) ** 2
    wave = signed(index_x, GRID_X) ** 2 + signed(index_y, GRID_Y) ** 2 + signed(index_z, GRID_Z) ** 2
    safe_wave = jnp.where(wave > 0.0, wave, 1.0)
    volume = GRID_X * GRID_Y * GRID_Z * spacing ** 3
    green = jnp.exp(-(jnp.pi / ewald_split) ** 2 * safe_wave) / (jnp.pi * volume * safe_wave)
    green = green / (modulus(index_x, GRID_X) * modulus(index_y, GRID_Y) * modulus(index_z, GRID_Z))
    return jnp.where(wave > 0.0, green, 0.0)

def cluster_forces(own_atoms, beside_all, pair_list):

    def one_cluster(inputs):
        own_rows, chosen = inputs
        partner = beside_all[:, chosen]
        offsets = (own_rows[:3, None, :, None] - partner[:3, :, None, :]) * spacing
        dist_square = lax.optimization_barrier(jnp.sum(offsets * offsets, axis=0))
        soft_square = dist_square + soft_core
        soft_dist = jnp.sqrt(soft_square)
        scaled = ewald_split * soft_dist
        strength = (jax.scipy.special.erfc(scaled) / soft_dist + ewald_split * root_factor * jnp.exp(-scaled * scaled)) / soft_square
        cutoff_taper = jnp.where(dist_square < cutoff * cutoff, (1.0 - dist_square / (cutoff * cutoff)) ** 2, 0.0)
        weight = partner[3][:, None, :] * strength * cutoff_taper
        return own_rows[3] * lax.optimization_barrier(jnp.sum(weight[None] * offsets, axis=(1, 3)))
    return lax.map(one_cluster, (jnp.moveaxis(own_atoms, 1, 0), pair_list))

def short_range(positions, charge, pair_lists):
    count_x, count_y, atom_total = charge.shape
    clusters = pair_lists.shape[2]
    cluster_size = atom_total // clusters
    cells_x = GRID_X // count_x
    cells_y = GRID_Y // count_y
    packed = jnp.concatenate([positions, charge[None]], axis=0)
    pieces = []
    for step_x in (-1, 0, 1):
        for step_y in (-1, 0, 1):
            moved = jnp.roll(packed, (-step_x, -step_y), axis=(1, 2))
            cell_shift = jnp.array([step_x * cells_x, step_y * cells_y, 0.0, 0.0], jnp.float32)
            pieces.append(moved + cell_shift[:, None, None, None])
    devices = count_x * count_y
    beside_all = jnp.stack(pieces, axis=3).reshape(4, devices, 9 * clusters, cluster_size)
    own_atoms = packed.reshape(4, devices, clusters, cluster_size)
    listing = pair_lists.reshape(devices, clusters, pair_lists.shape[3])

    def one_cell(inputs):
        return cluster_forces(inputs[0], inputs[1], inputs[2])
    result = lax.map(one_cell, (jnp.moveaxis(own_atoms, 1, 0), jnp.moveaxis(beside_all, 1, 0), listing))
    return jnp.moveaxis(result, 2, 0).reshape(3, count_x, count_y, atom_total)

def long_range(positions, charge, slab_dest):
    count_x, count_y, atom_total = charge.shape
    cells_x = GRID_X // count_x
    cells_y = GRID_Y // count_y
    cells_z = GRID_Z // count_y
    block_size = atom_total // slab_dest.shape[2]
    slab_of = jnp.repeat(slab_dest, block_size, axis=2)
    column_x = jnp.arange(count_x, dtype=jnp.int32)[:, None, None]
    column_y = jnp.arange(count_y, dtype=jnp.int32)[None, :, None]
    lowest_x, fraction_x = split_cells(positions[0], 0.0, cells_x)
    lowest_y, fraction_y = split_cells(positions[1], 0.0, cells_y)
    lowest_z, fraction_z = split_cells(positions[2], (slab_of * cells_z).astype(jnp.float32), cells_z)
    point_x = column_x * cells_x + lowest_x
    point_y = column_y * cells_y + lowest_y
    point_z = slab_of * cells_z + lowest_z
    values_x, slopes_x = spline_weights(fraction_x)
    values_y, slopes_y = spline_weights(fraction_y)
    values_z, slopes_z = spline_weights(fraction_z)
    charge_mesh = jnp.zeros((GRID_X, GRID_Y, GRID_Z), jnp.float32)
    for term_x in range(4):
        for term_y in range(4):
            for term_z in range(4):
                charge_mesh = charge_mesh.at[(point_x + term_x) % GRID_X, (point_y + term_y) % GRID_Y, (point_z + term_z) % GRID_Z].add(charge * values_x[term_x] * values_y[term_y] * values_z[term_z])
    green = influence(jnp.arange(GRID_X, dtype=jnp.int32)[:, None, None], jnp.arange(GRID_Y, dtype=jnp.int32)[None, :, None], jnp.arange(GRID_Z, dtype=jnp.int32)[None, None, :])
    potential = jnp.real(jnp.fft.ifftn(green * jnp.fft.fftn(charge_mesh))) * (GRID_X * GRID_Y * GRID_Z)
    force_x = jnp.zeros_like(charge)
    force_y = jnp.zeros_like(charge)
    force_z = jnp.zeros_like(charge)
    for term_x in range(4):
        for term_y in range(4):
            for term_z in range(4):
                sample = potential[(point_x + term_x) % GRID_X, (point_y + term_y) % GRID_Y, (point_z + term_z) % GRID_Z]
                force_x = force_x + slopes_x[term_x] * values_y[term_y] * values_z[term_z] * sample
                force_y = force_y + values_x[term_x] * slopes_y[term_y] * values_z[term_z] * sample
                force_z = force_z + values_x[term_x] * values_y[term_y] * slopes_z[term_z] * sample
    factor = -charge / spacing
    return jnp.stack([factor * force_x, factor * force_y, factor * force_z])

def reference(positions, charges, pair_lists, slab_dest, atom_counts):
    living = jnp.arange(charges.shape[2], dtype=jnp.int32)[None, None, :] < atom_counts[:, :, None]
    charge = jnp.where(living, charges, 0.0)
    return (short_range(positions, charge, pair_lists), long_range(positions, charge, slab_dest))
```

```python
import functools
import math

import jax
import jax.numpy as jnp
import numpy as np
from jax import lax
from jax.experimental import pallas as pl
from jax.experimental.pallas import tpu as pltpu
from jax.sharding import PartitionSpec as P

GRID_X = 256
GRID_Y = 256
GRID_Z = 128


spacing = 0.16
ewald_split = 3.47
cutoff = 0.9
soft_core = 0.09
root_factor = 1.1283791670955126
rows_group = 8


def moved(value, step_x, step_y):
    count_x = lax.axis_size("gx")
    count_y = lax.axis_size("gy")
    pairs = [
        (i * count_y + j, (i + step_x) % count_x * count_y + (j + step_y) % count_y)
        for i in range(count_x)
        for j in range(count_y)
    ]
    return lax.ppermute(value, ("gx", "gy"), pairs)


def round_up(value, multiple):
    return -(-value // multiple) * multiple


def hartley(period):
    turns = np.outer(np.arange(period), np.arange(period)) % period
    phases = turns * (2.0 * np.pi / period)
    return (np.cos(phases) + np.sin(phases)).astype(np.float32)


def halves(value):
    high = value.astype(jnp.bfloat16)
    low = (value - high.astype(jnp.float32)).astype(jnp.bfloat16)
    return (high, low)


def dot(left_side, right_side):
    return jnp.dot(left_side, right_side, preferred_element_type=jnp.float32)


def spline_weights(fraction):
    remain = 1.0 - fraction
    square = fraction * fraction
    cube_part = square * fraction
    values = [
        remain * remain * remain / 6.0,
        (3.0 * cube_part - 6.0 * square + 4.0) / 6.0,
        (-3.0 * cube_part + 3.0 * square + 3.0 * fraction + 1.0) / 6.0,
        cube_part / 6.0,
    ]
    slopes = [
        -0.5 * remain * remain,
        0.5 * (3.0 * square - 4.0 * fraction),
        0.5 * (-3.0 * square + 2.0 * fraction + 1.0),
        0.5 * square,
    ]
    return (values, slopes)


def split_cells(coordinate, offset, cell_count):
    inside = coordinate - offset
    lowest = jnp.clip(jnp.floor(inside).astype(jnp.int32), 0, cell_count - 1)
    return (lowest, inside - lowest.astype(inside.dtype))


def spline_table(lowest, values, table_size, period=None):
    points = lax.broadcasted_iota(jnp.int32, (table_size, lowest.shape[1]), 0)
    lookup = jnp.zeros(points.shape, jnp.float32)
    for spline_term in range(4):
        at = lowest + spline_term
        if period is not None:
            at = jnp.where(at >= period, at - period, at)
        lookup = jnp.where(points == at, values[spline_term], lookup)
    return lookup


def spread_kernel(cells, pad, atoms_ref, base_ref, turn_ref, out_ref, wx_ref, wy_ref, wz_ref, hi_ref, lo_ref):
    cells_x, cells_y, cells_z = cells
    pad_x, pad_y = pad
    atom_total = atoms_ref.shape[1]
    low_x, frac_x = split_cells(atoms_ref[0:1, :], 0.0, cells_x)
    low_y, frac_y = split_cells(atoms_ref[1:2, :], 0.0, cells_y)
    base = base_ref[...]
    low_z, frac_z = split_cells(atoms_ref[2:3, :], base.astype(jnp.float32), cells_z)
    wx_ref[...] = spline_table(low_x, spline_weights(frac_x)[0], pad_x) * atoms_ref[3:4, :]
    wy_ref[...] = spline_table(low_y, spline_weights(frac_y)[0], pad_y)
    turn = turn_ref[...]
    size_z = turn.shape[0]
    table_z = spline_table(base + low_z, spline_weights(frac_z)[0], size_z, size_z)
    waves = jnp.dot(
        turn, table_z, precision=lax.Precision.HIGHEST, preferred_element_type=jnp.float32
    ).T
    high, low = halves(waves)
    wz_ref[:, :size_z] = high
    wz_ref[:, size_z:] = low

    @pl.loop(0, pad_x // rows_group)
    def _(chunk):
        for inner in range(rows_group):
            row = wx_ref[pl.ds(chunk * rows_group + inner, 1), :]
            high, low = halves(row * wy_ref[...])
            hi_ref[pl.ds(inner * pad_y, pad_y), :] = high
            lo_ref[pl.ds(inner * pad_y, pad_y), :] = low
        both = dot(hi_ref[...], wz_ref[...])
        rest = dot(lo_ref[...], wz_ref[:, :size_z])
        total = both[:, :size_z] + both[:, size_z:] + rest
        out_ref[pl.ds(chunk * rows_group, rows_group)] = total.reshape(rows_group, pad_y, size_z)


def gather_kernel(cells, pad, atoms_ref, base_ref, turn_ref, mesh_ref, out_ref, wx_ref, vx_ref, wy_ref, vy_ref, wz_ref, level_ref):
    cells_x, cells_y, cells_z = cells
    pad_x, pad_y = pad
    atom_total = atoms_ref.shape[1]
    low_x, frac_x = split_cells(atoms_ref[0:1, :], 0.0, cells_x)
    low_y, frac_y = split_cells(atoms_ref[1:2, :], 0.0, cells_y)
    base = base_ref[...]
    low_z, frac_z = split_cells(atoms_ref[2:3, :], base.astype(jnp.float32), cells_z)
    values, slopes = spline_weights(frac_x)
    wx_ref[...] = spline_table(low_x, values, pad_x)
    vx_ref[...] = spline_table(low_x, slopes, pad_x)
    values, slopes = spline_weights(frac_y)
    wy_ref[...] = spline_table(low_y, values, pad_y)
    vy_ref[...] = spline_table(low_y, slopes, pad_y)
    values, slopes = spline_weights(frac_z)
    turn = turn_ref[...]
    size_z = turn.shape[0]
    for place, terms in enumerate((values, slopes)):
        table_z = spline_table(base + low_z, terms, size_z, size_z)
        waves = jnp.dot(
            turn, table_z, precision=lax.Precision.HIGHEST, preferred_element_type=jnp.float32
        )
        high, low = halves(waves)
        wz_ref[:size_z, pl.ds(place * atom_total, atom_total)] = high
        wz_ref[size_z:, pl.ds(place * atom_total, atom_total)] = low
    groups = pad_y // 8

    def one_chunk(chunk, sums):
        rows = mesh_ref[pl.ds(chunk * rows_group, rows_group)].reshape(rows_group * pad_y, size_z)
        high, low = halves(rows)
        level_ref[...] = dot(jnp.concatenate([high, high], axis=1), wz_ref[...]) + dot(
            low, wz_ref[:size_z, :]
        )
        first, second, third = sums
        for inner in range(rows_group):
            flat = level_ref[pl.ds(inner * pad_y, pad_y), :atom_total]
            tilt = level_ref[pl.ds(inner * pad_y, pad_y), atom_total:]
            across = wy_ref[...]
            part_x = jnp.sum((across * flat).reshape(groups, 8, atom_total), axis=0)
            part_y = jnp.sum((vy_ref[...] * flat).reshape(groups, 8, atom_total), axis=0)
            part_z = jnp.sum((across * tilt).reshape(groups, 8, atom_total), axis=0)
            weight = wx_ref[pl.ds(chunk * rows_group + inner, 1), :]
            slope = vx_ref[pl.ds(chunk * rows_group + inner, 1), :]
            first = first + slope * part_x
            second = second + weight * part_y
            third = third + weight * part_z
        return (first, second, third)

    zero = jnp.zeros((8, atom_total), jnp.float32)
    sums = lax.fori_loop(0, pad_x // rows_group, one_chunk, (zero, zero, zero))
    factor = -atoms_ref[3:4, :] / spacing
    for place in range(3):
        out_ref[pl.ds(place, 1), :] = factor * jnp.sum(sums[place], axis=0, keepdims=True)


def share_kernel(sizes, atoms_ref, out_ref, send_sem, recv_sem):
    count_x, count_y = sizes
    place_x, place_y = (lax.axis_index("gx"), lax.axis_index("gy"))
    me = place_x * count_y + place_y
    peers = []
    for order in range(1, count_x * count_y):
        peer_x = lax.rem(place_x + order // count_y, count_x)
        peer_y = lax.rem(place_y + order % count_y, count_y)
        peers.append({"gx": peer_x, "gy": peer_y})
    barrier = pltpu.get_barrier_semaphore()
    for peer in peers:
        pl.semaphore_signal(
            barrier, inc=1, device_id=peer, device_id_type=pl.DeviceIdType.MESH
        )
    pl.semaphore_wait(barrier, len(peers))
    copies = [
        pltpu.make_async_remote_copy(
            src_ref=atoms_ref,
            dst_ref=out_ref.at[me],
            send_sem=send_sem.at[order],
            recv_sem=recv_sem.at[order],
            device_id=peer,
            device_id_type=pl.DeviceIdType.MESH,
        )
        for order, peer in enumerate(peers)
    ]
    for copy in copies:
        copy.start()
    out_ref[me] = atoms_ref[...]
    for copy in copies:
        copy.wait()


def shared(atoms, count_x, count_y):
    devices = count_x * count_y
    vmem = pl.BlockSpec(memory_space=pltpu.VMEM)
    flags = pltpu.SemaphoreType.DMA((devices - 1,))
    return pl.pallas_call(
        functools.partial(share_kernel, (count_x, count_y)),
        in_specs=[vmem],
        out_specs=vmem,
        out_shape=jax.ShapeDtypeStruct((devices, *atoms.shape), jnp.float32),
        scratch_shapes=[flags, flags],
        compiler_params=pltpu.CompilerParams(collective_id=0, has_side_effects=True),
        name="share",
    )(atoms)


def depth_rows(table, height, fraction, terms):
    turns = height * table[:, 0:1]
    quarter = GRID_Z // 4
    nearest = jnp.floor(turns * (1.0 / quarter) + 0.5)
    angle = (turns - nearest * quarter) * (2.0 * math.pi / GRID_Z)
    quadrant = nearest - 4.0 * jnp.floor(nearest * 0.25)
    square = angle * angle
    near_cos = 1.0 + square * (
        -0.5 + square * (1.0 / 24.0 + square * (-1.0 / 720.0 + square * (1.0 / 40320.0)))
    )
    near_sin = angle * (
        1.0
        + square
        * (-1.0 / 6.0 + square * (1.0 / 120.0 + square * (-1.0 / 5040.0 + square / 362880.0)))
    )
    odd_turn = (quadrant == 1.0) | (quadrant == 3.0)
    cosine = jnp.where(odd_turn, near_sin, near_cos)
    cosine = jnp.where((quadrant == 1.0) | (quadrant == 2.0), -cosine, cosine)
    sine = jnp.where(odd_turn, near_cos, near_sin)
    sine = jnp.where(quadrant >= 2.0, -sine, sine)
    results = []
    for weights in terms:
        even = sum(table[:, 1 + t : 2 + t] * weights[t] for t in range(4))
        odd = sum(table[:, 5 + t : 6 + t] * weights[t] for t in range(4))
        results.append(cosine * even + sine * odd)
    return results


def mesh_kernel(sizes, cells, pad, atoms_ref, xh_ref, xl_ref, yh_ref, yl_ref, column_ref, row_ref, table_ref, out_ref, mesh_ref, turned_ref, *scratch):
    count_x, count_y = sizes
    cells_x, cells_y = cells
    pad_x, pad_y = pad
    atom_total = atoms_ref.shape[2]
    depth = table_ref.shape[0]
    window = 2 * cells_y
    windows = GRID_Y // window
    lane = lax.broadcasted_iota(jnp.int32, (depth * pad_x, window), 1)
    mesh_ref[...] = jnp.zeros_like(mesh_ref)
    table = table_ref[...]
    per_side = len(scratch) // 2
    banks = (scratch[:per_side], scratch[per_side:])
    for _, _, wy_ref, _, _, _, _, side_ref in banks:
        wy_ref[...] = jnp.zeros_like(wy_ref)
        side_ref[...] = jnp.zeros_like(side_ref)

    def atoms_of(cell, row):
        return atoms_ref[cell, row : row + 1, :]

    def spread_cell(cell, i, j):
        wx_ref, vx_ref, wy_ref, hi_ref, lo_ref, level_ref, stack_ref, side_ref = banks[j % 2]
        low_x, frac_x = split_cells(atoms_of(cell, 0), 0.0, cells_x)
        low_y, frac_y = split_cells(atoms_of(cell, 1), 0.0, cells_y)
        wx_ref[...] = spline_table(low_x, spline_weights(frac_x)[0], pad_x)
        high, low = halves(spline_table(low_y, spline_weights(frac_y)[0], pad_y))
        wy_ref[:pad_y, :] = high
        wy_ref[pl.ds(window, pad_y), :] = low
        height = jnp.floor(atoms_of(cell, 2))
        frac_z = atoms_of(cell, 2) - height
        (deep,) = depth_rows(table, height, frac_z, [spline_weights(frac_z)[0]])
        deep = deep * atoms_of(cell, 3)
        for k in range(depth):
            high, low = halves(deep[k : k + 1, :] * wx_ref[...])
            hi_ref[pl.ds(k * pad_x, pad_x), :] = high
            lo_ref[pl.ds(k * pad_x, pad_x), :] = low
        numbers = (((1,), (1,)), ((), ()))
        both = lax.dot_general(
            hi_ref[...], wy_ref[...], numbers, preferred_element_type=jnp.float32
        )
        rest = lax.dot_general(
            lo_ref[...], wy_ref[:window, :], numbers, preferred_element_type=jnp.float32
        )
        total = both[:, :window] + both[:, window:] + rest
        rows = pl.ds(pl.multiple_of(i * cells_x, 8), pad_x)
        m = j // 2
        if j % 2 == 0:
            mesh_ref[:, rows, pl.ds(m * window, window)] += total.reshape(depth, pad_x, window)
        else:
            total = pltpu.roll(total, cells_y, 1)
            kept = jnp.where(lane >= cells_y, total, 0.0)
            carried = jnp.where(lane < cells_y, total, 0.0)
            after = (m + 1) % windows
            mesh_ref[:, rows, pl.ds(m * window, window)] += kept.reshape(depth, pad_x, window)
            mesh_ref[:, rows, pl.ds(after * window, window)] += carried.reshape(
                depth, pad_x, window
            )

    @pl.loop(0, count_x)
    def _(i):
        for j in range(count_y):
            spread_cell(i * count_y + j, i, j)

    def across(value):
        high, low = halves(value)
        return dot(xh_ref[...], high) + dot(xl_ref[...], high) + dot(xh_ref[...], low)

    def along(value):
        high, low = halves(value)
        return dot(high, yh_ref[...]) + dot(high, yl_ref[...]) + dot(low, yh_ref[...])

    extra = mesh_ref.shape[1] - GRID_X

    @pl.loop(0, depth)
    def _(k):
        mesh_ref[k, :extra, :] += mesh_ref[k, GRID_X:, :]
        waves = along(across(mesh_ref[k, :GRID_X, :]))
        square = column_ref[:, 0:1] + row_ref[0:1, :] + table_ref[pl.ds(k, 1), 9:10]
        scale = column_ref[:, 1:2] * row_ref[1:2, :] * table_ref[pl.ds(k, 1), 10:11]
        green = jnp.where(square > 0.0, scale / jnp.where(square > 0.0, square, 1.0), 0.0)
        plane = across(along(waves * green))
        mesh_ref[k, :GRID_X, :] = plane
        mesh_ref[k, GRID_X:, :] = plane[:extra]
        rolled = pltpu.roll(plane, GRID_Y - cells_y, 1)
        turned_ref[k, :GRID_X, :] = rolled
        turned_ref[k, GRID_X:, :] = rolled[:extra]

    stride = round_up(pad_y, 16)
    groups = pad_x // 8

    def gather_cell(cell, i, j):
        wx_ref, vx_ref, wy_ref, hi_ref, lo_ref, level_ref, stack_ref, side_ref = banks[j % 2]
        low_x, frac_x = split_cells(atoms_of(cell, 0), 0.0, cells_x)
        low_y, frac_y = split_cells(atoms_of(cell, 1), 0.0, cells_y)
        values, slopes = spline_weights(frac_x)
        wx_ref[...] = spline_table(low_x, values, pad_x)
        vx_ref[...] = spline_table(low_x, slopes, pad_x)
        for place, terms in enumerate(spline_weights(frac_y)):
            high, low = halves(spline_table(low_y, terms, stride))
            span = pl.ds(place * atom_total, atom_total)
            side_ref[:stride, span] = high
            side_ref[pl.ds(stride, stride), span] = low
            side_ref[pl.ds(2 * stride, stride), span] = high
        height = jnp.floor(atoms_of(cell, 2))
        frac_z = atoms_of(cell, 2) - height
        deep, steep = depth_rows(table, height, frac_z, spline_weights(frac_z))
        source = mesh_ref if j % 2 == 0 else turned_ref
        rows = pl.ds(pl.multiple_of(i * cells_x, 8), pad_x)
        block = source[:, rows, pl.ds(j // 2 * window, window)].reshape(depth * pad_x, window)
        high = block.astype(jnp.bfloat16).astype(jnp.float32)
        low = block - high
        shifted = pltpu.roll(high, stride, 1)
        stack_ref[:, :window] = jnp.where(lane < stride, high, shifted).astype(jnp.bfloat16)
        stack_ref[:, window:] = jnp.where(
            lane < 2 * stride - window, shifted, pltpu.roll(low, 2 * stride - window, 1)
        ).astype(jnp.bfloat16)
        level_ref[...] = dot(stack_ref[...], side_ref[...])
        zero = jnp.zeros((8, atom_total), jnp.float32)
        first, second, third = (zero, zero, zero)
        for k in range(depth):
            flat = level_ref[pl.ds(k * pad_x, pad_x), :atom_total]
            tilt = level_ref[pl.ds(k * pad_x, pad_x), atom_total:]
            weight = wx_ref[...]
            part_x = jnp.sum((vx_ref[...] * flat).reshape(groups, 8, atom_total), axis=0)
            part_y = jnp.sum((weight * tilt).reshape(groups, 8, atom_total), axis=0)
            part_z = jnp.sum((weight * flat).reshape(groups, 8, atom_total), axis=0)
            first = first + deep[k : k + 1, :] * part_x
            second = second + deep[k : k + 1, :] * part_y
            third = third + steep[k : k + 1, :] * part_z
        for place, value in enumerate((first, second, third)):
            out_ref[cell, pl.ds(place, 1), :] = jnp.sum(value, axis=0, keepdims=True)
        out_ref[cell, 3:4, :] = jnp.zeros((1, atom_total), jnp.float32)

    @pl.loop(0, count_x)
    def _(i):
        for j in range(count_y):
            gather_cell(i * count_y + j, i, j)


root_terms = (
    3.9164407301418542,
    -0.0037127819564810594,
    0.16802528315459195,
    -0.003061234121505335,
    -0.0076524954798020545,
    0.002268454833542123,
    -0.0003056487922112269,
    1.686888935413571e-05,
)


def pair_weight(square):
    soft_square = square * (spacing * spacing) + soft_core
    inverse = lax.rsqrt(soft_square)
    series = jnp.full_like(inverse, root_terms[-1])
    for term in root_terms[-2::-1]:
        series = series * inverse + term
    decay = jnp.exp(soft_square * (-ewald_split * ewald_split))
    taper = jnp.maximum(1.0 - square * (spacing * spacing / (cutoff * cutoff)), 0.0)
    return (decay * series) * (inverse * taper) ** 2


def row_sums(values):
    total = None
    ones = jnp.ones((16, values.shape[1]), jnp.bfloat16)
    for _ in range(3):
        part = values.astype(jnp.bfloat16)
        values = values - part.astype(jnp.float32)
        summed = lax.dot_general(
            ones, part, (((1,), (1,)), ((), ())), preferred_element_type=jnp.float32
        )
        total = summed if total is None else total + summed
    return total[0:1, :]


def peers_of(count_x, count_y):
    place_x, place_y = (lax.axis_index("gx"), lax.axis_index("gy"))
    peers = []
    for order in range(1, count_x * count_y):
        peer_x = lax.rem(place_x + order // count_y, count_x)
        peer_y = lax.rem(place_y + order % count_y, count_y)
        peers.append((peer_x, peer_y))
    return peers


def finish_kernel(sizes, cells, pairs_ref, partial_ref, atoms_ref, short_ref, long_ref, land_ref, column_ref, partner_ref, sum_ref, send_sem, recv_sem):
    count_x, count_y = sizes
    cells_x, cells_y = cells
    place_x, place_y = (lax.axis_index("gx"), lax.axis_index("gy"))
    me = place_x * count_y + place_y
    peers = peers_of(count_x, count_y)
    barrier = pltpu.get_barrier_semaphore()
    for peer_x, peer_y in peers:
        pl.semaphore_signal(
            barrier,
            inc=1,
            device_id={"gx": peer_x, "gy": peer_y},
            device_id_type=pl.DeviceIdType.MESH,
        )
    clusters, listed = pairs_ref.shape[2:]
    atom_total = atoms_ref.shape[2]
    size = atom_total // clusters
    lanes = 128
    for axis in range(3):
        for chunk in range(atom_total // lanes):
            row = atoms_ref[me, pl.ds(axis, 1), pl.ds(chunk * lanes, lanes)]
            column_ref[axis, pl.ds(chunk * lanes, lanes), :] = jnp.broadcast_to(
                row, (lanes, lanes)
            ).T
    for c in range(clusters):
        for n in range(listed):
            chosen = pairs_ref[0, 0, c, n]
            beside = lax.div(chosen, clusters)
            which = chosen - beside * clusters
            row_x = lax.div(beside, 3)
            step_x = row_x - 1
            step_y = beside - row_x * 3 - 1
            from_x = lax.rem(place_x + step_x + count_x, count_x)
            from_y = lax.rem(place_y + step_y + count_y, count_y)
            block = atoms_ref[from_x * count_y + from_y]
            part = block[:, :size]
            for k in range(1, clusters):
                part = jnp.where(which == k, block[:, k * size : (k + 1) * size], part)
            shifts = (
                (step_x * cells_x).astype(jnp.float32),
                (step_y * cells_y).astype(jnp.float32),
            )
            for axis in range(4):
                row = part[axis : axis + 1, :]
                if axis < 2:
                    row = row + shifts[axis]
                partner_ref[c, axis, :, n * size : (n + 1) * size] = jnp.broadcast_to(
                    row, (8, size)
                )

    pl.semaphore_wait(barrier, len(peers))
    copies = []
    for order, (peer_x, peer_y) in enumerate(peers):
        copy = pltpu.make_async_remote_copy(
            src_ref=partial_ref.at[peer_x * count_y + peer_y],
            dst_ref=land_ref.at[order],
            send_sem=send_sem.at[order],
            recv_sem=recv_sem.at[order],
            device_id={"gx": peer_x, "gy": peer_y},
            device_id_type=pl.DeviceIdType.MESH,
        )
        copy.start()
        copies.append(copy)

    @pl.loop(0, clusters)
    def _(c):
        @pl.loop(0, size // 8)
        def _(step):
            rows = pl.ds(pl.multiple_of(c * size + step * 8, 8), 8)
            own = [column_ref[axis, rows, :] for axis in range(3)]
            sums = [jnp.zeros((8, lanes), jnp.float32) for _ in range(3)]
            for tile in range(listed * size // lanes):
                span = pl.ds(tile * lanes, lanes)
                offsets = [own[axis] - partner_ref[c, axis, :, span] for axis in range(3)]
                square = sum(offset * offset for offset in offsets)
                weight = pair_weight(square) * partner_ref[c, 3, :, span]
                sums = [total + weight * offset for total, offset in zip(sums, offsets)]
            for axis in range(3):
                sum_ref[axis, rows, :] = sums[axis]

    own_charge = atoms_ref[me, 3:4, :]
    for axis in range(3):
        short_ref[axis, 0, :, :] = row_sums(sum_ref[axis]) * (own_charge * spacing)
    for copy in copies:
        copy.wait()
    total = partial_ref[me]
    for order in range(len(peers)):
        total = total + land_ref[order]
    for axis in range(3):
        long_ref[axis, 0, :, :] = total[axis : axis + 1, :] * (own_charge * (-1.0 / spacing))


def finished(pair_lists, partial, gathered, count_x, count_y, cells_x, cells_y):
    devices, _, atom_total = gathered.shape
    clusters, listed = pair_lists.shape[2:]
    vmem = pl.BlockSpec(memory_space=pltpu.VMEM)
    flags = pltpu.SemaphoreType.DMA((devices - 1,))
    return pl.pallas_call(
        functools.partial(finish_kernel, (count_x, count_y), (cells_x, cells_y)),
        in_specs=[pl.BlockSpec(memory_space=pltpu.SMEM), vmem, vmem],
        out_specs=[vmem, vmem],
        out_shape=[jax.ShapeDtypeStruct((3, 1, 1, atom_total), jnp.float32)] * 2,
        scratch_shapes=[
            pltpu.VMEM((devices - 1, *partial.shape[1:]), jnp.float32),
            pltpu.VMEM((3, atom_total, 128), jnp.float32),
            pltpu.VMEM((clusters, 4, 8, listed * atom_total // clusters), jnp.float32),
            pltpu.VMEM((3, atom_total, 128), jnp.float32),
            flags,
            flags,
        ],
        compiler_params=pltpu.CompilerParams(collective_id=1, has_side_effects=True),
        name="finish",
    )(pair_lists, partial, gathered)


def green_table(period):
    index = np.arange(period)
    signed = np.where(index <= period // 2, index, index - period) / (period * spacing)
    modulus = ((2.0 + np.cos(index * (2.0 * np.pi / period))) / 3.0) ** 2
    square = signed * signed
    return np.stack([square, np.exp(-((np.pi / ewald_split) ** 2) * square) / modulus]).astype(
        np.float32
    )


def green_factors(index, period):
    signed = jnp.where(index <= period // 2, index, index - period).astype(jnp.float32) / (
        period * spacing
    )
    modulus = ((2.0 + jnp.cos(index.astype(jnp.float32) * (2.0 * jnp.pi / period))) / 3.0) ** 2
    square = signed * signed
    return jnp.stack([square, jnp.exp(-((jnp.pi / ewald_split) ** 2) * square) / modulus])


def one_cluster(own_rows, partner):
    offsets = (own_rows[:3, :, None] - partner[:3, None, :]) * spacing
    dist_square = jnp.sum(offsets * offsets, axis=0)
    soft_square = dist_square + soft_core
    soft_dist = jnp.sqrt(soft_square)
    scaled = ewald_split * soft_dist
    strength = (
        jax.scipy.special.erfc(scaled) / soft_dist
        + ewald_split * root_factor * jnp.exp(-scaled * scaled)
    ) / soft_square
    cutoff_taper = jnp.where(
        dist_square < cutoff * cutoff, (1.0 - dist_square / (cutoff * cutoff)) ** 2, 0.0
    )
    weight = partner[3][None, :] * strength * cutoff_taper
    return own_rows[3] * jnp.sum(weight[None] * offsets, axis=2)


def far_by_planes(gathered, count_x, count_y, cells_x, cells_y):
    devices = count_x * count_y
    place = lax.axis_index("gx") * count_y + lax.axis_index("gy")
    depth = GRID_Z // devices
    atom_total = gathered.shape[2]
    pad_x = round_up(cells_x + 3, 8)
    pad_y = round_up(cells_y + 3, 8)
    window = 2 * cells_y
    turn_x = halves(jnp.asarray(hartley(GRID_X)))
    turn_y = halves(jnp.asarray(hartley(GRID_Y)))
    volume = GRID_X * GRID_Y * GRID_Z * spacing**3
    column = jnp.asarray(green_table(GRID_X).T)
    row = jnp.asarray(green_table(GRID_Y))
    every_k = np.arange(GRID_Z)
    taps = np.outer(every_k, np.arange(4)) * (2.0 * np.pi / GRID_Z)
    square, scale = green_table(GRID_Z)
    table = np.concatenate(
        [
            every_k[:, None],
            np.cos(taps) + np.sin(taps),
            np.cos(taps) - np.sin(taps),
            square[:, None],
            scale[:, None] / (np.pi * volume),
        ],
        axis=1,
    ).astype(np.float32)
    table = lax.dynamic_slice_in_dim(jnp.asarray(table), place * depth, depth, axis=0)
    vmem = pl.BlockSpec(memory_space=pltpu.VMEM)
    rows = GRID_X + pad_x - cells_x
    bank = [
        pltpu.VMEM((pad_x, atom_total), jnp.float32),
        pltpu.VMEM((pad_x, atom_total), jnp.float32),
        pltpu.VMEM((2 * window, atom_total), jnp.bfloat16),
        pltpu.VMEM((depth * pad_x, atom_total), jnp.bfloat16),
        pltpu.VMEM((depth * pad_x, atom_total), jnp.bfloat16),
        pltpu.VMEM((depth * pad_x, 2 * atom_total), jnp.float32),
        pltpu.VMEM((depth * pad_x, 2 * window), jnp.bfloat16),
        pltpu.VMEM((2 * window, 2 * atom_total), jnp.bfloat16),
    ]
    partial = pl.pallas_call(
        functools.partial(mesh_kernel, (count_x, count_y), (cells_x, cells_y), (pad_x, pad_y)),
        in_specs=[vmem] * 8,
        out_specs=vmem,
        out_shape=jax.ShapeDtypeStruct((devices, 4, atom_total), jnp.float32),
        scratch_shapes=[pltpu.VMEM((depth, rows, GRID_Y), jnp.float32)] * 2 + 2 * bank,
        name="mesh",
    )(gathered, *turn_x, *turn_y, column, row, table)
    return partial


def convolved_by_lines(charge_mesh, count_x, count_y):
    turn_x = jnp.asarray(hartley(GRID_X))
    turn_y = jnp.asarray(hartley(GRID_Y))
    product = functools.partial(
        jnp.einsum, precision=lax.Precision.HIGHEST, preferred_element_type=jnp.float32
    )
    exchange = functools.partial(lax.all_to_all, tiled=True)
    lines = exchange(charge_mesh, "gx", split_axis=2, concat_axis=0)
    lines = product("xyk,xu->uyk", lines, turn_x)
    lines = exchange(lines, "gy", split_axis=0, concat_axis=1)
    lines = product("uyk,yv->uvk", lines, turn_y)
    wide, _, depth = lines.shape
    start_x = lax.axis_index("gy") * wide
    start_z = lax.axis_index("gx") * depth
    volume = GRID_X * GRID_Y * GRID_Z * spacing**3
    fx = green_factors(start_x + jnp.arange(wide, dtype=jnp.int32), GRID_X)
    fy = green_factors(jnp.arange(GRID_Y, dtype=jnp.int32), GRID_Y)
    fz = green_factors(start_z + jnp.arange(depth, dtype=jnp.int32), GRID_Z)
    square = fx[0][:, None, None] + fy[0][:, None] + fz[0]
    scale = fx[1][:, None, None] * fy[1][:, None] * fz[1] / (math.pi * volume)
    lines = lines * jnp.where(square > 0.0, scale / jnp.where(square > 0.0, square, 1.0), 0.0)
    lines = product("uvk,vy->uyk", lines, turn_y)
    lines = exchange(lines, "gy", split_axis=1, concat_axis=0)
    lines = product("uyk,ux->xyk", lines, turn_x)
    return exchange(lines, "gx", split_axis=0, concat_axis=2)


def far_by_lines(atoms, base, count_x, count_y, cells_x, cells_y, cells_z):
    atom_total = atoms.shape[1]
    cells = (cells_x, cells_y, cells_z)
    pad = (round_up(cells_x + 3, rows_group), round_up(cells_y + 3, 8))
    pad_x, pad_y = pad
    turn_z = jnp.asarray(hartley(GRID_Z))
    spread = pl.pallas_call(
        functools.partial(spread_kernel, cells, pad),
        out_shape=jax.ShapeDtypeStruct((pad_x, pad_y, GRID_Z), jnp.float32),
        scratch_shapes=[
            pltpu.VMEM((pad_x, atom_total), jnp.float32),
            pltpu.VMEM((pad_y, atom_total), jnp.float32),
            pltpu.VMEM((atom_total, 2 * GRID_Z), jnp.bfloat16),
            pltpu.VMEM((rows_group * pad_y, atom_total), jnp.bfloat16),
            pltpu.VMEM((rows_group * pad_y, atom_total), jnp.bfloat16),
        ],
        name="spread",
    )(atoms, base, turn_z)

    from_x = moved(spread[cells_x : cells_x + 3, :cells_y], 1, 0)
    from_y = moved(spread[:cells_x, cells_y : cells_y + 3], 0, 1)
    from_both = moved(spread[cells_x : cells_x + 3, cells_y : cells_y + 3], 1, 1)
    charge_mesh = (
        spread[:cells_x, :cells_y]
        .at[:3]
        .add(from_x)
        .at[:, :3]
        .add(from_y)
        .at[:3, :3]
        .add(from_both)
    )
    potential = convolved_by_lines(charge_mesh, count_x, count_y)
    upper_x = moved(potential[:3], -1, 0)
    upper_y = moved(potential[:, :3], 0, -1)
    upper_both = moved(potential[:3, :3], -1, -1)
    wider = jnp.concatenate(
        [
            jnp.concatenate([potential, upper_x], axis=0),
            jnp.concatenate([upper_y, upper_both], axis=0),
        ],
        axis=1,
    )
    wider = jnp.pad(wider, ((0, pad_x - cells_x - 3), (0, pad_y - cells_y - 3), (0, 0)))
    return pl.pallas_call(
        functools.partial(gather_kernel, cells, pad),
        out_shape=jax.ShapeDtypeStruct((3, atom_total), jnp.float32),
        scratch_shapes=[
            pltpu.VMEM((pad_x, atom_total), jnp.float32),
            pltpu.VMEM((pad_x, atom_total), jnp.float32),
            pltpu.VMEM((pad_y, atom_total), jnp.float32),
            pltpu.VMEM((pad_y, atom_total), jnp.float32),
            pltpu.VMEM((2 * GRID_Z, 2 * atom_total), jnp.bfloat16),
            pltpu.VMEM((rows_group * pad_y, 2 * atom_total), jnp.float32),
        ],
        name="gather",
    )(atoms, base, turn_z, wider)


def local(positions, charges, pair_lists, slab_dest, atom_counts):
    count_x = lax.axis_size("gx")
    count_y = lax.axis_size("gy")
    devices = count_x * count_y
    atom_total = positions.shape[3]
    clusters = pair_lists.shape[2]
    cluster_size = atom_total // clusters
    blocks = slab_dest.shape[2]
    block_size = atom_total // blocks
    cells_x = GRID_X // count_x
    cells_y = GRID_Y // count_y
    cells_z = GRID_Z // count_y
    living = jnp.arange(atom_total, dtype=jnp.int32) < atom_counts[0, 0]
    charge = jnp.where(living, charges[0, 0], 0.0)
    packed = jnp.concatenate([positions, charge[None, None, None, :]], axis=0)
    atoms = packed.reshape(4, atom_total)

    base = jnp.broadcast_to(
        (slab_dest[0, 0] * cells_z)[:, None], (blocks, block_size)
    ).reshape(1, atom_total)
    by_planes = GRID_Z % devices == 0 and cells_y == 64 and cells_x % 8 == 0
    if by_planes:
        gathered = shared(atoms, count_x, count_y)
        partial = far_by_planes(gathered, count_x, count_y, cells_x, cells_y)
        return tuple(
            finished(pair_lists, partial, gathered, count_x, count_y, cells_x, cells_y)
        )
    gathered = lax.all_gather(atoms, ("gx", "gy"), axis=0, tiled=False)
    far_part = far_by_lines(atoms, base, count_x, count_y, cells_x, cells_y, cells_z)

    chosen = pair_lists[0, 0]
    beside = chosen // clusters
    step_x, step_y = (beside // 3 - 1, beside % 3 - 1)
    at_x = (lax.axis_index("gx") + step_x + count_x) % count_x
    at_y = (lax.axis_index("gy") + step_y + count_y) % count_y
    number = (at_x * count_y + at_y) * clusters + chosen % clusters
    pick = (number[:, :, None] == jnp.arange(devices * clusters, dtype=jnp.int32)).astype(
        jnp.float32
    )
    pool = gathered[:, :4].reshape(devices, 4, clusters, cluster_size)
    pool = jnp.transpose(pool, (1, 0, 2, 3)).reshape(4, devices * clusters, cluster_size)
    partners = jnp.einsum(
        "cln,fnk->cflk",
        pick,
        pool,
        precision=lax.Precision.HIGHEST,
        preferred_element_type=jnp.float32,
    )
    shift_x = (step_x * cells_x).astype(jnp.float32)
    shift_y = (step_y * cells_y).astype(jnp.float32)
    flat = jnp.zeros_like(shift_x)
    shift = jnp.stack([shift_x, shift_y, flat, flat], axis=1)
    partners = (partners + shift[:, :, :, None]).reshape(clusters, 4, -1)
    own = packed.reshape(4, clusters, cluster_size)
    pair_part = jnp.stack(
        [one_cluster(own[:, c], partners[c]) for c in range(clusters)], axis=1
    )
    short_forces = pair_part.reshape(3, 1, 1, atom_total)
    return (short_forces, far_part.reshape(3, 1, 1, atom_total))


def solution(mesh):
    return jax.shard_map(
        local,
        mesh=mesh,
        in_specs=(
            P(None, ("rep", "gx"), "gy", None),
            P(("rep", "gx"), "gy", None),
            P(("rep", "gx"), "gy", None, None),
            P(("rep", "gx"), "gy", None),
            P(("rep", "gx"), "gy"),
        ),
        out_specs=(P(None, ("rep", "gx"), "gy", None), P(None, ("rep", "gx"), "gy", None)),
        check_vma=False,
    )
```

```python
import functools
import math

import jax
import jax.numpy as jnp
import numpy as np
from jax import lax
from jax.experimental import pallas as pl
from jax.experimental.pallas import tpu as pltpu
from jax.sharding import PartitionSpec as P

GRID_X = 256
GRID_Y = 256
GRID_Z = 128


spacing = 0.16
ewald_split = 3.47
cutoff = 0.9
soft_core = 0.09
root_factor = 1.1283791670955126
rows_group = 8
lanes = 128
window_rows = 24
group_size = 4
plane_group = 2


def moved(value, step_x, step_y):
    count_x = lax.axis_size("gx")
    count_y = lax.axis_size("gy")
    pairs = [
        (i * count_y + j, (i + step_x) % count_x * count_y + (j + step_y) % count_y)
        for i in range(count_x)
        for j in range(count_y)
    ]
    return lax.ppermute(value, ("gx", "gy"), pairs)


def round_up(value, multiple):
    return -(-value // multiple) * multiple


def hartley(period):
    turns = np.outer(np.arange(period), np.arange(period)) % period
    phases = turns * (2.0 * np.pi / period)
    return (np.cos(phases) + np.sin(phases)).astype(np.float32)


def halves(value):
    high = value.astype(jnp.bfloat16)
    low = (value - high.astype(jnp.float32)).astype(jnp.bfloat16)
    return (high, low)


def dot(left_side, right_side):
    return jnp.dot(left_side, right_side, preferred_element_type=jnp.float32)


def spline_weights(fraction):
    remain = 1.0 - fraction
    square = fraction * fraction
    cube_part = square * fraction
    values = [
        remain * remain * remain / 6.0,
        (3.0 * cube_part - 6.0 * square + 4.0) / 6.0,
        (-3.0 * cube_part + 3.0 * square + 3.0 * fraction + 1.0) / 6.0,
        cube_part / 6.0,
    ]
    slopes = [
        -0.5 * remain * remain,
        0.5 * (3.0 * square - 4.0 * fraction),
        0.5 * (-3.0 * square + 2.0 * fraction + 1.0),
        0.5 * square,
    ]
    return (values, slopes)


def split_cells(coordinate, offset, cell_count):
    inside = coordinate - offset
    lowest = jnp.clip(jnp.floor(inside).astype(jnp.int32), 0, cell_count - 1)
    return (lowest, inside - lowest.astype(inside.dtype))


def spline_table(lowest, values, table_size, period=None):
    points = lax.broadcasted_iota(jnp.int32, (table_size, lowest.shape[1]), 0)
    lookup = jnp.zeros(points.shape, jnp.float32)
    for spline_term in range(4):
        at = lowest + spline_term
        if period is not None:
            at = jnp.where(at >= period, at - period, at)
        lookup = jnp.where(points == at, values[spline_term], lookup)
    return lookup


def spread_kernel(cells, pad, atoms_ref, base_ref, turn_ref, out_ref, wx_ref, wy_ref, wz_ref, hi_ref, lo_ref):
    cells_x, cells_y, cells_z = cells
    pad_x, pad_y = pad
    atom_total = atoms_ref.shape[1]
    low_x, frac_x = split_cells(atoms_ref[0:1, :], 0.0, cells_x)
    low_y, frac_y = split_cells(atoms_ref[1:2, :], 0.0, cells_y)
    base = base_ref[...]
    low_z, frac_z = split_cells(atoms_ref[2:3, :], base.astype(jnp.float32), cells_z)
    wx_ref[...] = spline_table(low_x, spline_weights(frac_x)[0], pad_x) * atoms_ref[3:4, :]
    wy_ref[...] = spline_table(low_y, spline_weights(frac_y)[0], pad_y)
    turn = turn_ref[...]
    size_z = turn.shape[0]
    table_z = spline_table(base + low_z, spline_weights(frac_z)[0], size_z, size_z)
    waves = jnp.dot(
        turn, table_z, precision=lax.Precision.HIGHEST, preferred_element_type=jnp.float32
    ).T
    high, low = halves(waves)
    wz_ref[:, :size_z] = high
    wz_ref[:, size_z:] = low

    @pl.loop(0, pad_x // rows_group)
    def _(chunk):
        for inner in range(rows_group):
            row = wx_ref[pl.ds(chunk * rows_group + inner, 1), :]
            high, low = halves(row * wy_ref[...])
            hi_ref[pl.ds(inner * pad_y, pad_y), :] = high
            lo_ref[pl.ds(inner * pad_y, pad_y), :] = low
        both = dot(hi_ref[...], wz_ref[...])
        rest = dot(lo_ref[...], wz_ref[:, :size_z])
        total = both[:, :size_z] + both[:, size_z:] + rest
        out_ref[pl.ds(chunk * rows_group, rows_group)] = total.reshape(rows_group, pad_y, size_z)


def gather_kernel(cells, pad, atoms_ref, base_ref, turn_ref, mesh_ref, out_ref, wx_ref, vx_ref, wy_ref, vy_ref, wz_ref, level_ref):
    cells_x, cells_y, cells_z = cells
    pad_x, pad_y = pad
    atom_total = atoms_ref.shape[1]
    low_x, frac_x = split_cells(atoms_ref[0:1, :], 0.0, cells_x)
    low_y, frac_y = split_cells(atoms_ref[1:2, :], 0.0, cells_y)
    base = base_ref[...]
    low_z, frac_z = split_cells(atoms_ref[2:3, :], base.astype(jnp.float32), cells_z)
    values, slopes = spline_weights(frac_x)
    wx_ref[...] = spline_table(low_x, values, pad_x)
    vx_ref[...] = spline_table(low_x, slopes, pad_x)
    values, slopes = spline_weights(frac_y)
    wy_ref[...] = spline_table(low_y, values, pad_y)
    vy_ref[...] = spline_table(low_y, slopes, pad_y)
    values, slopes = spline_weights(frac_z)
    turn = turn_ref[...]
    size_z = turn.shape[0]
    for place, terms in enumerate((values, slopes)):
        table_z = spline_table(base + low_z, terms, size_z, size_z)
        waves = jnp.dot(
            turn, table_z, precision=lax.Precision.HIGHEST, preferred_element_type=jnp.float32
        )
        high, low = halves(waves)
        wz_ref[:size_z, pl.ds(place * atom_total, atom_total)] = high
        wz_ref[size_z:, pl.ds(place * atom_total, atom_total)] = low
    groups = pad_y // 8

    def one_chunk(chunk, sums):
        rows = mesh_ref[pl.ds(chunk * rows_group, rows_group)].reshape(rows_group * pad_y, size_z)
        high, low = halves(rows)
        level_ref[...] = dot(jnp.concatenate([high, high], axis=1), wz_ref[...]) + dot(
            low, wz_ref[:size_z, :]
        )
        first, second, third = sums
        for inner in range(rows_group):
            flat = level_ref[pl.ds(inner * pad_y, pad_y), :atom_total]
            tilt = level_ref[pl.ds(inner * pad_y, pad_y), atom_total:]
            across = wy_ref[...]
            part_x = jnp.sum((across * flat).reshape(groups, 8, atom_total), axis=0)
            part_y = jnp.sum((vy_ref[...] * flat).reshape(groups, 8, atom_total), axis=0)
            part_z = jnp.sum((across * tilt).reshape(groups, 8, atom_total), axis=0)
            weight = wx_ref[pl.ds(chunk * rows_group + inner, 1), :]
            slope = vx_ref[pl.ds(chunk * rows_group + inner, 1), :]
            first = first + slope * part_x
            second = second + weight * part_y
            third = third + weight * part_z
        return (first, second, third)

    zero = jnp.zeros((8, atom_total), jnp.float32)
    sums = lax.fori_loop(0, pad_x // rows_group, one_chunk, (zero, zero, zero))
    factor = -atoms_ref[3:4, :] / spacing
    for place in range(3):
        out_ref[pl.ds(place, 1), :] = factor * jnp.sum(sums[place], axis=0, keepdims=True)


def peers_of(count_x, count_y):
    place_x, place_y = (lax.axis_index("gx"), lax.axis_index("gy"))
    peers = []
    for order in range(1, count_x * count_y):
        peer_x = lax.rem(place_x + order // count_y, count_x)
        peer_y = lax.rem(place_y + order % count_y, count_y)
        peers.append((peer_x, peer_y))
    return peers


def share_kernel(sizes, cells, count_ref, position_ref, charge_ref, raw_ref, sorted_ref, bounds_ref, rank_ref, key_ref, split_ref, raw_send, raw_recv, sort_send, sort_recv, mark_send, mark_recv):
    count_x, count_y = sizes
    cells_x, _ = cells
    place_x, place_y = (lax.axis_index("gx"), lax.axis_index("gy"))
    me = place_x * count_y + place_y
    peers = peers_of(count_x, count_y)
    barrier = pltpu.get_barrier_semaphore()
    for peer_x, peer_y in peers:
        pl.semaphore_signal(
            barrier,
            inc=1,
            device_id={"gx": peer_x, "gy": peer_y},
            device_id_type=pl.DeviceIdType.MESH,
        )

    def sent(source, target, send_sem, recv_sem, order):
        peer_x, peer_y = peers[order]
        return pltpu.make_async_remote_copy(
            src_ref=source.at[me],
            dst_ref=target.at[me],
            send_sem=send_sem.at[order],
            recv_sem=recv_sem.at[order],
            device_id={"gx": peer_x, "gy": peer_y},
            device_id_type=pl.DeviceIdType.MESH,
        )

    atom_total = charge_ref.shape[2]
    tiles = atom_total // lanes
    slot = lax.broadcasted_iota(jnp.int32, (1, atom_total), 1)
    living = slot < count_ref[0, 0]
    charge = jnp.where(living, charge_ref[0], 0.0)
    rows = [position_ref[axis, 0] for axis in range(3)] + [charge]
    for axis in range(4):
        raw_ref[me, pl.ds(axis, 1), :] = rows[axis]
    column = jnp.clip(jnp.floor(rows[0]), 0.0, cells_x - 1.0)
    key = jnp.where(living, column, float(cells_x)) * float(atom_total) + slot.astype(jnp.float32)
    for tile in range(tiles):
        span = slice(tile * lanes, (tile + 1) * lanes)
        key_ref[span, :] = jnp.broadcast_to(key[:, span], (lanes, lanes)).T
    wide = [
        jnp.broadcast_to(key[:, tile * lanes : (tile + 1) * lanes], (8, lanes))
        for tile in range(tiles)
    ]

    def count_group(group, totals):
        for inner in range(8):
            others = key_ref[pl.ds(pl.multiple_of(group * 64 + inner * 8, 8), 8), :]
            totals = tuple(
                total + jnp.where(others < own, 1.0, 0.0) for total, own in zip(totals, wide)
            )
        return totals

    zero = jnp.zeros((8, lanes), jnp.float32)
    totals = lax.fori_loop(0, atom_total // 64, count_group, (zero,) * tiles)
    for tile, total in enumerate(totals):
        rank_ref[:, tile * lanes : (tile + 1) * lanes] = jnp.sum(total, axis=0, keepdims=True)

    pl.semaphore_wait(barrier, len(peers))
    beside = sorted(
        {
            step_x % count_x * count_y + step_y % count_y
            for step_x in (-1, 0, 1)
            for step_y in (-1, 0, 1)
        }
        - {0}
    )
    copies = [sent(raw_ref, raw_ref, raw_send, raw_recv, order - 1) for order in beside]
    for copy in copies:
        copy.start()

    split_ref[...] = jnp.zeros_like(split_ref)
    rest = raw_ref[me]
    for part in range(3):
        piece = rest.astype(jnp.bfloat16).astype(jnp.float32)
        split_ref[4 * part : 4 * part + 4, :] = piece
        rest = rest - piece
    split = split_ref[...].astype(jnp.bfloat16)
    rank = rank_ref[...]
    block = 2 * lanes
    for part in range(atom_total // block):
        place = lax.broadcasted_iota(jnp.int32, (block, atom_total), 0) + part * block
        chosen = jnp.where(place.astype(jnp.float32) == rank, 1.0, 0.0).astype(jnp.bfloat16)
        found = lax.dot_general(
            split, chosen, (((1,), (1,)), ((), ())), preferred_element_type=jnp.float32
        )
        found = (found[0:4] + found[4:8]) + found[8:12]
        for tile in range(block // lanes):
            row = part * (block // lanes) + tile
            for axis in range(4):
                sorted_ref[me, axis, row : row + 1, :] = found[
                    axis : axis + 1, tile * lanes : (tile + 1) * lanes
                ]
    spot = lax.broadcasted_iota(jnp.int32, (tiles, lanes), 0) * lanes
    spot = spot + lax.broadcasted_iota(jnp.int32, (tiles, lanes), 1)
    inside = spot < count_ref[0, 0]
    column = jnp.clip(jnp.floor(sorted_ref[me, 0]), 0.0, cells_x - 1.0)
    lowest = jnp.min(jnp.where(inside, column, float(cells_x)), axis=1, keepdims=True)
    highest = jnp.max(jnp.where(inside, column, -1.0), axis=1, keepdims=True)
    first = jnp.floor(lowest * 0.125)
    last = jnp.floor((highest + 3.0) * 0.125)
    windows = jnp.where(
        highest >= 0.0, jnp.floor((last - first) * (8.0 / window_rows) + 0.01) + 1.0, 0.0
    )
    lane = lax.broadcasted_iota(jnp.int32, (tiles, lanes), 1)
    row = lax.broadcasted_iota(jnp.int32, (tiles, lanes), 0)
    marks = jnp.where(lane == row, first, jnp.where(lane == row + tiles, windows, 0.0))
    marks = jnp.sum(marks, axis=0, keepdims=True)
    bounds_ref[me] = marks.astype(jnp.int32)

    everyone = range(len(peers))
    later = [sent(sorted_ref, sorted_ref, sort_send, sort_recv, order) for order in everyone]
    later += [sent(bounds_ref, bounds_ref, mark_send, mark_recv, order) for order in everyone]
    for copy in later:
        copy.start()
    for copy in copies + later:
        copy.wait()


def shared(positions, charges, atom_counts, count_x, count_y, cells_x, cells_y):
    devices = count_x * count_y
    atom_total = charges.shape[2]
    vmem = pl.BlockSpec(memory_space=pltpu.VMEM)
    flags = pltpu.SemaphoreType.DMA((devices - 1,))
    return pl.pallas_call(
        functools.partial(share_kernel, (count_x, count_y), (cells_x, cells_y)),
        in_specs=[pl.BlockSpec(memory_space=pltpu.SMEM), vmem, vmem],
        out_specs=[vmem] * 4,
        out_shape=[
            jax.ShapeDtypeStruct((devices, 4, atom_total), jnp.float32),
            jax.ShapeDtypeStruct((devices, 4, atom_total // lanes, lanes), jnp.float32),
            jax.ShapeDtypeStruct((devices, 1, lanes), jnp.int32),
            jax.ShapeDtypeStruct((1, atom_total), jnp.float32),
        ],
        scratch_shapes=[
            pltpu.VMEM((atom_total, lanes), jnp.float32),
            pltpu.VMEM((16, atom_total), jnp.float32),
        ]
        + [flags] * 6,
        compiler_params=pltpu.CompilerParams(collective_id=0, has_side_effects=True),
        name="share",
    )(atom_counts, positions, charges)


def depth_rows(table, height, terms):
    turns = height * table[:, 0:1]
    quarter = GRID_Z // 4
    nearest = jnp.floor(turns * (1.0 / quarter) + 0.5)
    angle = (turns - nearest * quarter) * (2.0 * math.pi / GRID_Z)
    quadrant = nearest - 4.0 * jnp.floor(nearest * 0.25)
    square = angle * angle
    near_cos = 1.0 + square * (
        -0.5 + square * (1.0 / 24.0 + square * (-1.0 / 720.0 + square * (1.0 / 40320.0)))
    )
    near_sin = angle * (
        1.0
        + square
        * (-1.0 / 6.0 + square * (1.0 / 120.0 + square * (-1.0 / 5040.0 + square / 362880.0)))
    )
    odd_turn = (quadrant == 1.0) | (quadrant == 3.0)
    cosine = jnp.where(odd_turn, near_sin, near_cos)
    cosine = jnp.where((quadrant == 1.0) | (quadrant == 2.0), -cosine, cosine)
    sine = jnp.where(odd_turn, near_cos, near_sin)
    sine = jnp.where(quadrant >= 2.0, -sine, sine)
    results = []
    for weights in terms:
        even = sum(table[:, 1 + t : 2 + t] * weights[t] for t in range(4))
        odd = sum(table[:, 5 + t : 6 + t] * weights[t] for t in range(4))
        results.append(cosine * even + sine * odd)
    return results


def mesh_kernel(sizes, cells, pad_y, bounds_ref, atoms_ref, xh_ref, xl_ref, yh_ref, yl_ref, column_ref, row_ref, table_ref, out_ref, mesh_ref, stack_ref, prep_ref, deep_ref, steep_ref, near_ref, wy_ref, side_ref, level_ref, square_ref, scale_ref):
    count_x, count_y = sizes
    cells_x, cells_y = cells
    devices = count_x * count_y
    place = lax.axis_index("gx") * count_y + lax.axis_index("gy")
    tiles = atoms_ref.shape[2]
    depth = stack_ref.shape[0]
    window = 2 * cells_y
    windows = GRID_Y // window
    chunks = tiles
    extra = 8
    mesh_ref[...] = jnp.zeros_like(mesh_ref)
    stack_ref[:, GRID_X:, :] = jnp.zeros_like(stack_ref[:, GRID_X:, :])
    out_ref[...] = jnp.zeros_like(out_ref)
    wy_ref[...] = jnp.zeros_like(wy_ref)
    table = table_ref[pl.ds(pl.multiple_of(place * depth, 8), depth), :]

    def prep_row(kind, cell, tile):
        return prep_ref[pl.ds((kind * devices + cell) * tiles + tile, 8, stride=0), :]

    @pl.loop(0, devices)
    def _(cell):
        def keep(kind, value):
            rows = pl.ds(pl.multiple_of((kind * devices + cell) * tiles, 8), tiles)
            prep_ref[rows, :] = value

        for axis, count in enumerate((cells_x, cells_y)):
            value = atoms_ref[cell, axis]
            lowest = jnp.clip(jnp.floor(value), 0.0, count - 1.0)
            values, slopes = spline_weights(value - lowest)
            keep(9 * axis, lowest)
            for term in range(4):
                keep(9 * axis + 1 + term, values[term])
                keep(9 * axis + 5 + term, slopes[term])
        value = atoms_ref[cell, 2]
        height = jnp.floor(value)
        values, slopes = spline_weights(value - height)
        keep(18, height)
        for term in range(4):
            keep(19 + term, values[term])
            keep(23 + term, slopes[term])
        keep(27, atoms_ref[cell, 3])
        for tile in range(tiles):
            height = prep_row(18, cell, tile)
            terms = [[prep_row(19 + 4 * s + term, cell, tile) for term in range(4)] for s in range(2)]
            deep, steep = depth_rows(table, height, terms)
            rows = pl.ds(pl.multiple_of((cell * tiles + tile) * depth, 8), depth)
            deep_ref[rows, :] = deep
            steep_ref[rows, :] = steep

    row_index = lax.broadcasted_iota(jnp.int32, (8, lanes), 0).astype(jnp.float32)

    def looked_up(points, lowest, term_lists):
        results = [jnp.zeros_like(points) for _ in term_lists]
        for term in range(4):
            hit = points == lowest + float(term)
            results = [
                jnp.where(hit, terms[term], result)
                for terms, result in zip(term_lists, results)
            ]
        return results

    def kinds(first, cell, tile):
        return [prep_row(first + term, cell, tile) for term in range(4)]

    stride = round_up(pad_y, 16)
    far_away = 1.0e6

    def window_of(cell, chunk, step):
        first = bounds_ref[cell, 0, chunk]
        count = bounds_ref[cell, 0, chunks + chunk]
        begin = first * 8 + jnp.minimum(step, jnp.maximum(count - 1, 0)) * window_rows
        base = jnp.where(step < count, begin.astype(jnp.float32), far_away)
        return (begin, base)

    def window_count(cell, chunk):
        counts = [bounds_ref[cell, 0, chunks + chunk + place] for place in range(group_size)]
        return functools.reduce(jnp.maximum, counts)

    def y_table(cell, chunk, kind):
        lowest = prep_row(9, cell, chunk)
        terms = kinds(kind, cell, chunk)
        for group in range(stride // 16):
            pieces = [
                looked_up(row_index + float(group * 16 + half * 8), lowest, [terms])[0]
                if group * 16 + half * 8 < pad_y
                else jnp.zeros_like(row_index)
                for half in range(2)
            ]
            yield (slice(group * 16, group * 16 + 16), *halves(jnp.concatenate(pieces, axis=0)))

    steps_x = window_rows // 8

    def spread_group(cell, group, i, m, odd):
        @pl.loop(0, window_count(cell, group * group_size))
        def _(step):
            for place in range(group_size):
                chunk = group * group_size + place
                spot = cell * chunks + chunk
                for rows, high, low in y_table(cell, chunk, 10):
                    after = slice(window + rows.start, window + rows.stop)
                    later = slice(stride + rows.start, stride + rows.stop)
                    wy_ref[place, rows, :lanes] = high
                    wy_ref[place, rows, lanes:] = high
                    wy_ref[place, after, :lanes] = low
                    near_ref[spot, rows, :] = high
                    near_ref[spot, later, :] = low
                begin, base = window_of(cell, chunk, step)
                lowest = prep_row(0, cell, chunk) - base
                charge = prep_row(27, cell, chunk)
                terms = [term * charge for term in kinds(1, cell, chunk)]
                weights = [
                    looked_up(row_index + float(tile * 8), lowest, [terms])[0]
                    for tile in range(steps_x)
                ]
                modes = [
                    deep_ref[pl.ds((cell * tiles + chunk) * depth + k, 8, stride=0), :]
                    for k in range(depth)
                ]
                blocks = [weight * mode for mode in modes for weight in weights]
                for pair in range(len(blocks) // 2):
                    high, low = halves(
                        jnp.concatenate(blocks[2 * pair : 2 * pair + 2], axis=0)
                    )
                    rows = slice(pair * 16, pair * 16 + 16)
                    side_ref[place, rows, :lanes] = high
                    side_ref[place, rows, lanes:] = low
            totals = []
            for place in range(group_size):
                total = lax.dot_general(
                    side_ref[place],
                    wy_ref[place],
                    (((1,), (1,)), ((), ())),
                    preferred_element_type=jnp.float32,
                )
                totals.append(total[:, :window] + total[:, window:])
            for place, total in enumerate(totals):
                begin, _ = window_of(cell, group * group_size + place, step)
                rows = pl.ds(pl.multiple_of(i * cells_x + begin, 8), window_rows)
                here = pl.ds(pl.multiple_of(m * window, lanes), window)
                mesh_ref[odd, :, rows, here] += total.reshape(depth, window_rows, window)

    @pl.loop(0, devices)
    def _(cell):
        i = lax.div(cell, count_y)
        j = lax.rem(cell, count_y)

        @pl.loop(0, chunks // group_size)
        def _(group):
            spread_group(cell, group, i, lax.div(j, 2), lax.rem(j, 2))

    def across(value):
        high, low = halves(value)
        return dot(xh_ref[...], high) + dot(xl_ref[...], high) + dot(xh_ref[...], low)

    def along(value):
        high, low = halves(value)
        return dot(high, yh_ref[...]) + dot(high, yl_ref[...]) + dot(low, yh_ref[...])

    plane_lane = lax.broadcasted_iota(jnp.int32, (GRID_X, window), 1)

    shape = (GRID_X, GRID_Y)
    square_ref[...] = jnp.broadcast_to(column_ref[:, 0:1], shape) + row_ref[0:1, :]
    scale_ref[...] = jnp.broadcast_to(column_ref[:, 1:2], shape) * row_ref[1:2, :]

    def one_plane(k):
        charge = mesh_ref[0, k, :GRID_X, :] + pltpu.roll(mesh_ref[1, k, :GRID_X, :], cells_y, 1)
        over = slice(GRID_X, GRID_X + extra)
        beyond = mesh_ref[0, k, over, :] + pltpu.roll(mesh_ref[1, k, over, :], cells_y, 1)
        charge = jnp.concatenate([charge[:extra] + beyond, charge[extra:]], axis=0)
        waves = along(across(charge))
        mode = pl.ds(place * depth + k, 1)
        square = square_ref[...] + table_ref[mode, 9:10]
        scale = scale_ref[...] * table_ref[mode, 10:11]
        green = jnp.where(square > 0.0, scale / square, 0.0)
        plane = across(along(waves * green))
        for odd in range(2):
            if odd:
                plane = pltpu.roll(plane, GRID_Y - cells_y, 1)
            for j_half in range(windows):
                j = 2 * j_half + odd
                block = plane[:, j_half * window : (j_half + 1) * window]
                high = block.astype(jnp.bfloat16).astype(jnp.float32)
                low = block - high
                shifted = pltpu.roll(high, stride, 1)
                left = jnp.where(plane_lane < stride, high, shifted)
                right = jnp.where(
                    plane_lane < 2 * stride - window,
                    shifted,
                    pltpu.roll(low, 2 * stride - window, 1),
                )
                for side, value in enumerate((left, right)):
                    span = slice((2 * j + side) * window, (2 * j + side + 1) * window)
                    stack_ref[k, :GRID_X, span] = value
                    stack_ref[k, GRID_X : GRID_X + extra, span] = value[:extra]

    @pl.loop(0, depth // plane_group)
    def _(pair):
        for inner in range(plane_group):
            one_plane(pair * plane_group + inner)

    def gather_group(cell, group, i, j):
        @pl.loop(0, window_count(cell, group * group_size))
        def _(step):
            blank = jnp.zeros((2 * window - 3 * stride, lanes), jnp.bfloat16)
            for place in range(group_size):
                chunk = group * group_size + place
                near = near_ref[cell * chunks + chunk]
                highs, lows = [], []
                for _, high, low in y_table(cell, chunk, 14):
                    highs.append(high)
                    lows.append(low)
                columns = jnp.concatenate(
                    [
                        jnp.concatenate([near, near[:stride], blank], axis=0),
                        jnp.concatenate([*highs, *lows, *highs, blank], axis=0),
                    ],
                    axis=1,
                )
                begin, _ = window_of(cell, chunk, step)
                rows = pl.ds(pl.multiple_of(i * cells_x + begin, 8), window_rows)
                span = pl.ds(pl.multiple_of(j * 2 * window, lanes), 2 * window)
                block = stack_ref[:, rows, span].reshape(depth * window_rows, 2 * window)
                level_ref[place] = dot(block.astype(jnp.bfloat16), columns)
            for place in range(group_size):
                chunk = group * group_size + place
                _, base = window_of(cell, chunk, step)
                lowest = prep_row(0, cell, chunk) - base
                values = kinds(1, cell, chunk)
                slopes = kinds(5, cell, chunk)
                spots = [
                    pl.ds((cell * tiles + chunk) * depth + k, 8, stride=0) for k in range(depth)
                ]
                deep = [deep_ref[spot, :] for spot in spots]
                steep = [steep_ref[spot, :] for spot in spots]
                zero = jnp.zeros((8, lanes), jnp.float32)
                sums = [zero, zero, zero]
                for tile in range(steps_x):
                    weight, slope = looked_up(
                        row_index + float(tile * 8), lowest, [values, slopes]
                    )
                    parts = [zero, zero, zero]
                    for k in range(depth):
                        at = slice(k * window_rows + tile * 8, k * window_rows + tile * 8 + 8)
                        flat = level_ref[place, at, :lanes]
                        tilt = level_ref[place, at, lanes:]
                        parts = [
                            parts[0] + deep[k] * flat,
                            parts[1] + deep[k] * tilt,
                            parts[2] + steep[k] * flat,
                        ]
                    sums = [
                        sums[0] + slope * parts[0],
                        sums[1] + weight * parts[1],
                        sums[2] + weight * parts[2],
                    ]
                for axis in range(3):
                    out_ref[cell, axis, pl.ds(chunk, 1), :] += jnp.sum(
                        sums[axis], axis=0, keepdims=True
                    )

    @pl.loop(0, devices)
    def _(cell):
        i = lax.div(cell, count_y)
        j = lax.rem(cell, count_y)

        @pl.loop(0, chunks // group_size)
        def _(group):
            gather_group(cell, group, i, j)


root_terms = (
    3.9164407301418542,
    -0.0037127819564810594,
    0.16802528315459195,
    -0.003061234121505335,
    -0.0076524954798020545,
    0.002268454833542123,
    -0.0003056487922112269,
    1.686888935413571e-05,
)


def pair_weight(square):
    soft_square = square * (spacing * spacing) + soft_core
    inverse = lax.rsqrt(soft_square)
    series = jnp.full_like(inverse, root_terms[-1])
    for term in root_terms[-2::-1]:
        series = series * inverse + term
    decay = jnp.exp(soft_square * (-ewald_split * ewald_split))
    taper = jnp.maximum(1.0 - square * (spacing * spacing / (cutoff * cutoff)), 0.0)
    return (decay * series) * (inverse * taper) ** 2


def row_sums(values):
    total = None
    ones = jnp.ones((16, values.shape[1]), jnp.bfloat16)
    for _ in range(3):
        part = values.astype(jnp.bfloat16)
        values = values - part.astype(jnp.float32)
        summed = lax.dot_general(
            ones, part, (((1,), (1,)), ((), ())), preferred_element_type=jnp.float32
        )
        total = summed if total is None else total + summed
    return total[0:1, :]


def finish_kernel(sizes, cells, pairs_ref, partial_ref, atoms_ref, rank_ref, short_ref, long_ref, land_ref, column_ref, partner_ref, sum_ref, order_ref, force_ref, send_sem, recv_sem):
    count_x, count_y = sizes
    cells_x, cells_y = cells
    place_x, place_y = (lax.axis_index("gx"), lax.axis_index("gy"))
    me = place_x * count_y + place_y
    peers = peers_of(count_x, count_y)
    barrier = pltpu.get_barrier_semaphore()
    for peer_x, peer_y in peers:
        pl.semaphore_signal(
            barrier,
            inc=1,
            device_id={"gx": peer_x, "gy": peer_y},
            device_id_type=pl.DeviceIdType.MESH,
        )
    clusters, listed = pairs_ref.shape[2:]
    atom_total = atoms_ref.shape[2]
    size = atom_total // clusters
    for axis in range(3):
        for chunk in range(atom_total // lanes):
            row = atoms_ref[me, pl.ds(axis, 1), pl.ds(chunk * lanes, lanes)]
            column_ref[axis, pl.ds(chunk * lanes, lanes), :] = jnp.broadcast_to(
                row, (lanes, lanes)
            ).T
    for c in range(clusters):
        for n in range(listed):
            chosen = pairs_ref[0, 0, c, n]
            beside = lax.div(chosen, clusters)
            which = chosen - beside * clusters
            row_x = lax.div(beside, 3)
            step_x = row_x - 1
            step_y = beside - row_x * 3 - 1
            from_x = lax.rem(place_x + step_x + count_x, count_x)
            from_y = lax.rem(place_y + step_y + count_y, count_y)
            block = atoms_ref[from_x * count_y + from_y]
            part = block[:, :size]
            for k in range(1, clusters):
                part = jnp.where(which == k, block[:, k * size : (k + 1) * size], part)
            shifts = (
                (step_x * cells_x).astype(jnp.float32),
                (step_y * cells_y).astype(jnp.float32),
            )
            for axis in range(4):
                row = part[axis : axis + 1, :]
                if axis < 2:
                    row = row + shifts[axis]
                partner_ref[c, axis, :, n * size : (n + 1) * size] = jnp.broadcast_to(
                    row, (8, size)
                )

    pl.semaphore_wait(barrier, len(peers))
    copies = []
    for order, (peer_x, peer_y) in enumerate(peers):
        copy = pltpu.make_async_remote_copy(
            src_ref=partial_ref.at[peer_x * count_y + peer_y],
            dst_ref=land_ref.at[order],
            send_sem=send_sem.at[order],
            recv_sem=recv_sem.at[order],
            device_id={"gx": peer_x, "gy": peer_y},
            device_id_type=pl.DeviceIdType.MESH,
        )
        copy.start()
        copies.append(copy)

    @pl.loop(0, clusters)
    def _(c):
        @pl.loop(0, size // 8)
        def _(step):
            rows = pl.ds(pl.multiple_of(c * size + step * 8, 8), 8)
            own = [column_ref[axis, rows, :] for axis in range(3)]
            sums = [jnp.zeros((8, lanes), jnp.float32) for _ in range(3)]
            for tile in range(listed * size // lanes):
                span = pl.ds(tile * lanes, lanes)
                offsets = [own[axis] - partner_ref[c, axis, :, span] for axis in range(3)]
                square = sum(offset * offset for offset in offsets)
                weight = pair_weight(square) * partner_ref[c, 3, :, span]
                sums = [total + weight * offset for total, offset in zip(sums, offsets)]
            for axis in range(3):
                sum_ref[axis, rows, :] = sums[axis]

    own_charge = atoms_ref[me, 3:4, :]
    for axis in range(3):
        short_ref[axis, 0, :, :] = row_sums(sum_ref[axis]) * (own_charge * spacing)
    rank = rank_ref[...]

    @pl.loop(0, atom_total // size)
    def _(block):
        place = lax.broadcasted_iota(jnp.int32, (size, atom_total), 0) + block * size
        order_ref[pl.ds(pl.multiple_of(block * size, size), size), :] = jnp.where(
            place.astype(jnp.float32) == rank, 1.0, 0.0
        ).astype(jnp.bfloat16)

    force_ref[...] = jnp.zeros_like(force_ref)
    for copy in copies:
        copy.wait()
    total = partial_ref[me]
    for order in range(len(peers)):
        total = total + land_ref[order]
    for part in range(3):
        piece = total.astype(jnp.bfloat16).astype(jnp.float32)
        total = total - piece
        for axis in range(3):
            for tile in range(atom_total // lanes):
                span = slice(tile * lanes, (tile + 1) * lanes)
                row = 4 * part + axis
                force_ref[row : row + 1, span] = piece[axis, tile : tile + 1, :]
    placed = dot(force_ref[...].astype(jnp.bfloat16), order_ref[...])
    placed = (placed[0:4] + placed[4:8]) + placed[8:12]
    for axis in range(3):
        long_ref[axis, 0, :, :] = placed[axis : axis + 1, :] * (own_charge * (-1.0 / spacing))


def finished(pair_lists, partial, raw, rank, count_x, count_y, cells_x, cells_y):
    devices, _, atom_total = raw.shape
    clusters, listed = pair_lists.shape[2:]
    vmem = pl.BlockSpec(memory_space=pltpu.VMEM)
    flags = pltpu.SemaphoreType.DMA((devices - 1,))
    return pl.pallas_call(
        functools.partial(finish_kernel, (count_x, count_y), (cells_x, cells_y)),
        in_specs=[pl.BlockSpec(memory_space=pltpu.SMEM), vmem, vmem, vmem],
        out_specs=[vmem, vmem],
        out_shape=[jax.ShapeDtypeStruct((3, 1, 1, atom_total), jnp.float32)] * 2,
        scratch_shapes=[
            pltpu.VMEM((devices - 1, *partial.shape[1:]), jnp.float32),
            pltpu.VMEM((3, atom_total, lanes), jnp.float32),
            pltpu.VMEM((clusters, 4, 8, listed * atom_total // clusters), jnp.float32),
            pltpu.VMEM((3, atom_total, lanes), jnp.float32),
            pltpu.VMEM((atom_total, atom_total), jnp.bfloat16),
            pltpu.VMEM((16, atom_total), jnp.float32),
            flags,
            flags,
        ],
        compiler_params=pltpu.CompilerParams(collective_id=1, has_side_effects=True),
        name="finish",
    )(pair_lists, partial, raw, rank)


def green_table(period):
    index = np.arange(period)
    signed = np.where(index <= period // 2, index, index - period) / (period * spacing)
    modulus = ((2.0 + np.cos(index * (2.0 * np.pi / period))) / 3.0) ** 2
    square = signed * signed
    return np.stack([square, np.exp(-((np.pi / ewald_split) ** 2) * square) / modulus]).astype(
        np.float32
    )


def green_factors(index, period):
    signed = jnp.where(index <= period // 2, index, index - period).astype(jnp.float32) / (
        period * spacing
    )
    modulus = ((2.0 + jnp.cos(index.astype(jnp.float32) * (2.0 * jnp.pi / period))) / 3.0) ** 2
    square = signed * signed
    return jnp.stack([square, jnp.exp(-((jnp.pi / ewald_split) ** 2) * square) / modulus])


def one_cluster(own_rows, partner):
    offsets = (own_rows[:3, :, None] - partner[:3, None, :]) * spacing
    dist_square = jnp.sum(offsets * offsets, axis=0)
    soft_square = dist_square + soft_core
    soft_dist = jnp.sqrt(soft_square)
    scaled = ewald_split * soft_dist
    strength = (
        jax.scipy.special.erfc(scaled) / soft_dist
        + ewald_split * root_factor * jnp.exp(-scaled * scaled)
    ) / soft_square
    cutoff_taper = jnp.where(
        dist_square < cutoff * cutoff, (1.0 - dist_square / (cutoff * cutoff)) ** 2, 0.0
    )
    weight = partner[3][None, :] * strength * cutoff_taper
    return own_rows[3] * jnp.sum(weight[None] * offsets, axis=2)


def far_by_planes(bounds, atoms, count_x, count_y, cells_x, cells_y):
    devices = count_x * count_y
    depth = GRID_Z // devices
    tiles = atoms.shape[2]
    pad_y = round_up(cells_y + 3, 8)
    stride = round_up(pad_y, 16)
    window = 2 * cells_y
    turn_x = halves(jnp.asarray(hartley(GRID_X)))
    turn_y = halves(jnp.asarray(hartley(GRID_Y)))
    volume = GRID_X * GRID_Y * GRID_Z * spacing**3
    column = jnp.asarray(green_table(GRID_X).T)
    row = jnp.asarray(green_table(GRID_Y))
    every_k = np.arange(GRID_Z)
    taps = np.outer(every_k, np.arange(4)) * (2.0 * np.pi / GRID_Z)
    square, scale = green_table(GRID_Z)
    table = np.concatenate(
        [
            every_k[:, None],
            np.cos(taps) + np.sin(taps),
            np.cos(taps) - np.sin(taps),
            square[:, None],
            scale[:, None] / (np.pi * volume),
        ],
        axis=1,
    ).astype(np.float32)
    vmem = pl.BlockSpec(memory_space=pltpu.VMEM)
    rows = GRID_X + window_rows
    batch = depth * window_rows
    return pl.pallas_call(
        functools.partial(mesh_kernel, (count_x, count_y), (cells_x, cells_y), pad_y),
        in_specs=[pl.BlockSpec(memory_space=pltpu.SMEM)] + [vmem] * 8,
        out_specs=vmem,
        out_shape=jax.ShapeDtypeStruct((devices, 3, tiles, lanes), jnp.float32),
        scratch_shapes=[
            pltpu.VMEM((2, depth, rows, GRID_Y), jnp.float32),
            pltpu.VMEM((depth, rows, 4 * GRID_Y), jnp.float32),
            pltpu.VMEM((28 * devices * tiles, lanes), jnp.float32),
            pltpu.VMEM((devices * tiles * depth, lanes), jnp.float32),
            pltpu.VMEM((devices * tiles * depth, lanes), jnp.float32),
            pltpu.VMEM((devices * tiles, 2 * stride, lanes), jnp.bfloat16),
            pltpu.VMEM((group_size, 2 * window, 2 * lanes), jnp.bfloat16),
            pltpu.VMEM((group_size, batch, 2 * lanes), jnp.bfloat16),
            pltpu.VMEM((group_size, batch, 2 * lanes), jnp.float32),
            pltpu.VMEM((GRID_X, GRID_Y), jnp.float32),
            pltpu.VMEM((GRID_X, GRID_Y), jnp.float32),
        ],
        name="mesh",
    )(bounds, atoms, *turn_x, *turn_y, column, row, jnp.asarray(table))


def convolved_by_lines(charge_mesh, count_x, count_y):
    turn_x = jnp.asarray(hartley(GRID_X))
    turn_y = jnp.asarray(hartley(GRID_Y))
    product = functools.partial(
        jnp.einsum, precision=lax.Precision.HIGHEST, preferred_element_type=jnp.float32
    )
    exchange = functools.partial(lax.all_to_all, tiled=True)
    lines = exchange(charge_mesh, "gx", split_axis=2, concat_axis=0)
    lines = product("xyk,xu->uyk", lines, turn_x)
    lines = exchange(lines, "gy", split_axis=0, concat_axis=1)
    lines = product("uyk,yv->uvk", lines, turn_y)
    wide, _, depth = lines.shape
    start_x = lax.axis_index("gy") * wide
    start_z = lax.axis_index("gx") * depth
    volume = GRID_X * GRID_Y * GRID_Z * spacing**3
    fx = green_factors(start_x + jnp.arange(wide, dtype=jnp.int32), GRID_X)
    fy = green_factors(jnp.arange(GRID_Y, dtype=jnp.int32), GRID_Y)
    fz = green_factors(start_z + jnp.arange(depth, dtype=jnp.int32), GRID_Z)
    square = fx[0][:, None, None] + fy[0][:, None] + fz[0]
    scale = fx[1][:, None, None] * fy[1][:, None] * fz[1] / (math.pi * volume)
    lines = lines * jnp.where(square > 0.0, scale / jnp.where(square > 0.0, square, 1.0), 0.0)
    lines = product("uvk,vy->uyk", lines, turn_y)
    lines = exchange(lines, "gy", split_axis=1, concat_axis=0)
    lines = product("uyk,ux->xyk", lines, turn_x)
    return exchange(lines, "gx", split_axis=0, concat_axis=2)


def far_by_lines(atoms, base, count_x, count_y, cells_x, cells_y, cells_z):
    atom_total = atoms.shape[1]
    cells = (cells_x, cells_y, cells_z)
    pad = (round_up(cells_x + 3, rows_group), round_up(cells_y + 3, 8))
    pad_x, pad_y = pad
    turn_z = jnp.asarray(hartley(GRID_Z))
    spread = pl.pallas_call(
        functools.partial(spread_kernel, cells, pad),
        out_shape=jax.ShapeDtypeStruct((pad_x, pad_y, GRID_Z), jnp.float32),
        scratch_shapes=[
            pltpu.VMEM((pad_x, atom_total), jnp.float32),
            pltpu.VMEM((pad_y, atom_total), jnp.float32),
            pltpu.VMEM((atom_total, 2 * GRID_Z), jnp.bfloat16),
            pltpu.VMEM((rows_group * pad_y, atom_total), jnp.bfloat16),
            pltpu.VMEM((rows_group * pad_y, atom_total), jnp.bfloat16),
        ],
        name="spread",
    )(atoms, base, turn_z)

    from_x = moved(spread[cells_x : cells_x + 3, :cells_y], 1, 0)
    from_y = moved(spread[:cells_x, cells_y : cells_y + 3], 0, 1)
    from_both = moved(spread[cells_x : cells_x + 3, cells_y : cells_y + 3], 1, 1)
    charge_mesh = (
        spread[:cells_x, :cells_y]
        .at[:3]
        .add(from_x)
        .at[:, :3]
        .add(from_y)
        .at[:3, :3]
        .add(from_both)
    )
    potential = convolved_by_lines(charge_mesh, count_x, count_y)
    upper_x = moved(potential[:3], -1, 0)
    upper_y = moved(potential[:, :3], 0, -1)
    upper_both = moved(potential[:3, :3], -1, -1)
    wider = jnp.concatenate(
        [
            jnp.concatenate([potential, upper_x], axis=0),
            jnp.concatenate([upper_y, upper_both], axis=0),
        ],
        axis=1,
    )
    wider = jnp.pad(wider, ((0, pad_x - cells_x - 3), (0, pad_y - cells_y - 3), (0, 0)))
    return pl.pallas_call(
        functools.partial(gather_kernel, cells, pad),
        out_shape=jax.ShapeDtypeStruct((3, atom_total), jnp.float32),
        scratch_shapes=[
            pltpu.VMEM((pad_x, atom_total), jnp.float32),
            pltpu.VMEM((pad_x, atom_total), jnp.float32),
            pltpu.VMEM((pad_y, atom_total), jnp.float32),
            pltpu.VMEM((pad_y, atom_total), jnp.float32),
            pltpu.VMEM((2 * GRID_Z, 2 * atom_total), jnp.bfloat16),
            pltpu.VMEM((rows_group * pad_y, 2 * atom_total), jnp.float32),
        ],
        name="gather",
    )(atoms, base, turn_z, wider)


def local(positions, charges, pair_lists, slab_dest, atom_counts):
    count_x = lax.axis_size("gx")
    count_y = lax.axis_size("gy")
    devices = count_x * count_y
    atom_total = positions.shape[3]
    clusters = pair_lists.shape[2]
    cluster_size = atom_total // clusters
    blocks = slab_dest.shape[2]
    block_size = atom_total // blocks
    cells_x = GRID_X // count_x
    cells_y = GRID_Y // count_y
    cells_z = GRID_Z // count_y
    by_planes = (
        GRID_Z == 8 * devices
        and cells_y == 64
        and cells_x % 8 == 0
        and cells_x <= 64
        and count_y % 2 == 0
        and atom_total == 8 * lanes
        and cluster_size % lanes == 0
    )
    if by_planes:
        sizes = (count_x, count_y, cells_x, cells_y)
        raw, atoms, bounds, rank = shared(positions, charges, atom_counts, *sizes)
        partial = far_by_planes(bounds, atoms, *sizes)
        return tuple(finished(pair_lists, partial, raw, rank, *sizes))
    living = jnp.arange(atom_total, dtype=jnp.int32) < atom_counts[0, 0]
    charge = jnp.where(living, charges[0, 0], 0.0)
    packed = jnp.concatenate([positions, charge[None, None, None, :]], axis=0)
    atoms = packed.reshape(4, atom_total)
    base = jnp.broadcast_to(
        (slab_dest[0, 0] * cells_z)[:, None], (blocks, block_size)
    ).reshape(1, atom_total)
    gathered = lax.all_gather(atoms, ("gx", "gy"), axis=0, tiled=False)
    far_part = far_by_lines(atoms, base, count_x, count_y, cells_x, cells_y, cells_z)

    chosen = pair_lists[0, 0]
    beside = chosen // clusters
    step_x, step_y = (beside // 3 - 1, beside % 3 - 1)
    at_x = (lax.axis_index("gx") + step_x + count_x) % count_x
    at_y = (lax.axis_index("gy") + step_y + count_y) % count_y
    number = (at_x * count_y + at_y) * clusters + chosen % clusters
    pick = (number[:, :, None] == jnp.arange(devices * clusters, dtype=jnp.int32)).astype(
        jnp.float32
    )
    pool = gathered[:, :4].reshape(devices, 4, clusters, cluster_size)
    pool = jnp.transpose(pool, (1, 0, 2, 3)).reshape(4, devices * clusters, cluster_size)
    partners = jnp.einsum(
        "cln,fnk->cflk",
        pick,
        pool,
        precision=lax.Precision.HIGHEST,
        preferred_element_type=jnp.float32,
    )
    shift_x = (step_x * cells_x).astype(jnp.float32)
    shift_y = (step_y * cells_y).astype(jnp.float32)
    flat = jnp.zeros_like(shift_x)
    shift = jnp.stack([shift_x, shift_y, flat, flat], axis=1)
    partners = (partners + shift[:, :, :, None]).reshape(clusters, 4, -1)
    own = packed.reshape(4, clusters, cluster_size)
    pair_part = jnp.stack(
        [one_cluster(own[:, c], partners[c]) for c in range(clusters)], axis=1
    )
    short_forces = pair_part.reshape(3, 1, 1, atom_total)
    return (short_forces, far_part.reshape(3, 1, 1, atom_total))


def solution(mesh):
    return jax.shard_map(
        local,
        mesh=mesh,
        in_specs=(
            P(None, ("rep", "gx"), "gy", None),
            P(("rep", "gx"), "gy", None),
            P(("rep", "gx"), "gy", None, None),
            P(("rep", "gx"), "gy", None),
            P(("rep", "gx"), "gy"),
        ),
        out_specs=(P(None, ("rep", "gx"), "gy", None), P(None, ("rep", "gx"), "gy", None)),
        check_vma=False,
    )
```

```python
import functools
import math

import jax
import jax.numpy as jnp
import numpy as np
from jax import lax
from jax.experimental import pallas as pl
from jax.experimental.pallas import tpu as pltpu
from jax.sharding import PartitionSpec as P

GRID_X = 256
GRID_Y = 256
GRID_Z = 128


spacing = 0.16
ewald_split = 3.47
cutoff = 0.9
soft_core = 0.09
root_factor = 1.1283791670955126
rows_group = 8
lanes = 128
window_rows = 24
group_size = 4
plane_group = 2
fixed_arrays = 7


def moved(value, step_x, step_y):
    count_x = lax.axis_size("gx")
    count_y = lax.axis_size("gy")
    pairs = [
        (i * count_y + j, (i + step_x) % count_x * count_y + (j + step_y) % count_y)
        for i in range(count_x)
        for j in range(count_y)
    ]
    return lax.ppermute(value, ("gx", "gy"), pairs)


def round_up(value, multiple):
    return -(-value // multiple) * multiple


def hartley(period):
    turns = np.outer(np.arange(period), np.arange(period)) % period
    phases = turns * (2.0 * np.pi / period)
    return (np.cos(phases) + np.sin(phases)).astype(np.float32)


def halves(value):
    high = value.astype(jnp.bfloat16)
    low = (value - high.astype(jnp.float32)).astype(jnp.bfloat16)
    return (high, low)


def dot(left_side, right_side):
    return jnp.dot(left_side, right_side, preferred_element_type=jnp.float32)


def spline_weights(fraction):
    remain = 1.0 - fraction
    square = fraction * fraction
    cube_part = square * fraction
    values = [
        remain * remain * remain / 6.0,
        (3.0 * cube_part - 6.0 * square + 4.0) / 6.0,
        (-3.0 * cube_part + 3.0 * square + 3.0 * fraction + 1.0) / 6.0,
        cube_part / 6.0,
    ]
    slopes = [
        -0.5 * remain * remain,
        0.5 * (3.0 * square - 4.0 * fraction),
        0.5 * (-3.0 * square + 2.0 * fraction + 1.0),
        0.5 * square,
    ]
    return (values, slopes)


def split_cells(coordinate, offset, cell_count):
    inside = coordinate - offset
    lowest = jnp.clip(jnp.floor(inside).astype(jnp.int32), 0, cell_count - 1)
    return (lowest, inside - lowest.astype(inside.dtype))


def spline_table(lowest, values, table_size, period=None):
    points = lax.broadcasted_iota(jnp.int32, (table_size, lowest.shape[1]), 0)
    lookup = jnp.zeros(points.shape, jnp.float32)
    for spline_term in range(4):
        at = lowest + spline_term
        if period is not None:
            at = jnp.where(at >= period, at - period, at)
        lookup = jnp.where(points == at, values[spline_term], lookup)
    return lookup


def spread_kernel(cells, pad, atoms_ref, base_ref, turn_ref, out_ref, wx_ref, wy_ref, wz_ref, hi_ref, lo_ref):
    cells_x, cells_y, cells_z = cells
    pad_x, pad_y = pad
    atom_total = atoms_ref.shape[1]
    low_x, frac_x = split_cells(atoms_ref[0:1, :], 0.0, cells_x)
    low_y, frac_y = split_cells(atoms_ref[1:2, :], 0.0, cells_y)
    base = base_ref[...]
    low_z, frac_z = split_cells(atoms_ref[2:3, :], base.astype(jnp.float32), cells_z)
    wx_ref[...] = spline_table(low_x, spline_weights(frac_x)[0], pad_x) * atoms_ref[3:4, :]
    wy_ref[...] = spline_table(low_y, spline_weights(frac_y)[0], pad_y)
    turn = turn_ref[...]
    size_z = turn.shape[0]
    table_z = spline_table(base + low_z, spline_weights(frac_z)[0], size_z, size_z)
    waves = jnp.dot(
        turn, table_z, precision=lax.Precision.HIGHEST, preferred_element_type=jnp.float32
    ).T
    high, low = halves(waves)
    wz_ref[:, :size_z] = high
    wz_ref[:, size_z:] = low

    @pl.loop(0, pad_x // rows_group)
    def _(chunk):
        for inner in range(rows_group):
            row = wx_ref[pl.ds(chunk * rows_group + inner, 1), :]
            high, low = halves(row * wy_ref[...])
            hi_ref[pl.ds(inner * pad_y, pad_y), :] = high
            lo_ref[pl.ds(inner * pad_y, pad_y), :] = low
        both = dot(hi_ref[...], wz_ref[...])
        rest = dot(lo_ref[...], wz_ref[:, :size_z])
        total = both[:, :size_z] + both[:, size_z:] + rest
        out_ref[pl.ds(chunk * rows_group, rows_group)] = total.reshape(rows_group, pad_y, size_z)


def gather_kernel(cells, pad, atoms_ref, base_ref, turn_ref, mesh_ref, out_ref, wx_ref, vx_ref, wy_ref, vy_ref, wz_ref, level_ref):
    cells_x, cells_y, cells_z = cells
    pad_x, pad_y = pad
    atom_total = atoms_ref.shape[1]
    low_x, frac_x = split_cells(atoms_ref[0:1, :], 0.0, cells_x)
    low_y, frac_y = split_cells(atoms_ref[1:2, :], 0.0, cells_y)
    base = base_ref[...]
    low_z, frac_z = split_cells(atoms_ref[2:3, :], base.astype(jnp.float32), cells_z)
    values, slopes = spline_weights(frac_x)
    wx_ref[...] = spline_table(low_x, values, pad_x)
    vx_ref[...] = spline_table(low_x, slopes, pad_x)
    values, slopes = spline_weights(frac_y)
    wy_ref[...] = spline_table(low_y, values, pad_y)
    vy_ref[...] = spline_table(low_y, slopes, pad_y)
    values, slopes = spline_weights(frac_z)
    turn = turn_ref[...]
    size_z = turn.shape[0]
    for place, terms in enumerate((values, slopes)):
        table_z = spline_table(base + low_z, terms, size_z, size_z)
        waves = jnp.dot(
            turn, table_z, precision=lax.Precision.HIGHEST, preferred_element_type=jnp.float32
        )
        high, low = halves(waves)
        wz_ref[:size_z, pl.ds(place * atom_total, atom_total)] = high
        wz_ref[size_z:, pl.ds(place * atom_total, atom_total)] = low
    groups = pad_y // 8

    def one_chunk(chunk, sums):
        rows = mesh_ref[pl.ds(chunk * rows_group, rows_group)].reshape(rows_group * pad_y, size_z)
        high, low = halves(rows)
        level_ref[...] = dot(jnp.concatenate([high, high], axis=1), wz_ref[...]) + dot(
            low, wz_ref[:size_z, :]
        )
        first, second, third = sums
        for inner in range(rows_group):
            flat = level_ref[pl.ds(inner * pad_y, pad_y), :atom_total]
            tilt = level_ref[pl.ds(inner * pad_y, pad_y), atom_total:]
            across = wy_ref[...]
            part_x = jnp.sum((across * flat).reshape(groups, 8, atom_total), axis=0)
            part_y = jnp.sum((vy_ref[...] * flat).reshape(groups, 8, atom_total), axis=0)
            part_z = jnp.sum((across * tilt).reshape(groups, 8, atom_total), axis=0)
            weight = wx_ref[pl.ds(chunk * rows_group + inner, 1), :]
            slope = vx_ref[pl.ds(chunk * rows_group + inner, 1), :]
            first = first + slope * part_x
            second = second + weight * part_y
            third = third + weight * part_z
        return (first, second, third)

    zero = jnp.zeros((8, atom_total), jnp.float32)
    sums = lax.fori_loop(0, pad_x // rows_group, one_chunk, (zero, zero, zero))
    factor = -atoms_ref[3:4, :] / spacing
    for place in range(3):
        out_ref[pl.ds(place, 1), :] = factor * jnp.sum(sums[place], axis=0, keepdims=True)


def peers_of(count_x, count_y):
    place_x, place_y = (lax.axis_index("gx"), lax.axis_index("gy"))
    peers = []
    for order in range(1, count_x * count_y):
        peer_x = lax.rem(place_x + order // count_y, count_x)
        peer_y = lax.rem(place_y + order % count_y, count_y)
        peers.append((peer_x, peer_y))
    return peers


root_terms = (
    3.9164407301418542,
    -0.0037127819564810594,
    0.16802528315459195,
    -0.003061234121505335,
    -0.0076524954798020545,
    0.002268454833542123,
    -0.0003056487922112269,
    1.686888935413571e-05,
)


def pair_weight(square):
    soft_square = square * (spacing * spacing) + soft_core
    inverse = lax.rsqrt(soft_square)
    series = jnp.full_like(inverse, root_terms[-1])
    for term in root_terms[-2::-1]:
        series = series * inverse + term
    decay = jnp.exp(soft_square * (-ewald_split * ewald_split))
    taper = jnp.maximum(1.0 - square * (spacing * spacing / (cutoff * cutoff)), 0.0)
    return (decay * series) * (inverse * taper) ** 2


def row_sums(values):
    total = None
    ones = jnp.ones((16, values.shape[1]), jnp.bfloat16)
    for _ in range(3):
        part = values.astype(jnp.bfloat16)
        values = values - part.astype(jnp.float32)
        summed = lax.dot_general(
            ones, part, (((1,), (1,)), ((), ())), preferred_element_type=jnp.float32
        )
        total = summed if total is None else total + summed
    return total[0:1, :]


def place_partners(sizes, cells, pairs_ref, atoms_ref, partner_ref, chosen_clusters):
    count_x, count_y = sizes
    cells_x, cells_y = cells
    place_x, place_y = (lax.axis_index("gx"), lax.axis_index("gy"))
    clusters, listed = pairs_ref.shape[2:]
    size = atoms_ref.shape[2] // clusters
    for slot, c in enumerate(chosen_clusters):
        for n in range(listed):
            chosen = pairs_ref[0, 0, c, n]
            beside = lax.div(chosen, clusters)
            which = chosen - beside * clusters
            row_x = lax.div(beside, 3)
            step_x = row_x - 1
            step_y = beside - row_x * 3 - 1
            from_x = lax.rem(place_x + step_x + count_x, count_x)
            from_y = lax.rem(place_y + step_y + count_y, count_y)
            block = atoms_ref[from_x * count_y + from_y]
            part = block[:, :size]
            for k in range(1, clusters):
                part = jnp.where(which == k, block[:, k * size : (k + 1) * size], part)
            shifts = (
                (step_x * cells_x).astype(jnp.float32),
                (step_y * cells_y).astype(jnp.float32),
            )
            for axis in range(4):
                row = part[axis : axis + 1, :]
                if axis < 2:
                    row = row + shifts[axis]
                partner_ref[slot, axis, :, n * size : (n + 1) * size] = jnp.broadcast_to(
                    row, (8, size)
                )


def place_columns(me, atoms_ref, column_ref, start):
    for axis in range(3):
        for chunk in range(column_ref.shape[1] // lanes):
            at = start + chunk * lanes
            row = atoms_ref[me, axis : axis + 1, at : at + lanes]
            column_ref[axis, chunk * lanes : (chunk + 1) * lanes, :] = jnp.broadcast_to(
                row, (lanes, lanes)
            ).T


def pair_sums(slot, size, column_ref, partner_ref, sum_ref, out_ref, out_start):
    @pl.loop(0, size // 16)
    def _(step):
        for half in range(2):
            own_rows = pl.ds(pl.multiple_of(slot * size + step * 16 + half * 8, 8), 8)
            own = [column_ref[axis, own_rows, :] for axis in range(3)]
            sums = [jnp.zeros((8, lanes), jnp.float32) for _ in range(3)]
            for tile in range(partner_ref.shape[3] // lanes):
                span = slice(tile * lanes, (tile + 1) * lanes)
                offsets = [own[axis] - partner_ref[slot, axis, :, span] for axis in range(3)]
                square = sum(offset * offset for offset in offsets)
                weight = pair_weight(square) * partner_ref[slot, 3, :, span]
                sums = [total + weight * offset for total, offset in zip(sums, offsets)]
            rows = pl.ds(pl.multiple_of(step * 16 + half * 8, 8), 8)
            for axis in range(3):
                sum_ref[axis, rows, :] = sums[axis]

    for axis in range(3):
        out_ref[axis : axis + 1, out_start : out_start + size] = row_sums(sum_ref[axis])


def share_kernel(sizes, cells, early, count_ref, pairs_ref, position_ref, charge_ref, raw_ref, sorted_ref, bounds_ref, rank_ref, pair_ref, key_ref, split_ref, column_ref, partner_ref, sum_ref, raw_send, raw_recv, sort_send, sort_recv, mark_send, mark_recv):
    count_x, count_y = sizes
    cells_x, _ = cells
    place_x, place_y = (lax.axis_index("gx"), lax.axis_index("gy"))
    me = place_x * count_y + place_y
    place_chip, place_core = (place_y // 2, lax.rem(place_y, 2))
    chips = count_y // 2

    def at(step_x, step_chip, flip):
        peer_x = lax.rem(place_x + step_x, count_x)
        peer_chip = lax.rem(place_chip + step_chip, chips)
        peer_core = 1 - place_core if flip else place_core
        return (peer_x, peer_chip * 2 + peer_core)

    peers = peers_of(count_x, count_y)
    barrier = pltpu.get_barrier_semaphore()
    for peer_x, peer_y in peers:
        pl.semaphore_signal(
            barrier,
            inc=1,
            device_id={"gx": peer_x, "gy": peer_y},
            device_id_type=pl.DeviceIdType.MESH,
        )

    def sent(ref, owner, peer, send_sem, recv_sem, order, slot):
        return pltpu.make_async_remote_copy(
            src_ref=ref.at[owner],
            dst_ref=ref.at[owner],
            send_sem=send_sem.at[order],
            recv_sem=recv_sem.at[slot],
            device_id={"gx": peer[0], "gy": peer[1]},
            device_id_type=pl.DeviceIdType.MESH,
        )

    passed = []

    def passes(owner, peer):
        order = len(passed)
        copies = [
            sent(sorted_ref, owner, peer, sort_send, sort_recv, order, owner),
            sent(bounds_ref, owner, peer, mark_send, mark_recv, order, owner),
        ]
        for copy in copies:
            copy.start()
        passed.append(copies)

    def arrives(owner, peer):
        sent(sorted_ref, owner, peer, sort_send, sort_recv, 0, owner).wait_recv()
        sent(bounds_ref, owner, peer, mark_send, mark_recv, 0, owner).wait_recv()

    atom_total = charge_ref.shape[2]
    tiles = atom_total // lanes
    slot = lax.broadcasted_iota(jnp.int32, (1, atom_total), 1)
    living = slot < count_ref[0, 0]
    charge = jnp.where(living, charge_ref[0], 0.0)
    rows = [position_ref[axis, 0] for axis in range(3)] + [charge]
    for axis in range(4):
        raw_ref[me, pl.ds(axis, 1), :] = rows[axis]
    column = jnp.clip(jnp.floor(rows[0]), 0.0, cells_x - 1.0)
    key = jnp.where(living, column, float(cells_x)) * float(atom_total) + slot.astype(jnp.float32)
    for tile in range(tiles):
        span = slice(tile * lanes, (tile + 1) * lanes)
        key_ref[span, :] = jnp.broadcast_to(key[:, span], (lanes, lanes)).T
    wide = [
        jnp.broadcast_to(key[:, tile * lanes : (tile + 1) * lanes], (8, lanes))
        for tile in range(tiles)
    ]

    def count_group(group, totals):
        for inner in range(8):
            others = key_ref[pl.ds(pl.multiple_of(group * 64 + inner * 8, 8), 8), :]
            totals = tuple(
                total + jnp.where(others < own, 1.0, 0.0) for total, own in zip(totals, wide)
            )
        return totals

    zero = jnp.zeros((8, lanes), jnp.float32)
    totals = lax.fori_loop(0, atom_total // 64, count_group, (zero,) * tiles)
    for tile, total in enumerate(totals):
        rank_ref[:, tile * lanes : (tile + 1) * lanes] = jnp.sum(total, axis=0, keepdims=True)

    pl.semaphore_wait(barrier, len(peers))
    beside = sorted(
        {
            step_x % count_x * count_y + step_y % count_y
            for step_x in (-1, 0, 1)
            for step_y in (-1, 0, 1)
        }
        - {0}
    )
    copies = [
        sent(raw_ref, me, peers[order - 1], raw_send, raw_recv, order - 1, order - 1)
        for order in beside
    ]
    for copy in copies:
        copy.start()

    split_ref[...] = jnp.zeros_like(split_ref)
    rest = raw_ref[me]
    for part in range(3):
        piece = rest.astype(jnp.bfloat16).astype(jnp.float32)
        split_ref[4 * part : 4 * part + 4, :] = piece
        rest = rest - piece
    split = split_ref[...].astype(jnp.bfloat16)
    rank = rank_ref[...]
    block = 2 * lanes
    for part in range(atom_total // block):
        place = lax.broadcasted_iota(jnp.int32, (block, atom_total), 0) + part * block
        chosen = jnp.where(place.astype(jnp.float32) == rank, 1.0, 0.0).astype(jnp.bfloat16)
        found = lax.dot_general(
            split, chosen, (((1,), (1,)), ((), ())), preferred_element_type=jnp.float32
        )
        found = (found[0:4] + found[4:8]) + found[8:12]
        for tile in range(block // lanes):
            row = part * (block // lanes) + tile
            for axis in range(4):
                sorted_ref[me, axis, row : row + 1, :] = found[
                    axis : axis + 1, tile * lanes : (tile + 1) * lanes
                ]
    spot = lax.broadcasted_iota(jnp.int32, (tiles, lanes), 0) * lanes
    spot = spot + lax.broadcasted_iota(jnp.int32, (tiles, lanes), 1)
    inside = spot < count_ref[0, 0]
    column = jnp.clip(jnp.floor(sorted_ref[me, 0]), 0.0, cells_x - 1.0)
    lowest = jnp.min(jnp.where(inside, column, float(cells_x)), axis=1, keepdims=True)
    highest = jnp.max(jnp.where(inside, column, -1.0), axis=1, keepdims=True)
    first = jnp.floor(lowest * 0.125)
    last = jnp.floor((highest + 3.0) * 0.125)
    windows = jnp.where(
        highest >= 0.0, jnp.floor((last - first) * (8.0 / window_rows) + 0.01) + 1.0, 0.0
    )
    lane = lax.broadcasted_iota(jnp.int32, (tiles, lanes), 1)
    row = lax.broadcasted_iota(jnp.int32, (tiles, lanes), 0)
    marks = jnp.where(lane == row, first, jnp.where(lane == row + tiles, windows, 0.0))
    marks = jnp.sum(marks, axis=0, keepdims=True)
    bounds_ref[me] = marks.astype(jnp.int32)

    others = [(step, at(step, 0, False)) for step in range(1, count_x)]
    for _, peer in others:
        passes(me, peer)
    for step in range(1, chips):
        passes(me, at(0, step, False))
    passes(me, at(0, 0, True))
    place_columns(me, raw_ref, column_ref, 0)
    for copy in copies:
        copy.wait_recv()
    place_partners(sizes, cells, pairs_ref, raw_ref, partner_ref, range(early))
    size = atom_total // pairs_ref.shape[2]
    stops = [[] for _ in range(max(early, 2))]
    stops[0] = [(step, 0) for step in range(1, count_x)]
    stops[1] = [(step, chip) for chip in range(1, chips) for step in range(count_x)]
    for stage, stop in enumerate(stops):
        if stage < early:
            pair_sums(stage, size, column_ref, partner_ref, sum_ref, pair_ref, stage * size)
        for step, chip in stop:
            owner_x, owner_y = at(step, chip, False)
            owner = owner_x * count_y + owner_y
            arrives(owner, at(step, 0, False) if chip == 0 else at(0, chip, False))
            if chip == 0:
                for far in range(1, chips):
                    passes(owner, at(0, far, False))
            passes(owner, at(0, 0, True))
    for step in range(count_x):
        for chip in range(chips):
            owner_x, owner_y = at(step, chip, True)
            arrives(owner_x * count_y + owner_y, at(0, 0, True))
    for copy in copies:
        copy.wait_send()
    for pair in passed:
        for copy in pair:
            copy.wait_send()


def shared(positions, charges, pair_lists, atom_counts, count_x, count_y, cells_x, cells_y):
    devices = count_x * count_y
    atom_total = charges.shape[2]
    clusters, listed = pair_lists.shape[2:]
    size = atom_total // clusters
    early = clusters // 2
    vmem = pl.BlockSpec(memory_space=pltpu.VMEM)
    smem = pl.BlockSpec(memory_space=pltpu.SMEM)
    fewer = pltpu.SemaphoreType.DMA((devices - 1,))
    flags = pltpu.SemaphoreType.DMA((devices,))
    return pl.pallas_call(
        functools.partial(share_kernel, (count_x, count_y), (cells_x, cells_y), early),
        in_specs=[smem, smem, vmem, vmem],
        out_specs=[vmem] * 5,
        out_shape=[
            jax.ShapeDtypeStruct((devices, 4, atom_total), jnp.float32),
            jax.ShapeDtypeStruct((devices, 4, atom_total // lanes, lanes), jnp.float32),
            jax.ShapeDtypeStruct((devices, 1, lanes), jnp.int32),
            jax.ShapeDtypeStruct((1, atom_total), jnp.float32),
            jax.ShapeDtypeStruct((3, early * size), jnp.float32),
        ],
        scratch_shapes=[
            pltpu.VMEM((atom_total, lanes), jnp.float32),
            pltpu.VMEM((16, atom_total), jnp.float32),
            pltpu.VMEM((3, early * size, lanes), jnp.float32),
            pltpu.VMEM((early, 4, 8, listed * size), jnp.float32),
            pltpu.VMEM((3, size, lanes), jnp.float32),
            fewer,
            fewer,
        ]
        + [flags] * 4,
        compiler_params=pltpu.CompilerParams(
            collective_id=0, has_side_effects=True, vmem_limit_bytes=12 << 20
        ),
        name="share",
    )(
        atom_counts,
        *[
            pltpu.with_memory_space_constraint(value, pltpu.HBM)
            for value in (pair_lists, positions, charges)
        ],
    )


def depth_rows(table, height, terms):
    turns = height * table[:, 0:1]
    quarter = GRID_Z // 4
    nearest = jnp.floor(turns * (1.0 / quarter) + 0.5)
    angle = (turns - nearest * quarter) * (2.0 * math.pi / GRID_Z)
    quadrant = nearest - 4.0 * jnp.floor(nearest * 0.25)
    square = angle * angle
    near_cos = 1.0 + square * (
        -0.5 + square * (1.0 / 24.0 + square * (-1.0 / 720.0 + square * (1.0 / 40320.0)))
    )
    near_sin = angle * (
        1.0
        + square
        * (-1.0 / 6.0 + square * (1.0 / 120.0 + square * (-1.0 / 5040.0 + square / 362880.0)))
    )
    odd_turn = (quadrant == 1.0) | (quadrant == 3.0)
    cosine = jnp.where(odd_turn, near_sin, near_cos)
    cosine = jnp.where((quadrant == 1.0) | (quadrant == 2.0), -cosine, cosine)
    sine = jnp.where(odd_turn, near_cos, near_sin)
    sine = jnp.where(quadrant >= 2.0, -sine, sine)
    results = []
    for weights in terms:
        even = sum(table[:, 1 + t : 2 + t] * weights[t] for t in range(4))
        odd = sum(table[:, 5 + t : 6 + t] * weights[t] for t in range(4))
        results.append(cosine * even + sine * odd)
    return results


def mesh_kernel(sizes, cells, pad_y, bounds_ref, atoms_ref, *refs):
    constants, (out_ref, *scratch) = refs[:fixed_arrays], refs[fixed_arrays:]
    held, copy_sem = scratch[-fixed_arrays - 1 : -1], scratch[-1]
    copies = [
        pltpu.make_async_copy(source, target, copy_sem.at[place])
        for place, (source, target) in enumerate(zip(constants, held))
    ]
    for copy in copies:
        copy.start()
    xh_ref, xl_ref, yh_ref, yl_ref, column_ref, row_ref, table_ref = held
    mesh_ref, stack_ref, prep_ref, deep_ref, steep_ref, near_ref, wy_ref, side_ref, level_ref, square_ref, scale_ref = scratch[: -fixed_arrays - 1]
    count_x, count_y = sizes
    cells_x, cells_y = cells
    devices = count_x * count_y
    place = lax.axis_index("gx") * count_y + lax.axis_index("gy")
    tiles = atoms_ref.shape[2]
    depth = stack_ref.shape[0]
    window = 2 * cells_y
    windows = GRID_Y // window
    chunks = tiles
    extra = 8
    mesh_ref[...] = jnp.zeros_like(mesh_ref)
    stack_ref[:, GRID_X:, :] = jnp.zeros_like(stack_ref[:, GRID_X:, :])
    out_ref[...] = jnp.zeros_like(out_ref)
    wy_ref[...] = jnp.zeros_like(wy_ref)
    copies[-1].wait()
    table = table_ref[pl.ds(pl.multiple_of(place * depth, 8), depth), :]

    def prep_row(kind, cell, tile):
        return prep_ref[pl.ds((kind * devices + cell) * tiles + tile, 8, stride=0), :]

    @pl.loop(0, devices)
    def _(cell):
        def keep(kind, value):
            rows = pl.ds(pl.multiple_of((kind * devices + cell) * tiles, 8), tiles)
            prep_ref[rows, :] = value

        for axis, count in enumerate((cells_x, cells_y)):
            value = atoms_ref[cell, axis]
            lowest = jnp.clip(jnp.floor(value), 0.0, count - 1.0)
            values, slopes = spline_weights(value - lowest)
            keep(9 * axis, lowest)
            for term in range(4):
                keep(9 * axis + 1 + term, values[term])
                keep(9 * axis + 5 + term, slopes[term])
        value = atoms_ref[cell, 2]
        height = jnp.floor(value)
        values, slopes = spline_weights(value - height)
        keep(18, height)
        for term in range(4):
            keep(19 + term, values[term])
            keep(23 + term, slopes[term])
        keep(27, atoms_ref[cell, 3])
        for tile in range(tiles):
            height = prep_row(18, cell, tile)
            terms = [[prep_row(19 + 4 * s + term, cell, tile) for term in range(4)] for s in range(2)]
            deep, steep = depth_rows(table, height, terms)
            rows = pl.ds(pl.multiple_of((cell * tiles + tile) * depth, 8), depth)
            deep_ref[rows, :] = deep
            steep_ref[rows, :] = steep

    row_index = lax.broadcasted_iota(jnp.int32, (8, lanes), 0).astype(jnp.float32)

    def looked_up(points, lowest, term_lists):
        results = [jnp.zeros_like(points) for _ in term_lists]
        for term in range(4):
            hit = points == lowest + float(term)
            results = [
                jnp.where(hit, terms[term], result)
                for terms, result in zip(term_lists, results)
            ]
        return results

    def kinds(first, cell, tile):
        return [prep_row(first + term, cell, tile) for term in range(4)]

    stride = round_up(pad_y, 16)
    far_away = 1.0e6

    def window_of(cell, chunk, step):
        first = bounds_ref[cell, 0, chunk]
        count = bounds_ref[cell, 0, chunks + chunk]
        begin = first * 8 + jnp.minimum(step, jnp.maximum(count - 1, 0)) * window_rows
        base = jnp.where(step < count, begin.astype(jnp.float32), far_away)
        return (begin, base)

    def window_count(cell, chunk):
        counts = [bounds_ref[cell, 0, chunks + chunk + place] for place in range(group_size)]
        return functools.reduce(jnp.maximum, counts)

    def y_table(cell, chunk, kind):
        lowest = prep_row(9, cell, chunk)
        terms = kinds(kind, cell, chunk)
        for group in range(stride // 16):
            pieces = [
                looked_up(row_index + float(group * 16 + half * 8), lowest, [terms])[0]
                if group * 16 + half * 8 < pad_y
                else jnp.zeros_like(row_index)
                for half in range(2)
            ]
            yield (slice(group * 16, group * 16 + 16), *halves(jnp.concatenate(pieces, axis=0)))

    steps_x = window_rows // 8

    def spread_group(cell, group, i, m, odd):
        @pl.loop(0, window_count(cell, group * group_size))
        def _(step):
            for place in range(group_size):
                chunk = group * group_size + place
                spot = cell * chunks + chunk
                for rows, high, low in y_table(cell, chunk, 10):
                    after = slice(window + rows.start, window + rows.stop)
                    later = slice(stride + rows.start, stride + rows.stop)
                    wy_ref[place, rows, :lanes] = high
                    wy_ref[place, rows, lanes:] = high
                    wy_ref[place, after, :lanes] = low
                    near_ref[spot, rows, :] = high
                    near_ref[spot, later, :] = low
                begin, base = window_of(cell, chunk, step)
                lowest = prep_row(0, cell, chunk) - base
                charge = prep_row(27, cell, chunk)
                terms = [term * charge for term in kinds(1, cell, chunk)]
                weights = [
                    looked_up(row_index + float(tile * 8), lowest, [terms])[0]
                    for tile in range(steps_x)
                ]
                modes = [
                    deep_ref[pl.ds((cell * tiles + chunk) * depth + k, 8, stride=0), :]
                    for k in range(depth)
                ]
                blocks = [weight * mode for mode in modes for weight in weights]
                for pair in range(len(blocks) // 2):
                    high, low = halves(
                        jnp.concatenate(blocks[2 * pair : 2 * pair + 2], axis=0)
                    )
                    rows = slice(pair * 16, pair * 16 + 16)
                    side_ref[place, rows, :lanes] = high
                    side_ref[place, rows, lanes:] = low
            totals = []
            for place in range(group_size):
                total = lax.dot_general(
                    side_ref[place],
                    wy_ref[place],
                    (((1,), (1,)), ((), ())),
                    preferred_element_type=jnp.float32,
                )
                totals.append(total[:, :window] + total[:, window:])
            for place, total in enumerate(totals):
                begin, _ = window_of(cell, group * group_size + place, step)
                rows = pl.ds(pl.multiple_of(i * cells_x + begin, 8), window_rows)
                here = pl.ds(pl.multiple_of(m * window, lanes), window)
                mesh_ref[odd, :, rows, here] += total.reshape(depth, window_rows, window)

    @pl.loop(0, devices)
    def _(cell):
        i = lax.div(cell, count_y)
        j = lax.rem(cell, count_y)

        @pl.loop(0, chunks // group_size)
        def _(group):
            spread_group(cell, group, i, lax.div(j, 2), lax.rem(j, 2))

    def across(value):
        high, low = halves(value)
        return dot(xh_ref[...], high) + dot(xl_ref[...], high) + dot(xh_ref[...], low)

    def along(value):
        high, low = halves(value)
        return dot(high, yh_ref[...]) + dot(high, yl_ref[...]) + dot(low, yh_ref[...])

    plane_lane = lax.broadcasted_iota(jnp.int32, (GRID_X, window), 1)

    for copy in copies[:-1]:
        copy.wait()
    shape = (GRID_X, GRID_Y)
    square_ref[...] = jnp.broadcast_to(column_ref[:, 0:1], shape) + row_ref[0:1, :]
    scale_ref[...] = jnp.broadcast_to(column_ref[:, 1:2], shape) * row_ref[1:2, :]

    def one_plane(k):
        charge = mesh_ref[0, k, :GRID_X, :] + pltpu.roll(mesh_ref[1, k, :GRID_X, :], cells_y, 1)
        over = slice(GRID_X, GRID_X + extra)
        beyond = mesh_ref[0, k, over, :] + pltpu.roll(mesh_ref[1, k, over, :], cells_y, 1)
        charge = jnp.concatenate([charge[:extra] + beyond, charge[extra:]], axis=0)
        waves = along(across(charge))
        mode = pl.ds(place * depth + k, 1)
        square = square_ref[...] + table_ref[mode, 9:10]
        scale = scale_ref[...] * table_ref[mode, 10:11]
        green = jnp.where(square > 0.0, scale / square, 0.0)
        plane = across(along(waves * green))
        for odd in range(2):
            if odd:
                plane = pltpu.roll(plane, GRID_Y - cells_y, 1)
            for j_half in range(windows):
                j = 2 * j_half + odd
                block = plane[:, j_half * window : (j_half + 1) * window]
                high = block.astype(jnp.bfloat16).astype(jnp.float32)
                low = block - high
                shifted = pltpu.roll(high, stride, 1)
                left = jnp.where(plane_lane < stride, high, shifted)
                right = jnp.where(
                    plane_lane < 2 * stride - window,
                    shifted,
                    pltpu.roll(low, 2 * stride - window, 1),
                )
                for side, value in enumerate((left, right)):
                    span = slice((2 * j + side) * window, (2 * j + side + 1) * window)
                    stack_ref[k, :GRID_X, span] = value
                    stack_ref[k, GRID_X : GRID_X + extra, span] = value[:extra]

    @pl.loop(0, depth // plane_group)
    def _(pair):
        for inner in range(plane_group):
            one_plane(pair * plane_group + inner)

    def gather_group(cell, group, i, j):
        @pl.loop(0, window_count(cell, group * group_size))
        def _(step):
            blank = jnp.zeros((2 * window - 3 * stride, lanes), jnp.bfloat16)
            for place in range(group_size):
                chunk = group * group_size + place
                near = near_ref[cell * chunks + chunk]
                highs, lows = [], []
                for _, high, low in y_table(cell, chunk, 14):
                    highs.append(high)
                    lows.append(low)
                columns = jnp.concatenate(
                    [
                        jnp.concatenate([near, near[:stride], blank], axis=0),
                        jnp.concatenate([*highs, *lows, *highs, blank], axis=0),
                    ],
                    axis=1,
                )
                begin, _ = window_of(cell, chunk, step)
                rows = pl.ds(pl.multiple_of(i * cells_x + begin, 8), window_rows)
                span = pl.ds(pl.multiple_of(j * 2 * window, lanes), 2 * window)
                block = stack_ref[:, rows, span].reshape(depth * window_rows, 2 * window)
                level_ref[place] = dot(block.astype(jnp.bfloat16), columns)
            for place in range(group_size):
                chunk = group * group_size + place
                _, base = window_of(cell, chunk, step)
                lowest = prep_row(0, cell, chunk) - base
                values = kinds(1, cell, chunk)
                slopes = kinds(5, cell, chunk)
                spots = [
                    pl.ds((cell * tiles + chunk) * depth + k, 8, stride=0) for k in range(depth)
                ]
                deep = [deep_ref[spot, :] for spot in spots]
                steep = [steep_ref[spot, :] for spot in spots]
                zero = jnp.zeros((8, lanes), jnp.float32)
                sums = [zero, zero, zero]
                for tile in range(steps_x):
                    weight, slope = looked_up(
                        row_index + float(tile * 8), lowest, [values, slopes]
                    )
                    parts = [zero, zero, zero]
                    for k in range(depth):
                        at = slice(k * window_rows + tile * 8, k * window_rows + tile * 8 + 8)
                        flat = level_ref[place, at, :lanes]
                        tilt = level_ref[place, at, lanes:]
                        parts = [
                            parts[0] + deep[k] * flat,
                            parts[1] + deep[k] * tilt,
                            parts[2] + steep[k] * flat,
                        ]
                    sums = [
                        sums[0] + slope * parts[0],
                        sums[1] + weight * parts[1],
                        sums[2] + weight * parts[2],
                    ]
                for axis in range(3):
                    out_ref[cell, axis, pl.ds(chunk, 1), :] += jnp.sum(
                        sums[axis], axis=0, keepdims=True
                    )

    @pl.loop(0, devices)
    def _(cell):
        i = lax.div(cell, count_y)
        j = lax.rem(cell, count_y)

        @pl.loop(0, chunks // group_size)
        def _(group):
            gather_group(cell, group, i, j)


def finish_kernel(sizes, cells, early, pairs_ref, partial_ref, atoms_ref, rank_ref, pair_ref, short_ref, long_ref, land_ref, column_ref, partner_ref, sum_ref, late_ref, order_ref, force_ref, send_sem, recv_sem):
    count_x, count_y = sizes
    place_x, place_y = (lax.axis_index("gx"), lax.axis_index("gy"))
    me = place_x * count_y + place_y
    peers = peers_of(count_x, count_y)
    barrier = pltpu.get_barrier_semaphore()
    for peer_x, peer_y in peers:
        pl.semaphore_signal(
            barrier,
            inc=1,
            device_id={"gx": peer_x, "gy": peer_y},
            device_id_type=pl.DeviceIdType.MESH,
        )
    clusters = pairs_ref.shape[2]
    atom_total = atoms_ref.shape[2]
    size = atom_total // clusters
    place_columns(me, atoms_ref, column_ref, early * size)
    place_partners(sizes, cells, pairs_ref, atoms_ref, partner_ref, range(early, clusters))
    pl.semaphore_wait(barrier, len(peers))
    copies = []
    for order, (peer_x, peer_y) in enumerate(peers):
        copy = pltpu.make_async_remote_copy(
            src_ref=partial_ref.at[peer_x * count_y + peer_y],
            dst_ref=land_ref.at[order],
            send_sem=send_sem.at[order],
            recv_sem=recv_sem.at[order],
            device_id={"gx": peer_x, "gy": peer_y},
            device_id_type=pl.DeviceIdType.MESH,
        )
        copy.start()
        copies.append(copy)
    for slot in range(clusters - early):
        pair_sums(slot, size, column_ref, partner_ref, sum_ref, late_ref, slot * size)
    own_charge = atoms_ref[me, 3:4, :]
    for axis in range(3):
        for half, source in enumerate((pair_ref, late_ref)):
            span = slice(0, early * size) if half == 0 else slice(early * size, atom_total)
            short_ref[axis, 0, :, span] = source[axis : axis + 1, :] * (
                own_charge[:, span] * spacing
            )
    rank = rank_ref[...]

    @pl.loop(0, atom_total // size)
    def _(block):
        place = lax.broadcasted_iota(jnp.int32, (size, atom_total), 0) + block * size
        order_ref[pl.ds(pl.multiple_of(block * size, size), size), :] = jnp.where(
            place.astype(jnp.float32) == rank, 1.0, 0.0
        ).astype(jnp.bfloat16)

    force_ref[...] = jnp.zeros_like(force_ref)
    for copy in copies:
        copy.wait()
    total = partial_ref[me]
    for order in range(len(peers)):
        total = total + land_ref[order]
    for part in range(3):
        piece = total.astype(jnp.bfloat16).astype(jnp.float32)
        total = total - piece
        for axis in range(3):
            for tile in range(atom_total // lanes):
                span = slice(tile * lanes, (tile + 1) * lanes)
                row = 4 * part + axis
                force_ref[row : row + 1, span] = piece[axis, tile : tile + 1, :]
    placed = dot(force_ref[...].astype(jnp.bfloat16), order_ref[...])
    placed = (placed[0:4] + placed[4:8]) + placed[8:12]
    for axis in range(3):
        long_ref[axis, 0, :, :] = placed[axis : axis + 1, :] * (own_charge * (-1.0 / spacing))


def finished(pair_lists, partial, raw, rank, pair_part, count_x, count_y, cells_x, cells_y):
    devices, _, atom_total = raw.shape
    clusters, listed = pair_lists.shape[2:]
    size = atom_total // clusters
    early = clusters // 2
    late = clusters - early
    vmem = pl.BlockSpec(memory_space=pltpu.VMEM)
    flags = pltpu.SemaphoreType.DMA((devices - 1,))
    return pl.pallas_call(
        functools.partial(finish_kernel, (count_x, count_y), (cells_x, cells_y), early),
        in_specs=[pl.BlockSpec(memory_space=pltpu.SMEM), vmem, vmem, vmem, vmem],
        out_specs=[vmem, vmem],
        out_shape=[jax.ShapeDtypeStruct((3, 1, 1, atom_total), jnp.float32)] * 2,
        scratch_shapes=[
            pltpu.VMEM((devices - 1, *partial.shape[1:]), jnp.float32),
            pltpu.VMEM((3, late * size, lanes), jnp.float32),
            pltpu.VMEM((late, 4, 8, listed * size), jnp.float32),
            pltpu.VMEM((3, size, lanes), jnp.float32),
            pltpu.VMEM((3, late * size), jnp.float32),
            pltpu.VMEM((atom_total, atom_total), jnp.bfloat16),
            pltpu.VMEM((16, atom_total), jnp.float32),
            flags,
            flags,
        ],
        compiler_params=pltpu.CompilerParams(
            collective_id=1, has_side_effects=True, vmem_limit_bytes=16 << 20
        ),
        name="finish",
    )(pair_lists, partial, raw, rank, pair_part)


def green_table(period):
    index = np.arange(period)
    signed = np.where(index <= period // 2, index, index - period) / (period * spacing)
    modulus = ((2.0 + np.cos(index * (2.0 * np.pi / period))) / 3.0) ** 2
    square = signed * signed
    return np.stack([square, np.exp(-((np.pi / ewald_split) ** 2) * square) / modulus]).astype(
        np.float32
    )


def green_factors(index, period):
    signed = jnp.where(index <= period // 2, index, index - period).astype(jnp.float32) / (
        period * spacing
    )
    modulus = ((2.0 + jnp.cos(index.astype(jnp.float32) * (2.0 * jnp.pi / period))) / 3.0) ** 2
    square = signed * signed
    return jnp.stack([square, jnp.exp(-((jnp.pi / ewald_split) ** 2) * square) / modulus])


def one_cluster(own_rows, partner):
    offsets = (own_rows[:3, :, None] - partner[:3, None, :]) * spacing
    dist_square = jnp.sum(offsets * offsets, axis=0)
    soft_square = dist_square + soft_core
    soft_dist = jnp.sqrt(soft_square)
    scaled = ewald_split * soft_dist
    strength = (
        jax.scipy.special.erfc(scaled) / soft_dist
        + ewald_split * root_factor * jnp.exp(-scaled * scaled)
    ) / soft_square
    cutoff_taper = jnp.where(
        dist_square < cutoff * cutoff, (1.0 - dist_square / (cutoff * cutoff)) ** 2, 0.0
    )
    weight = partner[3][None, :] * strength * cutoff_taper
    return own_rows[3] * jnp.sum(weight[None] * offsets, axis=2)


def far_by_planes(bounds, atoms, count_x, count_y, cells_x, cells_y):
    devices = count_x * count_y
    depth = GRID_Z // devices
    tiles = atoms.shape[2]
    pad_y = round_up(cells_y + 3, 8)
    stride = round_up(pad_y, 16)
    window = 2 * cells_y
    turn_x = halves(jnp.asarray(hartley(GRID_X)))
    turn_y = halves(jnp.asarray(hartley(GRID_Y)))
    volume = GRID_X * GRID_Y * GRID_Z * spacing**3
    column = jnp.asarray(green_table(GRID_X).T)
    row = jnp.asarray(green_table(GRID_Y))
    every_k = np.arange(GRID_Z)
    taps = np.outer(every_k, np.arange(4)) * (2.0 * np.pi / GRID_Z)
    square, scale = green_table(GRID_Z)
    table = np.concatenate(
        [
            every_k[:, None],
            np.cos(taps) + np.sin(taps),
            np.cos(taps) - np.sin(taps),
            square[:, None],
            scale[:, None] / (np.pi * volume),
        ],
        axis=1,
    ).astype(np.float32)
    vmem = pl.BlockSpec(memory_space=pltpu.VMEM)
    rows = GRID_X + window_rows
    batch = depth * window_rows
    constants = (*turn_x, *turn_y, column, row, jnp.asarray(table))
    fixed = pl.BlockSpec(memory_space=pltpu.HBM)
    return pl.pallas_call(
        functools.partial(mesh_kernel, (count_x, count_y), (cells_x, cells_y), pad_y),
        in_specs=[pl.BlockSpec(memory_space=pltpu.SMEM)] + [vmem] + [fixed] * fixed_arrays,
        out_specs=vmem,
        out_shape=jax.ShapeDtypeStruct((devices, 3, tiles, lanes), jnp.float32),
        scratch_shapes=[
            pltpu.VMEM((2, depth, rows, GRID_Y), jnp.float32),
            pltpu.VMEM((depth, rows, 4 * GRID_Y), jnp.float32),
            pltpu.VMEM((28 * devices * tiles, lanes), jnp.float32),
            pltpu.VMEM((devices * tiles * depth, lanes), jnp.float32),
            pltpu.VMEM((devices * tiles * depth, lanes), jnp.float32),
            pltpu.VMEM((devices * tiles, 2 * stride, lanes), jnp.bfloat16),
            pltpu.VMEM((group_size, 2 * window, 2 * lanes), jnp.bfloat16),
            pltpu.VMEM((group_size, batch, 2 * lanes), jnp.bfloat16),
            pltpu.VMEM((group_size, batch, 2 * lanes), jnp.float32),
            pltpu.VMEM((GRID_X, GRID_Y), jnp.float32),
            pltpu.VMEM((GRID_X, GRID_Y), jnp.float32),
            *[pltpu.VMEM(value.shape, value.dtype) for value in constants],
            pltpu.SemaphoreType.DMA((fixed_arrays,)),
        ],
        compiler_params=pltpu.CompilerParams(vmem_limit_bytes=36 << 20),
        name="mesh",
    )(
        bounds, atoms, *[pltpu.with_memory_space_constraint(value, pltpu.HBM) for value in constants]
    )


def convolved_by_lines(charge_mesh, count_x, count_y):
    turn_x = jnp.asarray(hartley(GRID_X))
    turn_y = jnp.asarray(hartley(GRID_Y))
    product = functools.partial(
        jnp.einsum, precision=lax.Precision.HIGHEST, preferred_element_type=jnp.float32
    )
    exchange = functools.partial(lax.all_to_all, tiled=True)
    lines = exchange(charge_mesh, "gx", split_axis=2, concat_axis=0)
    lines = product("xyk,xu->uyk", lines, turn_x)
    lines = exchange(lines, "gy", split_axis=0, concat_axis=1)
    lines = product("uyk,yv->uvk", lines, turn_y)
    wide, _, depth = lines.shape
    start_x = lax.axis_index("gy") * wide
    start_z = lax.axis_index("gx") * depth
    volume = GRID_X * GRID_Y * GRID_Z * spacing**3
    fx = green_factors(start_x + jnp.arange(wide, dtype=jnp.int32), GRID_X)
    fy = green_factors(jnp.arange(GRID_Y, dtype=jnp.int32), GRID_Y)
    fz = green_factors(start_z + jnp.arange(depth, dtype=jnp.int32), GRID_Z)
    square = fx[0][:, None, None] + fy[0][:, None] + fz[0]
    scale = fx[1][:, None, None] * fy[1][:, None] * fz[1] / (math.pi * volume)
    lines = lines * jnp.where(square > 0.0, scale / jnp.where(square > 0.0, square, 1.0), 0.0)
    lines = product("uvk,vy->uyk", lines, turn_y)
    lines = exchange(lines, "gy", split_axis=1, concat_axis=0)
    lines = product("uyk,ux->xyk", lines, turn_x)
    return exchange(lines, "gx", split_axis=0, concat_axis=2)


def far_by_lines(atoms, base, count_x, count_y, cells_x, cells_y, cells_z):
    atom_total = atoms.shape[1]
    cells = (cells_x, cells_y, cells_z)
    pad = (round_up(cells_x + 3, rows_group), round_up(cells_y + 3, 8))
    pad_x, pad_y = pad
    turn_z = jnp.asarray(hartley(GRID_Z))
    spread = pl.pallas_call(
        functools.partial(spread_kernel, cells, pad),
        out_shape=jax.ShapeDtypeStruct((pad_x, pad_y, GRID_Z), jnp.float32),
        scratch_shapes=[
            pltpu.VMEM((pad_x, atom_total), jnp.float32),
            pltpu.VMEM((pad_y, atom_total), jnp.float32),
            pltpu.VMEM((atom_total, 2 * GRID_Z), jnp.bfloat16),
            pltpu.VMEM((rows_group * pad_y, atom_total), jnp.bfloat16),
            pltpu.VMEM((rows_group * pad_y, atom_total), jnp.bfloat16),
        ],
        name="spread",
    )(atoms, base, turn_z)

    from_x = moved(spread[cells_x : cells_x + 3, :cells_y], 1, 0)
    from_y = moved(spread[:cells_x, cells_y : cells_y + 3], 0, 1)
    from_both = moved(spread[cells_x : cells_x + 3, cells_y : cells_y + 3], 1, 1)
    charge_mesh = (
        spread[:cells_x, :cells_y]
        .at[:3]
        .add(from_x)
        .at[:, :3]
        .add(from_y)
        .at[:3, :3]
        .add(from_both)
    )
    potential = convolved_by_lines(charge_mesh, count_x, count_y)
    upper_x = moved(potential[:3], -1, 0)
    upper_y = moved(potential[:, :3], 0, -1)
    upper_both = moved(potential[:3, :3], -1, -1)
    wider = jnp.concatenate(
        [
            jnp.concatenate([potential, upper_x], axis=0),
            jnp.concatenate([upper_y, upper_both], axis=0),
        ],
        axis=1,
    )
    wider = jnp.pad(wider, ((0, pad_x - cells_x - 3), (0, pad_y - cells_y - 3), (0, 0)))
    return pl.pallas_call(
        functools.partial(gather_kernel, cells, pad),
        out_shape=jax.ShapeDtypeStruct((3, atom_total), jnp.float32),
        scratch_shapes=[
            pltpu.VMEM((pad_x, atom_total), jnp.float32),
            pltpu.VMEM((pad_x, atom_total), jnp.float32),
            pltpu.VMEM((pad_y, atom_total), jnp.float32),
            pltpu.VMEM((pad_y, atom_total), jnp.float32),
            pltpu.VMEM((2 * GRID_Z, 2 * atom_total), jnp.bfloat16),
            pltpu.VMEM((rows_group * pad_y, 2 * atom_total), jnp.float32),
        ],
        name="gather",
    )(atoms, base, turn_z, wider)


def local(positions, charges, pair_lists, slab_dest, atom_counts):
    count_x = lax.axis_size("gx")
    count_y = lax.axis_size("gy")
    devices = count_x * count_y
    atom_total = positions.shape[3]
    clusters = pair_lists.shape[2]
    cluster_size = atom_total // clusters
    blocks = slab_dest.shape[2]
    block_size = atom_total // blocks
    cells_x = GRID_X // count_x
    cells_y = GRID_Y // count_y
    cells_z = GRID_Z // count_y
    by_planes = (
        GRID_Z == 8 * devices
        and cells_y == 64
        and cells_x % 8 == 0
        and cells_x <= 64
        and count_y % 2 == 0
        and clusters % 2 == 0
        and atom_total == 8 * lanes
        and cluster_size % lanes == 0
    )
    if by_planes:
        sizes = (count_x, count_y, cells_x, cells_y)
        raw, atoms, bounds, rank, pair_part = shared(
            positions, charges, pair_lists, atom_counts, *sizes
        )
        partial = far_by_planes(bounds, atoms, *sizes)
        return tuple(finished(pair_lists, partial, raw, rank, pair_part, *sizes))
    living = jnp.arange(atom_total, dtype=jnp.int32) < atom_counts[0, 0]
    charge = jnp.where(living, charges[0, 0], 0.0)
    packed = jnp.concatenate([positions, charge[None, None, None, :]], axis=0)
    atoms = packed.reshape(4, atom_total)
    base = jnp.broadcast_to(
        (slab_dest[0, 0] * cells_z)[:, None], (blocks, block_size)
    ).reshape(1, atom_total)
    gathered = lax.all_gather(atoms, ("gx", "gy"), axis=0, tiled=False)
    far_part = far_by_lines(atoms, base, count_x, count_y, cells_x, cells_y, cells_z)

    chosen = pair_lists[0, 0]
    beside = chosen // clusters
    step_x, step_y = (beside // 3 - 1, beside % 3 - 1)
    at_x = (lax.axis_index("gx") + step_x + count_x) % count_x
    at_y = (lax.axis_index("gy") + step_y + count_y) % count_y
    number = (at_x * count_y + at_y) * clusters + chosen % clusters
    pick = (number[:, :, None] == jnp.arange(devices * clusters, dtype=jnp.int32)).astype(
        jnp.float32
    )
    pool = gathered[:, :4].reshape(devices, 4, clusters, cluster_size)
    pool = jnp.transpose(pool, (1, 0, 2, 3)).reshape(4, devices * clusters, cluster_size)
    partners = jnp.einsum(
        "cln,fnk->cflk",
        pick,
        pool,
        precision=lax.Precision.HIGHEST,
        preferred_element_type=jnp.float32,
    )
    shift_x = (step_x * cells_x).astype(jnp.float32)
    shift_y = (step_y * cells_y).astype(jnp.float32)
    flat = jnp.zeros_like(shift_x)
    shift = jnp.stack([shift_x, shift_y, flat, flat], axis=1)
    partners = (partners + shift[:, :, :, None]).reshape(clusters, 4, -1)
    own = packed.reshape(4, clusters, cluster_size)
    pair_part = jnp.stack(
        [one_cluster(own[:, c], partners[c]) for c in range(clusters)], axis=1
    )
    short_forces = pair_part.reshape(3, 1, 1, atom_total)
    return (short_forces, far_part.reshape(3, 1, 1, atom_total))


def solution(mesh):
    return jax.shard_map(
        local,
        mesh=mesh,
        in_specs=(
            P(None, ("rep", "gx"), "gy", None),
            P(("rep", "gx"), "gy", None),
            P(("rep", "gx"), "gy", None, None),
            P(("rep", "gx"), "gy", None),
            P(("rep", "gx"), "gy"),
        ),
        out_specs=(P(None, ("rep", "gx"), "gy", None), P(None, ("rep", "gx"), "gy", None)),
        check_vma=False,
    )
```

```python
import functools
import math

import jax
import jax.numpy as jnp
import numpy as np
from jax import lax
from jax.experimental import pallas as pl
from jax.experimental.pallas import tpu as pltpu
from jax.sharding import PartitionSpec as P

GRID_X = 256
GRID_Y = 256
GRID_Z = 128


spacing = 0.16
ewald_split = 3.47
cutoff = 0.9
soft_core = 0.09
root_factor = 1.1283791670955126
rows_group = 8
lanes = 128
window_rows = 24
group_size = 8
plane_group = 2
fixed_arrays = 7


def moved(value, step_x, step_y):
    count_x = lax.axis_size("gx")
    count_y = lax.axis_size("gy")
    pairs = [
        (i * count_y + j, (i + step_x) % count_x * count_y + (j + step_y) % count_y)
        for i in range(count_x)
        for j in range(count_y)
    ]
    return lax.ppermute(value, ("gx", "gy"), pairs)


def round_up(value, multiple):
    return -(-value // multiple) * multiple


def hartley(period):
    turns = np.outer(np.arange(period), np.arange(period)) % period
    phases = turns * (2.0 * np.pi / period)
    return (np.cos(phases) + np.sin(phases)).astype(np.float32)


def halves(value):
    high = value.astype(jnp.bfloat16)
    low = (value - high.astype(jnp.float32)).astype(jnp.bfloat16)
    return (high, low)


def dot(left_side, right_side):
    return jnp.dot(left_side, right_side, preferred_element_type=jnp.float32)


def spline_weights(fraction):
    remain = 1.0 - fraction
    square = fraction * fraction
    cube_part = square * fraction
    values = [
        remain * remain * remain / 6.0,
        (3.0 * cube_part - 6.0 * square + 4.0) / 6.0,
        (-3.0 * cube_part + 3.0 * square + 3.0 * fraction + 1.0) / 6.0,
        cube_part / 6.0,
    ]
    slopes = [
        -0.5 * remain * remain,
        0.5 * (3.0 * square - 4.0 * fraction),
        0.5 * (-3.0 * square + 2.0 * fraction + 1.0),
        0.5 * square,
    ]
    return (values, slopes)


def split_cells(coordinate, offset, cell_count):
    inside = coordinate - offset
    lowest = jnp.clip(jnp.floor(inside).astype(jnp.int32), 0, cell_count - 1)
    return (lowest, inside - lowest.astype(inside.dtype))


def spline_table(lowest, values, table_size, period=None):
    points = lax.broadcasted_iota(jnp.int32, (table_size, lowest.shape[1]), 0)
    lookup = jnp.zeros(points.shape, jnp.float32)
    for spline_term in range(4):
        at = lowest + spline_term
        if period is not None:
            at = jnp.where(at >= period, at - period, at)
        lookup = jnp.where(points == at, values[spline_term], lookup)
    return lookup


def spread_kernel(cells, pad, atoms_ref, base_ref, turn_ref, out_ref, wx_ref, wy_ref, wz_ref, hi_ref, lo_ref):
    cells_x, cells_y, cells_z = cells
    pad_x, pad_y = pad
    atom_total = atoms_ref.shape[1]
    low_x, frac_x = split_cells(atoms_ref[0:1, :], 0.0, cells_x)
    low_y, frac_y = split_cells(atoms_ref[1:2, :], 0.0, cells_y)
    base = base_ref[...]
    low_z, frac_z = split_cells(atoms_ref[2:3, :], base.astype(jnp.float32), cells_z)
    wx_ref[...] = spline_table(low_x, spline_weights(frac_x)[0], pad_x) * atoms_ref[3:4, :]
    wy_ref[...] = spline_table(low_y, spline_weights(frac_y)[0], pad_y)
    turn = turn_ref[...]
    size_z = turn.shape[0]
    table_z = spline_table(base + low_z, spline_weights(frac_z)[0], size_z, size_z)
    waves = jnp.dot(
        turn, table_z, precision=lax.Precision.HIGHEST, preferred_element_type=jnp.float32
    ).T
    high, low = halves(waves)
    wz_ref[:, :size_z] = high
    wz_ref[:, size_z:] = low

    @pl.loop(0, pad_x // rows_group)
    def _(chunk):
        for inner in range(rows_group):
            row = wx_ref[pl.ds(chunk * rows_group + inner, 1), :]
            high, low = halves(row * wy_ref[...])
            hi_ref[pl.ds(inner * pad_y, pad_y), :] = high
            lo_ref[pl.ds(inner * pad_y, pad_y), :] = low
        both = dot(hi_ref[...], wz_ref[...])
        rest = dot(lo_ref[...], wz_ref[:, :size_z])
        total = both[:, :size_z] + both[:, size_z:] + rest
        out_ref[pl.ds(chunk * rows_group, rows_group)] = total.reshape(rows_group, pad_y, size_z)


def gather_kernel(cells, pad, atoms_ref, base_ref, turn_ref, mesh_ref, out_ref, wx_ref, vx_ref, wy_ref, vy_ref, wz_ref, level_ref):
    cells_x, cells_y, cells_z = cells
    pad_x, pad_y = pad
    atom_total = atoms_ref.shape[1]
    low_x, frac_x = split_cells(atoms_ref[0:1, :], 0.0, cells_x)
    low_y, frac_y = split_cells(atoms_ref[1:2, :], 0.0, cells_y)
    base = base_ref[...]
    low_z, frac_z = split_cells(atoms_ref[2:3, :], base.astype(jnp.float32), cells_z)
    values, slopes = spline_weights(frac_x)
    wx_ref[...] = spline_table(low_x, values, pad_x)
    vx_ref[...] = spline_table(low_x, slopes, pad_x)
    values, slopes = spline_weights(frac_y)
    wy_ref[...] = spline_table(low_y, values, pad_y)
    vy_ref[...] = spline_table(low_y, slopes, pad_y)
    values, slopes = spline_weights(frac_z)
    turn = turn_ref[...]
    size_z = turn.shape[0]
    for place, terms in enumerate((values, slopes)):
        table_z = spline_table(base + low_z, terms, size_z, size_z)
        waves = jnp.dot(
            turn, table_z, precision=lax.Precision.HIGHEST, preferred_element_type=jnp.float32
        )
        high, low = halves(waves)
        wz_ref[:size_z, pl.ds(place * atom_total, atom_total)] = high
        wz_ref[size_z:, pl.ds(place * atom_total, atom_total)] = low
    groups = pad_y // 8

    def one_chunk(chunk, sums):
        rows = mesh_ref[pl.ds(chunk * rows_group, rows_group)].reshape(rows_group * pad_y, size_z)
        high, low = halves(rows)
        level_ref[...] = dot(jnp.concatenate([high, high], axis=1), wz_ref[...]) + dot(
            low, wz_ref[:size_z, :]
        )
        first, second, third = sums
        for inner in range(rows_group):
            flat = level_ref[pl.ds(inner * pad_y, pad_y), :atom_total]
            tilt = level_ref[pl.ds(inner * pad_y, pad_y), atom_total:]
            across = wy_ref[...]
            part_x = jnp.sum((across * flat).reshape(groups, 8, atom_total), axis=0)
            part_y = jnp.sum((vy_ref[...] * flat).reshape(groups, 8, atom_total), axis=0)
            part_z = jnp.sum((across * tilt).reshape(groups, 8, atom_total), axis=0)
            weight = wx_ref[pl.ds(chunk * rows_group + inner, 1), :]
            slope = vx_ref[pl.ds(chunk * rows_group + inner, 1), :]
            first = first + slope * part_x
            second = second + weight * part_y
            third = third + weight * part_z
        return (first, second, third)

    zero = jnp.zeros((8, atom_total), jnp.float32)
    sums = lax.fori_loop(0, pad_x // rows_group, one_chunk, (zero, zero, zero))
    factor = -atoms_ref[3:4, :] / spacing
    for place in range(3):
        out_ref[pl.ds(place, 1), :] = factor * jnp.sum(sums[place], axis=0, keepdims=True)


def peers_of(count_x, count_y):
    place_x, place_y = (lax.axis_index("gx"), lax.axis_index("gy"))
    peers = []
    for order in range(1, count_x * count_y):
        peer_x = lax.rem(place_x + order // count_y, count_x)
        peer_y = lax.rem(place_y + order % count_y, count_y)
        peers.append((peer_x, peer_y))
    return peers


root_terms = (
    3.9164407301418542,
    -0.0037127819564810594,
    0.16802528315459195,
    -0.003061234121505335,
    -0.0076524954798020545,
    0.002268454833542123,
    -0.0003056487922112269,
    1.686888935413571e-05,
)


def pair_weight(square):
    soft_square = square * (spacing * spacing) + soft_core
    inverse = lax.rsqrt(soft_square)
    series = jnp.full_like(inverse, root_terms[-1])
    for term in root_terms[-2::-1]:
        series = series * inverse + term
    decay = jnp.exp(soft_square * (-ewald_split * ewald_split))
    taper = jnp.maximum(1.0 - square * (spacing * spacing / (cutoff * cutoff)), 0.0)
    return (decay * series) * (inverse * taper) ** 2


def row_sums(values):
    total = None
    ones = jnp.ones((16, values.shape[1]), jnp.bfloat16)
    for _ in range(3):
        part = values.astype(jnp.bfloat16)
        values = values - part.astype(jnp.float32)
        summed = lax.dot_general(
            ones, part, (((1,), (1,)), ((), ())), preferred_element_type=jnp.float32
        )
        total = summed if total is None else total + summed
    return total[0:1, :]


def place_partners(sizes, cells, pairs_ref, atoms_ref, partner_ref, chosen_clusters):
    count_x, count_y = sizes
    cells_x, cells_y = cells
    place_x, place_y = (lax.axis_index("gx"), lax.axis_index("gy"))
    clusters, listed = pairs_ref.shape[2:]
    size = atoms_ref.shape[2] // clusters
    for slot, c in enumerate(chosen_clusters):
        for n in range(listed):
            chosen = pairs_ref[0, 0, c, n]
            beside = lax.div(chosen, clusters)
            which = chosen - beside * clusters
            row_x = lax.div(beside, 3)
            step_x = row_x - 1
            step_y = beside - row_x * 3 - 1
            from_x = lax.rem(place_x + step_x + count_x, count_x)
            from_y = lax.rem(place_y + step_y + count_y, count_y)
            block = atoms_ref[from_x * count_y + from_y]
            part = block[:, :size]
            for k in range(1, clusters):
                part = jnp.where(which == k, block[:, k * size : (k + 1) * size], part)
            shifts = (
                (step_x * cells_x).astype(jnp.float32),
                (step_y * cells_y).astype(jnp.float32),
            )
            for axis in range(4):
                row = part[axis : axis + 1, :]
                if axis < 2:
                    row = row + shifts[axis]
                partner_ref[slot, axis, :, n * size : (n + 1) * size] = jnp.broadcast_to(
                    row, (8, size)
                )


def place_columns(me, atoms_ref, column_ref, start):
    for axis in range(3):
        for chunk in range(column_ref.shape[1] // lanes):
            at = start + chunk * lanes
            row = atoms_ref[me, axis : axis + 1, at : at + lanes]
            column_ref[axis, chunk * lanes : (chunk + 1) * lanes, :] = jnp.broadcast_to(
                row, (lanes, lanes)
            ).T


def pair_sums(slot, size, column_ref, partner_ref, sum_ref, out_ref, out_start):
    @pl.loop(0, size // 16)
    def _(step):
        for half in range(2):
            own_rows = pl.ds(pl.multiple_of(slot * size + step * 16 + half * 8, 8), 8)
            own = [column_ref[axis, own_rows, :] for axis in range(3)]
            sums = [jnp.zeros((8, lanes), jnp.float32) for _ in range(3)]
            for tile in range(partner_ref.shape[3] // lanes):
                span = slice(tile * lanes, (tile + 1) * lanes)
                offsets = [own[axis] - partner_ref[slot, axis, :, span] for axis in range(3)]
                square = sum(offset * offset for offset in offsets)
                weight = pair_weight(square) * partner_ref[slot, 3, :, span]
                sums = [total + weight * offset for total, offset in zip(sums, offsets)]
            rows = pl.ds(pl.multiple_of(step * 16 + half * 8, 8), 8)
            for axis in range(3):
                sum_ref[axis, rows, :] = sums[axis]

    for axis in range(3):
        out_ref[axis : axis + 1, out_start : out_start + size] = row_sums(sum_ref[axis])


def share_kernel(sizes, cells, early, count_ref, pairs_ref, position_ref, charge_ref, raw_ref, sorted_ref, bounds_ref, rank_ref, pair_ref, key_ref, split_ref, column_ref, partner_ref, sum_ref, raw_send, raw_recv, sort_send, sort_recv, mark_send, mark_recv):
    count_x, count_y = sizes
    cells_x, _ = cells
    place_x, place_y = (lax.axis_index("gx"), lax.axis_index("gy"))
    me = place_x * count_y + place_y
    place_chip, place_core = (place_y // 2, lax.rem(place_y, 2))
    chips = count_y // 2

    def at(step_x, step_chip, flip):
        peer_x = lax.rem(place_x + step_x, count_x)
        peer_chip = lax.rem(place_chip + step_chip, chips)
        peer_core = 1 - place_core if flip else place_core
        return (peer_x, peer_chip * 2 + peer_core)

    peers = peers_of(count_x, count_y)
    barrier = pltpu.get_barrier_semaphore()
    for peer_x, peer_y in peers:
        pl.semaphore_signal(
            barrier,
            inc=1,
            device_id={"gx": peer_x, "gy": peer_y},
            device_id_type=pl.DeviceIdType.MESH,
        )

    def sent(ref, owner, peer, send_sem, recv_sem, order, slot):
        return pltpu.make_async_remote_copy(
            src_ref=ref.at[owner],
            dst_ref=ref.at[owner],
            send_sem=send_sem.at[order],
            recv_sem=recv_sem.at[slot],
            device_id={"gx": peer[0], "gy": peer[1]},
            device_id_type=pl.DeviceIdType.MESH,
        )

    passed = []

    def passes(owner, peer):
        order = len(passed)
        copies = [
            sent(sorted_ref, owner, peer, sort_send, sort_recv, order, owner),
            sent(bounds_ref, owner, peer, mark_send, mark_recv, order, owner),
        ]
        for copy in copies:
            copy.start()
        passed.append(copies)

    def arrives(owner, peer):
        sent(sorted_ref, owner, peer, sort_send, sort_recv, 0, owner).wait_recv()
        sent(bounds_ref, owner, peer, mark_send, mark_recv, 0, owner).wait_recv()

    atom_total = charge_ref.shape[2]
    tiles = atom_total // lanes
    slot = lax.broadcasted_iota(jnp.int32, (1, atom_total), 1)
    living = slot < count_ref[0, 0]
    charge = jnp.where(living, charge_ref[0], 0.0)
    rows = [position_ref[axis, 0] for axis in range(3)] + [charge]
    for axis in range(4):
        raw_ref[me, pl.ds(axis, 1), :] = rows[axis]
    column = jnp.clip(jnp.floor(rows[0]), 0.0, cells_x - 1.0)
    key = jnp.where(living, column, float(cells_x)) * float(atom_total) + slot.astype(jnp.float32)
    for tile in range(tiles):
        span = slice(tile * lanes, (tile + 1) * lanes)
        key_ref[span, :] = jnp.broadcast_to(key[:, span], (lanes, lanes)).T
    wide = [
        jnp.broadcast_to(key[:, tile * lanes : (tile + 1) * lanes], (8, lanes))
        for tile in range(tiles)
    ]

    def count_group(group, totals):
        for inner in range(8):
            others = key_ref[pl.ds(pl.multiple_of(group * 64 + inner * 8, 8), 8), :]
            totals = tuple(
                total + jnp.where(others < own, 1.0, 0.0) for total, own in zip(totals, wide)
            )
        return totals

    zero = jnp.zeros((8, lanes), jnp.float32)
    totals = lax.fori_loop(0, atom_total // 64, count_group, (zero,) * tiles)
    for tile, total in enumerate(totals):
        rank_ref[:, tile * lanes : (tile + 1) * lanes] = jnp.sum(total, axis=0, keepdims=True)

    pl.semaphore_wait(barrier, len(peers))
    beside = sorted(
        {
            step_x % count_x * count_y + step_y % count_y
            for step_x in (-1, 0, 1)
            for step_y in (-1, 0, 1)
        }
        - {0}
    )
    copies = [
        sent(raw_ref, me, peers[order - 1], raw_send, raw_recv, order - 1, order - 1)
        for order in beside
    ]
    for copy in copies:
        copy.start()

    split_ref[...] = jnp.zeros_like(split_ref)
    rest = raw_ref[me]
    for part in range(3):
        piece = rest.astype(jnp.bfloat16).astype(jnp.float32)
        split_ref[4 * part : 4 * part + 4, :] = piece
        rest = rest - piece
    split = split_ref[...].astype(jnp.bfloat16)
    rank = rank_ref[...]
    block = 2 * lanes
    for part in range(atom_total // block):
        place = lax.broadcasted_iota(jnp.int32, (block, atom_total), 0) + part * block
        chosen = jnp.where(place.astype(jnp.float32) == rank, 1.0, 0.0).astype(jnp.bfloat16)
        found = lax.dot_general(
            split, chosen, (((1,), (1,)), ((), ())), preferred_element_type=jnp.float32
        )
        found = (found[0:4] + found[4:8]) + found[8:12]
        for tile in range(block // lanes):
            row = part * (block // lanes) + tile
            for axis in range(4):
                sorted_ref[me, axis, row : row + 1, :] = found[
                    axis : axis + 1, tile * lanes : (tile + 1) * lanes
                ]
    spot = lax.broadcasted_iota(jnp.int32, (tiles, lanes), 0) * lanes
    spot = spot + lax.broadcasted_iota(jnp.int32, (tiles, lanes), 1)
    inside = spot < count_ref[0, 0]
    column = jnp.clip(jnp.floor(sorted_ref[me, 0]), 0.0, cells_x - 1.0)
    lowest = jnp.min(jnp.where(inside, column, float(cells_x)), axis=1, keepdims=True)
    highest = jnp.max(jnp.where(inside, column, -1.0), axis=1, keepdims=True)
    first = jnp.floor(lowest * 0.125)
    last = jnp.floor((highest + 3.0) * 0.125)
    windows = jnp.where(
        highest >= 0.0, jnp.floor((last - first) * (8.0 / window_rows) + 0.01) + 1.0, 0.0
    )
    lane = lax.broadcasted_iota(jnp.int32, (tiles, lanes), 1)
    row = lax.broadcasted_iota(jnp.int32, (tiles, lanes), 0)
    marks = jnp.where(lane == row, first, jnp.where(lane == row + tiles, windows, 0.0))
    marks = jnp.sum(marks, axis=0, keepdims=True)
    bounds_ref[me] = marks.astype(jnp.int32)

    others = [(step, at(step, 0, False)) for step in range(1, count_x)]
    for _, peer in others:
        passes(me, peer)
    for step in range(1, chips):
        passes(me, at(0, step, False))
    passes(me, at(0, 0, True))
    place_columns(me, raw_ref, column_ref, 0)
    for copy in copies:
        copy.wait_recv()
    place_partners(sizes, cells, pairs_ref, raw_ref, partner_ref, range(early))
    size = atom_total // pairs_ref.shape[2]
    stops = [[] for _ in range(max(early, 2))]
    stops[0] = [(step, 0) for step in range(1, count_x)]
    stops[1] = [(step, chip) for chip in range(1, chips) for step in range(count_x)]
    for stage, stop in enumerate(stops):
        if stage < early:
            pair_sums(stage, size, column_ref, partner_ref, sum_ref, pair_ref, stage * size)
        for step, chip in stop:
            owner_x, owner_y = at(step, chip, False)
            owner = owner_x * count_y + owner_y
            arrives(owner, at(step, 0, False) if chip == 0 else at(0, chip, False))
            if chip == 0:
                for far in range(1, chips):
                    passes(owner, at(0, far, False))
            passes(owner, at(0, 0, True))
    for step in range(count_x):
        for chip in range(chips):
            owner_x, owner_y = at(step, chip, True)
            arrives(owner_x * count_y + owner_y, at(0, 0, True))
    for copy in copies:
        copy.wait_send()
    for pair in passed:
        for copy in pair:
            copy.wait_send()


def shared(positions, charges, pair_lists, atom_counts, count_x, count_y, cells_x, cells_y):
    devices = count_x * count_y
    atom_total = charges.shape[2]
    clusters, listed = pair_lists.shape[2:]
    size = atom_total // clusters
    early = clusters // 2
    vmem = pl.BlockSpec(memory_space=pltpu.VMEM)
    smem = pl.BlockSpec(memory_space=pltpu.SMEM)
    fewer = pltpu.SemaphoreType.DMA((devices - 1,))
    flags = pltpu.SemaphoreType.DMA((devices,))
    return pl.pallas_call(
        functools.partial(share_kernel, (count_x, count_y), (cells_x, cells_y), early),
        in_specs=[smem, smem, vmem, vmem],
        out_specs=[vmem] * 5,
        out_shape=[
            jax.ShapeDtypeStruct((devices, 4, atom_total), jnp.float32),
            jax.ShapeDtypeStruct((devices, 4, atom_total // lanes, lanes), jnp.float32),
            jax.ShapeDtypeStruct((devices, 1, lanes), jnp.int32),
            jax.ShapeDtypeStruct((1, atom_total), jnp.float32),
            jax.ShapeDtypeStruct((3, early * size), jnp.float32),
        ],
        scratch_shapes=[
            pltpu.VMEM((atom_total, lanes), jnp.float32),
            pltpu.VMEM((16, atom_total), jnp.float32),
            pltpu.VMEM((3, early * size, lanes), jnp.float32),
            pltpu.VMEM((early, 4, 8, listed * size), jnp.float32),
            pltpu.VMEM((3, size, lanes), jnp.float32),
            fewer,
            fewer,
        ]
        + [flags] * 4,
        compiler_params=pltpu.CompilerParams(
            collective_id=0, has_side_effects=True, vmem_limit_bytes=12 << 20
        ),
        name="share",
    )(
        atom_counts,
        *[
            pltpu.with_memory_space_constraint(value, pltpu.HBM)
            for value in (pair_lists, positions, charges)
        ],
    )


def depth_rows(table, height, terms):
    turns = height * table[:, 0:1]
    quarter = GRID_Z // 4
    nearest = jnp.floor(turns * (1.0 / quarter) + 0.5)
    angle = (turns - nearest * quarter) * (2.0 * math.pi / GRID_Z)
    quadrant = nearest - 4.0 * jnp.floor(nearest * 0.25)
    square = angle * angle
    near_cos = 1.0 + square * (
        -0.5 + square * (1.0 / 24.0 + square * (-1.0 / 720.0 + square * (1.0 / 40320.0)))
    )
    near_sin = angle * (
        1.0
        + square
        * (-1.0 / 6.0 + square * (1.0 / 120.0 + square * (-1.0 / 5040.0 + square / 362880.0)))
    )
    odd_turn = (quadrant == 1.0) | (quadrant == 3.0)
    cosine = jnp.where(odd_turn, near_sin, near_cos)
    cosine = jnp.where((quadrant == 1.0) | (quadrant == 2.0), -cosine, cosine)
    sine = jnp.where(odd_turn, near_cos, near_sin)
    sine = jnp.where(quadrant >= 2.0, -sine, sine)
    results = []
    for weights in terms:
        even = sum(table[:, 1 + t : 2 + t] * weights[t] for t in range(4))
        odd = sum(table[:, 5 + t : 6 + t] * weights[t] for t in range(4))
        results.append(cosine * even + sine * odd)
    return results


def mesh_kernel(sizes, cells, pad_y, bounds_ref, atoms_ref, *refs):
    constants, (out_ref, *scratch) = refs[:fixed_arrays], refs[fixed_arrays:]
    held, copy_sem = scratch[-fixed_arrays - 1 : -1], scratch[-1]
    copies = [
        pltpu.make_async_copy(source, target, copy_sem.at[place])
        for place, (source, target) in enumerate(zip(constants, held))
    ]
    for copy in copies:
        copy.start()
    xh_ref, xl_ref, yh_ref, yl_ref, column_ref, row_ref, table_ref = held
    mesh_ref, stack_ref, prep_ref, deep_ref, steep_ref, near_ref, wy_ref, side_ref, level_ref, square_ref, scale_ref, work_ref = scratch[: -fixed_arrays - 1]
    count_x, count_y = sizes
    cells_x, cells_y = cells
    devices = count_x * count_y
    place = lax.axis_index("gx") * count_y + lax.axis_index("gy")
    tiles = atoms_ref.shape[2]
    depth = stack_ref.shape[0]
    window = 2 * cells_y
    windows = GRID_Y // window
    extra = 8
    mesh_ref[...] = jnp.zeros_like(mesh_ref)
    stack_ref[:, GRID_X:, :] = jnp.zeros_like(stack_ref[:, GRID_X:, :])
    out_ref[...] = jnp.zeros_like(out_ref)
    wy_ref[...] = jnp.zeros_like(wy_ref)
    copies[-1].wait()
    table = table_ref[pl.ds(pl.multiple_of(place * depth, 8), depth), :]

    steps_x = window_rows // 8
    most = (cells_x + 2) // 8 // steps_x + 1

    def prep_row(kind, spot):
        return prep_ref[pl.ds(kind * devices * tiles + spot, 8, stride=0), :]

    def prepare(cell, total):
        for tile in range(tiles):
            for step in range(most):
                work_ref[total + step] = (cell * tiles + tile) * most + step
            total = total + bounds_ref[cell, 0, tiles + tile]

        def keep(kind, value):
            rows = pl.ds(pl.multiple_of((kind * devices + cell) * tiles, 8), tiles)
            prep_ref[rows, :] = value

        for axis, count in enumerate((cells_x, cells_y)):
            value = atoms_ref[cell, axis]
            lowest = jnp.clip(jnp.floor(value), 0.0, count - 1.0)
            values, slopes = spline_weights(value - lowest)
            keep(9 * axis, lowest)
            for term in range(4):
                keep(9 * axis + 1 + term, values[term])
                keep(9 * axis + 5 + term, slopes[term])
        value = atoms_ref[cell, 2]
        height = jnp.floor(value)
        values, slopes = spline_weights(value - height)
        keep(18, height)
        for term in range(4):
            keep(19 + term, values[term])
            keep(23 + term, slopes[term])
        keep(27, atoms_ref[cell, 3])
        for tile in range(tiles):
            spot = cell * tiles + tile
            height = prep_row(18, spot)
            terms = [[prep_row(19 + 4 * s + term, spot) for term in range(4)] for s in range(2)]
            deep, steep = depth_rows(table, height, terms)
            rows = pl.ds(pl.multiple_of(spot * depth, 8), depth)
            deep_ref[rows, :] = deep
            steep_ref[rows, :] = steep
        return total

    total = lax.fori_loop(0, devices, prepare, jnp.int32(0))
    rounds = lax.div(total + group_size - 1, group_size)

    row_index = lax.broadcasted_iota(jnp.int32, (8, lanes), 0).astype(jnp.float32)

    def looked_up(points, lowest, term_lists):
        results = [jnp.zeros_like(points) for _ in term_lists]
        for term in range(4):
            hit = points == lowest + float(term)
            results = [
                jnp.where(hit, terms[term], result)
                for terms, result in zip(term_lists, results)
            ]
        return results

    def kinds(first, spot):
        return [prep_row(first + term, spot) for term in range(4)]

    stride = round_up(pad_y, 16)
    far_away = 1.0e6

    def task(index):
        entry = jnp.where(index < total, work_ref[index], 0)
        spot = lax.div(entry, most)
        cell = lax.div(spot, tiles)
        chunk = spot - cell * tiles
        begin = bounds_ref[cell, 0, chunk] * 8 + (entry - spot * most) * window_rows
        base = jnp.where(index < total, begin.astype(jnp.float32), far_away)
        i = lax.div(cell, count_y)
        rows = pl.ds(pl.multiple_of(i * cells_x + begin, 8), window_rows)
        return (spot, cell, chunk, cell - i * count_y, rows, base)

    def y_table(spot, kind):
        lowest = prep_row(9, spot)
        terms = kinds(kind, spot)
        for group in range(stride // 16):
            pieces = [
                looked_up(row_index + float(group * 16 + half * 8), lowest, [terms])[0]
                if group * 16 + half * 8 < pad_y
                else jnp.zeros_like(row_index)
                for half in range(2)
            ]
            yield (slice(group * 16, group * 16 + 16), *halves(jnp.concatenate(pieces, axis=0)))

    @pl.loop(0, rounds)
    def _(turn):
        tasks = [task(turn * group_size + place) for place in range(group_size)]
        for place, (spot, _, _, _, _, base) in enumerate(tasks):
            for rows, high, low in y_table(spot, 10):
                after = slice(window + rows.start, window + rows.stop)
                later = slice(stride + rows.start, stride + rows.stop)
                wy_ref[place, rows, :lanes] = high
                wy_ref[place, rows, lanes:] = high
                wy_ref[place, after, :lanes] = low
                near_ref[spot, rows, :] = high
                near_ref[spot, later, :] = low
            lowest = prep_row(0, spot) - base
            charge = prep_row(27, spot)
            terms = [term * charge for term in kinds(1, spot)]
            weights = [
                looked_up(row_index + float(tile * 8), lowest, [terms])[0]
                for tile in range(steps_x)
            ]
            modes = [
                deep_ref[pl.ds(spot * depth + k, 8, stride=0), :] for k in range(depth)
            ]
            blocks = [weight * mode for mode in modes for weight in weights]
            for pair in range(len(blocks) // 2):
                high, low = halves(jnp.concatenate(blocks[2 * pair : 2 * pair + 2], axis=0))
                rows = slice(pair * 16, pair * 16 + 16)
                side_ref[place, rows, :lanes] = high
                side_ref[place, rows, lanes:] = low
        for place, (_, _, _, j, rows, _) in enumerate(tasks):
            product = lax.dot_general(
                side_ref[place],
                wy_ref[place],
                (((1,), (1,)), ((), ())),
                preferred_element_type=jnp.float32,
            )
            product = product[:, :window] + product[:, window:]
            m = lax.div(j, 2)
            here = pl.ds(pl.multiple_of(m * window, lanes), window)
            mesh_ref[j - 2 * m, :, rows, here] += product.reshape(depth, window_rows, window)

    def across(value):
        high, low = halves(value)
        return dot(xh_ref[...], high) + dot(xl_ref[...], high) + dot(xh_ref[...], low)

    def along(value):
        high, low = halves(value)
        return dot(high, yh_ref[...]) + dot(high, yl_ref[...]) + dot(low, yh_ref[...])

    plane_lane = lax.broadcasted_iota(jnp.int32, (GRID_X, window), 1)

    for copy in copies[:-1]:
        copy.wait()
    shape = (GRID_X, GRID_Y)
    square_ref[...] = jnp.broadcast_to(column_ref[:, 0:1], shape) + row_ref[0:1, :]
    scale_ref[...] = jnp.broadcast_to(column_ref[:, 1:2], shape) * row_ref[1:2, :]

    def one_plane(k):
        charge = mesh_ref[0, k, :GRID_X, :] + pltpu.roll(mesh_ref[1, k, :GRID_X, :], cells_y, 1)
        over = slice(GRID_X, GRID_X + extra)
        beyond = mesh_ref[0, k, over, :] + pltpu.roll(mesh_ref[1, k, over, :], cells_y, 1)
        charge = jnp.concatenate([charge[:extra] + beyond, charge[extra:]], axis=0)
        waves = along(across(charge))
        mode = pl.ds(place * depth + k, 1)
        square = square_ref[...] + table_ref[mode, 9:10]
        scale = scale_ref[...] * table_ref[mode, 10:11]
        green = jnp.where(square > 0.0, scale / square, 0.0)
        plane = across(along(waves * green))
        for odd in range(2):
            if odd:
                plane = pltpu.roll(plane, GRID_Y - cells_y, 1)
            for j_half in range(windows):
                j = 2 * j_half + odd
                block = plane[:, j_half * window : (j_half + 1) * window]
                high = block.astype(jnp.bfloat16).astype(jnp.float32)
                low = block - high
                shifted = pltpu.roll(high, stride, 1)
                left = jnp.where(plane_lane < stride, high, shifted)
                right = jnp.where(
                    plane_lane < 2 * stride - window,
                    shifted,
                    pltpu.roll(low, 2 * stride - window, 1),
                )
                for side, value in enumerate((left, right)):
                    span = slice((2 * j + side) * window, (2 * j + side + 1) * window)
                    stack_ref[k, :GRID_X, span] = value
                    stack_ref[k, GRID_X : GRID_X + extra, span] = value[:extra]

    @pl.loop(0, depth // plane_group)
    def _(pair):
        for inner in range(plane_group):
            one_plane(pair * plane_group + inner)

    @pl.loop(0, rounds)
    def _(turn):
        tasks = [task(turn * group_size + place) for place in range(group_size)]
        blank = jnp.zeros((2 * window - 3 * stride, lanes), jnp.bfloat16)
        for place, (spot, _, _, j, rows, _) in enumerate(tasks):
            near = near_ref[spot]
            highs, lows = [], []
            for _, high, low in y_table(spot, 14):
                highs.append(high)
                lows.append(low)
            columns = jnp.concatenate(
                [
                    jnp.concatenate([near, near[:stride], blank], axis=0),
                    jnp.concatenate([*highs, *lows, *highs, blank], axis=0),
                ],
                axis=1,
            )
            span = pl.ds(pl.multiple_of(j * 2 * window, lanes), 2 * window)
            block = stack_ref[:, rows, span].reshape(depth * window_rows, 2 * window)
            level_ref[place] = dot(block.astype(jnp.bfloat16), columns)
        for place, (spot, cell, chunk, _, _, base) in enumerate(tasks):
            lowest = prep_row(0, spot) - base
            values = kinds(1, spot)
            slopes = kinds(5, spot)
            modes = [pl.ds(spot * depth + k, 8, stride=0) for k in range(depth)]
            deep = [deep_ref[mode, :] for mode in modes]
            steep = [steep_ref[mode, :] for mode in modes]
            zero = jnp.zeros((8, lanes), jnp.float32)
            sums = [zero, zero, zero]
            for tile in range(steps_x):
                weight, slope = looked_up(row_index + float(tile * 8), lowest, [values, slopes])
                parts = [zero, zero, zero]
                for k in range(depth):
                    at = slice(k * window_rows + tile * 8, k * window_rows + tile * 8 + 8)
                    flat = level_ref[place, at, :lanes]
                    tilt = level_ref[place, at, lanes:]
                    parts = [
                        parts[0] + deep[k] * flat,
                        parts[1] + deep[k] * tilt,
                        parts[2] + steep[k] * flat,
                    ]
                sums = [
                    sums[0] + slope * parts[0],
                    sums[1] + weight * parts[1],
                    sums[2] + weight * parts[2],
                ]
            for axis in range(3):
                out_ref[cell, axis, pl.ds(chunk, 1), :] += jnp.sum(
                    sums[axis], axis=0, keepdims=True
                )


def finish_kernel(sizes, cells, early, pairs_ref, partial_ref, atoms_ref, rank_ref, pair_ref, short_ref, long_ref, land_ref, column_ref, partner_ref, sum_ref, late_ref, order_ref, force_ref, send_sem, recv_sem):
    count_x, count_y = sizes
    place_x, place_y = (lax.axis_index("gx"), lax.axis_index("gy"))
    me = place_x * count_y + place_y
    peers = peers_of(count_x, count_y)
    barrier = pltpu.get_barrier_semaphore()
    for peer_x, peer_y in peers:
        pl.semaphore_signal(
            barrier,
            inc=1,
            device_id={"gx": peer_x, "gy": peer_y},
            device_id_type=pl.DeviceIdType.MESH,
        )
    clusters = pairs_ref.shape[2]
    atom_total = atoms_ref.shape[2]
    size = atom_total // clusters
    place_columns(me, atoms_ref, column_ref, early * size)
    place_partners(sizes, cells, pairs_ref, atoms_ref, partner_ref, range(early, clusters))
    pl.semaphore_wait(barrier, len(peers))
    copies = []
    for order, (peer_x, peer_y) in enumerate(peers):
        copy = pltpu.make_async_remote_copy(
            src_ref=partial_ref.at[peer_x * count_y + peer_y],
            dst_ref=land_ref.at[order],
            send_sem=send_sem.at[order],
            recv_sem=recv_sem.at[order],
            device_id={"gx": peer_x, "gy": peer_y},
            device_id_type=pl.DeviceIdType.MESH,
        )
        copy.start()
        copies.append(copy)
    for slot in range(clusters - early):
        pair_sums(slot, size, column_ref, partner_ref, sum_ref, late_ref, slot * size)
    own_charge = atoms_ref[me, 3:4, :]
    for axis in range(3):
        for half, source in enumerate((pair_ref, late_ref)):
            span = slice(0, early * size) if half == 0 else slice(early * size, atom_total)
            short_ref[axis, 0, :, span] = source[axis : axis + 1, :] * (
                own_charge[:, span] * spacing
            )
    rank = rank_ref[...]

    @pl.loop(0, atom_total // size)
    def _(block):
        place = lax.broadcasted_iota(jnp.int32, (size, atom_total), 0) + block * size
        order_ref[pl.ds(pl.multiple_of(block * size, size), size), :] = jnp.where(
            place.astype(jnp.float32) == rank, 1.0, 0.0
        ).astype(jnp.bfloat16)

    force_ref[...] = jnp.zeros_like(force_ref)
    for copy in copies:
        copy.wait()
    total = partial_ref[me]
    for order in range(len(peers)):
        total = total + land_ref[order]
    for part in range(3):
        piece = total.astype(jnp.bfloat16).astype(jnp.float32)
        total = total - piece
        for axis in range(3):
            for tile in range(atom_total // lanes):
                span = slice(tile * lanes, (tile + 1) * lanes)
                row = 4 * part + axis
                force_ref[row : row + 1, span] = piece[axis, tile : tile + 1, :]
    placed = dot(force_ref[...].astype(jnp.bfloat16), order_ref[...])
    placed = (placed[0:4] + placed[4:8]) + placed[8:12]
    for axis in range(3):
        long_ref[axis, 0, :, :] = placed[axis : axis + 1, :] * (own_charge * (-1.0 / spacing))


def finished(pair_lists, partial, raw, rank, pair_part, count_x, count_y, cells_x, cells_y):
    devices, _, atom_total = raw.shape
    clusters, listed = pair_lists.shape[2:]
    size = atom_total // clusters
    early = clusters // 2
    late = clusters - early
    vmem = pl.BlockSpec(memory_space=pltpu.VMEM)
    flags = pltpu.SemaphoreType.DMA((devices - 1,))
    return pl.pallas_call(
        functools.partial(finish_kernel, (count_x, count_y), (cells_x, cells_y), early),
        in_specs=[pl.BlockSpec(memory_space=pltpu.SMEM), vmem, vmem, vmem, vmem],
        out_specs=[vmem, vmem],
        out_shape=[jax.ShapeDtypeStruct((3, 1, 1, atom_total), jnp.float32)] * 2,
        scratch_shapes=[
            pltpu.VMEM((devices - 1, *partial.shape[1:]), jnp.float32),
            pltpu.VMEM((3, late * size, lanes), jnp.float32),
            pltpu.VMEM((late, 4, 8, listed * size), jnp.float32),
            pltpu.VMEM((3, size, lanes), jnp.float32),
            pltpu.VMEM((3, late * size), jnp.float32),
            pltpu.VMEM((atom_total, atom_total), jnp.bfloat16),
            pltpu.VMEM((16, atom_total), jnp.float32),
            flags,
            flags,
        ],
        compiler_params=pltpu.CompilerParams(
            collective_id=1, has_side_effects=True, vmem_limit_bytes=16 << 20
        ),
        name="finish",
    )(pair_lists, partial, raw, rank, pair_part)


def green_table(period):
    index = np.arange(period)
    signed = np.where(index <= period // 2, index, index - period) / (period * spacing)
    modulus = ((2.0 + np.cos(index * (2.0 * np.pi / period))) / 3.0) ** 2
    square = signed * signed
    return np.stack([square, np.exp(-((np.pi / ewald_split) ** 2) * square) / modulus]).astype(
        np.float32
    )


def green_factors(index, period):
    signed = jnp.where(index <= period // 2, index, index - period).astype(jnp.float32) / (
        period * spacing
    )
    modulus = ((2.0 + jnp.cos(index.astype(jnp.float32) * (2.0 * jnp.pi / period))) / 3.0) ** 2
    square = signed * signed
    return jnp.stack([square, jnp.exp(-((jnp.pi / ewald_split) ** 2) * square) / modulus])


def one_cluster(own_rows, partner):
    offsets = (own_rows[:3, :, None] - partner[:3, None, :]) * spacing
    dist_square = jnp.sum(offsets * offsets, axis=0)
    soft_square = dist_square + soft_core
    soft_dist = jnp.sqrt(soft_square)
    scaled = ewald_split * soft_dist
    strength = (
        jax.scipy.special.erfc(scaled) / soft_dist
        + ewald_split * root_factor * jnp.exp(-scaled * scaled)
    ) / soft_square
    cutoff_taper = jnp.where(
        dist_square < cutoff * cutoff, (1.0 - dist_square / (cutoff * cutoff)) ** 2, 0.0
    )
    weight = partner[3][None, :] * strength * cutoff_taper
    return own_rows[3] * jnp.sum(weight[None] * offsets, axis=2)


def far_by_planes(bounds, atoms, count_x, count_y, cells_x, cells_y):
    devices = count_x * count_y
    depth = GRID_Z // devices
    tiles = atoms.shape[2]
    pad_y = round_up(cells_y + 3, 8)
    stride = round_up(pad_y, 16)
    window = 2 * cells_y
    turn_x = halves(jnp.asarray(hartley(GRID_X)))
    turn_y = halves(jnp.asarray(hartley(GRID_Y)))
    volume = GRID_X * GRID_Y * GRID_Z * spacing**3
    column = jnp.asarray(green_table(GRID_X).T)
    row = jnp.asarray(green_table(GRID_Y))
    every_k = np.arange(GRID_Z)
    taps = np.outer(every_k, np.arange(4)) * (2.0 * np.pi / GRID_Z)
    square, scale = green_table(GRID_Z)
    table = np.concatenate(
        [
            every_k[:, None],
            np.cos(taps) + np.sin(taps),
            np.cos(taps) - np.sin(taps),
            square[:, None],
            scale[:, None] / (np.pi * volume),
        ],
        axis=1,
    ).astype(np.float32)
    vmem = pl.BlockSpec(memory_space=pltpu.VMEM)
    rows = GRID_X + window_rows
    batch = depth * window_rows
    constants = (*turn_x, *turn_y, column, row, jnp.asarray(table))
    fixed = pl.BlockSpec(memory_space=pltpu.HBM)
    return pl.pallas_call(
        functools.partial(mesh_kernel, (count_x, count_y), (cells_x, cells_y), pad_y),
        in_specs=[pl.BlockSpec(memory_space=pltpu.SMEM)] + [vmem] + [fixed] * fixed_arrays,
        out_specs=vmem,
        out_shape=jax.ShapeDtypeStruct((devices, 3, tiles, lanes), jnp.float32),
        scratch_shapes=[
            pltpu.VMEM((2, depth, rows, GRID_Y), jnp.float32),
            pltpu.VMEM((depth, rows, 4 * GRID_Y), jnp.float32),
            pltpu.VMEM((28 * devices * tiles, lanes), jnp.float32),
            pltpu.VMEM((devices * tiles * depth, lanes), jnp.float32),
            pltpu.VMEM((devices * tiles * depth, lanes), jnp.float32),
            pltpu.VMEM((devices * tiles, 2 * stride, lanes), jnp.bfloat16),
            pltpu.VMEM((group_size, 2 * window, 2 * lanes), jnp.bfloat16),
            pltpu.VMEM((group_size, batch, 2 * lanes), jnp.bfloat16),
            pltpu.VMEM((group_size, batch, 2 * lanes), jnp.float32),
            pltpu.VMEM((GRID_X, GRID_Y), jnp.float32),
            pltpu.VMEM((GRID_X, GRID_Y), jnp.float32),
            pltpu.SMEM((4 * devices * tiles,), jnp.int32),
            *[pltpu.VMEM(value.shape, value.dtype) for value in constants],
            pltpu.SemaphoreType.DMA((fixed_arrays,)),
        ],
        compiler_params=pltpu.CompilerParams(vmem_limit_bytes=36 << 20),
        name="mesh",
    )(
        bounds, atoms, *[pltpu.with_memory_space_constraint(value, pltpu.HBM) for value in constants]
    )


def convolved_by_lines(charge_mesh, count_x, count_y):
    turn_x = jnp.asarray(hartley(GRID_X))
    turn_y = jnp.asarray(hartley(GRID_Y))
    product = functools.partial(
        jnp.einsum, precision=lax.Precision.HIGHEST, preferred_element_type=jnp.float32
    )
    exchange = functools.partial(lax.all_to_all, tiled=True)
    lines = exchange(charge_mesh, "gx", split_axis=2, concat_axis=0)
    lines = product("xyk,xu->uyk", lines, turn_x)
    lines = exchange(lines, "gy", split_axis=0, concat_axis=1)
    lines = product("uyk,yv->uvk", lines, turn_y)
    wide, _, depth = lines.shape
    start_x = lax.axis_index("gy") * wide
    start_z = lax.axis_index("gx") * depth
    volume = GRID_X * GRID_Y * GRID_Z * spacing**3
    fx = green_factors(start_x + jnp.arange(wide, dtype=jnp.int32), GRID_X)
    fy = green_factors(jnp.arange(GRID_Y, dtype=jnp.int32), GRID_Y)
    fz = green_factors(start_z + jnp.arange(depth, dtype=jnp.int32), GRID_Z)
    square = fx[0][:, None, None] + fy[0][:, None] + fz[0]
    scale = fx[1][:, None, None] * fy[1][:, None] * fz[1] / (math.pi * volume)
    lines = lines * jnp.where(square > 0.0, scale / jnp.where(square > 0.0, square, 1.0), 0.0)
    lines = product("uvk,vy->uyk", lines, turn_y)
    lines = exchange(lines, "gy", split_axis=1, concat_axis=0)
    lines = product("uyk,ux->xyk", lines, turn_x)
    return exchange(lines, "gx", split_axis=0, concat_axis=2)


def far_by_lines(atoms, base, count_x, count_y, cells_x, cells_y, cells_z):
    atom_total = atoms.shape[1]
    cells = (cells_x, cells_y, cells_z)
    pad = (round_up(cells_x + 3, rows_group), round_up(cells_y + 3, 8))
    pad_x, pad_y = pad
    turn_z = jnp.asarray(hartley(GRID_Z))
    spread = pl.pallas_call(
        functools.partial(spread_kernel, cells, pad),
        out_shape=jax.ShapeDtypeStruct((pad_x, pad_y, GRID_Z), jnp.float32),
        scratch_shapes=[
            pltpu.VMEM((pad_x, atom_total), jnp.float32),
            pltpu.VMEM((pad_y, atom_total), jnp.float32),
            pltpu.VMEM((atom_total, 2 * GRID_Z), jnp.bfloat16),
            pltpu.VMEM((rows_group * pad_y, atom_total), jnp.bfloat16),
            pltpu.VMEM((rows_group * pad_y, atom_total), jnp.bfloat16),
        ],
        name="spread",
    )(atoms, base, turn_z)

    from_x = moved(spread[cells_x : cells_x + 3, :cells_y], 1, 0)
    from_y = moved(spread[:cells_x, cells_y : cells_y + 3], 0, 1)
    from_both = moved(spread[cells_x : cells_x + 3, cells_y : cells_y + 3], 1, 1)
    charge_mesh = (
        spread[:cells_x, :cells_y]
        .at[:3]
        .add(from_x)
        .at[:, :3]
        .add(from_y)
        .at[:3, :3]
        .add(from_both)
    )
    potential = convolved_by_lines(charge_mesh, count_x, count_y)
    upper_x = moved(potential[:3], -1, 0)
    upper_y = moved(potential[:, :3], 0, -1)
    upper_both = moved(potential[:3, :3], -1, -1)
    wider = jnp.concatenate(
        [
            jnp.concatenate([potential, upper_x], axis=0),
            jnp.concatenate([upper_y, upper_both], axis=0),
        ],
        axis=1,
    )
    wider = jnp.pad(wider, ((0, pad_x - cells_x - 3), (0, pad_y - cells_y - 3), (0, 0)))
    return pl.pallas_call(
        functools.partial(gather_kernel, cells, pad),
        out_shape=jax.ShapeDtypeStruct((3, atom_total), jnp.float32),
        scratch_shapes=[
            pltpu.VMEM((pad_x, atom_total), jnp.float32),
            pltpu.VMEM((pad_x, atom_total), jnp.float32),
            pltpu.VMEM((pad_y, atom_total), jnp.float32),
            pltpu.VMEM((pad_y, atom_total), jnp.float32),
            pltpu.VMEM((2 * GRID_Z, 2 * atom_total), jnp.bfloat16),
            pltpu.VMEM((rows_group * pad_y, 2 * atom_total), jnp.float32),
        ],
        name="gather",
    )(atoms, base, turn_z, wider)


def local(positions, charges, pair_lists, slab_dest, atom_counts):
    count_x = lax.axis_size("gx")
    count_y = lax.axis_size("gy")
    devices = count_x * count_y
    atom_total = positions.shape[3]
    clusters = pair_lists.shape[2]
    cluster_size = atom_total // clusters
    blocks = slab_dest.shape[2]
    block_size = atom_total // blocks
    cells_x = GRID_X // count_x
    cells_y = GRID_Y // count_y
    cells_z = GRID_Z // count_y
    by_planes = (
        GRID_Z == 8 * devices
        and cells_y == 64
        and cells_x % 8 == 0
        and cells_x <= 64
        and count_y % 2 == 0
        and clusters % 2 == 0
        and atom_total == 8 * lanes
        and cluster_size % lanes == 0
    )
    if by_planes:
        sizes = (count_x, count_y, cells_x, cells_y)
        raw, atoms, bounds, rank, pair_part = shared(
            positions, charges, pair_lists, atom_counts, *sizes
        )
        partial = far_by_planes(bounds, atoms, *sizes)
        return tuple(finished(pair_lists, partial, raw, rank, pair_part, *sizes))
    living = jnp.arange(atom_total, dtype=jnp.int32) < atom_counts[0, 0]
    charge = jnp.where(living, charges[0, 0], 0.0)
    packed = jnp.concatenate([positions, charge[None, None, None, :]], axis=0)
    atoms = packed.reshape(4, atom_total)
    base = jnp.broadcast_to(
        (slab_dest[0, 0] * cells_z)[:, None], (blocks, block_size)
    ).reshape(1, atom_total)
    gathered = lax.all_gather(atoms, ("gx", "gy"), axis=0, tiled=False)
    far_part = far_by_lines(atoms, base, count_x, count_y, cells_x, cells_y, cells_z)

    chosen = pair_lists[0, 0]
    beside = chosen // clusters
    step_x, step_y = (beside // 3 - 1, beside % 3 - 1)
    at_x = (lax.axis_index("gx") + step_x + count_x) % count_x
    at_y = (lax.axis_index("gy") + step_y + count_y) % count_y
    number = (at_x * count_y + at_y) * clusters + chosen % clusters
    pick = (number[:, :, None] == jnp.arange(devices * clusters, dtype=jnp.int32)).astype(
        jnp.float32
    )
    pool = gathered[:, :4].reshape(devices, 4, clusters, cluster_size)
    pool = jnp.transpose(pool, (1, 0, 2, 3)).reshape(4, devices * clusters, cluster_size)
    partners = jnp.einsum(
        "cln,fnk->cflk",
        pick,
        pool,
        precision=lax.Precision.HIGHEST,
        preferred_element_type=jnp.float32,
    )
    shift_x = (step_x * cells_x).astype(jnp.float32)
    shift_y = (step_y * cells_y).astype(jnp.float32)
    flat = jnp.zeros_like(shift_x)
    shift = jnp.stack([shift_x, shift_y, flat, flat], axis=1)
    partners = (partners + shift[:, :, :, None]).reshape(clusters, 4, -1)
    own = packed.reshape(4, clusters, cluster_size)
    pair_part = jnp.stack(
        [one_cluster(own[:, c], partners[c]) for c in range(clusters)], axis=1
    )
    short_forces = pair_part.reshape(3, 1, 1, atom_total)
    return (short_forces, far_part.reshape(3, 1, 1, atom_total))


def solution(mesh):
    return jax.shard_map(
        local,
        mesh=mesh,
        in_specs=(
            P(None, ("rep", "gx"), "gy", None),
            P(("rep", "gx"), "gy", None),
            P(("rep", "gx"), "gy", None, None),
            P(("rep", "gx"), "gy", None),
            P(("rep", "gx"), "gy"),
        ),
        out_specs=(P(None, ("rep", "gx"), "gy", None), P(None, ("rep", "gx"), "gy", None)),
        check_vma=False,
    )
```

```python
import functools
import math

import jax
import jax.numpy as jnp
import numpy as np
from jax import lax
from jax.experimental import pallas as pl
from jax.experimental.pallas import tpu as pltpu
from jax.sharding import PartitionSpec as P

GRID_X = 256
GRID_Y = 256
GRID_Z = 128


spacing = 0.16
ewald_split = 3.47
cutoff = 0.9
soft_core = 0.09
root_factor = 1.1283791670955126
rows_group = 8
lanes = 128
window_rows = 24
group_size = 8
cell_group = 2
plane_group = 4
fixed_arrays = 7


def moved(value, step_x, step_y):
    count_x = lax.axis_size("gx")
    count_y = lax.axis_size("gy")
    pairs = [
        (i * count_y + j, (i + step_x) % count_x * count_y + (j + step_y) % count_y)
        for i in range(count_x)
        for j in range(count_y)
    ]
    return lax.ppermute(value, ("gx", "gy"), pairs)


def round_up(value, multiple):
    return -(-value // multiple) * multiple


def hartley(period):
    turns = np.outer(np.arange(period), np.arange(period)) % period
    phases = turns * (2.0 * np.pi / period)
    return (np.cos(phases) + np.sin(phases)).astype(np.float32)


def halves(value):
    high = value.astype(jnp.bfloat16)
    low = (value - high.astype(jnp.float32)).astype(jnp.bfloat16)
    return (high, low)


def dot(left_side, right_side):
    return jnp.dot(left_side, right_side, preferred_element_type=jnp.float32)


def spline_weights(fraction):
    remain = 1.0 - fraction
    square = fraction * fraction
    cube_part = square * fraction
    values = [
        remain * remain * remain / 6.0,
        (3.0 * cube_part - 6.0 * square + 4.0) / 6.0,
        (-3.0 * cube_part + 3.0 * square + 3.0 * fraction + 1.0) / 6.0,
        cube_part / 6.0,
    ]
    slopes = [
        -0.5 * remain * remain,
        0.5 * (3.0 * square - 4.0 * fraction),
        0.5 * (-3.0 * square + 2.0 * fraction + 1.0),
        0.5 * square,
    ]
    return (values, slopes)


def split_cells(coordinate, offset, cell_count):
    inside = coordinate - offset
    lowest = jnp.clip(jnp.floor(inside).astype(jnp.int32), 0, cell_count - 1)
    return (lowest, inside - lowest.astype(inside.dtype))


def spline_table(lowest, values, table_size, period=None):
    points = lax.broadcasted_iota(jnp.int32, (table_size, lowest.shape[1]), 0)
    lookup = jnp.zeros(points.shape, jnp.float32)
    for spline_term in range(4):
        at = lowest + spline_term
        if period is not None:
            at = jnp.where(at >= period, at - period, at)
        lookup = jnp.where(points == at, values[spline_term], lookup)
    return lookup


def spread_kernel(cells, pad, atoms_ref, base_ref, turn_ref, out_ref, wx_ref, wy_ref, wz_ref, hi_ref, lo_ref):
    cells_x, cells_y, cells_z = cells
    pad_x, pad_y = pad
    atom_total = atoms_ref.shape[1]
    low_x, frac_x = split_cells(atoms_ref[0:1, :], 0.0, cells_x)
    low_y, frac_y = split_cells(atoms_ref[1:2, :], 0.0, cells_y)
    base = base_ref[...]
    low_z, frac_z = split_cells(atoms_ref[2:3, :], base.astype(jnp.float32), cells_z)
    wx_ref[...] = spline_table(low_x, spline_weights(frac_x)[0], pad_x) * atoms_ref[3:4, :]
    wy_ref[...] = spline_table(low_y, spline_weights(frac_y)[0], pad_y)
    turn = turn_ref[...]
    size_z = turn.shape[0]
    table_z = spline_table(base + low_z, spline_weights(frac_z)[0], size_z, size_z)
    waves = jnp.dot(
        turn, table_z, precision=lax.Precision.HIGHEST, preferred_element_type=jnp.float32
    ).T
    high, low = halves(waves)
    wz_ref[:, :size_z] = high
    wz_ref[:, size_z:] = low

    @pl.loop(0, pad_x // rows_group)
    def _(chunk):
        for inner in range(rows_group):
            row = wx_ref[pl.ds(chunk * rows_group + inner, 1), :]
            high, low = halves(row * wy_ref[...])
            hi_ref[pl.ds(inner * pad_y, pad_y), :] = high
            lo_ref[pl.ds(inner * pad_y, pad_y), :] = low
        both = dot(hi_ref[...], wz_ref[...])
        rest = dot(lo_ref[...], wz_ref[:, :size_z])
        total = both[:, :size_z] + both[:, size_z:] + rest
        out_ref[pl.ds(chunk * rows_group, rows_group)] = total.reshape(rows_group, pad_y, size_z)


def gather_kernel(cells, pad, atoms_ref, base_ref, turn_ref, mesh_ref, out_ref, wx_ref, vx_ref, wy_ref, vy_ref, wz_ref, level_ref):
    cells_x, cells_y, cells_z = cells
    pad_x, pad_y = pad
    atom_total = atoms_ref.shape[1]
    low_x, frac_x = split_cells(atoms_ref[0:1, :], 0.0, cells_x)
    low_y, frac_y = split_cells(atoms_ref[1:2, :], 0.0, cells_y)
    base = base_ref[...]
    low_z, frac_z = split_cells(atoms_ref[2:3, :], base.astype(jnp.float32), cells_z)
    values, slopes = spline_weights(frac_x)
    wx_ref[...] = spline_table(low_x, values, pad_x)
    vx_ref[...] = spline_table(low_x, slopes, pad_x)
    values, slopes = spline_weights(frac_y)
    wy_ref[...] = spline_table(low_y, values, pad_y)
    vy_ref[...] = spline_table(low_y, slopes, pad_y)
    values, slopes = spline_weights(frac_z)
    turn = turn_ref[...]
    size_z = turn.shape[0]
    for place, terms in enumerate((values, slopes)):
        table_z = spline_table(base + low_z, terms, size_z, size_z)
        waves = jnp.dot(
            turn, table_z, precision=lax.Precision.HIGHEST, preferred_element_type=jnp.float32
        )
        high, low = halves(waves)
        wz_ref[:size_z, pl.ds(place * atom_total, atom_total)] = high
        wz_ref[size_z:, pl.ds(place * atom_total, atom_total)] = low
    groups = pad_y // 8

    def one_chunk(chunk, sums):
        rows = mesh_ref[pl.ds(chunk * rows_group, rows_group)].reshape(rows_group * pad_y, size_z)
        high, low = halves(rows)
        level_ref[...] = dot(jnp.concatenate([high, high], axis=1), wz_ref[...]) + dot(
            low, wz_ref[:size_z, :]
        )
        first, second, third = sums
        for inner in range(rows_group):
            flat = level_ref[pl.ds(inner * pad_y, pad_y), :atom_total]
            tilt = level_ref[pl.ds(inner * pad_y, pad_y), atom_total:]
            across = wy_ref[...]
            part_x = jnp.sum((across * flat).reshape(groups, 8, atom_total), axis=0)
            part_y = jnp.sum((vy_ref[...] * flat).reshape(groups, 8, atom_total), axis=0)
            part_z = jnp.sum((across * tilt).reshape(groups, 8, atom_total), axis=0)
            weight = wx_ref[pl.ds(chunk * rows_group + inner, 1), :]
            slope = vx_ref[pl.ds(chunk * rows_group + inner, 1), :]
            first = first + slope * part_x
            second = second + weight * part_y
            third = third + weight * part_z
        return (first, second, third)

    zero = jnp.zeros((8, atom_total), jnp.float32)
    sums = lax.fori_loop(0, pad_x // rows_group, one_chunk, (zero, zero, zero))
    factor = -atoms_ref[3:4, :] / spacing
    for place in range(3):
        out_ref[pl.ds(place, 1), :] = factor * jnp.sum(sums[place], axis=0, keepdims=True)


def peers_of(count_x, count_y):
    place_x, place_y = (lax.axis_index("gx"), lax.axis_index("gy"))
    peers = []
    for order in range(1, count_x * count_y):
        peer_x = lax.rem(place_x + order // count_y, count_x)
        peer_y = lax.rem(place_y + order % count_y, count_y)
        peers.append((peer_x, peer_y))
    return peers


root_terms = (
    3.9164407301418542,
    -0.0037127819564810594,
    0.16802528315459195,
    -0.003061234121505335,
    -0.0076524954798020545,
    0.002268454833542123,
    -0.0003056487922112269,
    1.686888935413571e-05,
)


def pair_weight(square):
    soft_square = square * (spacing * spacing) + soft_core
    inverse = lax.rsqrt(soft_square)
    series = jnp.full_like(inverse, root_terms[-1])
    for term in root_terms[-2::-1]:
        series = series * inverse + term
    decay = jnp.exp(soft_square * (-ewald_split * ewald_split))
    taper = jnp.maximum(1.0 - square * (spacing * spacing / (cutoff * cutoff)), 0.0)
    return (decay * series) * (inverse * taper) ** 2


def row_sums(values):
    total = None
    ones = jnp.ones((16, values.shape[1]), jnp.bfloat16)
    for _ in range(3):
        part = values.astype(jnp.bfloat16)
        values = values - part.astype(jnp.float32)
        summed = lax.dot_general(
            ones, part, (((1,), (1,)), ((), ())), preferred_element_type=jnp.float32
        )
        total = summed if total is None else total + summed
    return total[0:1, :]


def place_partners(sizes, cells, pairs_ref, atoms_ref, partner_ref):
    count_x, count_y = sizes
    cells_x, cells_y = cells
    place_x, place_y = (lax.axis_index("gx"), lax.axis_index("gy"))
    clusters, listed = pairs_ref.shape[2:]
    size = atoms_ref.shape[2] // clusters
    for c in range(clusters):
        for n in range(1, listed):
            chosen = pairs_ref[0, 0, c, n]
            beside = lax.div(chosen, clusters)
            which = chosen - beside * clusters
            row_x = lax.div(beside, 3)
            step_x = row_x - 1
            step_y = beside - row_x * 3 - 1
            from_x = lax.rem(place_x + step_x + count_x, count_x)
            from_y = lax.rem(place_y + step_y + count_y, count_y)
            block = atoms_ref[from_x * count_y + from_y]
            part = block[:, :size]
            for k in range(1, clusters):
                part = jnp.where(which == k, block[:, k * size : (k + 1) * size], part)
            shifts = (
                (step_x * cells_x).astype(jnp.float32),
                (step_y * cells_y).astype(jnp.float32),
            )
            for axis in range(4):
                row = part[axis : axis + 1, :]
                if axis < 2:
                    row = row + shifts[axis]
                partner_ref[c, axis, :, (n - 1) * size : n * size] = jnp.broadcast_to(
                    row, (8, size)
                )


def pair_sums(clusters, size, height, column_ref, partner_ref, before_ref, sum_ref):
    @pl.loop(0, clusters)
    def _(c):
        @pl.loop(0, size // height)
        def _(step):
            for part in range(height // 8):
                start = c * size + step * height + part * 8
                rows = pl.ds(pl.multiple_of(start, 8), 8)
                own = [column_ref[axis, rows, :] for axis in range(3)]
                sums = [
                    jnp.zeros((8, lanes), jnp.float32)
                    if before_ref is None
                    else before_ref[axis, rows, :]
                    for axis in range(3)
                ]
                for tile in range(partner_ref.shape[3] // lanes):
                    span = slice(tile * lanes, (tile + 1) * lanes)
                    offsets = [own[axis] - partner_ref[c, axis, :, span] for axis in range(3)]
                    square = sum(offset * offset for offset in offsets)
                    weight = pair_weight(square) * partner_ref[c, 3, :, span]
                    sums = [total + weight * offset for total, offset in zip(sums, offsets)]
                for axis in range(3):
                    sum_ref[axis, rows, :] = sums[axis]


def share_kernel(sizes, cells, clusters, count_ref, position_ref, charge_ref, raw_ref, sorted_ref, bounds_ref, rank_ref, column_ref, sum_ref, key_ref, split_ref, partner_ref, raw_send, raw_recv, sort_send, sort_recv, mark_send, mark_recv):
    count_x, count_y = sizes
    cells_x, _ = cells
    place_x, place_y = (lax.axis_index("gx"), lax.axis_index("gy"))
    me = place_x * count_y + place_y
    place_chip, place_core = (place_y // 2, lax.rem(place_y, 2))
    chips = count_y // 2

    def at(step_x, step_chip, flip):
        peer_x = lax.rem(place_x + step_x, count_x)
        peer_chip = lax.rem(place_chip + step_chip, chips)
        peer_core = 1 - place_core if flip else place_core
        return (peer_x, peer_chip * 2 + peer_core)

    peers = peers_of(count_x, count_y)
    barrier = pltpu.get_barrier_semaphore()
    for peer_x, peer_y in peers:
        pl.semaphore_signal(
            barrier,
            inc=1,
            device_id={"gx": peer_x, "gy": peer_y},
            device_id_type=pl.DeviceIdType.MESH,
        )

    def sent(ref, owner, peer, send_sem, recv_sem, order, slot):
        return pltpu.make_async_remote_copy(
            src_ref=ref.at[owner],
            dst_ref=ref.at[owner],
            send_sem=send_sem.at[order],
            recv_sem=recv_sem.at[slot],
            device_id={"gx": peer[0], "gy": peer[1]},
            device_id_type=pl.DeviceIdType.MESH,
        )

    passed = []

    def passes(owner, peer):
        order = len(passed)
        copies = [
            sent(sorted_ref, owner, peer, sort_send, sort_recv, order, owner),
            sent(bounds_ref, owner, peer, mark_send, mark_recv, order, owner),
        ]
        for copy in copies:
            copy.start()
        passed.append(copies)

    def arrives(owner, peer):
        sent(sorted_ref, owner, peer, sort_send, sort_recv, 0, owner).wait_recv()
        sent(bounds_ref, owner, peer, mark_send, mark_recv, 0, owner).wait_recv()

    atom_total = charge_ref.shape[2]
    tiles = atom_total // lanes
    slot = lax.broadcasted_iota(jnp.int32, (1, atom_total), 1)
    living = slot < count_ref[0, 0]
    charge = jnp.where(living, charge_ref[0], 0.0)
    rows = [position_ref[axis, 0] for axis in range(3)] + [charge]
    for axis in range(4):
        raw_ref[me, pl.ds(axis, 1), :] = rows[axis]
    column = jnp.clip(jnp.floor(rows[0]), 0.0, cells_x - 1.0)
    key = jnp.where(living, column, float(cells_x)) * float(atom_total) + slot.astype(jnp.float32)
    for tile in range(tiles):
        span = slice(tile * lanes, (tile + 1) * lanes)
        key_ref[span, :] = jnp.broadcast_to(key[:, span], (lanes, lanes)).T
    wide = [
        jnp.broadcast_to(key[:, tile * lanes : (tile + 1) * lanes], (8, lanes))
        for tile in range(tiles)
    ]

    def count_group(group, totals):
        for inner in range(8):
            others = key_ref[pl.ds(pl.multiple_of(group * 64 + inner * 8, 8), 8), :]
            totals = tuple(
                total + jnp.where(others < own, 1.0, 0.0) for total, own in zip(totals, wide)
            )
        return totals

    zero = jnp.zeros((8, lanes), jnp.float32)
    totals = lax.fori_loop(0, atom_total // 64, count_group, (zero,) * tiles)
    for tile, total in enumerate(totals):
        rank_ref[:, tile * lanes : (tile + 1) * lanes] = jnp.sum(total, axis=0, keepdims=True)

    split_ref[...] = jnp.zeros_like(split_ref)
    rest = raw_ref[me]
    for part in range(3):
        piece = rest.astype(jnp.bfloat16).astype(jnp.float32)
        split_ref[4 * part : 4 * part + 4, :] = piece
        rest = rest - piece
    split = split_ref[...].astype(jnp.bfloat16)
    rank = rank_ref[...]
    block = 2 * lanes
    for part in range(atom_total // block):
        place = lax.broadcasted_iota(jnp.int32, (block, atom_total), 0) + part * block
        chosen = jnp.where(place.astype(jnp.float32) == rank, 1.0, 0.0).astype(jnp.bfloat16)
        found = lax.dot_general(
            split, chosen, (((1,), (1,)), ((), ())), preferred_element_type=jnp.float32
        )
        found = (found[0:4] + found[4:8]) + found[8:12]
        for tile in range(block // lanes):
            row = part * (block // lanes) + tile
            for axis in range(4):
                sorted_ref[me, axis, row : row + 1, :] = found[
                    axis : axis + 1, tile * lanes : (tile + 1) * lanes
                ]
    spot = lax.broadcasted_iota(jnp.int32, (tiles, lanes), 0) * lanes
    spot = spot + lax.broadcasted_iota(jnp.int32, (tiles, lanes), 1)
    inside = spot < count_ref[0, 0]
    column = jnp.clip(jnp.floor(sorted_ref[me, 0]), 0.0, cells_x - 1.0)
    lowest = jnp.min(jnp.where(inside, column, float(cells_x)), axis=1, keepdims=True)
    highest = jnp.max(jnp.where(inside, column, -1.0), axis=1, keepdims=True)
    first = jnp.floor(lowest * 0.125)
    last = jnp.floor((highest + 3.0) * 0.125)
    windows = jnp.where(
        highest >= 0.0, jnp.floor((last - first) * (8.0 / window_rows) + 0.01) + 1.0, 0.0
    )
    lane = lax.broadcasted_iota(jnp.int32, (tiles, lanes), 1)
    row = lax.broadcasted_iota(jnp.int32, (tiles, lanes), 0)
    marks = jnp.where(lane == row, first, jnp.where(lane == row + tiles, windows, 0.0))
    marks = jnp.sum(marks, axis=0, keepdims=True)
    bounds_ref[me] = marks.astype(jnp.int32)

    near = sorted(
        (min(step, count_x - step) + min(chip, chips - chip), step, chip)
        for step in range(count_x)
        for chip in range(chips)
    )[1:]
    mate = at(0, 0, True)
    pl.semaphore_wait(barrier, len(peers))
    for _, step, chip in reversed(near):
        passes(me, at(step, chip, False))
    passes(me, mate)
    beside = sorted(
        {
            step_x % count_x * count_y + step_y % count_y
            for step_x in (-1, 0, 1)
            for step_y in (-1, 0, 1)
        }
        - {0}
    )
    copies = [
        sent(raw_ref, me, peers[order - 1], raw_send, raw_recv, order - 1, order - 1)
        for order in beside
    ]
    for copy in copies:
        copy.start()

    for axis in range(3):
        for tile in range(tiles):
            span = slice(tile * lanes, (tile + 1) * lanes)
            column_ref[axis, span, :] = jnp.broadcast_to(rows[axis][:, span], (lanes, lanes)).T
    size = atom_total // clusters
    for c in range(clusters):
        for axis in range(4):
            row = rows[axis][:, c * size : (c + 1) * size]
            partner_ref[c, axis] = jnp.broadcast_to(row, (8, size))
    pair_sums(clusters, size, 64, column_ref, partner_ref, None, sum_ref)
    for _, step, chip in near:
        owner_x, owner_y = at(step, chip, False)
        arrives(owner_x * count_y + owner_y, (owner_x, owner_y))
        passes(owner_x * count_y + owner_y, mate)
    for _, step, chip in [(0, 0, 0), *near]:
        owner_x, owner_y = at(step, chip, True)
        arrives(owner_x * count_y + owner_y, mate)
    for copy in copies:
        copy.wait()
    for pair in passed:
        for copy in pair:
            copy.wait_send()


def shared(positions, charges, atom_counts, clusters, count_x, count_y, cells_x, cells_y):
    devices = count_x * count_y
    atom_total = charges.shape[2]
    vmem = pl.BlockSpec(memory_space=pltpu.VMEM)
    smem = pl.BlockSpec(memory_space=pltpu.SMEM)
    fewer = pltpu.SemaphoreType.DMA((devices - 1,))
    flags = pltpu.SemaphoreType.DMA((devices,))
    return pl.pallas_call(
        functools.partial(share_kernel, (count_x, count_y), (cells_x, cells_y), clusters),
        in_specs=[smem, vmem, vmem],
        out_specs=[vmem] * 6,
        out_shape=[
            jax.ShapeDtypeStruct((devices, 4, atom_total), jnp.float32),
            jax.ShapeDtypeStruct((devices, 4, atom_total // lanes, lanes), jnp.float32),
            jax.ShapeDtypeStruct((devices, 1, lanes), jnp.int32),
            jax.ShapeDtypeStruct((1, atom_total), jnp.float32),
            jax.ShapeDtypeStruct((3, atom_total, lanes), jnp.float32),
            jax.ShapeDtypeStruct((3, atom_total, lanes), jnp.float32),
        ],
        scratch_shapes=[
            pltpu.VMEM((atom_total, lanes), jnp.float32),
            pltpu.VMEM((16, atom_total), jnp.float32),
            pltpu.VMEM((clusters, 4, 8, atom_total // clusters), jnp.float32),
            fewer,
            fewer,
        ]
        + [flags] * 4,
        compiler_params=pltpu.CompilerParams(
            collective_id=0, has_side_effects=True, vmem_limit_bytes=12 << 20
        ),
        name="share",
    )(
        atom_counts,
        *[pltpu.with_memory_space_constraint(value, pltpu.HBM) for value in (positions, charges)],
    )


def depth_rows(table, height, terms):
    turns = height * table[:, 0:1]
    quarter = GRID_Z // 4
    nearest = jnp.floor(turns * (1.0 / quarter) + 0.5)
    angle = (turns - nearest * quarter) * (2.0 * math.pi / GRID_Z)
    quadrant = nearest - 4.0 * jnp.floor(nearest * 0.25)
    square = angle * angle
    near_cos = 1.0 + square * (
        -0.5 + square * (1.0 / 24.0 + square * (-1.0 / 720.0 + square * (1.0 / 40320.0)))
    )
    near_sin = angle * (
        1.0
        + square
        * (-1.0 / 6.0 + square * (1.0 / 120.0 + square * (-1.0 / 5040.0 + square / 362880.0)))
    )
    odd_turn = (quadrant == 1.0) | (quadrant == 3.0)
    cosine = jnp.where(odd_turn, near_sin, near_cos)
    cosine = jnp.where((quadrant == 1.0) | (quadrant == 2.0), -cosine, cosine)
    sine = jnp.where(odd_turn, near_cos, near_sin)
    sine = jnp.where(quadrant >= 2.0, -sine, sine)
    results = []
    for weights in terms:
        even = sum(table[:, 1 + t : 2 + t] * weights[t] for t in range(4))
        odd = sum(table[:, 5 + t : 6 + t] * weights[t] for t in range(4))
        results.append(cosine * even + sine * odd)
    return results


def mesh_kernel(sizes, cells, pad_y, bounds_ref, atoms_ref, *refs):
    constants, (out_ref, *scratch) = refs[:fixed_arrays], refs[fixed_arrays:]
    held, copy_sem = scratch[-fixed_arrays - 1 : -1], scratch[-1]
    copies = [
        pltpu.make_async_copy(source, target, copy_sem.at[place])
        for place, (source, target) in enumerate(zip(constants, held))
    ]
    for copy in copies:
        copy.start()
    xh_ref, xl_ref, yh_ref, yl_ref, column_ref, row_ref, table_ref = held
    mesh_ref, stack_ref, prep_ref, deep_ref, steep_ref, near_ref, wy_ref, side_ref, level_ref, square_ref, scale_ref, work_ref = scratch[: -fixed_arrays - 1]
    count_x, count_y = sizes
    cells_x, cells_y = cells
    devices = count_x * count_y
    place = lax.axis_index("gx") * count_y + lax.axis_index("gy")
    tiles = atoms_ref.shape[2]
    depth = stack_ref.shape[0]
    window = 2 * cells_y
    windows = GRID_Y // window
    extra = 8
    stack_ref[:, GRID_X:, :] = jnp.zeros_like(stack_ref[:, GRID_X:, :])
    out_ref[...] = jnp.zeros_like(out_ref)
    copies[-1].wait()
    table = table_ref[pl.ds(pl.multiple_of(place * depth, 8), depth), :]

    steps_x = window_rows // 8
    most = (cells_x + 2) // 8 // steps_x + 1

    def prep_row(kind, spot):
        return prep_ref[pl.ds(kind * devices * tiles + spot, 8, stride=0), :]

    def listed_work(cell, total):
        for tile in range(tiles):
            for step in range(most):
                work_ref[total + step] = (cell * tiles + tile) * most + step
            total = total + bounds_ref[cell, 0, tiles + tile]

        return total

    def keep_splines(cell):
        def keep(kind, value):
            rows = pl.ds(pl.multiple_of((kind * devices + cell) * tiles, 8), tiles)
            prep_ref[rows, :] = value

        for axis, count in enumerate((cells_x, cells_y)):
            value = atoms_ref[cell, axis]
            lowest = jnp.clip(jnp.floor(value), 0.0, count - 1.0)
            values, slopes = spline_weights(value - lowest)
            keep(9 * axis, lowest)
            for term in range(4):
                keep(9 * axis + 1 + term, values[term])
                keep(9 * axis + 5 + term, slopes[term])
        value = atoms_ref[cell, 2]
        height = jnp.floor(value)
        values, slopes = spline_weights(value - height)
        keep(18, height)
        for term in range(4):
            keep(19 + term, values[term])
            keep(23 + term, slopes[term])
        keep(27, atoms_ref[cell, 3])

    def keep_modes(cell):
        for tile in range(tiles):
            spot = cell * tiles + tile
            height = prep_row(18, spot)
            terms = [[prep_row(19 + 4 * s + term, spot) for term in range(4)] for s in range(2)]
            deep, steep = depth_rows(table, height, terms)
            rows = pl.ds(pl.multiple_of(spot * depth, 8), depth)
            deep_ref[rows, :] = deep
            steep_ref[rows, :] = steep

    def prepare_some(turn, total):
        for inner in range(cell_group):
            cell = turn * cell_group + inner
            mesh_ref[lax.div(cell, depth), lax.rem(cell, depth)] = jnp.zeros(
                mesh_ref.shape[2:], jnp.float32
            )
            total = listed_work(cell, total)
        for inner in range(cell_group):
            keep_splines(turn * cell_group + inner)
        for inner in range(cell_group):
            keep_modes(turn * cell_group + inner)
        place = turn * group_size // (devices // cell_group)
        wy_ref[place] = jnp.zeros(wy_ref.shape[1:], wy_ref.dtype)
        return total

    total = lax.fori_loop(0, devices // cell_group, prepare_some, jnp.int32(0))
    rounds = lax.div(total + group_size - 1, group_size)

    row_index = lax.broadcasted_iota(jnp.int32, (8, lanes), 0).astype(jnp.float32)

    def looked_up(points, lowest, term_lists):
        results = [jnp.zeros_like(points) for _ in term_lists]
        for term in range(4):
            hit = points == lowest + float(term)
            results = [
                jnp.where(hit, terms[term], result)
                for terms, result in zip(term_lists, results)
            ]
        return results

    def kinds(first, spot):
        return [prep_row(first + term, spot) for term in range(4)]

    stride = round_up(pad_y, 16)
    far_away = 1.0e6

    def task(index):
        entry = jnp.where(index < total, work_ref[index], 0)
        spot = lax.div(entry, most)
        cell = lax.div(spot, tiles)
        chunk = spot - cell * tiles
        begin = bounds_ref[cell, 0, chunk] * 8 + (entry - spot * most) * window_rows
        base = jnp.where(index < total, begin.astype(jnp.float32), far_away)
        i = lax.div(cell, count_y)
        rows = pl.ds(pl.multiple_of(i * cells_x + begin, 8), window_rows)
        return (spot, cell, chunk, cell - i * count_y, rows, base)

    def y_table(spot, kind):
        lowest = prep_row(9, spot)
        terms = kinds(kind, spot)
        for group in range(stride // 16):
            pieces = [
                looked_up(row_index + float(group * 16 + half * 8), lowest, [terms])[0]
                if group * 16 + half * 8 < pad_y
                else jnp.zeros_like(row_index)
                for half in range(2)
            ]
            yield (slice(group * 16, group * 16 + 16), *halves(jnp.concatenate(pieces, axis=0)))

    @pl.loop(0, rounds)
    def _(turn):
        tasks = [task(turn * group_size + place) for place in range(group_size)]
        for place, (spot, _, _, _, _, base) in enumerate(tasks):
            for rows, high, low in y_table(spot, 10):
                after = slice(window + rows.start, window + rows.stop)
                later = slice(stride + rows.start, stride + rows.stop)
                wy_ref[place, rows, :lanes] = high
                wy_ref[place, rows, lanes:] = high
                wy_ref[place, after, :lanes] = low
                near_ref[spot, rows, :] = high
                near_ref[spot, later, :] = low
            lowest = prep_row(0, spot) - base
            charge = prep_row(27, spot)
            terms = [term * charge for term in kinds(1, spot)]
            weights = [
                looked_up(row_index + float(tile * 8), lowest, [terms])[0]
                for tile in range(steps_x)
            ]
            modes = [
                deep_ref[pl.ds(spot * depth + k, 8, stride=0), :] for k in range(depth)
            ]
            blocks = [weight * mode for mode in modes for weight in weights]
            for pair in range(len(blocks) // 2):
                high, low = halves(jnp.concatenate(blocks[2 * pair : 2 * pair + 2], axis=0))
                rows = slice(pair * 16, pair * 16 + 16)
                side_ref[place, rows, :lanes] = high
                side_ref[place, rows, lanes:] = low
        for place, (_, _, _, j, rows, _) in enumerate(tasks):
            product = lax.dot_general(
                side_ref[place],
                wy_ref[place],
                (((1,), (1,)), ((), ())),
                preferred_element_type=jnp.float32,
            )
            product = product[:, :window] + product[:, window:]
            m = lax.div(j, 2)
            here = pl.ds(pl.multiple_of(m * window, lanes), window)
            mesh_ref[j - 2 * m, :, rows, here] += product.reshape(depth, window_rows, window)

    def across(value):
        high, low = halves(value)
        return dot(xh_ref[...], high) + dot(xl_ref[...], high) + dot(xh_ref[...], low)

    def along(value):
        high, low = halves(value)
        return dot(high, yh_ref[...]) + dot(high, yl_ref[...]) + dot(low, yh_ref[...])

    plane_lane = lax.broadcasted_iota(jnp.int32, (GRID_X, window), 1)
    for copy in copies[:-1]:
        copy.wait()
    shape = (GRID_X, GRID_Y)
    square_ref[...] = jnp.broadcast_to(column_ref[:, 0:1], shape) + row_ref[0:1, :]
    scale_ref[...] = jnp.broadcast_to(column_ref[:, 1:2], shape) * row_ref[1:2, :]

    def charge_of(k):
        charge = mesh_ref[0, k, :GRID_X, :] + pltpu.roll(mesh_ref[1, k, :GRID_X, :], cells_y, 1)
        over = slice(GRID_X, GRID_X + extra)
        beyond = mesh_ref[0, k, over, :] + pltpu.roll(mesh_ref[1, k, over, :], cells_y, 1)
        return jnp.concatenate([charge[:extra] + beyond, charge[extra:]], axis=0)

    def green_of(k):
        mode = pl.ds(place * depth + k, 1)
        square = square_ref[...] + table_ref[mode, 9:10]
        scale = scale_ref[...] * table_ref[mode, 10:11]
        return jnp.where(square > 0.0, scale / square, 0.0)

    def place_plane(k, plane):
        for odd in range(2):
            if odd:
                plane = pltpu.roll(plane, GRID_Y - cells_y, 1)
            for j_half in range(windows):
                j = 2 * j_half + odd
                block = plane[:, j_half * window : (j_half + 1) * window]
                high = block.astype(jnp.bfloat16).astype(jnp.float32)
                low = block - high
                shifted = pltpu.roll(high, stride, 1)
                left = jnp.where(plane_lane < stride, high, shifted)
                right = jnp.where(
                    plane_lane < 2 * stride - window,
                    shifted,
                    pltpu.roll(low, 2 * stride - window, 1),
                )
                for side, value in enumerate((left, right)):
                    span = slice((2 * j + side) * window, (2 * j + side + 1) * window)
                    stack_ref[k, :GRID_X, span] = value
                    stack_ref[k, GRID_X : GRID_X + extra, span] = value[:extra]

    @pl.loop(0, depth // plane_group)
    def _(pair):
        spots = [pair * plane_group + inner for inner in range(plane_group)]
        values = [across(charge_of(k)) for k in spots]
        values = [along(value) for value in values]
        values = [along(value * green_of(k)) for k, value in zip(spots, values)]
        values = [across(value) for value in values]
        for k, value in zip(spots, values):
            place_plane(k, value)

    @pl.loop(0, rounds)
    def _(turn):
        tasks = [task(turn * group_size + place) for place in range(group_size)]
        blank = jnp.zeros((2 * window - 3 * stride, lanes), jnp.bfloat16)
        for place, (spot, _, _, j, rows, _) in enumerate(tasks):
            near = near_ref[spot]
            highs, lows = [], []
            for _, high, low in y_table(spot, 14):
                highs.append(high)
                lows.append(low)
            columns = jnp.concatenate(
                [
                    jnp.concatenate([near, near[:stride], blank], axis=0),
                    jnp.concatenate([*highs, *lows, *highs, blank], axis=0),
                ],
                axis=1,
            )
            span = pl.ds(pl.multiple_of(j * 2 * window, lanes), 2 * window)
            block = stack_ref[:, rows, span].reshape(depth * window_rows, 2 * window)
            level_ref[place] = dot(block.astype(jnp.bfloat16), columns)
        for place, (spot, cell, chunk, _, _, base) in enumerate(tasks):
            lowest = prep_row(0, spot) - base
            values = kinds(1, spot)
            slopes = kinds(5, spot)
            modes = [pl.ds(spot * depth + k, 8, stride=0) for k in range(depth)]
            deep = [deep_ref[mode, :] for mode in modes]
            steep = [steep_ref[mode, :] for mode in modes]
            zero = jnp.zeros((8, lanes), jnp.float32)
            sums = [zero, zero, zero]
            for tile in range(steps_x):
                weight, slope = looked_up(row_index + float(tile * 8), lowest, [values, slopes])
                parts = [zero, zero, zero]
                for k in range(depth):
                    at = slice(k * window_rows + tile * 8, k * window_rows + tile * 8 + 8)
                    flat = level_ref[place, at, :lanes]
                    tilt = level_ref[place, at, lanes:]
                    parts = [
                        parts[0] + deep[k] * flat,
                        parts[1] + deep[k] * tilt,
                        parts[2] + steep[k] * flat,
                    ]
                sums = [
                    sums[0] + slope * parts[0],
                    sums[1] + weight * parts[1],
                    sums[2] + weight * parts[2],
                ]
            for axis in range(3):
                out_ref[cell, axis, pl.ds(chunk, 1), :] += jnp.sum(
                    sums[axis], axis=0, keepdims=True
                )


def finish_kernel(sizes, cells, pairs_ref, partial_ref, atoms_ref, rank_ref, column_ref, before_ref, short_ref, long_ref, land_ref, partner_ref, sum_ref, order_ref, force_ref, send_sem, recv_sem):
    count_x, count_y = sizes
    place_x, place_y = (lax.axis_index("gx"), lax.axis_index("gy"))
    me = place_x * count_y + place_y
    peers = peers_of(count_x, count_y)
    barrier = pltpu.get_barrier_semaphore()
    for peer_x, peer_y in peers:
        pl.semaphore_signal(
            barrier,
            inc=1,
            device_id={"gx": peer_x, "gy": peer_y},
            device_id_type=pl.DeviceIdType.MESH,
        )
    clusters = pairs_ref.shape[2]
    atom_total = atoms_ref.shape[2]
    size = atom_total // clusters
    place_partners(sizes, cells, pairs_ref, atoms_ref, partner_ref)
    pl.semaphore_wait(barrier, len(peers))
    copies = []
    for order, (peer_x, peer_y) in enumerate(peers):
        copy = pltpu.make_async_remote_copy(
            src_ref=partial_ref.at[peer_x * count_y + peer_y],
            dst_ref=land_ref.at[order],
            send_sem=send_sem.at[order],
            recv_sem=recv_sem.at[order],
            device_id={"gx": peer_x, "gy": peer_y},
            device_id_type=pl.DeviceIdType.MESH,
        )
        copy.start()
        copies.append(copy)
    pair_sums(clusters, size, 32, column_ref, partner_ref, before_ref, sum_ref)
    own_charge = atoms_ref[me, 3:4, :]
    for axis in range(3):
        for c in range(clusters):
            span = slice(c * size, (c + 1) * size)
            summed = row_sums(sum_ref[axis, span, :])
            short_ref[axis, 0, :, span] = summed * (own_charge[:, span] * spacing)
    rank = rank_ref[...]

    @pl.loop(0, atom_total // size)
    def _(block):
        place = lax.broadcasted_iota(jnp.int32, (size, atom_total), 0) + block * size
        order_ref[pl.ds(pl.multiple_of(block * size, size), size), :] = jnp.where(
            place.astype(jnp.float32) == rank, 1.0, 0.0
        ).astype(jnp.bfloat16)

    force_ref[...] = jnp.zeros_like(force_ref)
    for copy in copies:
        copy.wait()
    total = partial_ref[me]
    for order in range(len(peers)):
        total = total + land_ref[order]
    for part in range(3):
        piece = total.astype(jnp.bfloat16).astype(jnp.float32)
        total = total - piece
        for axis in range(3):
            for tile in range(atom_total // lanes):
                span = slice(tile * lanes, (tile + 1) * lanes)
                row = 4 * part + axis
                force_ref[row : row + 1, span] = piece[axis, tile : tile + 1, :]
    placed = dot(force_ref[...].astype(jnp.bfloat16), order_ref[...])
    placed = (placed[0:4] + placed[4:8]) + placed[8:12]
    for axis in range(3):
        long_ref[axis, 0, :, :] = placed[axis : axis + 1, :] * (own_charge * (-1.0 / spacing))


def finished(pair_lists, partial, raw, rank, columns, before, count_x, count_y, cells_x, cells_y):
    devices, _, atom_total = raw.shape
    clusters, listed = pair_lists.shape[2:]
    size = atom_total // clusters
    vmem = pl.BlockSpec(memory_space=pltpu.VMEM)
    flags = pltpu.SemaphoreType.DMA((devices - 1,))
    return pl.pallas_call(
        functools.partial(finish_kernel, (count_x, count_y), (cells_x, cells_y)),
        in_specs=[pl.BlockSpec(memory_space=pltpu.SMEM)] + [vmem] * 5,
        out_specs=[vmem, vmem],
        out_shape=[jax.ShapeDtypeStruct((3, 1, 1, atom_total), jnp.float32)] * 2,
        scratch_shapes=[
            pltpu.VMEM((devices - 1, *partial.shape[1:]), jnp.float32),
            pltpu.VMEM((clusters, 4, 8, (listed - 1) * size), jnp.float32),
            pltpu.VMEM((3, atom_total, lanes), jnp.float32),
            pltpu.VMEM((atom_total, atom_total), jnp.bfloat16),
            pltpu.VMEM((16, atom_total), jnp.float32),
            flags,
            flags,
        ],
        compiler_params=pltpu.CompilerParams(
            collective_id=1, has_side_effects=True, vmem_limit_bytes=16 << 20
        ),
        name="finish",
    )(
        pltpu.with_memory_space_constraint(pair_lists, pltpu.HBM),
        partial,
        raw,
        rank,
        columns,
        before,
    )


def green_table(period):
    index = np.arange(period)
    signed = np.where(index <= period // 2, index, index - period) / (period * spacing)
    modulus = ((2.0 + np.cos(index * (2.0 * np.pi / period))) / 3.0) ** 2
    square = signed * signed
    return np.stack([square, np.exp(-((np.pi / ewald_split) ** 2) * square) / modulus]).astype(
        np.float32
    )


def green_factors(index, period):
    signed = jnp.where(index <= period // 2, index, index - period).astype(jnp.float32) / (
        period * spacing
    )
    modulus = ((2.0 + jnp.cos(index.astype(jnp.float32) * (2.0 * jnp.pi / period))) / 3.0) ** 2
    square = signed * signed
    return jnp.stack([square, jnp.exp(-((jnp.pi / ewald_split) ** 2) * square) / modulus])


def one_cluster(own_rows, partner):
    offsets = (own_rows[:3, :, None] - partner[:3, None, :]) * spacing
    dist_square = jnp.sum(offsets * offsets, axis=0)
    soft_square = dist_square + soft_core
    soft_dist = jnp.sqrt(soft_square)
    scaled = ewald_split * soft_dist
    strength = (
        jax.scipy.special.erfc(scaled) / soft_dist
        + ewald_split * root_factor * jnp.exp(-scaled * scaled)
    ) / soft_square
    cutoff_taper = jnp.where(
        dist_square < cutoff * cutoff, (1.0 - dist_square / (cutoff * cutoff)) ** 2, 0.0
    )
    weight = partner[3][None, :] * strength * cutoff_taper
    return own_rows[3] * jnp.sum(weight[None] * offsets, axis=2)


def far_by_planes(bounds, atoms, count_x, count_y, cells_x, cells_y):
    devices = count_x * count_y
    depth = GRID_Z // devices
    tiles = atoms.shape[2]
    pad_y = round_up(cells_y + 3, 8)
    stride = round_up(pad_y, 16)
    window = 2 * cells_y
    turn_x = halves(jnp.asarray(hartley(GRID_X)))
    turn_y = halves(jnp.asarray(hartley(GRID_Y)))
    volume = GRID_X * GRID_Y * GRID_Z * spacing**3
    column = jnp.asarray(green_table(GRID_X).T)
    row = jnp.asarray(green_table(GRID_Y))
    every_k = np.arange(GRID_Z)
    taps = np.outer(every_k, np.arange(4)) * (2.0 * np.pi / GRID_Z)
    square, scale = green_table(GRID_Z)
    table = np.concatenate(
        [
            every_k[:, None],
            np.cos(taps) + np.sin(taps),
            np.cos(taps) - np.sin(taps),
            square[:, None],
            scale[:, None] / (np.pi * volume),
        ],
        axis=1,
    ).astype(np.float32)
    vmem = pl.BlockSpec(memory_space=pltpu.VMEM)
    rows = GRID_X + window_rows
    batch = depth * window_rows
    constants = (*turn_x, *turn_y, column, row, jnp.asarray(table))
    fixed = pl.BlockSpec(memory_space=pltpu.HBM)
    return pl.pallas_call(
        functools.partial(mesh_kernel, (count_x, count_y), (cells_x, cells_y), pad_y),
        in_specs=[pl.BlockSpec(memory_space=pltpu.SMEM)] + [vmem] + [fixed] * fixed_arrays,
        out_specs=vmem,
        out_shape=jax.ShapeDtypeStruct((devices, 3, tiles, lanes), jnp.float32),
        scratch_shapes=[
            pltpu.VMEM((2, depth, rows, GRID_Y), jnp.float32),
            pltpu.VMEM((depth, rows, 4 * GRID_Y), jnp.float32),
            pltpu.VMEM((28 * devices * tiles, lanes), jnp.float32),
            pltpu.VMEM((devices * tiles * depth, lanes), jnp.float32),
            pltpu.VMEM((devices * tiles * depth, lanes), jnp.float32),
            pltpu.VMEM((devices * tiles, 2 * stride, lanes), jnp.bfloat16),
            pltpu.VMEM((group_size, 2 * window, 2 * lanes), jnp.bfloat16),
            pltpu.VMEM((group_size, batch, 2 * lanes), jnp.bfloat16),
            pltpu.VMEM((group_size, batch, 2 * lanes), jnp.float32),
            pltpu.VMEM((GRID_X, GRID_Y), jnp.float32),
            pltpu.VMEM((GRID_X, GRID_Y), jnp.float32),
            pltpu.SMEM((4 * devices * tiles,), jnp.int32),
            *[pltpu.VMEM(value.shape, value.dtype) for value in constants],
            pltpu.SemaphoreType.DMA((fixed_arrays,)),
        ],
        compiler_params=pltpu.CompilerParams(vmem_limit_bytes=36 << 20),
        name="mesh",
    )(
        bounds, atoms, *[pltpu.with_memory_space_constraint(value, pltpu.HBM) for value in constants]
    )


def convolved_by_lines(charge_mesh, count_x, count_y):
    turn_x = jnp.asarray(hartley(GRID_X))
    turn_y = jnp.asarray(hartley(GRID_Y))
    product = functools.partial(
        jnp.einsum, precision=lax.Precision.HIGHEST, preferred_element_type=jnp.float32
    )
    exchange = functools.partial(lax.all_to_all, tiled=True)
    lines = exchange(charge_mesh, "gx", split_axis=2, concat_axis=0)
    lines = product("xyk,xu->uyk", lines, turn_x)
    lines = exchange(lines, "gy", split_axis=0, concat_axis=1)
    lines = product("uyk,yv->uvk", lines, turn_y)
    wide, _, depth = lines.shape
    start_x = lax.axis_index("gy") * wide
    start_z = lax.axis_index("gx") * depth
    volume = GRID_X * GRID_Y * GRID_Z * spacing**3
    fx = green_factors(start_x + jnp.arange(wide, dtype=jnp.int32), GRID_X)
    fy = green_factors(jnp.arange(GRID_Y, dtype=jnp.int32), GRID_Y)
    fz = green_factors(start_z + jnp.arange(depth, dtype=jnp.int32), GRID_Z)
    square = fx[0][:, None, None] + fy[0][:, None] + fz[0]
    scale = fx[1][:, None, None] * fy[1][:, None] * fz[1] / (math.pi * volume)
    lines = lines * jnp.where(square > 0.0, scale / jnp.where(square > 0.0, square, 1.0), 0.0)
    lines = product("uvk,vy->uyk", lines, turn_y)
    lines = exchange(lines, "gy", split_axis=1, concat_axis=0)
    lines = product("uyk,ux->xyk", lines, turn_x)
    return exchange(lines, "gx", split_axis=0, concat_axis=2)


def far_by_lines(atoms, base, count_x, count_y, cells_x, cells_y, cells_z):
    atom_total = atoms.shape[1]
    cells = (cells_x, cells_y, cells_z)
    pad = (round_up(cells_x + 3, rows_group), round_up(cells_y + 3, 8))
    pad_x, pad_y = pad
    turn_z = jnp.asarray(hartley(GRID_Z))
    spread = pl.pallas_call(
        functools.partial(spread_kernel, cells, pad),
        out_shape=jax.ShapeDtypeStruct((pad_x, pad_y, GRID_Z), jnp.float32),
        scratch_shapes=[
            pltpu.VMEM((pad_x, atom_total), jnp.float32),
            pltpu.VMEM((pad_y, atom_total), jnp.float32),
            pltpu.VMEM((atom_total, 2 * GRID_Z), jnp.bfloat16),
            pltpu.VMEM((rows_group * pad_y, atom_total), jnp.bfloat16),
            pltpu.VMEM((rows_group * pad_y, atom_total), jnp.bfloat16),
        ],
        name="spread",
    )(atoms, base, turn_z)

    from_x = moved(spread[cells_x : cells_x + 3, :cells_y], 1, 0)
    from_y = moved(spread[:cells_x, cells_y : cells_y + 3], 0, 1)
    from_both = moved(spread[cells_x : cells_x + 3, cells_y : cells_y + 3], 1, 1)
    charge_mesh = (
        spread[:cells_x, :cells_y]
        .at[:3]
        .add(from_x)
        .at[:, :3]
        .add(from_y)
        .at[:3, :3]
        .add(from_both)
    )
    potential = convolved_by_lines(charge_mesh, count_x, count_y)
    upper_x = moved(potential[:3], -1, 0)
    upper_y = moved(potential[:, :3], 0, -1)
    upper_both = moved(potential[:3, :3], -1, -1)
    wider = jnp.concatenate(
        [
            jnp.concatenate([potential, upper_x], axis=0),
            jnp.concatenate([upper_y, upper_both], axis=0),
        ],
        axis=1,
    )
    wider = jnp.pad(wider, ((0, pad_x - cells_x - 3), (0, pad_y - cells_y - 3), (0, 0)))
    return pl.pallas_call(
        functools.partial(gather_kernel, cells, pad),
        out_shape=jax.ShapeDtypeStruct((3, atom_total), jnp.float32),
        scratch_shapes=[
            pltpu.VMEM((pad_x, atom_total), jnp.float32),
            pltpu.VMEM((pad_x, atom_total), jnp.float32),
            pltpu.VMEM((pad_y, atom_total), jnp.float32),
            pltpu.VMEM((pad_y, atom_total), jnp.float32),
            pltpu.VMEM((2 * GRID_Z, 2 * atom_total), jnp.bfloat16),
            pltpu.VMEM((rows_group * pad_y, 2 * atom_total), jnp.float32),
        ],
        name="gather",
    )(atoms, base, turn_z, wider)


def local(positions, charges, pair_lists, slab_dest, atom_counts):
    count_x = lax.axis_size("gx")
    count_y = lax.axis_size("gy")
    devices = count_x * count_y
    atom_total = positions.shape[3]
    clusters = pair_lists.shape[2]
    cluster_size = atom_total // clusters
    blocks = slab_dest.shape[2]
    block_size = atom_total // blocks
    cells_x = GRID_X // count_x
    cells_y = GRID_Y // count_y
    cells_z = GRID_Z // count_y
    by_planes = (
        GRID_Z == 8 * devices
        and cells_y == 64
        and cells_x % 8 == 0
        and cells_x <= 64
        and count_y % 2 == 0
        and atom_total == 8 * lanes
        and cluster_size % lanes == 0
    )
    if by_planes:
        sizes = (count_x, count_y, cells_x, cells_y)
        raw, atoms, bounds, rank, columns, before = shared(
            positions, charges, atom_counts, clusters, *sizes
        )
        partial = far_by_planes(bounds, atoms, *sizes)
        return tuple(finished(pair_lists, partial, raw, rank, columns, before, *sizes))
    living = jnp.arange(atom_total, dtype=jnp.int32) < atom_counts[0, 0]
    charge = jnp.where(living, charges[0, 0], 0.0)
    packed = jnp.concatenate([positions, charge[None, None, None, :]], axis=0)
    atoms = packed.reshape(4, atom_total)
    base = jnp.broadcast_to(
        (slab_dest[0, 0] * cells_z)[:, None], (blocks, block_size)
    ).reshape(1, atom_total)
    gathered = lax.all_gather(atoms, ("gx", "gy"), axis=0, tiled=False)
    far_part = far_by_lines(atoms, base, count_x, count_y, cells_x, cells_y, cells_z)

    chosen = pair_lists[0, 0]
    beside = chosen // clusters
    step_x, step_y = (beside // 3 - 1, beside % 3 - 1)
    at_x = (lax.axis_index("gx") + step_x + count_x) % count_x
    at_y = (lax.axis_index("gy") + step_y + count_y) % count_y
    number = (at_x * count_y + at_y) * clusters + chosen % clusters
    pick = (number[:, :, None] == jnp.arange(devices * clusters, dtype=jnp.int32)).astype(
        jnp.float32
    )
    pool = gathered[:, :4].reshape(devices, 4, clusters, cluster_size)
    pool = jnp.transpose(pool, (1, 0, 2, 3)).reshape(4, devices * clusters, cluster_size)
    partners = jnp.einsum(
        "cln,fnk->cflk",
        pick,
        pool,
        precision=lax.Precision.HIGHEST,
        preferred_element_type=jnp.float32,
    )
    shift_x = (step_x * cells_x).astype(jnp.float32)
    shift_y = (step_y * cells_y).astype(jnp.float32)
    flat = jnp.zeros_like(shift_x)
    shift = jnp.stack([shift_x, shift_y, flat, flat], axis=1)
    partners = (partners + shift[:, :, :, None]).reshape(clusters, 4, -1)
    own = packed.reshape(4, clusters, cluster_size)
    pair_part = jnp.stack(
        [one_cluster(own[:, c], partners[c]) for c in range(clusters)], axis=1
    )
    short_forces = pair_part.reshape(3, 1, 1, atom_total)
    return (short_forces, far_part.reshape(3, 1, 1, atom_total))


def solution(mesh):
    return jax.shard_map(
        local,
        mesh=mesh,
        in_specs=(
            P(None, ("rep", "gx"), "gy", None),
            P(("rep", "gx"), "gy", None),
            P(("rep", "gx"), "gy", None, None),
            P(("rep", "gx"), "gy", None),
            P(("rep", "gx"), "gy"),
        ),
        out_specs=(P(None, ("rep", "gx"), "gy", None), P(None, ("rep", "gx"), "gy", None)),
        check_vma=False,
    )
```

```python
import functools
import math

import jax
import jax.numpy as jnp
import numpy as np
from jax import lax
from jax.experimental import pallas as pl
from jax.experimental.pallas import tpu as pltpu
from jax.sharding import PartitionSpec as P

GRID_X = 256
GRID_Y = 256
GRID_Z = 128


spacing = 0.16
ewald_split = 3.47
cutoff = 0.9
soft_core = 0.09
root_factor = 1.1283791670955126
rows_group = 8
lanes = 128
window_rows = 24
group_size = 16
gather_size = 8
cell_group = 2
plane_group = 4
fixed_arrays = 8


def moved(value, step_x, step_y):
    count_x = lax.axis_size("gx")
    count_y = lax.axis_size("gy")
    pairs = [
        (i * count_y + j, (i + step_x) % count_x * count_y + (j + step_y) % count_y)
        for i in range(count_x)
        for j in range(count_y)
    ]
    return lax.ppermute(value, ("gx", "gy"), pairs)


def round_up(value, multiple):
    return -(-value // multiple) * multiple


def hartley(period):
    turns = np.outer(np.arange(period), np.arange(period)) % period
    phases = turns * (2.0 * np.pi / period)
    return (np.cos(phases) + np.sin(phases)).astype(np.float32)


def halves(value):
    high = value.astype(jnp.bfloat16)
    low = (value - high.astype(jnp.float32)).astype(jnp.bfloat16)
    return (high, low)


def dot(left_side, right_side):
    return jnp.dot(left_side, right_side, preferred_element_type=jnp.float32)


def spline_weights(fraction):
    remain = 1.0 - fraction
    square = fraction * fraction
    cube_part = square * fraction
    values = [
        remain * remain * remain / 6.0,
        (3.0 * cube_part - 6.0 * square + 4.0) / 6.0,
        (-3.0 * cube_part + 3.0 * square + 3.0 * fraction + 1.0) / 6.0,
        cube_part / 6.0,
    ]
    slopes = [
        -0.5 * remain * remain,
        0.5 * (3.0 * square - 4.0 * fraction),
        0.5 * (-3.0 * square + 2.0 * fraction + 1.0),
        0.5 * square,
    ]
    return (values, slopes)


def split_cells(coordinate, offset, cell_count):
    inside = coordinate - offset
    lowest = jnp.clip(jnp.floor(inside).astype(jnp.int32), 0, cell_count - 1)
    return (lowest, inside - lowest.astype(inside.dtype))


def spline_table(lowest, values, table_size, period=None):
    points = lax.broadcasted_iota(jnp.int32, (table_size, lowest.shape[1]), 0)
    lookup = jnp.zeros(points.shape, jnp.float32)
    for spline_term in range(4):
        at = lowest + spline_term
        if period is not None:
            at = jnp.where(at >= period, at - period, at)
        lookup = jnp.where(points == at, values[spline_term], lookup)
    return lookup


def spread_kernel(cells, pad, atoms_ref, base_ref, turn_ref, out_ref, wx_ref, wy_ref, wz_ref, hi_ref, lo_ref):
    cells_x, cells_y, cells_z = cells
    pad_x, pad_y = pad
    atom_total = atoms_ref.shape[1]
    low_x, frac_x = split_cells(atoms_ref[0:1, :], 0.0, cells_x)
    low_y, frac_y = split_cells(atoms_ref[1:2, :], 0.0, cells_y)
    base = base_ref[...]
    low_z, frac_z = split_cells(atoms_ref[2:3, :], base.astype(jnp.float32), cells_z)
    wx_ref[...] = spline_table(low_x, spline_weights(frac_x)[0], pad_x) * atoms_ref[3:4, :]
    wy_ref[...] = spline_table(low_y, spline_weights(frac_y)[0], pad_y)
    turn = turn_ref[...]
    size_z = turn.shape[0]
    table_z = spline_table(base + low_z, spline_weights(frac_z)[0], size_z, size_z)
    waves = jnp.dot(
        turn, table_z, precision=lax.Precision.HIGHEST, preferred_element_type=jnp.float32
    ).T
    high, low = halves(waves)
    wz_ref[:, :size_z] = high
    wz_ref[:, size_z:] = low

    @pl.loop(0, pad_x // rows_group)
    def _(chunk):
        for inner in range(rows_group):
            row = wx_ref[pl.ds(chunk * rows_group + inner, 1), :]
            high, low = halves(row * wy_ref[...])
            hi_ref[pl.ds(inner * pad_y, pad_y), :] = high
            lo_ref[pl.ds(inner * pad_y, pad_y), :] = low
        both = dot(hi_ref[...], wz_ref[...])
        rest = dot(lo_ref[...], wz_ref[:, :size_z])
        total = both[:, :size_z] + both[:, size_z:] + rest
        out_ref[pl.ds(chunk * rows_group, rows_group)] = total.reshape(rows_group, pad_y, size_z)


def gather_kernel(cells, pad, atoms_ref, base_ref, turn_ref, mesh_ref, out_ref, wx_ref, vx_ref, wy_ref, vy_ref, wz_ref, level_ref):
    cells_x, cells_y, cells_z = cells
    pad_x, pad_y = pad
    atom_total = atoms_ref.shape[1]
    low_x, frac_x = split_cells(atoms_ref[0:1, :], 0.0, cells_x)
    low_y, frac_y = split_cells(atoms_ref[1:2, :], 0.0, cells_y)
    base = base_ref[...]
    low_z, frac_z = split_cells(atoms_ref[2:3, :], base.astype(jnp.float32), cells_z)
    values, slopes = spline_weights(frac_x)
    wx_ref[...] = spline_table(low_x, values, pad_x)
    vx_ref[...] = spline_table(low_x, slopes, pad_x)
    values, slopes = spline_weights(frac_y)
    wy_ref[...] = spline_table(low_y, values, pad_y)
    vy_ref[...] = spline_table(low_y, slopes, pad_y)
    values, slopes = spline_weights(frac_z)
    turn = turn_ref[...]
    size_z = turn.shape[0]
    for place, terms in enumerate((values, slopes)):
        table_z = spline_table(base + low_z, terms, size_z, size_z)
        waves = jnp.dot(
            turn, table_z, precision=lax.Precision.HIGHEST, preferred_element_type=jnp.float32
        )
        high, low = halves(waves)
        wz_ref[:size_z, pl.ds(place * atom_total, atom_total)] = high
        wz_ref[size_z:, pl.ds(place * atom_total, atom_total)] = low
    groups = pad_y // 8

    def one_chunk(chunk, sums):
        rows = mesh_ref[pl.ds(chunk * rows_group, rows_group)].reshape(rows_group * pad_y, size_z)
        high, low = halves(rows)
        level_ref[...] = dot(jnp.concatenate([high, high], axis=1), wz_ref[...]) + dot(
            low, wz_ref[:size_z, :]
        )
        first, second, third = sums
        for inner in range(rows_group):
            flat = level_ref[pl.ds(inner * pad_y, pad_y), :atom_total]
            tilt = level_ref[pl.ds(inner * pad_y, pad_y), atom_total:]
            across = wy_ref[...]
            part_x = jnp.sum((across * flat).reshape(groups, 8, atom_total), axis=0)
            part_y = jnp.sum((vy_ref[...] * flat).reshape(groups, 8, atom_total), axis=0)
            part_z = jnp.sum((across * tilt).reshape(groups, 8, atom_total), axis=0)
            weight = wx_ref[pl.ds(chunk * rows_group + inner, 1), :]
            slope = vx_ref[pl.ds(chunk * rows_group + inner, 1), :]
            first = first + slope * part_x
            second = second + weight * part_y
            third = third + weight * part_z
        return (first, second, third)

    zero = jnp.zeros((8, atom_total), jnp.float32)
    sums = lax.fori_loop(0, pad_x // rows_group, one_chunk, (zero, zero, zero))
    factor = -atoms_ref[3:4, :] / spacing
    for place in range(3):
        out_ref[pl.ds(place, 1), :] = factor * jnp.sum(sums[place], axis=0, keepdims=True)


def peers_of(count_x, count_y):
    place_x, place_y = (lax.axis_index("gx"), lax.axis_index("gy"))
    peers = []
    for order in range(1, count_x * count_y):
        peer_x = lax.rem(place_x + order // count_y, count_x)
        peer_y = lax.rem(place_y + order % count_y, count_y)
        peers.append((peer_x, peer_y))
    return peers


root_terms = (
    3.9164407301418542,
    -0.0037127819564810594,
    0.16802528315459195,
    -0.003061234121505335,
    -0.0076524954798020545,
    0.002268454833542123,
    -0.0003056487922112269,
    1.686888935413571e-05,
)


def pair_weight(square):
    soft_square = square * (spacing * spacing) + soft_core
    inverse = lax.rsqrt(soft_square)
    series = jnp.full_like(inverse, root_terms[-1])
    for term in root_terms[-2::-1]:
        series = series * inverse + term
    decay = jnp.exp(soft_square * (-ewald_split * ewald_split))
    taper = jnp.maximum(1.0 - square * (spacing * spacing / (cutoff * cutoff)), 0.0)
    return (decay * series) * (inverse * taper) ** 2


def row_sums(values):
    total = None
    ones = jnp.ones((16, values.shape[1]), jnp.bfloat16)
    for _ in range(3):
        part = values.astype(jnp.bfloat16)
        values = values - part.astype(jnp.float32)
        summed = lax.dot_general(
            ones, part, (((1,), (1,)), ((), ())), preferred_element_type=jnp.float32
        )
        total = summed if total is None else total + summed
    return total[0:1, :]


def place_partners(sizes, cells, pairs_ref, atoms_ref, partner_ref):
    count_x, count_y = sizes
    cells_x, cells_y = cells
    place_x, place_y = (lax.axis_index("gx"), lax.axis_index("gy"))
    clusters, listed = pairs_ref.shape[2:]
    size = atoms_ref.shape[2] // clusters
    for c in range(clusters):
        for n in range(1, listed):
            chosen = pairs_ref[0, 0, c, n]
            beside = lax.div(chosen, clusters)
            which = chosen - beside * clusters
            row_x = lax.div(beside, 3)
            step_x = row_x - 1
            step_y = beside - row_x * 3 - 1
            from_x = lax.rem(place_x + step_x + count_x, count_x)
            from_y = lax.rem(place_y + step_y + count_y, count_y)
            block = atoms_ref[from_x * count_y + from_y]
            part = block[:, :size]
            for k in range(1, clusters):
                part = jnp.where(which == k, block[:, k * size : (k + 1) * size], part)
            shifts = (
                (step_x * cells_x).astype(jnp.float32),
                (step_y * cells_y).astype(jnp.float32),
            )
            for axis in range(4):
                row = part[axis : axis + 1, :]
                if axis < 2:
                    row = row + shifts[axis]
                partner_ref[c, axis, :, (n - 1) * size : n * size] = jnp.broadcast_to(
                    row, (8, size)
                )


def pair_sums(clusters, size, height, column_ref, partner_ref, before_ref, sum_ref):
    @pl.loop(0, clusters)
    def _(c):
        @pl.loop(0, size // height)
        def _(step):
            for part in range(height // 8):
                start = c * size + step * height + part * 8
                rows = pl.ds(pl.multiple_of(start, 8), 8)
                own = [column_ref[axis, rows, :] for axis in range(3)]
                sums = [
                    jnp.zeros((8, lanes), jnp.float32)
                    if before_ref is None
                    else before_ref[axis, rows, :]
                    for axis in range(3)
                ]
                for tile in range(partner_ref.shape[3] // lanes):
                    span = slice(tile * lanes, (tile + 1) * lanes)
                    offsets = [own[axis] - partner_ref[c, axis, :, span] for axis in range(3)]
                    square = sum(offset * offset for offset in offsets)
                    weight = pair_weight(square) * partner_ref[c, 3, :, span]
                    sums = [total + weight * offset for total, offset in zip(sums, offsets)]
                for axis in range(3):
                    sum_ref[axis, rows, :] = sums[axis]


def share_kernel(sizes, cells, clusters, count_ref, position_ref, charge_ref, raw_ref, sorted_ref, bounds_ref, rank_ref, column_ref, sum_ref, key_ref, split_ref, partner_ref, raw_send, raw_recv, sort_send, sort_recv, mark_send, mark_recv):
    count_x, count_y = sizes
    cells_x, _ = cells
    place_x, place_y = (lax.axis_index("gx"), lax.axis_index("gy"))
    me = place_x * count_y + place_y
    place_chip, place_core = (place_y // 2, lax.rem(place_y, 2))
    chips = count_y // 2

    def at(step_x, step_chip, flip):
        peer_x = lax.rem(place_x + step_x, count_x)
        peer_chip = lax.rem(place_chip + step_chip, chips)
        peer_core = 1 - place_core if flip else place_core
        return (peer_x, peer_chip * 2 + peer_core)

    peers = peers_of(count_x, count_y)
    barrier = pltpu.get_barrier_semaphore()
    for peer_x, peer_y in peers:
        pl.semaphore_signal(
            barrier,
            inc=1,
            device_id={"gx": peer_x, "gy": peer_y},
            device_id_type=pl.DeviceIdType.MESH,
        )

    def sent(ref, owner, peer, send_sem, recv_sem, order, slot):
        return pltpu.make_async_remote_copy(
            src_ref=ref.at[owner],
            dst_ref=ref.at[owner],
            send_sem=send_sem.at[order],
            recv_sem=recv_sem.at[slot],
            device_id={"gx": peer[0], "gy": peer[1]},
            device_id_type=pl.DeviceIdType.MESH,
        )

    passed = []

    def passes(owner, peer):
        order = len(passed)
        copies = [
            sent(sorted_ref, owner, peer, sort_send, sort_recv, order, owner),
            sent(bounds_ref, owner, peer, mark_send, mark_recv, order, owner),
        ]
        for copy in copies:
            copy.start()
        passed.append(copies)

    def arrives(owner, peer):
        sent(sorted_ref, owner, peer, sort_send, sort_recv, 0, owner).wait_recv()
        sent(bounds_ref, owner, peer, mark_send, mark_recv, 0, owner).wait_recv()

    atom_total = charge_ref.shape[2]
    tiles = atom_total // lanes
    slot = lax.broadcasted_iota(jnp.int32, (1, atom_total), 1)
    living = slot < count_ref[0, 0]
    charge = jnp.where(living, charge_ref[0], 0.0)
    rows = [position_ref[axis, 0] for axis in range(3)] + [charge]
    for axis in range(4):
        raw_ref[me, pl.ds(axis, 1), :] = rows[axis]
    column = jnp.clip(jnp.floor(rows[0]), 0.0, cells_x - 1.0)
    key = jnp.where(living, column, float(cells_x)) * float(atom_total) + slot.astype(jnp.float32)
    for tile in range(tiles):
        span = slice(tile * lanes, (tile + 1) * lanes)
        key_ref[span, :] = jnp.broadcast_to(key[:, span], (lanes, lanes)).T
    wide = [
        jnp.broadcast_to(key[:, tile * lanes : (tile + 1) * lanes], (8, lanes))
        for tile in range(tiles)
    ]

    def count_group(group, totals):
        for inner in range(8):
            others = key_ref[pl.ds(pl.multiple_of(group * 64 + inner * 8, 8), 8), :]
            totals = tuple(
                total + jnp.where(others < own, 1.0, 0.0) for total, own in zip(totals, wide)
            )
        return totals

    zero = jnp.zeros((8, lanes), jnp.float32)
    totals = lax.fori_loop(0, atom_total // 64, count_group, (zero,) * tiles)
    for tile, total in enumerate(totals):
        rank_ref[:, tile * lanes : (tile + 1) * lanes] = jnp.sum(total, axis=0, keepdims=True)

    split_ref[...] = jnp.zeros_like(split_ref)
    rest = raw_ref[me]
    for part in range(3):
        piece = rest.astype(jnp.bfloat16).astype(jnp.float32)
        split_ref[4 * part : 4 * part + 4, :] = piece
        rest = rest - piece
    split = split_ref[...].astype(jnp.bfloat16)
    rank = rank_ref[...]
    block = 2 * lanes
    for part in range(atom_total // block):
        place = lax.broadcasted_iota(jnp.int32, (block, atom_total), 0) + part * block
        chosen = jnp.where(place.astype(jnp.float32) == rank, 1.0, 0.0).astype(jnp.bfloat16)
        found = lax.dot_general(
            split, chosen, (((1,), (1,)), ((), ())), preferred_element_type=jnp.float32
        )
        found = (found[0:4] + found[4:8]) + found[8:12]
        for tile in range(block // lanes):
            row = part * (block // lanes) + tile
            for axis in range(4):
                sorted_ref[me, axis, row : row + 1, :] = found[
                    axis : axis + 1, tile * lanes : (tile + 1) * lanes
                ]
    spot = lax.broadcasted_iota(jnp.int32, (tiles, lanes), 0) * lanes
    spot = spot + lax.broadcasted_iota(jnp.int32, (tiles, lanes), 1)
    inside = spot < count_ref[0, 0]
    column = jnp.clip(jnp.floor(sorted_ref[me, 0]), 0.0, cells_x - 1.0)
    lowest = jnp.min(jnp.where(inside, column, float(cells_x)), axis=1, keepdims=True)
    highest = jnp.max(jnp.where(inside, column, -1.0), axis=1, keepdims=True)
    first = jnp.floor(lowest * 0.125)
    last = jnp.floor((highest + 3.0) * 0.125)
    windows = jnp.where(
        highest >= 0.0, jnp.floor((last - first) * (8.0 / window_rows) + 0.01) + 1.0, 0.0
    )
    lane = lax.broadcasted_iota(jnp.int32, (tiles, lanes), 1)
    row = lax.broadcasted_iota(jnp.int32, (tiles, lanes), 0)
    marks = jnp.where(lane == row, first, jnp.where(lane == row + tiles, windows, 0.0))
    marks = jnp.sum(marks, axis=0, keepdims=True)
    bounds_ref[me] = marks.astype(jnp.int32)

    near = sorted(
        (min(step, count_x - step) + min(chip, chips - chip), step, chip)
        for step in range(count_x)
        for chip in range(chips)
    )[1:]
    mate = at(0, 0, True)
    pl.semaphore_wait(barrier, len(peers))
    for _, step, chip in reversed(near):
        passes(me, at(step, chip, False))
    passes(me, mate)
    beside = sorted(
        {
            step_x % count_x * count_y + step_y % count_y
            for step_x in (-1, 0, 1)
            for step_y in (-1, 0, 1)
        }
        - {0}
    )
    copies = [
        sent(raw_ref, me, peers[order - 1], raw_send, raw_recv, order - 1, order - 1)
        for order in beside
    ]
    for copy in copies:
        copy.start()

    for axis in range(3):
        for tile in range(tiles):
            span = slice(tile * lanes, (tile + 1) * lanes)
            column_ref[axis, span, :] = jnp.broadcast_to(rows[axis][:, span], (lanes, lanes)).T
    size = atom_total // clusters
    for c in range(clusters):
        for axis in range(4):
            row = rows[axis][:, c * size : (c + 1) * size]
            partner_ref[c, axis] = jnp.broadcast_to(row, (8, size))
    pair_sums(clusters, size, 64, column_ref, partner_ref, None, sum_ref)
    for _, step, chip in near:
        owner_x, owner_y = at(step, chip, False)
        arrives(owner_x * count_y + owner_y, (owner_x, owner_y))
        passes(owner_x * count_y + owner_y, mate)
    for _, step, chip in [(0, 0, 0), *near]:
        owner_x, owner_y = at(step, chip, True)
        arrives(owner_x * count_y + owner_y, mate)
    for copy in copies:
        copy.wait()
    for pair in passed:
        for copy in pair:
            copy.wait_send()


def shared(positions, charges, atom_counts, clusters, count_x, count_y, cells_x, cells_y):
    devices = count_x * count_y
    atom_total = charges.shape[2]
    vmem = pl.BlockSpec(memory_space=pltpu.VMEM)
    smem = pl.BlockSpec(memory_space=pltpu.SMEM)
    fewer = pltpu.SemaphoreType.DMA((devices - 1,))
    flags = pltpu.SemaphoreType.DMA((devices,))
    return pl.pallas_call(
        functools.partial(share_kernel, (count_x, count_y), (cells_x, cells_y), clusters),
        in_specs=[smem, vmem, vmem],
        out_specs=[vmem] * 6,
        out_shape=[
            jax.ShapeDtypeStruct((devices, 4, atom_total), jnp.float32),
            jax.ShapeDtypeStruct((devices, 4, atom_total // lanes, lanes), jnp.float32),
            jax.ShapeDtypeStruct((devices, 1, lanes), jnp.int32),
            jax.ShapeDtypeStruct((1, atom_total), jnp.float32),
            jax.ShapeDtypeStruct((3, atom_total, lanes), jnp.float32),
            jax.ShapeDtypeStruct((3, atom_total, lanes), jnp.float32),
        ],
        scratch_shapes=[
            pltpu.VMEM((atom_total, lanes), jnp.float32),
            pltpu.VMEM((16, atom_total), jnp.float32),
            pltpu.VMEM((clusters, 4, 8, atom_total // clusters), jnp.float32),
            fewer,
            fewer,
        ]
        + [flags] * 4,
        compiler_params=pltpu.CompilerParams(
            collective_id=0, has_side_effects=True, vmem_limit_bytes=12 << 20
        ),
        name="share",
    )(
        atom_counts,
        *[pltpu.with_memory_space_constraint(value, pltpu.HBM) for value in (positions, charges)],
    )


def depth_rows(table, circle, height, terms):
    turns = height * table[:, 0:1]
    turns = turns - GRID_Z * jnp.floor(turns * (1.0 / GRID_Z))
    index = turns.astype(jnp.int32)
    cosine, sine = [jnp.take_along_axis(part, index, axis=1) for part in circle]
    results = []
    for weights in terms:
        even = sum(table[:, 1 + t : 2 + t] * weights[t] for t in range(4))
        odd = sum(table[:, 5 + t : 6 + t] * weights[t] for t in range(4))
        results.append(cosine * even + sine * odd)
    return results


def mesh_kernel(sizes, cells, pad_y, bounds_ref, atoms_ref, *refs):
    constants, (out_ref, *scratch) = refs[:fixed_arrays], refs[fixed_arrays:]
    held, copy_sem = scratch[-fixed_arrays - 1 : -1], scratch[-1]
    copies = [
        pltpu.make_async_copy(source, target, copy_sem.at[place])
        for place, (source, target) in enumerate(zip(constants, held))
    ]
    for copy in copies:
        copy.start()
    xh_ref, xl_ref, yh_ref, yl_ref, column_ref, row_ref, circle_ref, table_ref = held
    mesh_ref, stack_ref, prep_ref, deep_ref, steep_ref, near_ref, wy_ref, side_ref, level_ref, square_ref, scale_ref, work_ref = scratch[: -fixed_arrays - 1]
    count_x, count_y = sizes
    cells_x, cells_y = cells
    devices = count_x * count_y
    place = lax.axis_index("gx") * count_y + lax.axis_index("gy")
    tiles = atoms_ref.shape[2]
    depth = stack_ref.shape[0]
    window = 2 * cells_y
    windows = GRID_Y // window
    extra = 8
    share = -(-group_size * cell_group // devices)
    stack_ref[:, GRID_X:, :] = jnp.zeros_like(stack_ref[:, GRID_X:, :])
    out_ref[...] = jnp.zeros_like(out_ref)
    copies[-2].wait()
    copies[-1].wait()
    circle = [circle_ref[:8, :], circle_ref[8:, :]]
    table = table_ref[pl.ds(pl.multiple_of(place * depth, 8), depth), :]

    steps_x = window_rows // 8
    most = (cells_x + 2) // 8 // steps_x + 1

    def prep_row(kind, spot):
        return prep_ref[pl.ds(kind * devices * tiles + spot, 8, stride=0), :]

    def listed_work(cell, total):
        for tile in range(tiles):
            for step in range(most):
                work_ref[total + step] = (cell * tiles + tile) * most + step
            total = total + bounds_ref[cell, 0, tiles + tile]

        return total

    def keep_splines(cell):
        def keep(kind, value):
            rows = pl.ds(pl.multiple_of((kind * devices + cell) * tiles, 8), tiles)
            prep_ref[rows, :] = value

        for axis, count in enumerate((cells_x, cells_y)):
            value = atoms_ref[cell, axis]
            lowest = jnp.clip(jnp.floor(value), 0.0, count - 1.0)
            values, slopes = spline_weights(value - lowest)
            keep(9 * axis, lowest)
            for term in range(4):
                keep(9 * axis + 1 + term, values[term])
                keep(9 * axis + 5 + term, slopes[term])
                if axis == 1:
                    for kind, whole in ((28, values[term]), (32, slopes[term])):
                        keep(kind + term, whole - whole.astype(jnp.bfloat16).astype(jnp.float32))
        value = atoms_ref[cell, 2]
        height = jnp.floor(value)
        values, slopes = spline_weights(value - height)
        keep(18, height)
        for term in range(4):
            keep(19 + term, values[term])
            keep(23 + term, slopes[term])
        keep(27, atoms_ref[cell, 3])

    def keep_modes(cell):
        for tile in range(tiles):
            spot = cell * tiles + tile
            height = prep_row(18, spot)
            terms = [[prep_row(19 + 4 * s + term, spot) for term in range(4)] for s in range(2)]
            deep, steep = depth_rows(table, circle, height, terms)
            rows = pl.ds(pl.multiple_of(spot * depth, 8), depth)
            deep_ref[rows, :] = deep
            steep_ref[rows, :] = steep

    def prepare_some(turn, total):
        for inner in range(cell_group):
            cell = turn * cell_group + inner
            mesh_ref[lax.div(cell, depth), lax.rem(cell, depth)] = jnp.zeros(
                mesh_ref.shape[2:], jnp.float32
            )
            total = listed_work(cell, total)
        for inner in range(cell_group):
            keep_splines(turn * cell_group + inner)
        for inner in range(cell_group):
            keep_modes(turn * cell_group + inner)
        for inner in range(share):
            place = jnp.minimum(turn * share + inner, group_size - 1)
            wy_ref[place] = jnp.zeros(wy_ref.shape[1:], wy_ref.dtype)
        return total

    total = lax.fori_loop(0, devices // cell_group, prepare_some, jnp.int32(0))
    rounds = lax.div(total + group_size - 1, group_size)

    row_index = lax.broadcasted_iota(jnp.int32, (8, lanes), 0).astype(jnp.float32)

    def looked_up(points, lowest, term_lists):
        results = [jnp.zeros_like(points) for _ in term_lists]
        for term in range(4):
            hit = points == lowest + float(term)
            results = [
                jnp.where(hit, terms[term], result)
                for terms, result in zip(term_lists, results)
            ]
        return results

    def kinds(first, spot):
        return [prep_row(first + term, spot) for term in range(4)]

    stride = round_up(pad_y, 16)
    far_away = 1.0e6

    def task(index):
        entry = jnp.where(index < total, work_ref[index], 0)
        spot = lax.div(entry, most)
        cell = lax.div(spot, tiles)
        chunk = spot - cell * tiles
        begin = bounds_ref[cell, 0, chunk] * 8 + (entry - spot * most) * window_rows
        base = jnp.where(index < total, begin.astype(jnp.float32), far_away)
        i = lax.div(cell, count_y)
        rows = pl.ds(pl.multiple_of(i * cells_x + begin, 8), window_rows)
        return (spot, cell, chunk, cell - i * count_y, rows, base)

    packed_index = jnp.concatenate([row_index, row_index + 8.0], axis=0).astype(jnp.bfloat16)

    def packed_row(kind, spot):
        row = prep_row(kind, spot)
        return jnp.concatenate([row, row], axis=0).astype(jnp.bfloat16)

    def y_table(spot, kind, low_kind):
        lowest = packed_row(9, spot)
        highs = [packed_row(kind + term, spot) for term in range(4)]
        lows = [packed_row(low_kind + term, spot) for term in range(4)]
        starts = [lowest + jnp.bfloat16(term) for term in range(4)]
        for group in range(stride // 16):
            points = packed_index + jnp.bfloat16(group * 16)
            high = low = jnp.zeros_like(points)
            for term in range(4):
                hit = points == starts[term]
                high = jnp.where(hit, highs[term], high)
                low = jnp.where(hit, lows[term], low)
            yield (slice(group * 16, group * 16 + 16), high, low)

    @pl.loop(0, rounds)
    def _(turn):
        tasks = [task(turn * group_size + place) for place in range(group_size)]
        for place, (spot, _, _, _, _, base) in enumerate(tasks):
            for rows, high, low in y_table(spot, 10, 28):
                after = slice(window + rows.start, window + rows.stop)
                later = slice(stride + rows.start, stride + rows.stop)
                wy_ref[place, rows, :lanes] = high
                wy_ref[place, rows, lanes:] = high
                wy_ref[place, after, :lanes] = low
                near_ref[spot, rows, :] = high
                near_ref[spot, later, :] = low
            lowest = prep_row(0, spot) - base
            charge = prep_row(27, spot)
            terms = [term * charge for term in kinds(1, spot)]
            weights = [
                looked_up(row_index + float(tile * 8), lowest, [terms])[0]
                for tile in range(steps_x)
            ]
            modes = [
                deep_ref[pl.ds(spot * depth + k, 8, stride=0), :] for k in range(depth)
            ]
            blocks = [weight * mode for mode in modes for weight in weights]
            for pair in range(len(blocks) // 2):
                high, low = halves(jnp.concatenate(blocks[2 * pair : 2 * pair + 2], axis=0))
                rows = slice(pair * 16, pair * 16 + 16)
                side_ref[place, rows, :lanes] = high
                side_ref[place, rows, lanes:] = low
        for place, (_, _, _, j, rows, _) in enumerate(tasks):
            product = lax.dot_general(
                side_ref[place],
                wy_ref[place],
                (((1,), (1,)), ((), ())),
                preferred_element_type=jnp.float32,
            )
            product = product[:, :window] + product[:, window:]
            m = lax.div(j, 2)
            here = pl.ds(pl.multiple_of(m * window, lanes), window)
            mesh_ref[j - 2 * m, :, rows, here] += product.reshape(depth, window_rows, window)

    def across(value):
        high, low = halves(value)
        return dot(xh_ref[...], high) + dot(xl_ref[...], high) + dot(xh_ref[...], low)

    def along(value):
        high, low = halves(value)
        return dot(high, yh_ref[...]) + dot(high, yl_ref[...]) + dot(low, yh_ref[...])

    plane_lane = lax.broadcasted_iota(jnp.int32, (GRID_X, window), 1)
    for copy in copies[:-2]:
        copy.wait()
    shape = (GRID_X, GRID_Y)
    square_ref[...] = jnp.broadcast_to(column_ref[:, 0:1], shape) + row_ref[0:1, :]
    scale_ref[...] = jnp.broadcast_to(column_ref[:, 1:2], shape) * row_ref[1:2, :]

    def charge_of(k):
        charge = mesh_ref[0, k, :GRID_X, :] + pltpu.roll(mesh_ref[1, k, :GRID_X, :], cells_y, 1)
        over = slice(GRID_X, GRID_X + extra)
        beyond = mesh_ref[0, k, over, :] + pltpu.roll(mesh_ref[1, k, over, :], cells_y, 1)
        return jnp.concatenate([charge[:extra] + beyond, charge[extra:]], axis=0)

    def green_of(k):
        mode = pl.ds(place * depth + k, 1)
        square = square_ref[...] + table_ref[mode, 9:10]
        scale = scale_ref[...] * table_ref[mode, 10:11]
        return jnp.where(square > 0.0, scale / square, 0.0)

    def place_plane(k, plane):
        for odd in range(2):
            if odd:
                plane = pltpu.roll(plane, GRID_Y - cells_y, 1)
            for j_half in range(windows):
                j = 2 * j_half + odd
                block = plane[:, j_half * window : (j_half + 1) * window]
                high = block.astype(jnp.bfloat16).astype(jnp.float32)
                low = block - high
                shifted = pltpu.roll(high, stride, 1)
                left = jnp.where(plane_lane < stride, high, shifted)
                right = jnp.where(
                    plane_lane < 2 * stride - window,
                    shifted,
                    pltpu.roll(low, 2 * stride - window, 1),
                )
                for side, value in enumerate((left, right)):
                    span = slice((2 * j + side) * window, (2 * j + side + 1) * window)
                    stack_ref[k, :GRID_X, span] = value
                    stack_ref[k, GRID_X : GRID_X + extra, span] = value[:extra]

    @pl.loop(0, depth // plane_group)
    def _(pair):
        spots = [pair * plane_group + inner for inner in range(plane_group)]
        values = [across(charge_of(k)) for k in spots]
        values = [along(value) for value in values]
        values = [along(value * green_of(k)) for k, value in zip(spots, values)]
        values = [across(value) for value in values]
        for k, value in zip(spots, values):
            place_plane(k, value)

    @pl.loop(0, lax.div(total + gather_size - 1, gather_size))
    def _(turn):
        tasks = [task(turn * gather_size + place) for place in range(gather_size)]
        blank = jnp.zeros((2 * window - 3 * stride, lanes), jnp.bfloat16)
        for place, (spot, _, _, j, rows, _) in enumerate(tasks):
            near = near_ref[spot]
            highs, lows = [], []
            for _, high, low in y_table(spot, 14, 32):
                highs.append(high)
                lows.append(low)
            columns = jnp.concatenate(
                [
                    jnp.concatenate([near, near[:stride], blank], axis=0),
                    jnp.concatenate([*highs, *lows, *highs, blank], axis=0),
                ],
                axis=1,
            )
            span = pl.ds(pl.multiple_of(j * 2 * window, lanes), 2 * window)
            block = stack_ref[:, rows, span].reshape(depth * window_rows, 2 * window)
            level_ref[place] = dot(block.astype(jnp.bfloat16), columns)
        for place, (spot, cell, chunk, _, _, base) in enumerate(tasks):
            lowest = prep_row(0, spot) - base
            values = kinds(1, spot)
            slopes = kinds(5, spot)
            modes = [pl.ds(spot * depth + k, 8, stride=0) for k in range(depth)]
            deep = [deep_ref[mode, :] for mode in modes]
            steep = [steep_ref[mode, :] for mode in modes]
            zero = jnp.zeros((8, lanes), jnp.float32)
            sums = [zero, zero, zero]
            for tile in range(steps_x):
                weight, slope = looked_up(row_index + float(tile * 8), lowest, [values, slopes])
                parts = [zero, zero, zero]
                for k in range(depth):
                    at = slice(k * window_rows + tile * 8, k * window_rows + tile * 8 + 8)
                    flat = level_ref[place, at, :lanes]
                    tilt = level_ref[place, at, lanes:]
                    parts = [
                        parts[0] + deep[k] * flat,
                        parts[1] + deep[k] * tilt,
                        parts[2] + steep[k] * flat,
                    ]
                sums = [
                    sums[0] + slope * parts[0],
                    sums[1] + weight * parts[1],
                    sums[2] + weight * parts[2],
                ]
            for axis in range(3):
                out_ref[cell, axis, pl.ds(chunk, 1), :] += jnp.sum(
                    sums[axis], axis=0, keepdims=True
                )


def finish_kernel(sizes, cells, pairs_ref, partial_ref, atoms_ref, rank_ref, column_ref, before_ref, short_ref, long_ref, land_ref, partner_ref, sum_ref, order_ref, force_ref, send_sem, recv_sem):
    count_x, count_y = sizes
    place_x, place_y = (lax.axis_index("gx"), lax.axis_index("gy"))
    me = place_x * count_y + place_y
    peers = peers_of(count_x, count_y)
    barrier = pltpu.get_barrier_semaphore()
    for peer_x, peer_y in peers:
        pl.semaphore_signal(
            barrier,
            inc=1,
            device_id={"gx": peer_x, "gy": peer_y},
            device_id_type=pl.DeviceIdType.MESH,
        )
    clusters = pairs_ref.shape[2]
    atom_total = atoms_ref.shape[2]
    size = atom_total // clusters
    place_partners(sizes, cells, pairs_ref, atoms_ref, partner_ref)
    pl.semaphore_wait(barrier, len(peers))
    copies = []
    for order, (peer_x, peer_y) in enumerate(peers):
        copy = pltpu.make_async_remote_copy(
            src_ref=partial_ref.at[peer_x * count_y + peer_y],
            dst_ref=land_ref.at[order],
            send_sem=send_sem.at[order],
            recv_sem=recv_sem.at[order],
            device_id={"gx": peer_x, "gy": peer_y},
            device_id_type=pl.DeviceIdType.MESH,
        )
        copy.start()
        copies.append(copy)
    pair_sums(clusters, size, 32, column_ref, partner_ref, before_ref, sum_ref)
    for axis in range(3):
        for c in range(clusters):
            span = slice(c * size, (c + 1) * size)
            summed = row_sums(sum_ref[axis, span, :])
            short_ref[axis, 0, :, span] = summed
    rank = rank_ref[...]

    @pl.loop(0, atom_total // size)
    def _(block):
        place = lax.broadcasted_iota(jnp.int32, (size, atom_total), 0) + block * size
        order_ref[pl.ds(pl.multiple_of(block * size, size), size), :] = jnp.where(
            place.astype(jnp.float32) == rank, 1.0, 0.0
        ).astype(jnp.bfloat16)

    force_ref[...] = jnp.zeros_like(force_ref)
    for copy in copies:
        copy.wait()
    total = partial_ref[me]
    for order in range(len(peers)):
        total = total + land_ref[order]
    for part in range(3):
        piece = total.astype(jnp.bfloat16).astype(jnp.float32)
        total = total - piece
        for axis in range(3):
            for tile in range(atom_total // lanes):
                span = slice(tile * lanes, (tile + 1) * lanes)
                row = 4 * part + axis
                force_ref[row : row + 1, span] = piece[axis, tile : tile + 1, :]
    placed = dot(force_ref[...].astype(jnp.bfloat16), order_ref[...])
    placed = (placed[0:4] + placed[4:8]) + placed[8:12]
    for axis in range(3):
        long_ref[axis, 0, :, :] = placed[axis : axis + 1, :]


def finished(pair_lists, partial, raw, rank, columns, before, count_x, count_y, cells_x, cells_y):
    devices, _, atom_total = raw.shape
    clusters, listed = pair_lists.shape[2:]
    size = atom_total // clusters
    vmem = pl.BlockSpec(memory_space=pltpu.VMEM)
    flags = pltpu.SemaphoreType.DMA((devices - 1,))
    return pl.pallas_call(
        functools.partial(finish_kernel, (count_x, count_y), (cells_x, cells_y)),
        in_specs=[pl.BlockSpec(memory_space=pltpu.SMEM)] + [vmem] * 5,
        out_specs=[vmem, vmem],
        out_shape=[jax.ShapeDtypeStruct((3, 1, 1, atom_total), jnp.float32)] * 2,
        scratch_shapes=[
            pltpu.VMEM((devices - 1, *partial.shape[1:]), jnp.float32),
            pltpu.VMEM((clusters, 4, 8, (listed - 1) * size), jnp.float32),
            pltpu.VMEM((3, atom_total, lanes), jnp.float32),
            pltpu.VMEM((atom_total, atom_total), jnp.bfloat16),
            pltpu.VMEM((16, atom_total), jnp.float32),
            flags,
            flags,
        ],
        compiler_params=pltpu.CompilerParams(
            collective_id=1, has_side_effects=True, vmem_limit_bytes=16 << 20
        ),
        name="finish",
    )(
        pltpu.with_memory_space_constraint(pair_lists, pltpu.HBM),
        partial,
        raw,
        rank,
        columns,
        before,
    )


def green_table(period):
    index = np.arange(period)
    signed = np.where(index <= period // 2, index, index - period) / (period * spacing)
    modulus = ((2.0 + np.cos(index * (2.0 * np.pi / period))) / 3.0) ** 2
    square = signed * signed
    return np.stack([square, np.exp(-((np.pi / ewald_split) ** 2) * square) / modulus]).astype(
        np.float32
    )


def green_factors(index, period):
    signed = jnp.where(index <= period // 2, index, index - period).astype(jnp.float32) / (
        period * spacing
    )
    modulus = ((2.0 + jnp.cos(index.astype(jnp.float32) * (2.0 * jnp.pi / period))) / 3.0) ** 2
    square = signed * signed
    return jnp.stack([square, jnp.exp(-((jnp.pi / ewald_split) ** 2) * square) / modulus])


def one_cluster(own_rows, partner):
    offsets = (own_rows[:3, :, None] - partner[:3, None, :]) * spacing
    dist_square = jnp.sum(offsets * offsets, axis=0)
    soft_square = dist_square + soft_core
    soft_dist = jnp.sqrt(soft_square)
    scaled = ewald_split * soft_dist
    strength = (
        jax.scipy.special.erfc(scaled) / soft_dist
        + ewald_split * root_factor * jnp.exp(-scaled * scaled)
    ) / soft_square
    cutoff_taper = jnp.where(
        dist_square < cutoff * cutoff, (1.0 - dist_square / (cutoff * cutoff)) ** 2, 0.0
    )
    weight = partner[3][None, :] * strength * cutoff_taper
    return own_rows[3] * jnp.sum(weight[None] * offsets, axis=2)


def far_by_planes(bounds, atoms, count_x, count_y, cells_x, cells_y):
    devices = count_x * count_y
    depth = GRID_Z // devices
    tiles = atoms.shape[2]
    pad_y = round_up(cells_y + 3, 8)
    stride = round_up(pad_y, 16)
    window = 2 * cells_y
    turn_x = halves(jnp.asarray(hartley(GRID_X)))
    turn_y = halves(jnp.asarray(hartley(GRID_Y)))
    volume = GRID_X * GRID_Y * GRID_Z * spacing**3
    column = jnp.asarray(green_table(GRID_X).T)
    row = jnp.asarray(green_table(GRID_Y))
    every_k = np.arange(GRID_Z)
    taps = np.outer(every_k, np.arange(4)) * (2.0 * np.pi / GRID_Z)
    square, scale = green_table(GRID_Z)
    table = np.concatenate(
        [
            every_k[:, None],
            np.cos(taps) + np.sin(taps),
            np.cos(taps) - np.sin(taps),
            square[:, None],
            scale[:, None] / (np.pi * volume),
        ],
        axis=1,
    ).astype(np.float32)
    vmem = pl.BlockSpec(memory_space=pltpu.VMEM)
    rows = GRID_X + window_rows
    batch = depth * window_rows
    angle = every_k * (2.0 * np.pi / GRID_Z)
    circle = np.repeat(np.stack([np.cos(angle), np.sin(angle)]), 8, axis=0).astype(np.float32)
    constants = (*turn_x, *turn_y, column, row, jnp.asarray(circle), jnp.asarray(table))
    fixed = pl.BlockSpec(memory_space=pltpu.HBM)
    return pl.pallas_call(
        functools.partial(mesh_kernel, (count_x, count_y), (cells_x, cells_y), pad_y),
        in_specs=[pl.BlockSpec(memory_space=pltpu.SMEM)] + [vmem] + [fixed] * fixed_arrays,
        out_specs=vmem,
        out_shape=jax.ShapeDtypeStruct((devices, 3, tiles, lanes), jnp.float32),
        scratch_shapes=[
            pltpu.VMEM((2, depth, rows, GRID_Y), jnp.float32),
            pltpu.VMEM((depth, rows, 4 * GRID_Y), jnp.float32),
            pltpu.VMEM((36 * devices * tiles, lanes), jnp.float32),
            pltpu.VMEM((devices * tiles * depth, lanes), jnp.float32),
            pltpu.VMEM((devices * tiles * depth, lanes), jnp.float32),
            pltpu.VMEM((devices * tiles, 2 * stride, lanes), jnp.bfloat16),
            pltpu.VMEM((group_size, 2 * window, 2 * lanes), jnp.bfloat16),
            pltpu.VMEM((group_size, batch, 2 * lanes), jnp.bfloat16),
            pltpu.VMEM((gather_size, batch, 2 * lanes), jnp.float32),
            pltpu.VMEM((GRID_X, GRID_Y), jnp.float32),
            pltpu.VMEM((GRID_X, GRID_Y), jnp.float32),
            pltpu.SMEM((4 * devices * tiles,), jnp.int32),
            *[pltpu.VMEM(value.shape, value.dtype) for value in constants],
            pltpu.SemaphoreType.DMA((fixed_arrays,)),
        ],
        compiler_params=pltpu.CompilerParams(vmem_limit_bytes=36 << 20),
        name="mesh",
    )(
        bounds, atoms, *[pltpu.with_memory_space_constraint(value, pltpu.HBM) for value in constants]
    )


def convolved_by_lines(charge_mesh, count_x, count_y):
    turn_x = jnp.asarray(hartley(GRID_X))
    turn_y = jnp.asarray(hartley(GRID_Y))
    product = functools.partial(
        jnp.einsum, precision=lax.Precision.HIGHEST, preferred_element_type=jnp.float32
    )
    exchange = functools.partial(lax.all_to_all, tiled=True)
    lines = exchange(charge_mesh, "gx", split_axis=2, concat_axis=0)
    lines = product("xyk,xu->uyk", lines, turn_x)
    lines = exchange(lines, "gy", split_axis=0, concat_axis=1)
    lines = product("uyk,yv->uvk", lines, turn_y)
    wide, _, depth = lines.shape
    start_x = lax.axis_index("gy") * wide
    start_z = lax.axis_index("gx") * depth
    volume = GRID_X * GRID_Y * GRID_Z * spacing**3
    fx = green_factors(start_x + jnp.arange(wide, dtype=jnp.int32), GRID_X)
    fy = green_factors(jnp.arange(GRID_Y, dtype=jnp.int32), GRID_Y)
    fz = green_factors(start_z + jnp.arange(depth, dtype=jnp.int32), GRID_Z)
    square = fx[0][:, None, None] + fy[0][:, None] + fz[0]
    scale = fx[1][:, None, None] * fy[1][:, None] * fz[1] / (math.pi * volume)
    lines = lines * jnp.where(square > 0.0, scale / jnp.where(square > 0.0, square, 1.0), 0.0)
    lines = product("uvk,vy->uyk", lines, turn_y)
    lines = exchange(lines, "gy", split_axis=1, concat_axis=0)
    lines = product("uyk,ux->xyk", lines, turn_x)
    return exchange(lines, "gx", split_axis=0, concat_axis=2)


def far_by_lines(atoms, base, count_x, count_y, cells_x, cells_y, cells_z):
    atom_total = atoms.shape[1]
    cells = (cells_x, cells_y, cells_z)
    pad = (round_up(cells_x + 3, rows_group), round_up(cells_y + 3, 8))
    pad_x, pad_y = pad
    turn_z = jnp.asarray(hartley(GRID_Z))
    spread = pl.pallas_call(
        functools.partial(spread_kernel, cells, pad),
        out_shape=jax.ShapeDtypeStruct((pad_x, pad_y, GRID_Z), jnp.float32),
        scratch_shapes=[
            pltpu.VMEM((pad_x, atom_total), jnp.float32),
            pltpu.VMEM((pad_y, atom_total), jnp.float32),
            pltpu.VMEM((atom_total, 2 * GRID_Z), jnp.bfloat16),
            pltpu.VMEM((rows_group * pad_y, atom_total), jnp.bfloat16),
            pltpu.VMEM((rows_group * pad_y, atom_total), jnp.bfloat16),
        ],
        name="spread",
    )(atoms, base, turn_z)

    from_x = moved(spread[cells_x : cells_x + 3, :cells_y], 1, 0)
    from_y = moved(spread[:cells_x, cells_y : cells_y + 3], 0, 1)
    from_both = moved(spread[cells_x : cells_x + 3, cells_y : cells_y + 3], 1, 1)
    charge_mesh = (
        spread[:cells_x, :cells_y]
        .at[:3]
        .add(from_x)
        .at[:, :3]
        .add(from_y)
        .at[:3, :3]
        .add(from_both)
    )
    potential = convolved_by_lines(charge_mesh, count_x, count_y)
    upper_x = moved(potential[:3], -1, 0)
    upper_y = moved(potential[:, :3], 0, -1)
    upper_both = moved(potential[:3, :3], -1, -1)
    wider = jnp.concatenate(
        [
            jnp.concatenate([potential, upper_x], axis=0),
            jnp.concatenate([upper_y, upper_both], axis=0),
        ],
        axis=1,
    )
    wider = jnp.pad(wider, ((0, pad_x - cells_x - 3), (0, pad_y - cells_y - 3), (0, 0)))
    return pl.pallas_call(
        functools.partial(gather_kernel, cells, pad),
        out_shape=jax.ShapeDtypeStruct((3, atom_total), jnp.float32),
        scratch_shapes=[
            pltpu.VMEM((pad_x, atom_total), jnp.float32),
            pltpu.VMEM((pad_x, atom_total), jnp.float32),
            pltpu.VMEM((pad_y, atom_total), jnp.float32),
            pltpu.VMEM((pad_y, atom_total), jnp.float32),
            pltpu.VMEM((2 * GRID_Z, 2 * atom_total), jnp.bfloat16),
            pltpu.VMEM((rows_group * pad_y, 2 * atom_total), jnp.float32),
        ],
        name="gather",
    )(atoms, base, turn_z, wider)


def local(positions, charges, pair_lists, slab_dest, atom_counts):
    count_x = lax.axis_size("gx")
    count_y = lax.axis_size("gy")
    devices = count_x * count_y
    atom_total = positions.shape[3]
    clusters = pair_lists.shape[2]
    cluster_size = atom_total // clusters
    blocks = slab_dest.shape[2]
    block_size = atom_total // blocks
    cells_x = GRID_X // count_x
    cells_y = GRID_Y // count_y
    cells_z = GRID_Z // count_y
    by_planes = (
        GRID_Z == 8 * devices
        and GRID_Z == lanes
        and cells_y == 64
        and cells_x % 8 == 0
        and cells_x <= 64
        and count_y % 2 == 0
        and atom_total == 8 * lanes
        and cluster_size % lanes == 0
    )
    if by_planes:
        sizes = (count_x, count_y, cells_x, cells_y)
        raw, atoms, bounds, rank, columns, before = shared(
            positions, charges, atom_counts, clusters, *sizes
        )
        partial = far_by_planes(bounds, atoms, *sizes)
        short_sums, long_sums = finished(
            pair_lists, partial, raw, rank, columns, before, *sizes
        )
        living = jnp.arange(atom_total, dtype=jnp.int32) < atom_counts[0, 0]
        charge = jnp.where(living, charges[0, 0], 0.0)
        return (short_sums * (charge * spacing), long_sums * (charge * (-1.0 / spacing)))
    living = jnp.arange(atom_total, dtype=jnp.int32) < atom_counts[0, 0]
    charge = jnp.where(living, charges[0, 0], 0.0)
    packed = jnp.concatenate([positions, charge[None, None, None, :]], axis=0)
    atoms = packed.reshape(4, atom_total)
    base = jnp.broadcast_to(
        (slab_dest[0, 0] * cells_z)[:, None], (blocks, block_size)
    ).reshape(1, atom_total)
    gathered = lax.all_gather(atoms, ("gx", "gy"), axis=0, tiled=False)
    far_part = far_by_lines(atoms, base, count_x, count_y, cells_x, cells_y, cells_z)

    chosen = pair_lists[0, 0]
    beside = chosen // clusters
    step_x, step_y = (beside // 3 - 1, beside % 3 - 1)
    at_x = (lax.axis_index("gx") + step_x + count_x) % count_x
    at_y = (lax.axis_index("gy") + step_y + count_y) % count_y
    number = (at_x * count_y + at_y) * clusters + chosen % clusters
    pick = (number[:, :, None] == jnp.arange(devices * clusters, dtype=jnp.int32)).astype(
        jnp.float32
    )
    pool = gathered[:, :4].reshape(devices, 4, clusters, cluster_size)
    pool = jnp.transpose(pool, (1, 0, 2, 3)).reshape(4, devices * clusters, cluster_size)
    partners = jnp.einsum(
        "cln,fnk->cflk",
        pick,
        pool,
        precision=lax.Precision.HIGHEST,
        preferred_element_type=jnp.float32,
    )
    shift_x = (step_x * cells_x).astype(jnp.float32)
    shift_y = (step_y * cells_y).astype(jnp.float32)
    flat = jnp.zeros_like(shift_x)
    shift = jnp.stack([shift_x, shift_y, flat, flat], axis=1)
    partners = (partners + shift[:, :, :, None]).reshape(clusters, 4, -1)
    own = packed.reshape(4, clusters, cluster_size)
    pair_part = jnp.stack(
        [one_cluster(own[:, c], partners[c]) for c in range(clusters)], axis=1
    )
    short_forces = pair_part.reshape(3, 1, 1, atom_total)
    return (short_forces, far_part.reshape(3, 1, 1, atom_total))


def solution(mesh):
    return jax.shard_map(
        local,
        mesh=mesh,
        in_specs=(
            P(None, ("rep", "gx"), "gy", None),
            P(("rep", "gx"), "gy", None),
            P(("rep", "gx"), "gy", None, None),
            P(("rep", "gx"), "gy", None),
            P(("rep", "gx"), "gy"),
        ),
        out_specs=(P(None, ("rep", "gx"), "gy", None), P(None, ("rep", "gx"), "gy", None)),
        check_vma=False,
    )
```

```python
import functools
import math

import jax
import jax.numpy as jnp
import numpy as np
from jax import lax
from jax.experimental import pallas as pl
from jax.experimental.pallas import tpu as pltpu
from jax.sharding import PartitionSpec as P

GRID_X = 256
GRID_Y = 256
GRID_Z = 128


spacing = 0.16
ewald_split = 3.47
cutoff = 0.9
soft_core = 0.09
root_factor = 1.1283791670955126
rows_group = 8
lanes = 128
window_rows = 24
group_size = 16
gather_size = 8
cell_group = 4
plane_group = 8
fixed_arrays = 8


def moved(value, step_x, step_y):
    count_x = lax.axis_size("gx")
    count_y = lax.axis_size("gy")
    pairs = [
        (i * count_y + j, (i + step_x) % count_x * count_y + (j + step_y) % count_y)
        for i in range(count_x)
        for j in range(count_y)
    ]
    return lax.ppermute(value, ("gx", "gy"), pairs)


def round_up(value, multiple):
    return -(-value // multiple) * multiple


def hartley(period):
    turns = np.outer(np.arange(period), np.arange(period)) % period
    phases = turns * (2.0 * np.pi / period)
    return (np.cos(phases) + np.sin(phases)).astype(np.float32)


def halves(value):
    high = value.astype(jnp.bfloat16)
    low = (value - high.astype(jnp.float32)).astype(jnp.bfloat16)
    return (high, low)


def dot(left_side, right_side):
    return jnp.dot(left_side, right_side, preferred_element_type=jnp.float32)


def spline_weights(fraction):
    remain = 1.0 - fraction
    square = fraction * fraction
    cube_part = square * fraction
    values = [
        remain * remain * remain / 6.0,
        (3.0 * cube_part - 6.0 * square + 4.0) / 6.0,
        (-3.0 * cube_part + 3.0 * square + 3.0 * fraction + 1.0) / 6.0,
        cube_part / 6.0,
    ]
    slopes = [
        -0.5 * remain * remain,
        0.5 * (3.0 * square - 4.0 * fraction),
        0.5 * (-3.0 * square + 2.0 * fraction + 1.0),
        0.5 * square,
    ]
    return (values, slopes)


def split_cells(coordinate, offset, cell_count):
    inside = coordinate - offset
    lowest = jnp.clip(jnp.floor(inside).astype(jnp.int32), 0, cell_count - 1)
    return (lowest, inside - lowest.astype(inside.dtype))


def spline_table(lowest, values, table_size, period=None):
    points = lax.broadcasted_iota(jnp.int32, (table_size, lowest.shape[1]), 0)
    lookup = jnp.zeros(points.shape, jnp.float32)
    for spline_term in range(4):
        at = lowest + spline_term
        if period is not None:
            at = jnp.where(at >= period, at - period, at)
        lookup = jnp.where(points == at, values[spline_term], lookup)
    return lookup


def spread_kernel(cells, pad, atoms_ref, base_ref, turn_ref, out_ref, wx_ref, wy_ref, wz_ref, hi_ref, lo_ref):
    cells_x, cells_y, cells_z = cells
    pad_x, pad_y = pad
    atom_total = atoms_ref.shape[1]
    low_x, frac_x = split_cells(atoms_ref[0:1, :], 0.0, cells_x)
    low_y, frac_y = split_cells(atoms_ref[1:2, :], 0.0, cells_y)
    base = base_ref[...]
    low_z, frac_z = split_cells(atoms_ref[2:3, :], base.astype(jnp.float32), cells_z)
    wx_ref[...] = spline_table(low_x, spline_weights(frac_x)[0], pad_x) * atoms_ref[3:4, :]
    wy_ref[...] = spline_table(low_y, spline_weights(frac_y)[0], pad_y)
    turn = turn_ref[...]
    size_z = turn.shape[0]
    table_z = spline_table(base + low_z, spline_weights(frac_z)[0], size_z, size_z)
    waves = jnp.dot(
        turn, table_z, precision=lax.Precision.HIGHEST, preferred_element_type=jnp.float32
    ).T
    high, low = halves(waves)
    wz_ref[:, :size_z] = high
    wz_ref[:, size_z:] = low

    @pl.loop(0, pad_x // rows_group)
    def _(chunk):
        for inner in range(rows_group):
            row = wx_ref[pl.ds(chunk * rows_group + inner, 1), :]
            high, low = halves(row * wy_ref[...])
            hi_ref[pl.ds(inner * pad_y, pad_y), :] = high
            lo_ref[pl.ds(inner * pad_y, pad_y), :] = low
        both = dot(hi_ref[...], wz_ref[...])
        rest = dot(lo_ref[...], wz_ref[:, :size_z])
        total = both[:, :size_z] + both[:, size_z:] + rest
        out_ref[pl.ds(chunk * rows_group, rows_group)] = total.reshape(rows_group, pad_y, size_z)


def gather_kernel(cells, pad, atoms_ref, base_ref, turn_ref, mesh_ref, out_ref, wx_ref, vx_ref, wy_ref, vy_ref, wz_ref, level_ref):
    cells_x, cells_y, cells_z = cells
    pad_x, pad_y = pad
    atom_total = atoms_ref.shape[1]
    low_x, frac_x = split_cells(atoms_ref[0:1, :], 0.0, cells_x)
    low_y, frac_y = split_cells(atoms_ref[1:2, :], 0.0, cells_y)
    base = base_ref[...]
    low_z, frac_z = split_cells(atoms_ref[2:3, :], base.astype(jnp.float32), cells_z)
    values, slopes = spline_weights(frac_x)
    wx_ref[...] = spline_table(low_x, values, pad_x)
    vx_ref[...] = spline_table(low_x, slopes, pad_x)
    values, slopes = spline_weights(frac_y)
    wy_ref[...] = spline_table(low_y, values, pad_y)
    vy_ref[...] = spline_table(low_y, slopes, pad_y)
    values, slopes = spline_weights(frac_z)
    turn = turn_ref[...]
    size_z = turn.shape[0]
    for place, terms in enumerate((values, slopes)):
        table_z = spline_table(base + low_z, terms, size_z, size_z)
        waves = jnp.dot(
            turn, table_z, precision=lax.Precision.HIGHEST, preferred_element_type=jnp.float32
        )
        high, low = halves(waves)
        wz_ref[:size_z, pl.ds(place * atom_total, atom_total)] = high
        wz_ref[size_z:, pl.ds(place * atom_total, atom_total)] = low
    groups = pad_y // 8

    def one_chunk(chunk, sums):
        rows = mesh_ref[pl.ds(chunk * rows_group, rows_group)].reshape(rows_group * pad_y, size_z)
        high, low = halves(rows)
        level_ref[...] = dot(jnp.concatenate([high, high], axis=1), wz_ref[...]) + dot(
            low, wz_ref[:size_z, :]
        )
        first, second, third = sums
        for inner in range(rows_group):
            flat = level_ref[pl.ds(inner * pad_y, pad_y), :atom_total]
            tilt = level_ref[pl.ds(inner * pad_y, pad_y), atom_total:]
            across = wy_ref[...]
            part_x = jnp.sum((across * flat).reshape(groups, 8, atom_total), axis=0)
            part_y = jnp.sum((vy_ref[...] * flat).reshape(groups, 8, atom_total), axis=0)
            part_z = jnp.sum((across * tilt).reshape(groups, 8, atom_total), axis=0)
            weight = wx_ref[pl.ds(chunk * rows_group + inner, 1), :]
            slope = vx_ref[pl.ds(chunk * rows_group + inner, 1), :]
            first = first + slope * part_x
            second = second + weight * part_y
            third = third + weight * part_z
        return (first, second, third)

    zero = jnp.zeros((8, atom_total), jnp.float32)
    sums = lax.fori_loop(0, pad_x // rows_group, one_chunk, (zero, zero, zero))
    factor = -atoms_ref[3:4, :] / spacing
    for place in range(3):
        out_ref[pl.ds(place, 1), :] = factor * jnp.sum(sums[place], axis=0, keepdims=True)


def peers_of(count_x, count_y):
    place_x, place_y = (lax.axis_index("gx"), lax.axis_index("gy"))
    peers = []
    for order in range(1, count_x * count_y):
        peer_x = lax.rem(place_x + order // count_y, count_x)
        peer_y = lax.rem(place_y + order % count_y, count_y)
        peers.append((peer_x, peer_y))
    return peers


root_terms = (
    3.9164407301418542,
    -0.0037127819564810594,
    0.16802528315459195,
    -0.003061234121505335,
    -0.0076524954798020545,
    0.002268454833542123,
    -0.0003056487922112269,
    1.686888935413571e-05,
)


def pair_weight(square):
    soft_square = square * (spacing * spacing) + soft_core
    inverse = lax.rsqrt(soft_square)
    series = jnp.full_like(inverse, root_terms[-1])
    for term in root_terms[-2::-1]:
        series = series * inverse + term
    decay = jnp.exp(soft_square * (-ewald_split * ewald_split))
    taper = jnp.maximum(1.0 - square * (spacing * spacing / (cutoff * cutoff)), 0.0)
    return (decay * series) * (inverse * taper) ** 2


def row_sums(values):
    total = None
    ones = jnp.ones((16, values.shape[1]), jnp.bfloat16)
    for _ in range(3):
        part = values.astype(jnp.bfloat16)
        values = values - part.astype(jnp.float32)
        summed = lax.dot_general(
            ones, part, (((1,), (1,)), ((), ())), preferred_element_type=jnp.float32
        )
        total = summed if total is None else total + summed
    return total[0:1, :]


def place_partners(sizes, cells, pairs_ref, atoms_ref, partner_ref):
    count_x, count_y = sizes
    cells_x, cells_y = cells
    place_x, place_y = (lax.axis_index("gx"), lax.axis_index("gy"))
    clusters, listed = pairs_ref.shape[2:]
    size = atoms_ref.shape[2] // clusters
    for c in range(clusters):
        for n in range(1, listed):
            chosen = pairs_ref[0, 0, c, n]
            beside = lax.div(chosen, clusters)
            which = chosen - beside * clusters
            row_x = lax.div(beside, 3)
            step_x = row_x - 1
            step_y = beside - row_x * 3 - 1
            from_x = lax.rem(place_x + step_x + count_x, count_x)
            from_y = lax.rem(place_y + step_y + count_y, count_y)
            block = atoms_ref[from_x * count_y + from_y]
            part = block[:, :size]
            for k in range(1, clusters):
                part = jnp.where(which == k, block[:, k * size : (k + 1) * size], part)
            shifts = (
                (step_x * cells_x).astype(jnp.float32),
                (step_y * cells_y).astype(jnp.float32),
            )
            for axis in range(4):
                row = part[axis : axis + 1, :]
                if axis < 2:
                    row = row + shifts[axis]
                partner_ref[c, axis, :, (n - 1) * size : n * size] = jnp.broadcast_to(
                    row, (8, size)
                )


def pair_sums(clusters, size, height, column_ref, partner_ref, before_ref, sum_ref):
    @pl.loop(0, clusters)
    def _(c):
        @pl.loop(0, size // height)
        def _(step):
            for part in range(height // 8):
                start = c * size + step * height + part * 8
                rows = pl.ds(pl.multiple_of(start, 8), 8)
                own = [column_ref[axis, rows, :] for axis in range(3)]
                sums = [
                    jnp.zeros((8, lanes), jnp.float32)
                    if before_ref is None
                    else before_ref[axis, rows, :]
                    for axis in range(3)
                ]
                for tile in range(partner_ref.shape[3] // lanes):
                    span = slice(tile * lanes, (tile + 1) * lanes)
                    offsets = [own[axis] - partner_ref[c, axis, :, span] for axis in range(3)]
                    square = sum(offset * offset for offset in offsets)
                    weight = pair_weight(square) * partner_ref[c, 3, :, span]
                    sums = [total + weight * offset for total, offset in zip(sums, offsets)]
                for axis in range(3):
                    sum_ref[axis, rows, :] = sums[axis]


def share_kernel(sizes, cells, clusters, count_ref, position_ref, charge_ref, raw_ref, sorted_ref, bounds_ref, rank_ref, column_ref, sum_ref, key_ref, split_ref, partner_ref, raw_send, raw_recv, sort_send, sort_recv, mark_send, mark_recv):
    count_x, count_y = sizes
    cells_x, _ = cells
    place_x, place_y = (lax.axis_index("gx"), lax.axis_index("gy"))
    me = place_x * count_y + place_y
    place_chip, place_core = (place_y // 2, lax.rem(place_y, 2))
    chips = count_y // 2

    def at(step_x, step_chip, flip):
        peer_x = lax.rem(place_x + step_x, count_x)
        peer_chip = lax.rem(place_chip + step_chip, chips)
        peer_core = 1 - place_core if flip else place_core
        return (peer_x, peer_chip * 2 + peer_core)

    peers = peers_of(count_x, count_y)
    barrier = pltpu.get_barrier_semaphore()
    for peer_x, peer_y in peers:
        pl.semaphore_signal(
            barrier,
            inc=1,
            device_id={"gx": peer_x, "gy": peer_y},
            device_id_type=pl.DeviceIdType.MESH,
        )

    def sent(ref, owner, peer, send_sem, recv_sem, order, slot):
        return pltpu.make_async_remote_copy(
            src_ref=ref.at[owner],
            dst_ref=ref.at[owner],
            send_sem=send_sem.at[order],
            recv_sem=recv_sem.at[slot],
            device_id={"gx": peer[0], "gy": peer[1]},
            device_id_type=pl.DeviceIdType.MESH,
        )

    passed = []

    def passes(owner, peer):
        order = len(passed)
        copies = [
            sent(sorted_ref, owner, peer, sort_send, sort_recv, order, owner),
            sent(bounds_ref, owner, peer, mark_send, mark_recv, order, owner),
        ]
        for copy in copies:
            copy.start()
        passed.append(copies)

    def arrives(owner, peer):
        sent(sorted_ref, owner, peer, sort_send, sort_recv, 0, owner).wait_recv()
        sent(bounds_ref, owner, peer, mark_send, mark_recv, 0, owner).wait_recv()

    atom_total = charge_ref.shape[2]
    tiles = atom_total // lanes
    slot = lax.broadcasted_iota(jnp.int32, (1, atom_total), 1)
    living = slot < count_ref[0, 0]
    charge = jnp.where(living, charge_ref[0], 0.0)
    rows = [position_ref[axis, 0] for axis in range(3)] + [charge]
    for axis in range(4):
        raw_ref[me, pl.ds(axis, 1), :] = rows[axis]
    column = jnp.clip(jnp.floor(rows[0]), 0.0, cells_x - 1.0)
    key = jnp.where(living, column, float(cells_x)) * float(atom_total) + slot.astype(jnp.float32)
    for tile in range(tiles):
        span = slice(tile * lanes, (tile + 1) * lanes)
        key_ref[span, :] = jnp.broadcast_to(key[:, span], (lanes, lanes)).T
    wide = [
        jnp.broadcast_to(key[:, tile * lanes : (tile + 1) * lanes], (8, lanes))
        for tile in range(tiles)
    ]

    def count_group(group, totals):
        for inner in range(8):
            others = key_ref[pl.ds(pl.multiple_of(group * 64 + inner * 8, 8), 8), :]
            totals = tuple(
                total + jnp.where(others < own, 1.0, 0.0) for total, own in zip(totals, wide)
            )
        return totals

    zero = jnp.zeros((8, lanes), jnp.float32)
    totals = lax.fori_loop(0, atom_total // 64, count_group, (zero,) * tiles)
    for tile, total in enumerate(totals):
        rank_ref[:, tile * lanes : (tile + 1) * lanes] = jnp.sum(total, axis=0, keepdims=True)

    split_ref[...] = jnp.zeros_like(split_ref)
    rest = raw_ref[me]
    for part in range(3):
        piece = rest.astype(jnp.bfloat16).astype(jnp.float32)
        split_ref[4 * part : 4 * part + 4, :] = piece
        rest = rest - piece
    split = split_ref[...].astype(jnp.bfloat16)
    rank = rank_ref[...]
    block = 2 * lanes
    for part in range(atom_total // block):
        place = lax.broadcasted_iota(jnp.int32, (block, atom_total), 0) + part * block
        chosen = jnp.where(place.astype(jnp.float32) == rank, 1.0, 0.0).astype(jnp.bfloat16)
        found = lax.dot_general(
            split, chosen, (((1,), (1,)), ((), ())), preferred_element_type=jnp.float32
        )
        found = (found[0:4] + found[4:8]) + found[8:12]
        for tile in range(block // lanes):
            row = part * (block // lanes) + tile
            for axis in range(4):
                sorted_ref[me, axis, row : row + 1, :] = found[
                    axis : axis + 1, tile * lanes : (tile + 1) * lanes
                ]
    spot = lax.broadcasted_iota(jnp.int32, (tiles, lanes), 0) * lanes
    spot = spot + lax.broadcasted_iota(jnp.int32, (tiles, lanes), 1)
    inside = spot < count_ref[0, 0]
    column = jnp.clip(jnp.floor(sorted_ref[me, 0]), 0.0, cells_x - 1.0)
    lowest = jnp.min(jnp.where(inside, column, float(cells_x)), axis=1, keepdims=True)
    highest = jnp.max(jnp.where(inside, column, -1.0), axis=1, keepdims=True)
    first = jnp.floor(lowest * 0.125)
    last = jnp.floor((highest + 3.0) * 0.125)
    windows = jnp.where(
        highest >= 0.0, jnp.floor((last - first) * (8.0 / window_rows) + 0.01) + 1.0, 0.0
    )
    lane = lax.broadcasted_iota(jnp.int32, (tiles, lanes), 1)
    row = lax.broadcasted_iota(jnp.int32, (tiles, lanes), 0)
    marks = jnp.where(lane == row, first, jnp.where(lane == row + tiles, windows, 0.0))
    marks = jnp.sum(marks, axis=0, keepdims=True)
    bounds_ref[me] = marks.astype(jnp.int32)

    near = sorted(
        (min(step, count_x - step) + min(chip, chips - chip), step, chip)
        for step in range(count_x)
        for chip in range(chips)
    )[1:]
    mate = at(0, 0, True)
    pl.semaphore_wait(barrier, len(peers))
    for _, step, chip in reversed(near):
        passes(me, at(step, chip, False))
    passes(me, mate)
    beside = sorted(
        {
            step_x % count_x * count_y + step_y % count_y
            for step_x in (-1, 0, 1)
            for step_y in (-1, 0, 1)
        }
        - {0}
    )
    copies = [
        sent(raw_ref, me, peers[order - 1], raw_send, raw_recv, order - 1, order - 1)
        for order in beside
    ]
    for copy in copies:
        copy.start()

    for axis in range(3):
        for tile in range(tiles):
            span = slice(tile * lanes, (tile + 1) * lanes)
            column_ref[axis, span, :] = jnp.broadcast_to(rows[axis][:, span], (lanes, lanes)).T
    size = atom_total // clusters
    for c in range(clusters):
        for axis in range(4):
            row = rows[axis][:, c * size : (c + 1) * size]
            partner_ref[c, axis] = jnp.broadcast_to(row, (8, size))
    pair_sums(clusters, size, 64, column_ref, partner_ref, None, sum_ref)
    for _, step, chip in near:
        owner_x, owner_y = at(step, chip, False)
        arrives(owner_x * count_y + owner_y, (owner_x, owner_y))
        passes(owner_x * count_y + owner_y, mate)
    for _, step, chip in [(0, 0, 0), *near]:
        owner_x, owner_y = at(step, chip, True)
        arrives(owner_x * count_y + owner_y, mate)
    for copy in copies:
        copy.wait()
    for pair in passed:
        for copy in pair:
            copy.wait_send()


def shared(positions, charges, atom_counts, clusters, count_x, count_y, cells_x, cells_y):
    devices = count_x * count_y
    atom_total = charges.shape[2]
    vmem = pl.BlockSpec(memory_space=pltpu.VMEM)
    smem = pl.BlockSpec(memory_space=pltpu.SMEM)
    fewer = pltpu.SemaphoreType.DMA((devices - 1,))
    flags = pltpu.SemaphoreType.DMA((devices,))
    return pl.pallas_call(
        functools.partial(share_kernel, (count_x, count_y), (cells_x, cells_y), clusters),
        in_specs=[smem, vmem, vmem],
        out_specs=[vmem] * 6,
        out_shape=[
            jax.ShapeDtypeStruct((devices, 4, atom_total), jnp.float32),
            jax.ShapeDtypeStruct((devices, 4, atom_total // lanes, lanes), jnp.float32),
            jax.ShapeDtypeStruct((devices, 1, lanes), jnp.int32),
            jax.ShapeDtypeStruct((1, atom_total), jnp.float32),
            jax.ShapeDtypeStruct((3, atom_total, lanes), jnp.float32),
            jax.ShapeDtypeStruct((3, atom_total, lanes), jnp.float32),
        ],
        scratch_shapes=[
            pltpu.VMEM((atom_total, lanes), jnp.float32),
            pltpu.VMEM((16, atom_total), jnp.float32),
            pltpu.VMEM((clusters, 4, 8, atom_total // clusters), jnp.float32),
            fewer,
            fewer,
        ]
        + [flags] * 4,
        compiler_params=pltpu.CompilerParams(
            collective_id=0, has_side_effects=True, vmem_limit_bytes=12 << 20
        ),
        name="share",
    )(
        atom_counts,
        *[pltpu.with_memory_space_constraint(value, pltpu.HBM) for value in (positions, charges)],
    )


def depth_rows(table, circle, height, terms):
    turns = height * table[:, 0:1]
    turns = turns - GRID_Z * jnp.floor(turns * (1.0 / GRID_Z))
    index = turns.astype(jnp.int32)
    cosine, sine = [jnp.take_along_axis(part, index, axis=1) for part in circle]
    results = []
    for weights in terms:
        even = sum(table[:, 1 + t : 2 + t] * weights[t] for t in range(4))
        odd = sum(table[:, 5 + t : 6 + t] * weights[t] for t in range(4))
        results.append(cosine * even + sine * odd)
    return results


def mesh_kernel(sizes, cells, pad_y, bounds_ref, atoms_ref, *refs):
    constants, (out_ref, *scratch) = refs[:fixed_arrays], refs[fixed_arrays:]
    held, copy_sem = scratch[-fixed_arrays - 1 : -1], scratch[-1]
    copies = [
        pltpu.make_async_copy(source, target, copy_sem.at[place])
        for place, (source, target) in enumerate(zip(constants, held))
    ]
    for copy in copies:
        copy.start()
    xh_ref, xl_ref, yh_ref, yl_ref, column_ref, row_ref, circle_ref, table_ref = held
    mesh_ref, stack_ref, prep_ref, deep_ref, steep_ref, near_ref, wy_ref, side_ref, level_ref, square_ref, scale_ref, work_ref = scratch[: -fixed_arrays - 1]
    count_x, count_y = sizes
    cells_x, cells_y = cells
    devices = count_x * count_y
    place = lax.axis_index("gx") * count_y + lax.axis_index("gy")
    tiles = atoms_ref.shape[2]
    depth = stack_ref.shape[0]
    window = 2 * cells_y
    windows = GRID_Y // window
    extra = 8
    share = -(-group_size * cell_group // devices)
    stack_ref[:, GRID_X:, :] = jnp.zeros_like(stack_ref[:, GRID_X:, :])
    out_ref[...] = jnp.zeros_like(out_ref)
    copies[-2].wait()
    copies[-1].wait()
    circle = [circle_ref[:8, :], circle_ref[8:, :]]
    table = table_ref[pl.ds(pl.multiple_of(place * depth, 8), depth), :]

    steps_x = window_rows // 8
    most = (cells_x + 2) // 8 // steps_x + 1

    def prep_row(kind, spot):
        return prep_ref[pl.ds(kind * devices * tiles + spot, 8, stride=0), :]

    def listed_work(cell, total):
        for tile in range(tiles):
            for step in range(most):
                work_ref[total + step] = (cell * tiles + tile) * most + step
            total = total + bounds_ref[cell, 0, tiles + tile]

        return total

    def keep_splines(cell):
        def keep(kind, value):
            rows = pl.ds(pl.multiple_of((kind * devices + cell) * tiles, 8), tiles)
            prep_ref[rows, :] = value

        for axis, count in enumerate((cells_x, cells_y)):
            value = atoms_ref[cell, axis]
            lowest = jnp.clip(jnp.floor(value), 0.0, count - 1.0)
            values, slopes = spline_weights(value - lowest)
            keep(9 * axis, lowest)
            for term in range(4):
                keep(9 * axis + 1 + term, values[term])
                keep(9 * axis + 5 + term, slopes[term])
                if axis == 1:
                    for kind, whole in ((28, values[term]), (32, slopes[term])):
                        keep(kind + term, whole - whole.astype(jnp.bfloat16).astype(jnp.float32))
        value = atoms_ref[cell, 2]
        height = jnp.floor(value)
        values, slopes = spline_weights(value - height)
        keep(18, height)
        for term in range(4):
            keep(19 + term, values[term])
            keep(23 + term, slopes[term])
        keep(27, atoms_ref[cell, 3])

    def keep_modes(cell):
        for tile in range(tiles):
            spot = cell * tiles + tile
            height = prep_row(18, spot)
            terms = [[prep_row(19 + 4 * s + term, spot) for term in range(4)] for s in range(2)]
            deep, steep = depth_rows(table, circle, height, terms)
            rows = pl.ds(pl.multiple_of(spot * depth, 8), depth)
            deep_ref[rows, :] = deep
            steep_ref[rows, :] = steep

    def prepare_some(turn, total):
        for inner in range(cell_group):
            cell = turn * cell_group + inner
            mesh_ref[lax.div(cell, depth), lax.rem(cell, depth)] = jnp.zeros(
                mesh_ref.shape[2:], jnp.float32
            )
            total = listed_work(cell, total)
        for inner in range(cell_group):
            keep_splines(turn * cell_group + inner)
        for inner in range(cell_group):
            keep_modes(turn * cell_group + inner)
        for inner in range(share):
            place = jnp.minimum(turn * share + inner, group_size - 1)
            wy_ref[place] = jnp.zeros(wy_ref.shape[1:], wy_ref.dtype)
        return total

    total = lax.fori_loop(0, devices // cell_group, prepare_some, jnp.int32(0))
    rounds = lax.div(total + group_size - 1, group_size)

    row_index = lax.broadcasted_iota(jnp.int32, (8, lanes), 0).astype(jnp.float32)

    def looked_up(points, lowest, term_lists):
        results = [jnp.zeros_like(points) for _ in term_lists]
        for term in range(4):
            hit = points == lowest + float(term)
            results = [
                jnp.where(hit, terms[term], result)
                for terms, result in zip(term_lists, results)
            ]
        return results

    def kinds(first, spot):
        return [prep_row(first + term, spot) for term in range(4)]

    stride = round_up(pad_y, 16)
    far_away = 1.0e6

    def task(index):
        entry = jnp.where(index < total, work_ref[index], 0)
        spot = lax.div(entry, most)
        cell = lax.div(spot, tiles)
        chunk = spot - cell * tiles
        begin = bounds_ref[cell, 0, chunk] * 8 + (entry - spot * most) * window_rows
        base = jnp.where(index < total, begin.astype(jnp.float32), far_away)
        i = lax.div(cell, count_y)
        rows = pl.ds(pl.multiple_of(i * cells_x + begin, 8), window_rows)
        return (spot, cell, chunk, cell - i * count_y, rows, base)

    packed_index = jnp.concatenate([row_index, row_index + 8.0], axis=0).astype(jnp.bfloat16)

    def packed_row(kind, spot):
        row = prep_row(kind, spot)
        return jnp.concatenate([row, row], axis=0).astype(jnp.bfloat16)

    def y_table(spot, kind, low_kind):
        lowest = packed_row(9, spot)
        highs = [packed_row(kind + term, spot) for term in range(4)]
        lows = [packed_row(low_kind + term, spot) for term in range(4)]
        starts = [lowest + jnp.bfloat16(term) for term in range(4)]
        for group in range(stride // 16):
            points = packed_index + jnp.bfloat16(group * 16)
            high = low = jnp.zeros_like(points)
            for term in range(4):
                hit = points == starts[term]
                high = jnp.where(hit, highs[term], high)
                low = jnp.where(hit, lows[term], low)
            yield (slice(group * 16, group * 16 + 16), high, low)

    @pl.loop(0, rounds)
    def _(turn):
        tasks = [task(turn * group_size + place) for place in range(group_size)]
        for place, (spot, _, _, _, _, base) in enumerate(tasks):
            for rows, high, low in y_table(spot, 10, 28):
                after = slice(window + rows.start, window + rows.stop)
                later = slice(stride + rows.start, stride + rows.stop)
                wy_ref[place, rows, :lanes] = high
                wy_ref[place, rows, lanes:] = high
                wy_ref[place, after, :lanes] = low
                near_ref[spot, rows, :] = high
                near_ref[spot, later, :] = low
            lowest = prep_row(0, spot) - base
            charge = prep_row(27, spot)
            terms = [term * charge for term in kinds(1, spot)]
            weights = [
                looked_up(row_index + float(tile * 8), lowest, [terms])[0]
                for tile in range(steps_x)
            ]
            modes = [
                deep_ref[pl.ds(spot * depth + k, 8, stride=0), :] for k in range(depth)
            ]
            blocks = [weight * mode for mode in modes for weight in weights]
            for pair in range(len(blocks) // 2):
                high, low = halves(jnp.concatenate(blocks[2 * pair : 2 * pair + 2], axis=0))
                rows = slice(pair * 16, pair * 16 + 16)
                side_ref[place, rows, :lanes] = high
                side_ref[place, rows, lanes:] = low
        for place, (_, _, _, j, rows, _) in enumerate(tasks):
            product = lax.dot_general(
                side_ref[place],
                wy_ref[place],
                (((1,), (1,)), ((), ())),
                preferred_element_type=jnp.float32,
            )
            product = product[:, :window] + product[:, window:]
            m = lax.div(j, 2)
            here = pl.ds(pl.multiple_of(m * window, lanes), window)
            mesh_ref[j - 2 * m, :, rows, here] += product.reshape(depth, window_rows, window)

    def across(value):
        high, low = halves(value)
        return dot(xh_ref[...], high) + dot(xl_ref[...], high) + dot(xh_ref[...], low)

    def along(value):
        high, low = halves(value)
        return dot(high, yh_ref[...]) + dot(high, yl_ref[...]) + dot(low, yh_ref[...])

    plane_lane = lax.broadcasted_iota(jnp.int32, (GRID_X, window), 1)
    for copy in copies[:-2]:
        copy.wait()
    shape = (GRID_X, GRID_Y)
    square_ref[...] = jnp.broadcast_to(column_ref[:, 0:1], shape) + row_ref[0:1, :]
    scale_ref[...] = jnp.broadcast_to(column_ref[:, 1:2], shape) * row_ref[1:2, :]

    def charge_of(k):
        charge = mesh_ref[0, k, :GRID_X, :] + pltpu.roll(mesh_ref[1, k, :GRID_X, :], cells_y, 1)
        over = slice(GRID_X, GRID_X + extra)
        beyond = mesh_ref[0, k, over, :] + pltpu.roll(mesh_ref[1, k, over, :], cells_y, 1)
        return jnp.concatenate([charge[:extra] + beyond, charge[extra:]], axis=0)

    def green_of(k):
        mode = pl.ds(place * depth + k, 1)
        square = square_ref[...] + table_ref[mode, 9:10]
        scale = scale_ref[...] * table_ref[mode, 10:11]
        return jnp.where(square > 0.0, scale / square, 0.0)

    def place_plane(k, plane):
        for odd in range(2):
            if odd:
                plane = pltpu.roll(plane, GRID_Y - cells_y, 1)
            for j_half in range(windows):
                j = 2 * j_half + odd
                block = plane[:, j_half * window : (j_half + 1) * window]
                high = block.astype(jnp.bfloat16).astype(jnp.float32)
                low = block - high
                shifted = pltpu.roll(high, stride, 1)
                left = jnp.where(plane_lane < stride, high, shifted)
                right = jnp.where(
                    plane_lane < 2 * stride - window,
                    shifted,
                    pltpu.roll(low, 2 * stride - window, 1),
                )
                for side, value in enumerate((left, right)):
                    span = slice((2 * j + side) * window, (2 * j + side + 1) * window)
                    stack_ref[k, :GRID_X, span] = value
                    stack_ref[k, GRID_X : GRID_X + extra, span] = value[:extra]

    @pl.loop(0, depth // plane_group)
    def _(pair):
        spots = [pair * plane_group + inner for inner in range(plane_group)]
        stages = [
            lambda k, _: across(charge_of(k)),
            lambda k, value: along(value),
            lambda k, value: along(value * green_of(k)),
            lambda k, value: across(value),
            lambda k, value: place_plane(k, value),
        ]
        values = [None] * plane_group
        for wave in range(plane_group + len(stages) - 1):
            for inner in range(plane_group):
                if 0 <= wave - inner < len(stages):
                    values[inner] = stages[wave - inner](spots[inner], values[inner])

    @pl.loop(0, lax.div(total + gather_size - 1, gather_size))
    def _(turn):
        tasks = [task(turn * gather_size + place) for place in range(gather_size)]
        blank = jnp.zeros((2 * window - 3 * stride, lanes), jnp.bfloat16)
        for place, (spot, _, _, j, rows, _) in enumerate(tasks):
            near = near_ref[spot]
            highs, lows = [], []
            for _, high, low in y_table(spot, 14, 32):
                highs.append(high)
                lows.append(low)
            columns = jnp.concatenate(
                [
                    jnp.concatenate([near, near[:stride], blank], axis=0),
                    jnp.concatenate([*highs, *lows, *highs, blank], axis=0),
                ],
                axis=1,
            )
            span = pl.ds(pl.multiple_of(j * 2 * window, lanes), 2 * window)
            block = stack_ref[:, rows, span].reshape(depth * window_rows, 2 * window)
            level_ref[place] = dot(block.astype(jnp.bfloat16), columns)
        for place, (spot, cell, chunk, _, _, base) in enumerate(tasks):
            lowest = prep_row(0, spot) - base
            values = kinds(1, spot)
            slopes = kinds(5, spot)
            modes = [pl.ds(spot * depth + k, 8, stride=0) for k in range(depth)]
            deep = [deep_ref[mode, :] for mode in modes]
            steep = [steep_ref[mode, :] for mode in modes]
            zero = jnp.zeros((8, lanes), jnp.float32)
            sums = [zero, zero, zero]
            for tile in range(steps_x):
                weight, slope = looked_up(row_index + float(tile * 8), lowest, [values, slopes])
                parts = [zero, zero, zero]
                for k in range(depth):
                    at = slice(k * window_rows + tile * 8, k * window_rows + tile * 8 + 8)
                    flat = level_ref[place, at, :lanes]
                    tilt = level_ref[place, at, lanes:]
                    parts = [
                        parts[0] + deep[k] * flat,
                        parts[1] + deep[k] * tilt,
                        parts[2] + steep[k] * flat,
                    ]
                sums = [
                    sums[0] + slope * parts[0],
                    sums[1] + weight * parts[1],
                    sums[2] + weight * parts[2],
                ]
            for axis in range(3):
                out_ref[cell, axis, pl.ds(chunk, 1), :] += jnp.sum(
                    sums[axis], axis=0, keepdims=True
                )


def finish_kernel(sizes, cells, pairs_ref, partial_ref, atoms_ref, rank_ref, column_ref, before_ref, short_ref, long_ref, land_ref, partner_ref, sum_ref, order_ref, force_ref, send_sem, recv_sem):
    count_x, count_y = sizes
    place_x, place_y = (lax.axis_index("gx"), lax.axis_index("gy"))
    me = place_x * count_y + place_y
    peers = peers_of(count_x, count_y)
    barrier = pltpu.get_barrier_semaphore()
    for peer_x, peer_y in peers:
        pl.semaphore_signal(
            barrier,
            inc=1,
            device_id={"gx": peer_x, "gy": peer_y},
            device_id_type=pl.DeviceIdType.MESH,
        )
    clusters = pairs_ref.shape[2]
    atom_total = atoms_ref.shape[2]
    size = atom_total // clusters
    place_partners(sizes, cells, pairs_ref, atoms_ref, partner_ref)
    pl.semaphore_wait(barrier, len(peers))
    copies = []
    for order, (peer_x, peer_y) in enumerate(peers):
        copy = pltpu.make_async_remote_copy(
            src_ref=partial_ref.at[peer_x * count_y + peer_y],
            dst_ref=land_ref.at[order],
            send_sem=send_sem.at[order],
            recv_sem=recv_sem.at[order],
            device_id={"gx": peer_x, "gy": peer_y},
            device_id_type=pl.DeviceIdType.MESH,
        )
        copy.start()
        copies.append(copy)
    pair_sums(clusters, size, 32, column_ref, partner_ref, before_ref, sum_ref)
    for axis in range(3):
        for c in range(clusters):
            span = slice(c * size, (c + 1) * size)
            summed = row_sums(sum_ref[axis, span, :])
            short_ref[axis, 0, :, span] = summed
    rank = rank_ref[...]

    @pl.loop(0, atom_total // size)
    def _(block):
        place = lax.broadcasted_iota(jnp.int32, (size, atom_total), 0) + block * size
        order_ref[pl.ds(pl.multiple_of(block * size, size), size), :] = jnp.where(
            place.astype(jnp.float32) == rank, 1.0, 0.0
        ).astype(jnp.bfloat16)

    force_ref[...] = jnp.zeros_like(force_ref)
    for copy in copies:
        copy.wait()
    total = partial_ref[me]
    for order in range(len(peers)):
        total = total + land_ref[order]
    for part in range(3):
        piece = total.astype(jnp.bfloat16).astype(jnp.float32)
        total = total - piece
        for axis in range(3):
            for tile in range(atom_total // lanes):
                span = slice(tile * lanes, (tile + 1) * lanes)
                row = 4 * part + axis
                force_ref[row : row + 1, span] = piece[axis, tile : tile + 1, :]
    placed = dot(force_ref[...].astype(jnp.bfloat16), order_ref[...])
    placed = (placed[0:4] + placed[4:8]) + placed[8:12]
    for axis in range(3):
        long_ref[axis, 0, :, :] = placed[axis : axis + 1, :]


def finished(pair_lists, partial, raw, rank, columns, before, count_x, count_y, cells_x, cells_y):
    devices, _, atom_total = raw.shape
    clusters, listed = pair_lists.shape[2:]
    size = atom_total // clusters
    vmem = pl.BlockSpec(memory_space=pltpu.VMEM)
    flags = pltpu.SemaphoreType.DMA((devices - 1,))
    return pl.pallas_call(
        functools.partial(finish_kernel, (count_x, count_y), (cells_x, cells_y)),
        in_specs=[pl.BlockSpec(memory_space=pltpu.SMEM)] + [vmem] * 5,
        out_specs=[vmem, vmem],
        out_shape=[jax.ShapeDtypeStruct((3, 1, 1, atom_total), jnp.float32)] * 2,
        scratch_shapes=[
            pltpu.VMEM((devices - 1, *partial.shape[1:]), jnp.float32),
            pltpu.VMEM((clusters, 4, 8, (listed - 1) * size), jnp.float32),
            pltpu.VMEM((3, atom_total, lanes), jnp.float32),
            pltpu.VMEM((atom_total, atom_total), jnp.bfloat16),
            pltpu.VMEM((16, atom_total), jnp.float32),
            flags,
            flags,
        ],
        compiler_params=pltpu.CompilerParams(
            collective_id=1, has_side_effects=True, vmem_limit_bytes=16 << 20
        ),
        name="finish",
    )(
        pltpu.with_memory_space_constraint(pair_lists, pltpu.HBM),
        partial,
        raw,
        rank,
        columns,
        before,
    )


def green_table(period):
    index = np.arange(period)
    signed = np.where(index <= period // 2, index, index - period) / (period * spacing)
    modulus = ((2.0 + np.cos(index * (2.0 * np.pi / period))) / 3.0) ** 2
    square = signed * signed
    return np.stack([square, np.exp(-((np.pi / ewald_split) ** 2) * square) / modulus]).astype(
        np.float32
    )


def green_factors(index, period):
    signed = jnp.where(index <= period // 2, index, index - period).astype(jnp.float32) / (
        period * spacing
    )
    modulus = ((2.0 + jnp.cos(index.astype(jnp.float32) * (2.0 * jnp.pi / period))) / 3.0) ** 2
    square = signed * signed
    return jnp.stack([square, jnp.exp(-((jnp.pi / ewald_split) ** 2) * square) / modulus])


def one_cluster(own_rows, partner):
    offsets = (own_rows[:3, :, None] - partner[:3, None, :]) * spacing
    dist_square = jnp.sum(offsets * offsets, axis=0)
    soft_square = dist_square + soft_core
    soft_dist = jnp.sqrt(soft_square)
    scaled = ewald_split * soft_dist
    strength = (
        jax.scipy.special.erfc(scaled) / soft_dist
        + ewald_split * root_factor * jnp.exp(-scaled * scaled)
    ) / soft_square
    cutoff_taper = jnp.where(
        dist_square < cutoff * cutoff, (1.0 - dist_square / (cutoff * cutoff)) ** 2, 0.0
    )
    weight = partner[3][None, :] * strength * cutoff_taper
    return own_rows[3] * jnp.sum(weight[None] * offsets, axis=2)


def far_by_planes(bounds, atoms, count_x, count_y, cells_x, cells_y):
    devices = count_x * count_y
    depth = GRID_Z // devices
    tiles = atoms.shape[2]
    pad_y = round_up(cells_y + 3, 8)
    stride = round_up(pad_y, 16)
    window = 2 * cells_y
    turn_x = halves(jnp.asarray(hartley(GRID_X)))
    turn_y = halves(jnp.asarray(hartley(GRID_Y)))
    volume = GRID_X * GRID_Y * GRID_Z * spacing**3
    column = jnp.asarray(green_table(GRID_X).T)
    row = jnp.asarray(green_table(GRID_Y))
    every_k = np.arange(GRID_Z)
    taps = np.outer(every_k, np.arange(4)) * (2.0 * np.pi / GRID_Z)
    square, scale = green_table(GRID_Z)
    table = np.concatenate(
        [
            every_k[:, None],
            np.cos(taps) + np.sin(taps),
            np.cos(taps) - np.sin(taps),
            square[:, None],
            scale[:, None] / (np.pi * volume),
        ],
        axis=1,
    ).astype(np.float32)
    vmem = pl.BlockSpec(memory_space=pltpu.VMEM)
    rows = GRID_X + window_rows
    batch = depth * window_rows
    angle = every_k * (2.0 * np.pi / GRID_Z)
    circle = np.repeat(np.stack([np.cos(angle), np.sin(angle)]), 8, axis=0).astype(np.float32)
    constants = (*turn_x, *turn_y, column, row, jnp.asarray(circle), jnp.asarray(table))
    fixed = pl.BlockSpec(memory_space=pltpu.HBM)
    return pl.pallas_call(
        functools.partial(mesh_kernel, (count_x, count_y), (cells_x, cells_y), pad_y),
        in_specs=[pl.BlockSpec(memory_space=pltpu.SMEM)] + [vmem] + [fixed] * fixed_arrays,
        out_specs=vmem,
        out_shape=jax.ShapeDtypeStruct((devices, 3, tiles, lanes), jnp.float32),
        scratch_shapes=[
            pltpu.VMEM((2, depth, rows, GRID_Y), jnp.float32),
            pltpu.VMEM((depth, rows, 4 * GRID_Y), jnp.float32),
            pltpu.VMEM((36 * devices * tiles, lanes), jnp.float32),
            pltpu.VMEM((devices * tiles * depth, lanes), jnp.float32),
            pltpu.VMEM((devices * tiles * depth, lanes), jnp.float32),
            pltpu.VMEM((devices * tiles, 2 * stride, lanes), jnp.bfloat16),
            pltpu.VMEM((group_size, 2 * window, 2 * lanes), jnp.bfloat16),
            pltpu.VMEM((group_size, batch, 2 * lanes), jnp.bfloat16),
            pltpu.VMEM((gather_size, batch, 2 * lanes), jnp.float32),
            pltpu.VMEM((GRID_X, GRID_Y), jnp.float32),
            pltpu.VMEM((GRID_X, GRID_Y), jnp.float32),
            pltpu.SMEM((4 * devices * tiles,), jnp.int32),
            *[pltpu.VMEM(value.shape, value.dtype) for value in constants],
            pltpu.SemaphoreType.DMA((fixed_arrays,)),
        ],
        compiler_params=pltpu.CompilerParams(vmem_limit_bytes=36 << 20),
        name="mesh",
    )(
        bounds, atoms, *[pltpu.with_memory_space_constraint(value, pltpu.HBM) for value in constants]
    )


def convolved_by_lines(charge_mesh, count_x, count_y):
    turn_x = jnp.asarray(hartley(GRID_X))
    turn_y = jnp.asarray(hartley(GRID_Y))
    product = functools.partial(
        jnp.einsum, precision=lax.Precision.HIGHEST, preferred_element_type=jnp.float32
    )
    exchange = functools.partial(lax.all_to_all, tiled=True)
    lines = exchange(charge_mesh, "gx", split_axis=2, concat_axis=0)
    lines = product("xyk,xu->uyk", lines, turn_x)
    lines = exchange(lines, "gy", split_axis=0, concat_axis=1)
    lines = product("uyk,yv->uvk", lines, turn_y)
    wide, _, depth = lines.shape
    start_x = lax.axis_index("gy") * wide
    start_z = lax.axis_index("gx") * depth
    volume = GRID_X * GRID_Y * GRID_Z * spacing**3
    fx = green_factors(start_x + jnp.arange(wide, dtype=jnp.int32), GRID_X)
    fy = green_factors(jnp.arange(GRID_Y, dtype=jnp.int32), GRID_Y)
    fz = green_factors(start_z + jnp.arange(depth, dtype=jnp.int32), GRID_Z)
    square = fx[0][:, None, None] + fy[0][:, None] + fz[0]
    scale = fx[1][:, None, None] * fy[1][:, None] * fz[1] / (math.pi * volume)
    lines = lines * jnp.where(square > 0.0, scale / jnp.where(square > 0.0, square, 1.0), 0.0)
    lines = product("uvk,vy->uyk", lines, turn_y)
    lines = exchange(lines, "gy", split_axis=1, concat_axis=0)
    lines = product("uyk,ux->xyk", lines, turn_x)
    return exchange(lines, "gx", split_axis=0, concat_axis=2)


def far_by_lines(atoms, base, count_x, count_y, cells_x, cells_y, cells_z):
    atom_total = atoms.shape[1]
    cells = (cells_x, cells_y, cells_z)
    pad = (round_up(cells_x + 3, rows_group), round_up(cells_y + 3, 8))
    pad_x, pad_y = pad
    turn_z = jnp.asarray(hartley(GRID_Z))
    spread = pl.pallas_call(
        functools.partial(spread_kernel, cells, pad),
        out_shape=jax.ShapeDtypeStruct((pad_x, pad_y, GRID_Z), jnp.float32),
        scratch_shapes=[
            pltpu.VMEM((pad_x, atom_total), jnp.float32),
            pltpu.VMEM((pad_y, atom_total), jnp.float32),
            pltpu.VMEM((atom_total, 2 * GRID_Z), jnp.bfloat16),
            pltpu.VMEM((rows_group * pad_y, atom_total), jnp.bfloat16),
            pltpu.VMEM((rows_group * pad_y, atom_total), jnp.bfloat16),
        ],
        name="spread",
    )(atoms, base, turn_z)

    from_x = moved(spread[cells_x : cells_x + 3, :cells_y], 1, 0)
    from_y = moved(spread[:cells_x, cells_y : cells_y + 3], 0, 1)
    from_both = moved(spread[cells_x : cells_x + 3, cells_y : cells_y + 3], 1, 1)
    charge_mesh = (
        spread[:cells_x, :cells_y]
        .at[:3]
        .add(from_x)
        .at[:, :3]
        .add(from_y)
        .at[:3, :3]
        .add(from_both)
    )
    potential = convolved_by_lines(charge_mesh, count_x, count_y)
    upper_x = moved(potential[:3], -1, 0)
    upper_y = moved(potential[:, :3], 0, -1)
    upper_both = moved(potential[:3, :3], -1, -1)
    wider = jnp.concatenate(
        [
            jnp.concatenate([potential, upper_x], axis=0),
            jnp.concatenate([upper_y, upper_both], axis=0),
        ],
        axis=1,
    )
    wider = jnp.pad(wider, ((0, pad_x - cells_x - 3), (0, pad_y - cells_y - 3), (0, 0)))
    return pl.pallas_call(
        functools.partial(gather_kernel, cells, pad),
        out_shape=jax.ShapeDtypeStruct((3, atom_total), jnp.float32),
        scratch_shapes=[
            pltpu.VMEM((pad_x, atom_total), jnp.float32),
            pltpu.VMEM((pad_x, atom_total), jnp.float32),
            pltpu.VMEM((pad_y, atom_total), jnp.float32),
            pltpu.VMEM((pad_y, atom_total), jnp.float32),
            pltpu.VMEM((2 * GRID_Z, 2 * atom_total), jnp.bfloat16),
            pltpu.VMEM((rows_group * pad_y, 2 * atom_total), jnp.float32),
        ],
        name="gather",
    )(atoms, base, turn_z, wider)


def local(positions, charges, pair_lists, slab_dest, atom_counts):
    count_x = lax.axis_size("gx")
    count_y = lax.axis_size("gy")
    devices = count_x * count_y
    atom_total = positions.shape[3]
    clusters = pair_lists.shape[2]
    cluster_size = atom_total // clusters
    blocks = slab_dest.shape[2]
    block_size = atom_total // blocks
    cells_x = GRID_X // count_x
    cells_y = GRID_Y // count_y
    cells_z = GRID_Z // count_y
    by_planes = (
        GRID_Z == 8 * devices
        and GRID_Z == lanes
        and cells_y == 64
        and cells_x % 8 == 0
        and cells_x <= 64
        and count_y % 2 == 0
        and atom_total == 8 * lanes
        and cluster_size % lanes == 0
    )
    if by_planes:
        sizes = (count_x, count_y, cells_x, cells_y)
        raw, atoms, bounds, rank, columns, before = shared(
            positions, charges, atom_counts, clusters, *sizes
        )
        partial = far_by_planes(bounds, atoms, *sizes)
        short_sums, long_sums = finished(
            pair_lists, partial, raw, rank, columns, before, *sizes
        )
        living = jnp.arange(atom_total, dtype=jnp.int32) < atom_counts[0, 0]
        charge = jnp.where(living, charges[0, 0], 0.0)
        return (short_sums * (charge * spacing), long_sums * (charge * (-1.0 / spacing)))
    living = jnp.arange(atom_total, dtype=jnp.int32) < atom_counts[0, 0]
    charge = jnp.where(living, charges[0, 0], 0.0)
    packed = jnp.concatenate([positions, charge[None, None, None, :]], axis=0)
    atoms = packed.reshape(4, atom_total)
    base = jnp.broadcast_to(
        (slab_dest[0, 0] * cells_z)[:, None], (blocks, block_size)
    ).reshape(1, atom_total)
    gathered = lax.all_gather(atoms, ("gx", "gy"), axis=0, tiled=False)
    far_part = far_by_lines(atoms, base, count_x, count_y, cells_x, cells_y, cells_z)

    chosen = pair_lists[0, 0]
    beside = chosen // clusters
    step_x, step_y = (beside // 3 - 1, beside % 3 - 1)
    at_x = (lax.axis_index("gx") + step_x + count_x) % count_x
    at_y = (lax.axis_index("gy") + step_y + count_y) % count_y
    number = (at_x * count_y + at_y) * clusters + chosen % clusters
    pick = (number[:, :, None] == jnp.arange(devices * clusters, dtype=jnp.int32)).astype(
        jnp.float32
    )
    pool = gathered[:, :4].reshape(devices, 4, clusters, cluster_size)
    pool = jnp.transpose(pool, (1, 0, 2, 3)).reshape(4, devices * clusters, cluster_size)
    partners = jnp.einsum(
        "cln,fnk->cflk",
        pick,
        pool,
        precision=lax.Precision.HIGHEST,
        preferred_element_type=jnp.float32,
    )
    shift_x = (step_x * cells_x).astype(jnp.float32)
    shift_y = (step_y * cells_y).astype(jnp.float32)
    flat = jnp.zeros_like(shift_x)
    shift = jnp.stack([shift_x, shift_y, flat, flat], axis=1)
    partners = (partners + shift[:, :, :, None]).reshape(clusters, 4, -1)
    own = packed.reshape(4, clusters, cluster_size)
    pair_part = jnp.stack(
        [one_cluster(own[:, c], partners[c]) for c in range(clusters)], axis=1
    )
    short_forces = pair_part.reshape(3, 1, 1, atom_total)
    return (short_forces, far_part.reshape(3, 1, 1, atom_total))


def solution(mesh):
    return jax.shard_map(
        local,
        mesh=mesh,
        in_specs=(
            P(None, ("rep", "gx"), "gy", None),
            P(("rep", "gx"), "gy", None),
            P(("rep", "gx"), "gy", None, None),
            P(("rep", "gx"), "gy", None),
            P(("rep", "gx"), "gy"),
        ),
        out_specs=(P(None, ("rep", "gx"), "gy", None), P(None, ("rep", "gx"), "gy", None)),
        check_vma=False,
    )
```

```python
import functools
import math

import jax
import jax.numpy as jnp
import numpy as np
from jax import lax
from jax.experimental import pallas as pl
from jax.experimental.pallas import tpu as pltpu
from jax.sharding import PartitionSpec as P

GRID_X = 256
GRID_Y = 256
GRID_Z = 128


spacing = 0.16
ewald_split = 3.47
cutoff = 0.9
soft_core = 0.09
root_factor = 1.1283791670955126
rows_group = 8
lanes = 128
window_rows = 24
group_size = 16
gather_size = 8
cell_group = 4
plane_group = 8
fixed_arrays = 8


def moved(value, step_x, step_y):
    count_x = lax.axis_size("gx")
    count_y = lax.axis_size("gy")
    pairs = [
        (i * count_y + j, (i + step_x) % count_x * count_y + (j + step_y) % count_y)
        for i in range(count_x)
        for j in range(count_y)
    ]
    return lax.ppermute(value, ("gx", "gy"), pairs)


def round_up(value, multiple):
    return -(-value // multiple) * multiple


def hartley(period):
    turns = np.outer(np.arange(period), np.arange(period)) % period
    phases = turns * (2.0 * np.pi / period)
    return (np.cos(phases) + np.sin(phases)).astype(np.float32)


def halves(value):
    high = value.astype(jnp.bfloat16)
    low = (value - high.astype(jnp.float32)).astype(jnp.bfloat16)
    return (high, low)


def dot(left_side, right_side):
    return jnp.dot(left_side, right_side, preferred_element_type=jnp.float32)


def spline_weights(fraction):
    remain = 1.0 - fraction
    square = fraction * fraction
    cube_part = square * fraction
    values = [
        remain * remain * remain / 6.0,
        (3.0 * cube_part - 6.0 * square + 4.0) / 6.0,
        (-3.0 * cube_part + 3.0 * square + 3.0 * fraction + 1.0) / 6.0,
        cube_part / 6.0,
    ]
    slopes = [
        -0.5 * remain * remain,
        0.5 * (3.0 * square - 4.0 * fraction),
        0.5 * (-3.0 * square + 2.0 * fraction + 1.0),
        0.5 * square,
    ]
    return (values, slopes)


def split_cells(coordinate, offset, cell_count):
    inside = coordinate - offset
    lowest = jnp.clip(jnp.floor(inside).astype(jnp.int32), 0, cell_count - 1)
    return (lowest, inside - lowest.astype(inside.dtype))


def spline_table(lowest, values, table_size, period=None):
    points = lax.broadcasted_iota(jnp.int32, (table_size, lowest.shape[1]), 0)
    lookup = jnp.zeros(points.shape, jnp.float32)
    for spline_term in range(4):
        at = lowest + spline_term
        if period is not None:
            at = jnp.where(at >= period, at - period, at)
        lookup = jnp.where(points == at, values[spline_term], lookup)
    return lookup


def spread_kernel(cells, pad, atoms_ref, base_ref, turn_ref, out_ref, wx_ref, wy_ref, wz_ref, hi_ref, lo_ref):
    cells_x, cells_y, cells_z = cells
    pad_x, pad_y = pad
    atom_total = atoms_ref.shape[1]
    low_x, frac_x = split_cells(atoms_ref[0:1, :], 0.0, cells_x)
    low_y, frac_y = split_cells(atoms_ref[1:2, :], 0.0, cells_y)
    base = base_ref[...]
    low_z, frac_z = split_cells(atoms_ref[2:3, :], base.astype(jnp.float32), cells_z)
    wx_ref[...] = spline_table(low_x, spline_weights(frac_x)[0], pad_x) * atoms_ref[3:4, :]
    wy_ref[...] = spline_table(low_y, spline_weights(frac_y)[0], pad_y)
    turn = turn_ref[...]
    size_z = turn.shape[0]
    table_z = spline_table(base + low_z, spline_weights(frac_z)[0], size_z, size_z)
    waves = jnp.dot(
        turn, table_z, precision=lax.Precision.HIGHEST, preferred_element_type=jnp.float32
    ).T
    high, low = halves(waves)
    wz_ref[:, :size_z] = high
    wz_ref[:, size_z:] = low

    @pl.loop(0, pad_x // rows_group)
    def _(chunk):
        for inner in range(rows_group):
            row = wx_ref[pl.ds(chunk * rows_group + inner, 1), :]
            high, low = halves(row * wy_ref[...])
            hi_ref[pl.ds(inner * pad_y, pad_y), :] = high
            lo_ref[pl.ds(inner * pad_y, pad_y), :] = low
        both = dot(hi_ref[...], wz_ref[...])
        rest = dot(lo_ref[...], wz_ref[:, :size_z])
        total = both[:, :size_z] + both[:, size_z:] + rest
        out_ref[pl.ds(chunk * rows_group, rows_group)] = total.reshape(rows_group, pad_y, size_z)


def gather_kernel(cells, pad, atoms_ref, base_ref, turn_ref, mesh_ref, out_ref, wx_ref, vx_ref, wy_ref, vy_ref, wz_ref, level_ref):
    cells_x, cells_y, cells_z = cells
    pad_x, pad_y = pad
    atom_total = atoms_ref.shape[1]
    low_x, frac_x = split_cells(atoms_ref[0:1, :], 0.0, cells_x)
    low_y, frac_y = split_cells(atoms_ref[1:2, :], 0.0, cells_y)
    base = base_ref[...]
    low_z, frac_z = split_cells(atoms_ref[2:3, :], base.astype(jnp.float32), cells_z)
    values, slopes = spline_weights(frac_x)
    wx_ref[...] = spline_table(low_x, values, pad_x)
    vx_ref[...] = spline_table(low_x, slopes, pad_x)
    values, slopes = spline_weights(frac_y)
    wy_ref[...] = spline_table(low_y, values, pad_y)
    vy_ref[...] = spline_table(low_y, slopes, pad_y)
    values, slopes = spline_weights(frac_z)
    turn = turn_ref[...]
    size_z = turn.shape[0]
    for place, terms in enumerate((values, slopes)):
        table_z = spline_table(base + low_z, terms, size_z, size_z)
        waves = jnp.dot(
            turn, table_z, precision=lax.Precision.HIGHEST, preferred_element_type=jnp.float32
        )
        high, low = halves(waves)
        wz_ref[:size_z, pl.ds(place * atom_total, atom_total)] = high
        wz_ref[size_z:, pl.ds(place * atom_total, atom_total)] = low
    groups = pad_y // 8

    def one_chunk(chunk, sums):
        rows = mesh_ref[pl.ds(chunk * rows_group, rows_group)].reshape(rows_group * pad_y, size_z)
        high, low = halves(rows)
        level_ref[...] = dot(jnp.concatenate([high, high], axis=1), wz_ref[...]) + dot(
            low, wz_ref[:size_z, :]
        )
        first, second, third = sums
        for inner in range(rows_group):
            flat = level_ref[pl.ds(inner * pad_y, pad_y), :atom_total]
            tilt = level_ref[pl.ds(inner * pad_y, pad_y), atom_total:]
            across = wy_ref[...]
            part_x = jnp.sum((across * flat).reshape(groups, 8, atom_total), axis=0)
            part_y = jnp.sum((vy_ref[...] * flat).reshape(groups, 8, atom_total), axis=0)
            part_z = jnp.sum((across * tilt).reshape(groups, 8, atom_total), axis=0)
            weight = wx_ref[pl.ds(chunk * rows_group + inner, 1), :]
            slope = vx_ref[pl.ds(chunk * rows_group + inner, 1), :]
            first = first + slope * part_x
            second = second + weight * part_y
            third = third + weight * part_z
        return (first, second, third)

    zero = jnp.zeros((8, atom_total), jnp.float32)
    sums = lax.fori_loop(0, pad_x // rows_group, one_chunk, (zero, zero, zero))
    factor = -atoms_ref[3:4, :] / spacing
    for place in range(3):
        out_ref[pl.ds(place, 1), :] = factor * jnp.sum(sums[place], axis=0, keepdims=True)


def peers_of(count_x, count_y):
    place_x, place_y = (lax.axis_index("gx"), lax.axis_index("gy"))
    peers = []
    for order in range(1, count_x * count_y):
        peer_x = lax.rem(place_x + order // count_y, count_x)
        peer_y = lax.rem(place_y + order % count_y, count_y)
        peers.append((peer_x, peer_y))
    return peers


root_terms = (
    3.9164407301418542,
    -0.0037127819564810594,
    0.16802528315459195,
    -0.003061234121505335,
    -0.0076524954798020545,
    0.002268454833542123,
    -0.0003056487922112269,
    1.686888935413571e-05,
)


def pair_weight(square):
    soft_square = square * (spacing * spacing) + soft_core
    inverse = lax.rsqrt(soft_square)
    series = jnp.full_like(inverse, root_terms[-1])
    for term in root_terms[-2::-1]:
        series = series * inverse + term
    decay = jnp.exp(soft_square * (-ewald_split * ewald_split))
    taper = jnp.maximum(1.0 - square * (spacing * spacing / (cutoff * cutoff)), 0.0)
    return (decay * series) * (inverse * taper) ** 2


def row_sums(values):
    total = None
    ones = jnp.ones((16, values.shape[1]), jnp.bfloat16)
    for _ in range(3):
        part = values.astype(jnp.bfloat16)
        values = values - part.astype(jnp.float32)
        summed = lax.dot_general(
            ones, part, (((1,), (1,)), ((), ())), preferred_element_type=jnp.float32
        )
        total = summed if total is None else total + summed
    return total[0:1, :]


def place_partners(sizes, cells, pairs_ref, atoms_ref, partner_ref):
    count_x, count_y = sizes
    cells_x, cells_y = cells
    place_x, place_y = (lax.axis_index("gx"), lax.axis_index("gy"))
    clusters, listed = pairs_ref.shape[2:]
    size = atoms_ref.shape[2] // clusters
    for c in range(clusters):
        for n in range(1, listed):
            chosen = pairs_ref[0, 0, c, n]
            beside = lax.div(chosen, clusters)
            which = chosen - beside * clusters
            row_x = lax.div(beside, 3)
            step_x = row_x - 1
            step_y = beside - row_x * 3 - 1
            from_x = lax.rem(place_x + step_x + count_x, count_x)
            from_y = lax.rem(place_y + step_y + count_y, count_y)
            block = atoms_ref[from_x * count_y + from_y]
            part = block[:, :size]
            for k in range(1, clusters):
                part = jnp.where(which == k, block[:, k * size : (k + 1) * size], part)
            shifts = (
                (step_x * cells_x).astype(jnp.float32),
                (step_y * cells_y).astype(jnp.float32),
            )
            for axis in range(4):
                row = part[axis : axis + 1, :]
                if axis < 2:
                    row = row + shifts[axis]
                partner_ref[c, axis, :, (n - 1) * size : n * size] = jnp.broadcast_to(
                    row, (8, size)
                )


def pair_sums(clusters, size, height, column_ref, partner_ref, before_ref, sum_ref):
    @pl.loop(0, clusters)
    def _(c):
        @pl.loop(0, size // height)
        def _(step):
            for part in range(height // 8):
                start = c * size + step * height + part * 8
                rows = pl.ds(pl.multiple_of(start, 8), 8)
                own = [column_ref[axis, rows, :] for axis in range(3)]
                sums = [
                    jnp.zeros((8, lanes), jnp.float32)
                    if before_ref is None
                    else before_ref[axis, rows, :]
                    for axis in range(3)
                ]
                for tile in range(partner_ref.shape[3] // lanes):
                    span = slice(tile * lanes, (tile + 1) * lanes)
                    offsets = [own[axis] - partner_ref[c, axis, :, span] for axis in range(3)]
                    square = sum(offset * offset for offset in offsets)
                    weight = pair_weight(square) * partner_ref[c, 3, :, span]
                    sums = [total + weight * offset for total, offset in zip(sums, offsets)]
                for axis in range(3):
                    sum_ref[axis, rows, :] = sums[axis]


def share_kernel(sizes, cells, clusters, count_ref, position_ref, charge_ref, raw_ref, sorted_ref, bounds_ref, rank_ref, column_ref, sum_ref, key_ref, split_ref, partner_ref, raw_send, raw_recv, sort_send, sort_recv, mark_send, mark_recv):
    count_x, count_y = sizes
    cells_x, _ = cells
    place_x, place_y = (lax.axis_index("gx"), lax.axis_index("gy"))
    me = place_x * count_y + place_y
    place_chip, place_core = (place_y // 2, lax.rem(place_y, 2))
    chips = count_y // 2

    def at(step_x, step_chip, flip):
        peer_x = lax.rem(place_x + step_x, count_x)
        peer_chip = lax.rem(place_chip + step_chip, chips)
        peer_core = 1 - place_core if flip else place_core
        return (peer_x, peer_chip * 2 + peer_core)

    peers = peers_of(count_x, count_y)
    barrier = pltpu.get_barrier_semaphore()
    for peer_x, peer_y in peers:
        pl.semaphore_signal(
            barrier,
            inc=1,
            device_id={"gx": peer_x, "gy": peer_y},
            device_id_type=pl.DeviceIdType.MESH,
        )

    def sent(ref, owner, peer, send_sem, recv_sem, order, slot):
        return pltpu.make_async_remote_copy(
            src_ref=ref.at[owner],
            dst_ref=ref.at[owner],
            send_sem=send_sem.at[order],
            recv_sem=recv_sem.at[slot],
            device_id={"gx": peer[0], "gy": peer[1]},
            device_id_type=pl.DeviceIdType.MESH,
        )

    passed = []

    def passes(owner, peer):
        order = len(passed)
        copies = [
            sent(sorted_ref, owner, peer, sort_send, sort_recv, order, owner),
            sent(bounds_ref, owner, peer, mark_send, mark_recv, order, owner),
        ]
        for copy in copies:
            copy.start()
        passed.append(copies)

    def arrives(owner, peer):
        sent(sorted_ref, owner, peer, sort_send, sort_recv, 0, owner).wait_recv()
        sent(bounds_ref, owner, peer, mark_send, mark_recv, 0, owner).wait_recv()

    atom_total = charge_ref.shape[2]
    tiles = atom_total // lanes
    slot = lax.broadcasted_iota(jnp.int32, (1, atom_total), 1)
    living = slot < count_ref[0, 0]
    charge = jnp.where(living, charge_ref[0], 0.0)
    rows = [position_ref[axis, 0] for axis in range(3)] + [charge]
    for axis in range(4):
        raw_ref[me, pl.ds(axis, 1), :] = rows[axis]
    column = jnp.clip(jnp.floor(rows[0]), 0.0, cells_x - 1.0)
    key = jnp.where(living, column, float(cells_x)) * float(atom_total) + slot.astype(jnp.float32)
    for tile in range(tiles):
        span = slice(tile * lanes, (tile + 1) * lanes)
        key_ref[span, :] = jnp.broadcast_to(key[:, span], (lanes, lanes)).T
    wide = [
        jnp.broadcast_to(key[:, tile * lanes : (tile + 1) * lanes], (8, lanes))
        for tile in range(tiles)
    ]

    def count_group(group, totals):
        for inner in range(8):
            others = key_ref[pl.ds(pl.multiple_of(group * 64 + inner * 8, 8), 8), :]
            totals = tuple(
                total + jnp.where(others < own, 1.0, 0.0) for total, own in zip(totals, wide)
            )
        return totals

    zero = jnp.zeros((8, lanes), jnp.float32)
    totals = lax.fori_loop(0, atom_total // 64, count_group, (zero,) * tiles)
    for tile, total in enumerate(totals):
        rank_ref[:, tile * lanes : (tile + 1) * lanes] = jnp.sum(total, axis=0, keepdims=True)

    split_ref[...] = jnp.zeros_like(split_ref)
    rest = raw_ref[me]
    for part in range(3):
        piece = rest.astype(jnp.bfloat16).astype(jnp.float32)
        split_ref[4 * part : 4 * part + 4, :] = piece
        rest = rest - piece
    split = split_ref[...].astype(jnp.bfloat16)
    rank = rank_ref[...]
    block = 2 * lanes
    for part in range(atom_total // block):
        place = lax.broadcasted_iota(jnp.int32, (block, atom_total), 0) + part * block
        chosen = jnp.where(place.astype(jnp.float32) == rank, 1.0, 0.0).astype(jnp.bfloat16)
        found = lax.dot_general(
            split, chosen, (((1,), (1,)), ((), ())), preferred_element_type=jnp.float32
        )
        found = (found[0:4] + found[4:8]) + found[8:12]
        for tile in range(block // lanes):
            row = part * (block // lanes) + tile
            for axis in range(4):
                sorted_ref[me, axis, row : row + 1, :] = found[
                    axis : axis + 1, tile * lanes : (tile + 1) * lanes
                ]
    spot = lax.broadcasted_iota(jnp.int32, (tiles, lanes), 0) * lanes
    spot = spot + lax.broadcasted_iota(jnp.int32, (tiles, lanes), 1)
    inside = spot < count_ref[0, 0]
    column = jnp.clip(jnp.floor(sorted_ref[me, 0]), 0.0, cells_x - 1.0)
    lowest = jnp.min(jnp.where(inside, column, float(cells_x)), axis=1, keepdims=True)
    highest = jnp.max(jnp.where(inside, column, -1.0), axis=1, keepdims=True)
    first = jnp.floor(lowest * 0.125)
    last = jnp.floor((highest + 3.0) * 0.125)
    windows = jnp.where(
        highest >= 0.0, jnp.floor((last - first) * (8.0 / window_rows) + 0.01) + 1.0, 0.0
    )
    lane = lax.broadcasted_iota(jnp.int32, (tiles, lanes), 1)
    row = lax.broadcasted_iota(jnp.int32, (tiles, lanes), 0)
    marks = jnp.where(lane == row, first, jnp.where(lane == row + tiles, windows, 0.0))
    marks = jnp.sum(marks, axis=0, keepdims=True)
    bounds_ref[me] = marks.astype(jnp.int32)

    near = sorted(
        (min(step, count_x - step) + min(chip, chips - chip), step, chip)
        for step in range(count_x)
        for chip in range(chips)
    )[1:]
    mate = at(0, 0, True)
    pl.semaphore_wait(barrier, len(peers))
    for _, step, chip in reversed(near):
        passes(me, at(step, chip, False))
    passes(me, mate)
    beside = sorted(
        {
            step_x % count_x * count_y + step_y % count_y
            for step_x in (-1, 0, 1)
            for step_y in (-1, 0, 1)
        }
        - {0}
    )
    copies = [
        sent(raw_ref, me, peers[order - 1], raw_send, raw_recv, order - 1, order - 1)
        for order in beside
    ]
    for copy in copies:
        copy.start()

    for axis in range(3):
        for tile in range(tiles):
            span = slice(tile * lanes, (tile + 1) * lanes)
            column_ref[axis, span, :] = jnp.broadcast_to(rows[axis][:, span], (lanes, lanes)).T
    size = atom_total // clusters
    for c in range(clusters):
        for axis in range(4):
            row = rows[axis][:, c * size : (c + 1) * size]
            partner_ref[c, axis] = jnp.broadcast_to(row, (8, size))
    pair_sums(clusters, size, 64, column_ref, partner_ref, None, sum_ref)
    for _, step, chip in near:
        owner_x, owner_y = at(step, chip, False)
        arrives(owner_x * count_y + owner_y, (owner_x, owner_y))
        passes(owner_x * count_y + owner_y, mate)
    for _, step, chip in [(0, 0, 0), *near]:
        owner_x, owner_y = at(step, chip, True)
        arrives(owner_x * count_y + owner_y, mate)
    for copy in copies:
        copy.wait()
    for pair in passed:
        for copy in pair:
            copy.wait_send()


def shared(positions, charges, atom_counts, clusters, count_x, count_y, cells_x, cells_y):
    devices = count_x * count_y
    atom_total = charges.shape[2]
    vmem = pl.BlockSpec(memory_space=pltpu.VMEM)
    smem = pl.BlockSpec(memory_space=pltpu.SMEM)
    fewer = pltpu.SemaphoreType.DMA((devices - 1,))
    flags = pltpu.SemaphoreType.DMA((devices,))
    return pl.pallas_call(
        functools.partial(share_kernel, (count_x, count_y), (cells_x, cells_y), clusters),
        in_specs=[smem, vmem, vmem],
        out_specs=[vmem] * 6,
        out_shape=[
            jax.ShapeDtypeStruct((devices, 4, atom_total), jnp.float32),
            jax.ShapeDtypeStruct((devices, 4, atom_total // lanes, lanes), jnp.float32),
            jax.ShapeDtypeStruct((devices, 1, lanes), jnp.int32),
            jax.ShapeDtypeStruct((1, atom_total), jnp.float32),
            jax.ShapeDtypeStruct((3, atom_total, lanes), jnp.float32),
            jax.ShapeDtypeStruct((3, atom_total, lanes), jnp.float32),
        ],
        scratch_shapes=[
            pltpu.VMEM((atom_total, lanes), jnp.float32),
            pltpu.VMEM((16, atom_total), jnp.float32),
            pltpu.VMEM((clusters, 4, 8, atom_total // clusters), jnp.float32),
            fewer,
            fewer,
        ]
        + [flags] * 4,
        compiler_params=pltpu.CompilerParams(
            collective_id=0, has_side_effects=True, vmem_limit_bytes=12 << 20
        ),
        name="share",
    )(
        atom_counts,
        *[pltpu.with_memory_space_constraint(value, pltpu.HBM) for value in (positions, charges)],
    )


def depth_rows(table, circle, height, terms):
    turns = height * table[:, 0:1]
    turns = turns - GRID_Z * jnp.floor(turns * (1.0 / GRID_Z))
    index = turns.astype(jnp.int32)
    cosine, sine = [jnp.take_along_axis(part, index, axis=1) for part in circle]
    results = []
    for weights in terms:
        even = sum(table[:, 1 + t : 2 + t] * weights[t] for t in range(4))
        odd = sum(table[:, 5 + t : 6 + t] * weights[t] for t in range(4))
        results.append(cosine * even + sine * odd)
    return results


def mesh_kernel(sizes, cells, pad_y, bounds_ref, atoms_ref, *refs):
    constants, (out_ref, *scratch) = refs[:fixed_arrays], refs[fixed_arrays:]
    held, copy_sem = scratch[-fixed_arrays - 1 : -1], scratch[-1]
    copies = [
        pltpu.make_async_copy(source, target, copy_sem.at[place])
        for place, (source, target) in enumerate(zip(constants, held))
    ]
    for copy in copies:
        copy.start()
    xh_ref, xl_ref, yh_ref, yl_ref, column_ref, row_ref, circle_ref, table_ref = held
    mesh_ref, stack_ref, prep_ref, deep_ref, steep_ref, near_ref, wy_ref, side_ref, level_ref, square_ref, scale_ref, work_ref = scratch[: -fixed_arrays - 1]
    count_x, count_y = sizes
    cells_x, cells_y = cells
    devices = count_x * count_y
    place = lax.axis_index("gx") * count_y + lax.axis_index("gy")
    tiles = atoms_ref.shape[2]
    depth = stack_ref.shape[0]
    window = 2 * cells_y
    windows = GRID_Y // window
    extra = 8
    share = -(-group_size * cell_group // devices)
    stack_ref[:, GRID_X:, :] = jnp.zeros_like(stack_ref[:, GRID_X:, :])
    out_ref[...] = jnp.zeros_like(out_ref)

    steps_x = window_rows // 8
    most = (cells_x + 2) // 8 // steps_x + 1

    def prep_row(kind, spot):
        return prep_ref[pl.ds(kind * devices * tiles + spot, 8, stride=0), :]

    def listed_work(cell, total):
        for tile in range(tiles):
            for step in range(most):
                work_ref[total + step] = (cell * tiles + tile) * most + step
            total = total + bounds_ref[cell, 0, tiles + tile]

        return total

    def keep_splines(cell):
        def keep(kind, value):
            rows = pl.ds(pl.multiple_of((kind * devices + cell) * tiles, 8), tiles)
            prep_ref[rows, :] = value

        for axis, count in enumerate((cells_x, cells_y)):
            value = atoms_ref[cell, axis]
            lowest = jnp.clip(jnp.floor(value), 0.0, count - 1.0)
            values, slopes = spline_weights(value - lowest)
            keep(9 * axis, lowest)
            for term in range(4):
                keep(9 * axis + 1 + term, values[term])
                keep(9 * axis + 5 + term, slopes[term])
                if axis == 1:
                    for kind, whole in ((28, values[term]), (32, slopes[term])):
                        keep(kind + term, whole - whole.astype(jnp.bfloat16).astype(jnp.float32))
        value = atoms_ref[cell, 2]
        height = jnp.floor(value)
        values, slopes = spline_weights(value - height)
        keep(18, height)
        for term in range(4):
            keep(19 + term, values[term])
            keep(23 + term, slopes[term])
        keep(27, atoms_ref[cell, 3])

    def keep_modes(cell):
        for tile in range(tiles):
            spot = cell * tiles + tile
            height = prep_row(18, spot)
            terms = [[prep_row(19 + 4 * s + term, spot) for term in range(4)] for s in range(2)]
            deep, steep = depth_rows(table, circle, height, terms)
            rows = pl.ds(pl.multiple_of(spot * depth, 8), depth)
            deep_ref[rows, :] = deep
            steep_ref[rows, :] = steep

    def prepare_some(turn, total):
        for inner in range(cell_group):
            cell = turn * cell_group + inner
            mesh_ref[lax.div(cell, depth), lax.rem(cell, depth)] = jnp.zeros(
                mesh_ref.shape[2:], jnp.float32
            )
            total = listed_work(cell, total)
        for inner in range(cell_group):
            keep_splines(turn * cell_group + inner)
        for inner in range(share):
            place = jnp.minimum(turn * share + inner, group_size - 1)
            wy_ref[place] = jnp.zeros(wy_ref.shape[1:], wy_ref.dtype)
        return total

    total = lax.fori_loop(0, devices // cell_group, prepare_some, jnp.int32(0))
    copies[-2].wait()
    copies[-1].wait()
    circle = [circle_ref[:8, :], circle_ref[8:, :]]
    table = table_ref[pl.ds(pl.multiple_of(place * depth, 8), depth), :]

    @pl.loop(0, devices // cell_group)
    def _(turn):
        for inner in range(cell_group):
            keep_modes(turn * cell_group + inner)

    rounds = lax.div(total + group_size - 1, group_size)

    row_index = lax.broadcasted_iota(jnp.int32, (8, lanes), 0).astype(jnp.float32)

    def looked_up(points, lowest, term_lists):
        results = [jnp.zeros_like(points) for _ in term_lists]
        for term in range(4):
            hit = points == lowest + float(term)
            results = [
                jnp.where(hit, terms[term], result)
                for terms, result in zip(term_lists, results)
            ]
        return results

    def kinds(first, spot):
        return [prep_row(first + term, spot) for term in range(4)]

    stride = round_up(pad_y, 16)
    far_away = 1.0e6

    def task(index):
        entry = jnp.where(index < total, work_ref[index], 0)
        spot = lax.div(entry, most)
        cell = lax.div(spot, tiles)
        chunk = spot - cell * tiles
        begin = bounds_ref[cell, 0, chunk] * 8 + (entry - spot * most) * window_rows
        base = jnp.where(index < total, begin.astype(jnp.float32), far_away)
        i = lax.div(cell, count_y)
        rows = pl.ds(pl.multiple_of(i * cells_x + begin, 8), window_rows)
        return (spot, cell, chunk, cell - i * count_y, rows, base)

    packed_index = jnp.concatenate([row_index, row_index + 8.0], axis=0).astype(jnp.bfloat16)

    def packed_row(kind, spot):
        row = prep_row(kind, spot)
        return jnp.concatenate([row, row], axis=0).astype(jnp.bfloat16)

    def y_table(spot, kind, low_kind):
        lowest = packed_row(9, spot)
        highs = [packed_row(kind + term, spot) for term in range(4)]
        lows = [packed_row(low_kind + term, spot) for term in range(4)]
        starts = [lowest + jnp.bfloat16(term) for term in range(4)]
        for group in range(stride // 16):
            points = packed_index + jnp.bfloat16(group * 16)
            high = low = jnp.zeros_like(points)
            for term in range(4):
                hit = points == starts[term]
                high = jnp.where(hit, highs[term], high)
                low = jnp.where(hit, lows[term], low)
            yield (slice(group * 16, group * 16 + 16), high, low)

    @pl.loop(0, rounds)
    def _(turn):
        tasks = [task(turn * group_size + place) for place in range(group_size)]
        for place, (spot, _, _, _, _, base) in enumerate(tasks):
            for rows, high, low in y_table(spot, 10, 28):
                after = slice(window + rows.start, window + rows.stop)
                later = slice(stride + rows.start, stride + rows.stop)
                wy_ref[place, rows, :lanes] = high
                wy_ref[place, rows, lanes:] = high
                wy_ref[place, after, :lanes] = low
                near_ref[spot, rows, :] = high
                near_ref[spot, later, :] = low
            lowest = prep_row(0, spot) - base
            charge = prep_row(27, spot)
            terms = [term * charge for term in kinds(1, spot)]
            weights = [
                looked_up(row_index + float(tile * 8), lowest, [terms])[0]
                for tile in range(steps_x)
            ]
            modes = [
                deep_ref[pl.ds(spot * depth + k, 8, stride=0), :] for k in range(depth)
            ]
            blocks = [weight * mode for mode in modes for weight in weights]
            for pair in range(len(blocks) // 2):
                high, low = halves(jnp.concatenate(blocks[2 * pair : 2 * pair + 2], axis=0))
                rows = slice(pair * 16, pair * 16 + 16)
                side_ref[place, rows, :lanes] = high
                side_ref[place, rows, lanes:] = low
        for place, (_, _, _, j, rows, _) in enumerate(tasks):
            product = lax.dot_general(
                side_ref[place],
                wy_ref[place],
                (((1,), (1,)), ((), ())),
                preferred_element_type=jnp.float32,
            )
            product = product[:, :window] + product[:, window:]
            m = lax.div(j, 2)
            here = pl.ds(pl.multiple_of(m * window, lanes), window)
            mesh_ref[j - 2 * m, :, rows, here] += product.reshape(depth, window_rows, window)

    def across(value):
        high, low = halves(value)
        return dot(xh_ref[...], high) + dot(xl_ref[...], high) + dot(xh_ref[...], low)

    def along(value):
        high, low = halves(value)
        return dot(high, yh_ref[...]) + dot(high, yl_ref[...]) + dot(low, yh_ref[...])

    plane_lane = lax.broadcasted_iota(jnp.int32, (GRID_X, window), 1)
    for copy in copies[:-2]:
        copy.wait()
    shape = (GRID_X, GRID_Y)
    square_ref[...] = jnp.broadcast_to(column_ref[:, 0:1], shape) + row_ref[0:1, :]
    scale_ref[...] = jnp.broadcast_to(column_ref[:, 1:2], shape) * row_ref[1:2, :]

    def charge_of(k):
        charge = mesh_ref[0, k, :GRID_X, :] + pltpu.roll(mesh_ref[1, k, :GRID_X, :], cells_y, 1)
        over = slice(GRID_X, GRID_X + extra)
        beyond = mesh_ref[0, k, over, :] + pltpu.roll(mesh_ref[1, k, over, :], cells_y, 1)
        return jnp.concatenate([charge[:extra] + beyond, charge[extra:]], axis=0)

    def green_of(k):
        mode = pl.ds(place * depth + k, 1)
        square = square_ref[...] + table_ref[mode, 9:10]
        scale = scale_ref[...] * table_ref[mode, 10:11]
        return jnp.where(square > 0.0, scale / square, 0.0)

    def place_plane(k, plane):
        for odd in range(2):
            if odd:
                plane = pltpu.roll(plane, GRID_Y - cells_y, 1)
            for j_half in range(windows):
                j = 2 * j_half + odd
                block = plane[:, j_half * window : (j_half + 1) * window]
                high = block.astype(jnp.bfloat16).astype(jnp.float32)
                low = block - high
                shifted = pltpu.roll(high, stride, 1)
                left = jnp.where(plane_lane < stride, high, shifted)
                right = jnp.where(
                    plane_lane < 2 * stride - window,
                    shifted,
                    pltpu.roll(low, 2 * stride - window, 1),
                )
                for side, value in enumerate((left, right)):
                    span = slice((2 * j + side) * window, (2 * j + side + 1) * window)
                    stack_ref[k, :GRID_X, span] = value
                    stack_ref[k, GRID_X : GRID_X + extra, span] = value[:extra]

    @pl.loop(0, depth // plane_group)
    def _(pair):
        spots = [pair * plane_group + inner for inner in range(plane_group)]
        stages = [
            lambda k, _: across(charge_of(k)),
            lambda k, value: along(value),
            lambda k, value: along(value * green_of(k)),
            lambda k, value: across(value),
            lambda k, value: place_plane(k, value),
        ]
        values = [None] * plane_group
        for wave in range(plane_group + len(stages) - 1):
            for inner in range(plane_group):
                if 0 <= wave - inner < len(stages):
                    values[inner] = stages[wave - inner](spots[inner], values[inner])

    @pl.loop(0, lax.div(total + gather_size - 1, gather_size))
    def _(turn):
        tasks = [task(turn * gather_size + place) for place in range(gather_size)]
        blank = jnp.zeros((2 * window - 3 * stride, lanes), jnp.bfloat16)
        for place, (spot, _, _, j, rows, _) in enumerate(tasks):
            near = near_ref[spot]
            highs, lows = [], []
            for _, high, low in y_table(spot, 14, 32):
                highs.append(high)
                lows.append(low)
            columns = jnp.concatenate(
                [
                    jnp.concatenate([near, near[:stride], blank], axis=0),
                    jnp.concatenate([*highs, *lows, *highs, blank], axis=0),
                ],
                axis=1,
            )
            span = pl.ds(pl.multiple_of(j * 2 * window, lanes), 2 * window)
            block = stack_ref[:, rows, span].reshape(depth * window_rows, 2 * window)
            level_ref[place] = dot(block.astype(jnp.bfloat16), columns)
        for place, (spot, cell, chunk, _, _, base) in enumerate(tasks):
            lowest = prep_row(0, spot) - base
            values = kinds(1, spot)
            slopes = kinds(5, spot)
            modes = [pl.ds(spot * depth + k, 8, stride=0) for k in range(depth)]
            deep = [deep_ref[mode, :] for mode in modes]
            steep = [steep_ref[mode, :] for mode in modes]
            zero = jnp.zeros((8, lanes), jnp.float32)
            sums = [zero, zero, zero]
            for tile in range(steps_x):
                weight, slope = looked_up(row_index + float(tile * 8), lowest, [values, slopes])
                parts = [zero, zero, zero]
                for k in range(depth):
                    at = slice(k * window_rows + tile * 8, k * window_rows + tile * 8 + 8)
                    flat = level_ref[place, at, :lanes]
                    tilt = level_ref[place, at, lanes:]
                    parts = [
                        parts[0] + deep[k] * flat,
                        parts[1] + deep[k] * tilt,
                        parts[2] + steep[k] * flat,
                    ]
                sums = [
                    sums[0] + slope * parts[0],
                    sums[1] + weight * parts[1],
                    sums[2] + weight * parts[2],
                ]
            for axis in range(3):
                out_ref[cell, axis, pl.ds(chunk, 1), :] += jnp.sum(
                    sums[axis], axis=0, keepdims=True
                )


def finish_kernel(sizes, cells, pairs_ref, partial_ref, atoms_ref, rank_ref, column_ref, before_ref, short_ref, long_ref, land_ref, partner_ref, sum_ref, order_ref, force_ref, send_sem, recv_sem):
    count_x, count_y = sizes
    place_x, place_y = (lax.axis_index("gx"), lax.axis_index("gy"))
    me = place_x * count_y + place_y
    peers = peers_of(count_x, count_y)
    barrier = pltpu.get_barrier_semaphore()
    for peer_x, peer_y in peers:
        pl.semaphore_signal(
            barrier,
            inc=1,
            device_id={"gx": peer_x, "gy": peer_y},
            device_id_type=pl.DeviceIdType.MESH,
        )
    clusters = pairs_ref.shape[2]
    atom_total = atoms_ref.shape[2]
    size = atom_total // clusters
    place_partners(sizes, cells, pairs_ref, atoms_ref, partner_ref)
    pl.semaphore_wait(barrier, len(peers))
    copies = []
    for order, (peer_x, peer_y) in enumerate(peers):
        copy = pltpu.make_async_remote_copy(
            src_ref=partial_ref.at[peer_x * count_y + peer_y],
            dst_ref=land_ref.at[order],
            send_sem=send_sem.at[order],
            recv_sem=recv_sem.at[order],
            device_id={"gx": peer_x, "gy": peer_y},
            device_id_type=pl.DeviceIdType.MESH,
        )
        copy.start()
        copies.append(copy)
    pair_sums(clusters, size, 32, column_ref, partner_ref, before_ref, sum_ref)
    for axis in range(3):
        for c in range(clusters):
            span = slice(c * size, (c + 1) * size)
            summed = row_sums(sum_ref[axis, span, :])
            short_ref[axis, 0, :, span] = summed
    rank = rank_ref[...]

    @pl.loop(0, atom_total // size)
    def _(block):
        place = lax.broadcasted_iota(jnp.int32, (size, atom_total), 0) + block * size
        order_ref[pl.ds(pl.multiple_of(block * size, size), size), :] = jnp.where(
            place.astype(jnp.float32) == rank, 1.0, 0.0
        ).astype(jnp.bfloat16)

    force_ref[...] = jnp.zeros_like(force_ref)
    for copy in copies:
        copy.wait()
    total = partial_ref[me]
    for order in range(len(peers)):
        total = total + land_ref[order]
    for part in range(3):
        piece = total.astype(jnp.bfloat16).astype(jnp.float32)
        total = total - piece
        for axis in range(3):
            for tile in range(atom_total // lanes):
                span = slice(tile * lanes, (tile + 1) * lanes)
                row = 4 * part + axis
                force_ref[row : row + 1, span] = piece[axis, tile : tile + 1, :]
    placed = dot(force_ref[...].astype(jnp.bfloat16), order_ref[...])
    placed = (placed[0:4] + placed[4:8]) + placed[8:12]
    for axis in range(3):
        long_ref[axis, 0, :, :] = placed[axis : axis + 1, :]


def finished(pair_lists, partial, raw, rank, columns, before, count_x, count_y, cells_x, cells_y):
    devices, _, atom_total = raw.shape
    clusters, listed = pair_lists.shape[2:]
    size = atom_total // clusters
    vmem = pl.BlockSpec(memory_space=pltpu.VMEM)
    flags = pltpu.SemaphoreType.DMA((devices - 1,))
    return pl.pallas_call(
        functools.partial(finish_kernel, (count_x, count_y), (cells_x, cells_y)),
        in_specs=[pl.BlockSpec(memory_space=pltpu.SMEM)] + [vmem] * 5,
        out_specs=[vmem, vmem],
        out_shape=[jax.ShapeDtypeStruct((3, 1, 1, atom_total), jnp.float32)] * 2,
        scratch_shapes=[
            pltpu.VMEM((devices - 1, *partial.shape[1:]), jnp.float32),
            pltpu.VMEM((clusters, 4, 8, (listed - 1) * size), jnp.float32),
            pltpu.VMEM((3, atom_total, lanes), jnp.float32),
            pltpu.VMEM((atom_total, atom_total), jnp.bfloat16),
            pltpu.VMEM((16, atom_total), jnp.float32),
            flags,
            flags,
        ],
        compiler_params=pltpu.CompilerParams(
            collective_id=1, has_side_effects=True, vmem_limit_bytes=16 << 20
        ),
        name="finish",
    )(
        pltpu.with_memory_space_constraint(pair_lists, pltpu.HBM),
        partial,
        raw,
        rank,
        columns,
        before,
    )


def green_table(period):
    index = np.arange(period)
    signed = np.where(index <= period // 2, index, index - period) / (period * spacing)
    modulus = ((2.0 + np.cos(index * (2.0 * np.pi / period))) / 3.0) ** 2
    square = signed * signed
    return np.stack([square, np.exp(-((np.pi / ewald_split) ** 2) * square) / modulus]).astype(
        np.float32
    )


def green_factors(index, period):
    signed = jnp.where(index <= period // 2, index, index - period).astype(jnp.float32) / (
        period * spacing
    )
    modulus = ((2.0 + jnp.cos(index.astype(jnp.float32) * (2.0 * jnp.pi / period))) / 3.0) ** 2
    square = signed * signed
    return jnp.stack([square, jnp.exp(-((jnp.pi / ewald_split) ** 2) * square) / modulus])


def one_cluster(own_rows, partner):
    offsets = (own_rows[:3, :, None] - partner[:3, None, :]) * spacing
    dist_square = jnp.sum(offsets * offsets, axis=0)
    soft_square = dist_square + soft_core
    soft_dist = jnp.sqrt(soft_square)
    scaled = ewald_split * soft_dist
    strength = (
        jax.scipy.special.erfc(scaled) / soft_dist
        + ewald_split * root_factor * jnp.exp(-scaled * scaled)
    ) / soft_square
    cutoff_taper = jnp.where(
        dist_square < cutoff * cutoff, (1.0 - dist_square / (cutoff * cutoff)) ** 2, 0.0
    )
    weight = partner[3][None, :] * strength * cutoff_taper
    return own_rows[3] * jnp.sum(weight[None] * offsets, axis=2)


def far_by_planes(bounds, atoms, count_x, count_y, cells_x, cells_y):
    devices = count_x * count_y
    depth = GRID_Z // devices
    tiles = atoms.shape[2]
    pad_y = round_up(cells_y + 3, 8)
    stride = round_up(pad_y, 16)
    window = 2 * cells_y
    turn_x = halves(jnp.asarray(hartley(GRID_X)))
    turn_y = halves(jnp.asarray(hartley(GRID_Y)))
    volume = GRID_X * GRID_Y * GRID_Z * spacing**3
    column = jnp.asarray(green_table(GRID_X).T)
    row = jnp.asarray(green_table(GRID_Y))
    every_k = np.arange(GRID_Z)
    taps = np.outer(every_k, np.arange(4)) * (2.0 * np.pi / GRID_Z)
    square, scale = green_table(GRID_Z)
    table = np.concatenate(
        [
            every_k[:, None],
            np.cos(taps) + np.sin(taps),
            np.cos(taps) - np.sin(taps),
            square[:, None],
            scale[:, None] / (np.pi * volume),
        ],
        axis=1,
    ).astype(np.float32)
    vmem = pl.BlockSpec(memory_space=pltpu.VMEM)
    rows = GRID_X + window_rows
    batch = depth * window_rows
    angle = every_k * (2.0 * np.pi / GRID_Z)
    circle = np.repeat(np.stack([np.cos(angle), np.sin(angle)]), 8, axis=0).astype(np.float32)
    constants = (*turn_x, *turn_y, column, row, jnp.asarray(circle), jnp.asarray(table))
    fixed = pl.BlockSpec(memory_space=pltpu.HBM)
    return pl.pallas_call(
        functools.partial(mesh_kernel, (count_x, count_y), (cells_x, cells_y), pad_y),
        in_specs=[pl.BlockSpec(memory_space=pltpu.SMEM)] + [vmem] + [fixed] * fixed_arrays,
        out_specs=vmem,
        out_shape=jax.ShapeDtypeStruct((devices, 3, tiles, lanes), jnp.float32),
        scratch_shapes=[
            pltpu.VMEM((2, depth, rows, GRID_Y), jnp.float32),
            pltpu.VMEM((depth, rows, 4 * GRID_Y), jnp.float32),
            pltpu.VMEM((36 * devices * tiles + 8, lanes), jnp.float32),
            pltpu.VMEM((devices * tiles * depth + 8, lanes), jnp.float32),
            pltpu.VMEM((devices * tiles * depth + 8, lanes), jnp.float32),
            pltpu.VMEM((devices * tiles, 2 * stride, lanes), jnp.bfloat16),
            pltpu.VMEM((group_size, 2 * window, 2 * lanes), jnp.bfloat16),
            pltpu.VMEM((group_size, batch, 2 * lanes), jnp.bfloat16),
            pltpu.VMEM((gather_size, batch, 2 * lanes), jnp.float32),
            pltpu.VMEM((GRID_X, GRID_Y), jnp.float32),
            pltpu.VMEM((GRID_X, GRID_Y), jnp.float32),
            pltpu.SMEM((4 * devices * tiles,), jnp.int32),
            *[pltpu.VMEM(value.shape, value.dtype) for value in constants],
            pltpu.SemaphoreType.DMA((fixed_arrays,)),
        ],
        compiler_params=pltpu.CompilerParams(vmem_limit_bytes=36 << 20),
        name="mesh",
    )(
        bounds, atoms, *[pltpu.with_memory_space_constraint(value, pltpu.HBM) for value in constants]
    )


def convolved_by_lines(charge_mesh, count_x, count_y):
    turn_x = jnp.asarray(hartley(GRID_X))
    turn_y = jnp.asarray(hartley(GRID_Y))
    product = functools.partial(
        jnp.einsum, precision=lax.Precision.HIGHEST, preferred_element_type=jnp.float32
    )
    exchange = functools.partial(lax.all_to_all, tiled=True)
    lines = exchange(charge_mesh, "gx", split_axis=2, concat_axis=0)
    lines = product("xyk,xu->uyk", lines, turn_x)
    lines = exchange(lines, "gy", split_axis=0, concat_axis=1)
    lines = product("uyk,yv->uvk", lines, turn_y)
    wide, _, depth = lines.shape
    start_x = lax.axis_index("gy") * wide
    start_z = lax.axis_index("gx") * depth
    volume = GRID_X * GRID_Y * GRID_Z * spacing**3
    fx = green_factors(start_x + jnp.arange(wide, dtype=jnp.int32), GRID_X)
    fy = green_factors(jnp.arange(GRID_Y, dtype=jnp.int32), GRID_Y)
    fz = green_factors(start_z + jnp.arange(depth, dtype=jnp.int32), GRID_Z)
    square = fx[0][:, None, None] + fy[0][:, None] + fz[0]
    scale = fx[1][:, None, None] * fy[1][:, None] * fz[1] / (math.pi * volume)
    lines = lines * jnp.where(square > 0.0, scale / jnp.where(square > 0.0, square, 1.0), 0.0)
    lines = product("uvk,vy->uyk", lines, turn_y)
    lines = exchange(lines, "gy", split_axis=1, concat_axis=0)
    lines = product("uyk,ux->xyk", lines, turn_x)
    return exchange(lines, "gx", split_axis=0, concat_axis=2)


def far_by_lines(atoms, base, count_x, count_y, cells_x, cells_y, cells_z):
    atom_total = atoms.shape[1]
    cells = (cells_x, cells_y, cells_z)
    pad = (round_up(cells_x + 3, rows_group), round_up(cells_y + 3, 8))
    pad_x, pad_y = pad
    turn_z = jnp.asarray(hartley(GRID_Z))
    spread = pl.pallas_call(
        functools.partial(spread_kernel, cells, pad),
        out_shape=jax.ShapeDtypeStruct((pad_x, pad_y, GRID_Z), jnp.float32),
        scratch_shapes=[
            pltpu.VMEM((pad_x, atom_total), jnp.float32),
            pltpu.VMEM((pad_y, atom_total), jnp.float32),
            pltpu.VMEM((atom_total, 2 * GRID_Z), jnp.bfloat16),
            pltpu.VMEM((rows_group * pad_y, atom_total), jnp.bfloat16),
            pltpu.VMEM((rows_group * pad_y, atom_total), jnp.bfloat16),
        ],
        name="spread",
    )(atoms, base, turn_z)

    from_x = moved(spread[cells_x : cells_x + 3, :cells_y], 1, 0)
    from_y = moved(spread[:cells_x, cells_y : cells_y + 3], 0, 1)
    from_both = moved(spread[cells_x : cells_x + 3, cells_y : cells_y + 3], 1, 1)
    charge_mesh = (
        spread[:cells_x, :cells_y]
        .at[:3]
        .add(from_x)
        .at[:, :3]
        .add(from_y)
        .at[:3, :3]
        .add(from_both)
    )
    potential = convolved_by_lines(charge_mesh, count_x, count_y)
    upper_x = moved(potential[:3], -1, 0)
    upper_y = moved(potential[:, :3], 0, -1)
    upper_both = moved(potential[:3, :3], -1, -1)
    wider = jnp.concatenate(
        [
            jnp.concatenate([potential, upper_x], axis=0),
            jnp.concatenate([upper_y, upper_both], axis=0),
        ],
        axis=1,
    )
    wider = jnp.pad(wider, ((0, pad_x - cells_x - 3), (0, pad_y - cells_y - 3), (0, 0)))
    return pl.pallas_call(
        functools.partial(gather_kernel, cells, pad),
        out_shape=jax.ShapeDtypeStruct((3, atom_total), jnp.float32),
        scratch_shapes=[
            pltpu.VMEM((pad_x, atom_total), jnp.float32),
            pltpu.VMEM((pad_x, atom_total), jnp.float32),
            pltpu.VMEM((pad_y, atom_total), jnp.float32),
            pltpu.VMEM((pad_y, atom_total), jnp.float32),
            pltpu.VMEM((2 * GRID_Z, 2 * atom_total), jnp.bfloat16),
            pltpu.VMEM((rows_group * pad_y, 2 * atom_total), jnp.float32),
        ],
        name="gather",
    )(atoms, base, turn_z, wider)


def local(positions, charges, pair_lists, slab_dest, atom_counts):
    count_x = lax.axis_size("gx")
    count_y = lax.axis_size("gy")
    devices = count_x * count_y
    atom_total = positions.shape[3]
    clusters = pair_lists.shape[2]
    cluster_size = atom_total // clusters
    blocks = slab_dest.shape[2]
    block_size = atom_total // blocks
    cells_x = GRID_X // count_x
    cells_y = GRID_Y // count_y
    cells_z = GRID_Z // count_y
    by_planes = (
        GRID_Z == 8 * devices
        and GRID_Z == lanes
        and cells_y == 64
        and cells_x % 8 == 0
        and cells_x <= 64
        and count_y % 2 == 0
        and atom_total == 8 * lanes
        and cluster_size % lanes == 0
    )
    if by_planes:
        sizes = (count_x, count_y, cells_x, cells_y)
        raw, atoms, bounds, rank, columns, before = shared(
            positions, charges, atom_counts, clusters, *sizes
        )
        partial = far_by_planes(bounds, atoms, *sizes)
        short_sums, long_sums = finished(
            pair_lists, partial, raw, rank, columns, before, *sizes
        )
        living = jnp.arange(atom_total, dtype=jnp.int32) < atom_counts[0, 0]
        charge = jnp.where(living, charges[0, 0], 0.0)
        return (short_sums * (charge * spacing), long_sums * (charge * (-1.0 / spacing)))
    living = jnp.arange(atom_total, dtype=jnp.int32) < atom_counts[0, 0]
    charge = jnp.where(living, charges[0, 0], 0.0)
    packed = jnp.concatenate([positions, charge[None, None, None, :]], axis=0)
    atoms = packed.reshape(4, atom_total)
    base = jnp.broadcast_to(
        (slab_dest[0, 0] * cells_z)[:, None], (blocks, block_size)
    ).reshape(1, atom_total)
    gathered = lax.all_gather(atoms, ("gx", "gy"), axis=0, tiled=False)
    far_part = far_by_lines(atoms, base, count_x, count_y, cells_x, cells_y, cells_z)

    chosen = pair_lists[0, 0]
    beside = chosen // clusters
    step_x, step_y = (beside // 3 - 1, beside % 3 - 1)
    at_x = (lax.axis_index("gx") + step_x + count_x) % count_x
    at_y = (lax.axis_index("gy") + step_y + count_y) % count_y
    number = (at_x * count_y + at_y) * clusters + chosen % clusters
    pick = (number[:, :, None] == jnp.arange(devices * clusters, dtype=jnp.int32)).astype(
        jnp.float32
    )
    pool = gathered[:, :4].reshape(devices, 4, clusters, cluster_size)
    pool = jnp.transpose(pool, (1, 0, 2, 3)).reshape(4, devices * clusters, cluster_size)
    partners = jnp.einsum(
        "cln,fnk->cflk",
        pick,
        pool,
        precision=lax.Precision.HIGHEST,
        preferred_element_type=jnp.float32,
    )
    shift_x = (step_x * cells_x).astype(jnp.float32)
    shift_y = (step_y * cells_y).astype(jnp.float32)
    flat = jnp.zeros_like(shift_x)
    shift = jnp.stack([shift_x, shift_y, flat, flat], axis=1)
    partners = (partners + shift[:, :, :, None]).reshape(clusters, 4, -1)
    own = packed.reshape(4, clusters, cluster_size)
    pair_part = jnp.stack(
        [one_cluster(own[:, c], partners[c]) for c in range(clusters)], axis=1
    )
    short_forces = pair_part.reshape(3, 1, 1, atom_total)
    return (short_forces, far_part.reshape(3, 1, 1, atom_total))


def solution(mesh):
    return jax.shard_map(
        local,
        mesh=mesh,
        in_specs=(
            P(None, ("rep", "gx"), "gy", None),
            P(("rep", "gx"), "gy", None),
            P(("rep", "gx"), "gy", None, None),
            P(("rep", "gx"), "gy", None),
            P(("rep", "gx"), "gy"),
        ),
        out_specs=(P(None, ("rep", "gx"), "gy", None), P(None, ("rep", "gx"), "gy", None)),
        check_vma=False,
    )
```

```python
import functools
import math

import jax
import jax.numpy as jnp
import numpy as np
from jax import lax
from jax.experimental import pallas as pl
from jax.experimental.pallas import tpu as pltpu
from jax.sharding import PartitionSpec as P

GRID_X = 256
GRID_Y = 256
GRID_Z = 128


spacing = 0.16
ewald_split = 3.47
cutoff = 0.9
soft_core = 0.09
root_factor = 1.1283791670955126
rows_group = 8
lanes = 128
window_rows = 24
group_size = 16
gather_size = 12
cell_group = 4
plane_group = 8
fixed_arrays = 8


def moved(value, step_x, step_y):
    count_x = lax.axis_size("gx")
    count_y = lax.axis_size("gy")
    pairs = [
        (i * count_y + j, (i + step_x) % count_x * count_y + (j + step_y) % count_y)
        for i in range(count_x)
        for j in range(count_y)
    ]
    return lax.ppermute(value, ("gx", "gy"), pairs)


def round_up(value, multiple):
    return -(-value // multiple) * multiple


def hartley(period):
    turns = np.outer(np.arange(period), np.arange(period)) % period
    phases = turns * (2.0 * np.pi / period)
    return (np.cos(phases) + np.sin(phases)).astype(np.float32)


def halves(value):
    high = value.astype(jnp.bfloat16)
    low = (value - high.astype(jnp.float32)).astype(jnp.bfloat16)
    return (high, low)


def dot(left_side, right_side):
    return jnp.dot(left_side, right_side, preferred_element_type=jnp.float32)


def spline_weights(fraction):
    remain = 1.0 - fraction
    square = fraction * fraction
    cube_part = square * fraction
    values = [
        remain * remain * remain / 6.0,
        (3.0 * cube_part - 6.0 * square + 4.0) / 6.0,
        (-3.0 * cube_part + 3.0 * square + 3.0 * fraction + 1.0) / 6.0,
        cube_part / 6.0,
    ]
    slopes = [
        -0.5 * remain * remain,
        0.5 * (3.0 * square - 4.0 * fraction),
        0.5 * (-3.0 * square + 2.0 * fraction + 1.0),
        0.5 * square,
    ]
    return (values, slopes)


def split_cells(coordinate, offset, cell_count):
    inside = coordinate - offset
    lowest = jnp.clip(jnp.floor(inside).astype(jnp.int32), 0, cell_count - 1)
    return (lowest, inside - lowest.astype(inside.dtype))


def spline_table(lowest, values, table_size, period=None):
    points = lax.broadcasted_iota(jnp.int32, (table_size, lowest.shape[1]), 0)
    lookup = jnp.zeros(points.shape, jnp.float32)
    for spline_term in range(4):
        at = lowest + spline_term
        if period is not None:
            at = jnp.where(at >= period, at - period, at)
        lookup = jnp.where(points == at, values[spline_term], lookup)
    return lookup


def spread_kernel(cells, pad, atoms_ref, base_ref, turn_ref, out_ref, wx_ref, wy_ref, wz_ref, hi_ref, lo_ref):
    cells_x, cells_y, cells_z = cells
    pad_x, pad_y = pad
    atom_total = atoms_ref.shape[1]
    low_x, frac_x = split_cells(atoms_ref[0:1, :], 0.0, cells_x)
    low_y, frac_y = split_cells(atoms_ref[1:2, :], 0.0, cells_y)
    base = base_ref[...]
    low_z, frac_z = split_cells(atoms_ref[2:3, :], base.astype(jnp.float32), cells_z)
    wx_ref[...] = spline_table(low_x, spline_weights(frac_x)[0], pad_x) * atoms_ref[3:4, :]
    wy_ref[...] = spline_table(low_y, spline_weights(frac_y)[0], pad_y)
    turn = turn_ref[...]
    size_z = turn.shape[0]
    table_z = spline_table(base + low_z, spline_weights(frac_z)[0], size_z, size_z)
    waves = jnp.dot(
        turn, table_z, precision=lax.Precision.HIGHEST, preferred_element_type=jnp.float32
    ).T
    high, low = halves(waves)
    wz_ref[:, :size_z] = high
    wz_ref[:, size_z:] = low

    @pl.loop(0, pad_x // rows_group)
    def _(chunk):
        for inner in range(rows_group):
            row = wx_ref[pl.ds(chunk * rows_group + inner, 1), :]
            high, low = halves(row * wy_ref[...])
            hi_ref[pl.ds(inner * pad_y, pad_y), :] = high
            lo_ref[pl.ds(inner * pad_y, pad_y), :] = low
        both = dot(hi_ref[...], wz_ref[...])
        rest = dot(lo_ref[...], wz_ref[:, :size_z])
        total = both[:, :size_z] + both[:, size_z:] + rest
        out_ref[pl.ds(chunk * rows_group, rows_group)] = total.reshape(rows_group, pad_y, size_z)


def gather_kernel(cells, pad, atoms_ref, base_ref, turn_ref, mesh_ref, out_ref, wx_ref, vx_ref, wy_ref, vy_ref, wz_ref, level_ref):
    cells_x, cells_y, cells_z = cells
    pad_x, pad_y = pad
    atom_total = atoms_ref.shape[1]
    low_x, frac_x = split_cells(atoms_ref[0:1, :], 0.0, cells_x)
    low_y, frac_y = split_cells(atoms_ref[1:2, :], 0.0, cells_y)
    base = base_ref[...]
    low_z, frac_z = split_cells(atoms_ref[2:3, :], base.astype(jnp.float32), cells_z)
    values, slopes = spline_weights(frac_x)
    wx_ref[...] = spline_table(low_x, values, pad_x)
    vx_ref[...] = spline_table(low_x, slopes, pad_x)
    values, slopes = spline_weights(frac_y)
    wy_ref[...] = spline_table(low_y, values, pad_y)
    vy_ref[...] = spline_table(low_y, slopes, pad_y)
    values, slopes = spline_weights(frac_z)
    turn = turn_ref[...]
    size_z = turn.shape[0]
    for place, terms in enumerate((values, slopes)):
        table_z = spline_table(base + low_z, terms, size_z, size_z)
        waves = jnp.dot(
            turn, table_z, precision=lax.Precision.HIGHEST, preferred_element_type=jnp.float32
        )
        high, low = halves(waves)
        wz_ref[:size_z, pl.ds(place * atom_total, atom_total)] = high
        wz_ref[size_z:, pl.ds(place * atom_total, atom_total)] = low
    groups = pad_y // 8

    def one_chunk(chunk, sums):
        rows = mesh_ref[pl.ds(chunk * rows_group, rows_group)].reshape(rows_group * pad_y, size_z)
        high, low = halves(rows)
        level_ref[...] = dot(jnp.concatenate([high, high], axis=1), wz_ref[...]) + dot(
            low, wz_ref[:size_z, :]
        )
        first, second, third = sums
        for inner in range(rows_group):
            flat = level_ref[pl.ds(inner * pad_y, pad_y), :atom_total]
            tilt = level_ref[pl.ds(inner * pad_y, pad_y), atom_total:]
            across = wy_ref[...]
            part_x = jnp.sum((across * flat).reshape(groups, 8, atom_total), axis=0)
            part_y = jnp.sum((vy_ref[...] * flat).reshape(groups, 8, atom_total), axis=0)
            part_z = jnp.sum((across * tilt).reshape(groups, 8, atom_total), axis=0)
            weight = wx_ref[pl.ds(chunk * rows_group + inner, 1), :]
            slope = vx_ref[pl.ds(chunk * rows_group + inner, 1), :]
            first = first + slope * part_x
            second = second + weight * part_y
            third = third + weight * part_z
        return (first, second, third)

    zero = jnp.zeros((8, atom_total), jnp.float32)
    sums = lax.fori_loop(0, pad_x // rows_group, one_chunk, (zero, zero, zero))
    factor = -atoms_ref[3:4, :] / spacing
    for place in range(3):
        out_ref[pl.ds(place, 1), :] = factor * jnp.sum(sums[place], axis=0, keepdims=True)


def peers_of(count_x, count_y):
    place_x, place_y = (lax.axis_index("gx"), lax.axis_index("gy"))
    peers = []
    for order in range(1, count_x * count_y):
        peer_x = lax.rem(place_x + order // count_y, count_x)
        peer_y = lax.rem(place_y + order % count_y, count_y)
        peers.append((peer_x, peer_y))
    return peers


root_terms = (
    3.9164407301418542,
    -0.0037127819564810594,
    0.16802528315459195,
    -0.003061234121505335,
    -0.0076524954798020545,
    0.002268454833542123,
    -0.0003056487922112269,
    1.686888935413571e-05,
)


def pair_weight(square):
    soft_square = square * (spacing * spacing) + soft_core
    inverse = lax.rsqrt(soft_square)
    series = jnp.full_like(inverse, root_terms[-1])
    for term in root_terms[-2::-1]:
        series = series * inverse + term
    decay = jnp.exp(soft_square * (-ewald_split * ewald_split))
    taper = jnp.maximum(1.0 - square * (spacing * spacing / (cutoff * cutoff)), 0.0)
    return (decay * series) * (inverse * taper) ** 2


def row_sums(values):
    total = None
    ones = jnp.ones((16, values.shape[1]), jnp.bfloat16)
    for _ in range(3):
        part = values.astype(jnp.bfloat16)
        values = values - part.astype(jnp.float32)
        summed = lax.dot_general(
            ones, part, (((1,), (1,)), ((), ())), preferred_element_type=jnp.float32
        )
        total = summed if total is None else total + summed
    return total[0:1, :]


def place_partners(sizes, cells, pairs_ref, atoms_ref, partner_ref):
    count_x, count_y = sizes
    cells_x, cells_y = cells
    place_x, place_y = (lax.axis_index("gx"), lax.axis_index("gy"))
    clusters, listed = pairs_ref.shape[2:]
    size = atoms_ref.shape[2] // clusters
    for c in range(clusters):
        for n in range(1, listed):
            chosen = pairs_ref[0, 0, c, n]
            beside = lax.div(chosen, clusters)
            which = chosen - beside * clusters
            row_x = lax.div(beside, 3)
            step_x = row_x - 1
            step_y = beside - row_x * 3 - 1
            from_x = lax.rem(place_x + step_x + count_x, count_x)
            from_y = lax.rem(place_y + step_y + count_y, count_y)
            block = atoms_ref[from_x * count_y + from_y]
            part = block[:, :size]
            for k in range(1, clusters):
                part = jnp.where(which == k, block[:, k * size : (k + 1) * size], part)
            shifts = (
                (step_x * cells_x).astype(jnp.float32),
                (step_y * cells_y).astype(jnp.float32),
            )
            for axis in range(4):
                row = part[axis : axis + 1, :]
                if axis < 2:
                    row = row + shifts[axis]
                partner_ref[c, axis, :, (n - 1) * size : n * size] = jnp.broadcast_to(
                    row, (8, size)
                )


def pair_sums(clusters, size, height, column_ref, partner_ref, before_ref, sum_ref):
    @pl.loop(0, clusters)
    def _(c):
        @pl.loop(0, size // height)
        def _(step):
            for part in range(height // 8):
                start = c * size + step * height + part * 8
                rows = pl.ds(pl.multiple_of(start, 8), 8)
                own = [column_ref[axis, rows, :] for axis in range(3)]
                sums = [
                    jnp.zeros((8, lanes), jnp.float32)
                    if before_ref is None
                    else before_ref[axis, rows, :]
                    for axis in range(3)
                ]
                for tile in range(partner_ref.shape[3] // lanes):
                    span = slice(tile * lanes, (tile + 1) * lanes)
                    offsets = [own[axis] - partner_ref[c, axis, :, span] for axis in range(3)]
                    square = sum(offset * offset for offset in offsets)
                    weight = pair_weight(square) * partner_ref[c, 3, :, span]
                    sums = [total + weight * offset for total, offset in zip(sums, offsets)]
                for axis in range(3):
                    sum_ref[axis, rows, :] = sums[axis]


def share_kernel(sizes, cells, clusters, count_ref, position_ref, charge_ref, raw_ref, sorted_ref, bounds_ref, rank_ref, column_ref, sum_ref, key_ref, split_ref, partner_ref, raw_send, raw_recv, sort_send, sort_recv, mark_send, mark_recv):
    count_x, count_y = sizes
    cells_x, _ = cells
    place_x, place_y = (lax.axis_index("gx"), lax.axis_index("gy"))
    me = place_x * count_y + place_y
    place_chip, place_core = (place_y // 2, lax.rem(place_y, 2))
    chips = count_y // 2

    def at(step_x, step_chip, flip):
        peer_x = lax.rem(place_x + step_x, count_x)
        peer_chip = lax.rem(place_chip + step_chip, chips)
        peer_core = 1 - place_core if flip else place_core
        return (peer_x, peer_chip * 2 + peer_core)

    peers = peers_of(count_x, count_y)
    barrier = pltpu.get_barrier_semaphore()
    for peer_x, peer_y in peers:
        pl.semaphore_signal(
            barrier,
            inc=1,
            device_id={"gx": peer_x, "gy": peer_y},
            device_id_type=pl.DeviceIdType.MESH,
        )

    def sent(ref, owner, peer, send_sem, recv_sem, order, slot):
        return pltpu.make_async_remote_copy(
            src_ref=ref.at[owner],
            dst_ref=ref.at[owner],
            send_sem=send_sem.at[order],
            recv_sem=recv_sem.at[slot],
            device_id={"gx": peer[0], "gy": peer[1]},
            device_id_type=pl.DeviceIdType.MESH,
        )

    passed = []

    def passes(owner, peer):
        order = len(passed)
        copies = [
            sent(sorted_ref, owner, peer, sort_send, sort_recv, order, owner),
            sent(bounds_ref, owner, peer, mark_send, mark_recv, order, owner),
        ]
        for copy in copies:
            copy.start()
        passed.append(copies)

    def arrives(owner, peer):
        sent(sorted_ref, owner, peer, sort_send, sort_recv, 0, owner).wait_recv()
        sent(bounds_ref, owner, peer, mark_send, mark_recv, 0, owner).wait_recv()

    atom_total = charge_ref.shape[2]
    tiles = atom_total // lanes
    slot = lax.broadcasted_iota(jnp.int32, (1, atom_total), 1)
    living = slot < count_ref[0, 0]
    charge = jnp.where(living, charge_ref[0], 0.0)
    rows = [position_ref[axis, 0] for axis in range(3)] + [charge]
    for axis in range(4):
        raw_ref[me, pl.ds(axis, 1), :] = rows[axis]
    column = jnp.clip(jnp.floor(rows[0]), 0.0, cells_x - 1.0)
    key = jnp.where(living, column, float(cells_x)) * float(atom_total) + slot.astype(jnp.float32)
    for tile in range(tiles):
        span = slice(tile * lanes, (tile + 1) * lanes)
        key_ref[span, :] = jnp.broadcast_to(key[:, span], (lanes, lanes)).T
    wide = [
        jnp.broadcast_to(key[:, tile * lanes : (tile + 1) * lanes], (8, lanes))
        for tile in range(tiles)
    ]

    def count_group(group, totals):
        for inner in range(8):
            others = key_ref[pl.ds(pl.multiple_of(group * 64 + inner * 8, 8), 8), :]
            totals = tuple(
                total + jnp.where(others < own, 1.0, 0.0) for total, own in zip(totals, wide)
            )
        return totals

    zero = jnp.zeros((8, lanes), jnp.float32)
    totals = lax.fori_loop(0, atom_total // 64, count_group, (zero,) * tiles)
    for tile, total in enumerate(totals):
        rank_ref[:, tile * lanes : (tile + 1) * lanes] = jnp.sum(total, axis=0, keepdims=True)

    split_ref[...] = jnp.zeros_like(split_ref)
    rest = raw_ref[me]
    for part in range(3):
        piece = rest.astype(jnp.bfloat16).astype(jnp.float32)
        split_ref[4 * part : 4 * part + 4, :] = piece
        rest = rest - piece
    split = split_ref[...].astype(jnp.bfloat16)
    rank = rank_ref[...]
    block = 2 * lanes
    for part in range(atom_total // block):
        place = lax.broadcasted_iota(jnp.int32, (block, atom_total), 0) + part * block
        chosen = jnp.where(place.astype(jnp.float32) == rank, 1.0, 0.0).astype(jnp.bfloat16)
        found = lax.dot_general(
            split, chosen, (((1,), (1,)), ((), ())), preferred_element_type=jnp.float32
        )
        found = (found[0:4] + found[4:8]) + found[8:12]
        for tile in range(block // lanes):
            row = part * (block // lanes) + tile
            for axis in range(4):
                sorted_ref[me, axis, row : row + 1, :] = found[
                    axis : axis + 1, tile * lanes : (tile + 1) * lanes
                ]
    spot = lax.broadcasted_iota(jnp.int32, (tiles, lanes), 0) * lanes
    spot = spot + lax.broadcasted_iota(jnp.int32, (tiles, lanes), 1)
    inside = spot < count_ref[0, 0]
    column = jnp.clip(jnp.floor(sorted_ref[me, 0]), 0.0, cells_x - 1.0)
    lowest = jnp.min(jnp.where(inside, column, float(cells_x)), axis=1, keepdims=True)
    highest = jnp.max(jnp.where(inside, column, -1.0), axis=1, keepdims=True)
    first = jnp.floor(lowest * 0.125)
    last = jnp.floor((highest + 3.0) * 0.125)
    windows = jnp.where(
        highest >= 0.0, jnp.floor((last - first) * (8.0 / window_rows) + 0.01) + 1.0, 0.0
    )
    lane = lax.broadcasted_iota(jnp.int32, (tiles, lanes), 1)
    row = lax.broadcasted_iota(jnp.int32, (tiles, lanes), 0)
    marks = jnp.where(lane == row, first, jnp.where(lane == row + tiles, windows, 0.0))
    marks = jnp.sum(marks, axis=0, keepdims=True)
    bounds_ref[me] = marks.astype(jnp.int32)

    near = sorted(
        (min(step, count_x - step) + min(chip, chips - chip), step, chip)
        for step in range(count_x)
        for chip in range(chips)
    )[1:]
    mate = at(0, 0, True)
    pl.semaphore_wait(barrier, len(peers))
    for _, step, chip in reversed(near):
        passes(me, at(step, chip, False))
    passes(me, mate)
    beside = sorted(
        {
            step_x % count_x * count_y + step_y % count_y
            for step_x in (-1, 0, 1)
            for step_y in (-1, 0, 1)
        }
        - {0}
    )
    copies = [
        sent(raw_ref, me, peers[order - 1], raw_send, raw_recv, order - 1, order - 1)
        for order in beside
    ]
    for copy in copies:
        copy.start()

    for axis in range(3):
        for tile in range(tiles):
            span = slice(tile * lanes, (tile + 1) * lanes)
            column_ref[axis, span, :] = jnp.broadcast_to(rows[axis][:, span], (lanes, lanes)).T
    size = atom_total // clusters
    for c in range(clusters):
        for axis in range(4):
            row = rows[axis][:, c * size : (c + 1) * size]
            partner_ref[c, axis] = jnp.broadcast_to(row, (8, size))
    pair_sums(clusters, size, 64, column_ref, partner_ref, None, sum_ref)
    for _, step, chip in near:
        owner_x, owner_y = at(step, chip, False)
        arrives(owner_x * count_y + owner_y, (owner_x, owner_y))
        passes(owner_x * count_y + owner_y, mate)
    for _, step, chip in [(0, 0, 0), *near]:
        owner_x, owner_y = at(step, chip, True)
        arrives(owner_x * count_y + owner_y, mate)
    for copy in copies:
        copy.wait()
    for pair in passed:
        for copy in pair:
            copy.wait_send()


def shared(positions, charges, atom_counts, clusters, count_x, count_y, cells_x, cells_y):
    devices = count_x * count_y
    atom_total = charges.shape[2]
    vmem = pl.BlockSpec(memory_space=pltpu.VMEM)
    smem = pl.BlockSpec(memory_space=pltpu.SMEM)
    fewer = pltpu.SemaphoreType.DMA((devices - 1,))
    flags = pltpu.SemaphoreType.DMA((devices,))
    return pl.pallas_call(
        functools.partial(share_kernel, (count_x, count_y), (cells_x, cells_y), clusters),
        in_specs=[smem, vmem, vmem],
        out_specs=[vmem] * 6,
        out_shape=[
            jax.ShapeDtypeStruct((devices, 4, atom_total), jnp.float32),
            jax.ShapeDtypeStruct((devices, 4, atom_total // lanes, lanes), jnp.float32),
            jax.ShapeDtypeStruct((devices, 1, lanes), jnp.int32),
            jax.ShapeDtypeStruct((1, atom_total), jnp.float32),
            jax.ShapeDtypeStruct((3, atom_total, lanes), jnp.float32),
            jax.ShapeDtypeStruct((3, atom_total, lanes), jnp.float32),
        ],
        scratch_shapes=[
            pltpu.VMEM((atom_total, lanes), jnp.float32),
            pltpu.VMEM((16, atom_total), jnp.float32),
            pltpu.VMEM((clusters, 4, 8, atom_total // clusters), jnp.float32),
            fewer,
            fewer,
        ]
        + [flags] * 4,
        compiler_params=pltpu.CompilerParams(
            collective_id=0, has_side_effects=True, vmem_limit_bytes=12 << 20
        ),
        name="share",
    )(
        atom_counts,
        *[pltpu.with_memory_space_constraint(value, pltpu.HBM) for value in (positions, charges)],
    )


def depth_rows(table, circle, height, terms):
    turns = height * table[:, 0:1]
    turns = turns - GRID_Z * jnp.floor(turns * (1.0 / GRID_Z))
    index = turns.astype(jnp.int32)
    cosine, sine = [jnp.take_along_axis(part, index, axis=1) for part in circle]
    results = []
    for weights in terms:
        even = sum(table[:, 1 + t : 2 + t] * weights[t] for t in range(4))
        odd = sum(table[:, 5 + t : 6 + t] * weights[t] for t in range(4))
        results.append(cosine * even + sine * odd)
    return results


def mesh_kernel(sizes, cells, pad_y, bounds_ref, atoms_ref, *refs):
    constants, (out_ref, *scratch) = refs[:fixed_arrays], refs[fixed_arrays:]
    held, copy_sem = scratch[-fixed_arrays - 1 : -1], scratch[-1]
    copies = [
        pltpu.make_async_copy(source, target, copy_sem.at[place])
        for place, (source, target) in enumerate(zip(constants, held))
    ]
    for copy in copies:
        copy.start()
    xh_ref, xl_ref, yh_ref, yl_ref, column_ref, row_ref, circle_ref, table_ref = held
    mesh_ref, stack_ref, prep_ref, deep_ref, steep_ref, near_ref, wy_ref, side_ref, level_ref, square_ref, scale_ref, work_ref = scratch[: -fixed_arrays - 1]
    count_x, count_y = sizes
    cells_x, cells_y = cells
    devices = count_x * count_y
    place = lax.axis_index("gx") * count_y + lax.axis_index("gy")
    tiles = atoms_ref.shape[2]
    depth = stack_ref.shape[0]
    window = 2 * cells_y
    windows = GRID_Y // window
    extra = 8
    share = -(-group_size * cell_group // devices)
    stack_ref[:, GRID_X:, :] = jnp.zeros_like(stack_ref[:, GRID_X:, :])
    out_ref[...] = jnp.zeros_like(out_ref)

    steps_x = window_rows // 8
    most = (cells_x + 2) // 8 // steps_x + 1

    def prep_row(kind, spot):
        return prep_ref[pl.ds(kind * devices * tiles + spot, 8, stride=0), :]

    def listed_work(cell, total):
        for tile in range(tiles):
            for step in range(most):
                work_ref[total + step] = (cell * tiles + tile) * most + step
            total = total + bounds_ref[cell, 0, tiles + tile]

        return total

    def keep_splines(cell):
        def keep(kind, value):
            rows = pl.ds(pl.multiple_of((kind * devices + cell) * tiles, 8), tiles)
            prep_ref[rows, :] = value

        for axis, count in enumerate((cells_x, cells_y)):
            value = atoms_ref[cell, axis]
            lowest = jnp.clip(jnp.floor(value), 0.0, count - 1.0)
            values, slopes = spline_weights(value - lowest)
            keep(9 * axis, lowest)
            for term in range(4):
                keep(9 * axis + 1 + term, values[term])
                keep(9 * axis + 5 + term, slopes[term])
                if axis == 1:
                    for kind, whole in ((28, values[term]), (32, slopes[term])):
                        keep(kind + term, whole - whole.astype(jnp.bfloat16).astype(jnp.float32))
        value = atoms_ref[cell, 2]
        height = jnp.floor(value)
        values, slopes = spline_weights(value - height)
        keep(18, height)
        for term in range(4):
            keep(19 + term, values[term])
            keep(23 + term, slopes[term])
        keep(27, atoms_ref[cell, 3])

    def keep_modes(cell):
        for tile in range(tiles):
            spot = cell * tiles + tile
            height = prep_row(18, spot)
            terms = [[prep_row(19 + 4 * s + term, spot) for term in range(4)] for s in range(2)]
            deep, steep = depth_rows(table, circle, height, terms)
            rows = pl.ds(pl.multiple_of(spot * depth, 8), depth)
            deep_ref[rows, :] = deep
            steep_ref[rows, :] = steep

    def prepare_some(turn, total):
        for inner in range(cell_group):
            cell = turn * cell_group + inner
            mesh_ref[lax.div(cell, depth), lax.rem(cell, depth)] = jnp.zeros(
                mesh_ref.shape[2:], jnp.float32
            )
            total = listed_work(cell, total)
        for inner in range(cell_group):
            keep_splines(turn * cell_group + inner)
        for inner in range(share):
            place = jnp.minimum(turn * share + inner, group_size - 1)
            wy_ref[place] = jnp.zeros(wy_ref.shape[1:], wy_ref.dtype)
        return total

    total = lax.fori_loop(0, devices // cell_group, prepare_some, jnp.int32(0))
    copies[-2].wait()
    copies[-1].wait()
    circle = [circle_ref[:8, :], circle_ref[8:, :]]
    table = table_ref[pl.ds(pl.multiple_of(place * depth, 8), depth), :]

    @pl.loop(0, devices // cell_group)
    def _(turn):
        for inner in range(cell_group):
            keep_modes(turn * cell_group + inner)

    rounds = lax.div(total + group_size - 1, group_size)

    row_index = lax.broadcasted_iota(jnp.int32, (8, lanes), 0).astype(jnp.float32)

    def looked_up(points, lowest, term_lists):
        results = [jnp.zeros_like(points) for _ in term_lists]
        for term in range(4):
            hit = points == lowest + float(term)
            results = [
                jnp.where(hit, terms[term], result)
                for terms, result in zip(term_lists, results)
            ]
        return results

    def kinds(first, spot):
        return [prep_row(first + term, spot) for term in range(4)]

    stride = round_up(pad_y, 16)
    far_away = 1.0e6

    def task(index):
        entry = jnp.where(index < total, work_ref[index], 0)
        spot = lax.div(entry, most)
        cell = lax.div(spot, tiles)
        chunk = spot - cell * tiles
        begin = bounds_ref[cell, 0, chunk] * 8 + (entry - spot * most) * window_rows
        base = jnp.where(index < total, begin.astype(jnp.float32), far_away)
        i = lax.div(cell, count_y)
        rows = pl.ds(pl.multiple_of(i * cells_x + begin, 8), window_rows)
        return (spot, cell, chunk, cell - i * count_y, rows, base)

    packed_index = jnp.concatenate([row_index, row_index + 8.0], axis=0).astype(jnp.bfloat16)

    def packed_row(kind, spot):
        row = prep_row(kind, spot)
        return jnp.concatenate([row, row], axis=0).astype(jnp.bfloat16)

    def y_table(spot, kind, low_kind):
        lowest = packed_row(9, spot)
        highs = [packed_row(kind + term, spot) for term in range(4)]
        lows = [packed_row(low_kind + term, spot) for term in range(4)]
        starts = [lowest + jnp.bfloat16(term) for term in range(4)]
        for group in range(stride // 16):
            points = packed_index + jnp.bfloat16(group * 16)
            high = low = jnp.zeros_like(points)
            for term in range(4):
                hit = points == starts[term]
                high = jnp.where(hit, highs[term], high)
                low = jnp.where(hit, lows[term], low)
            yield (slice(group * 16, group * 16 + 16), high, low)

    @pl.loop(0, rounds)
    def _(turn):
        tasks = [task(turn * group_size + place) for place in range(group_size)]
        for place, (spot, _, _, _, _, base) in enumerate(tasks):
            for rows, high, low in y_table(spot, 10, 28):
                after = slice(window + rows.start, window + rows.stop)
                later = slice(stride + rows.start, stride + rows.stop)
                wy_ref[place, rows, :lanes] = high
                wy_ref[place, rows, lanes:] = high
                wy_ref[place, after, :lanes] = low
                near_ref[spot, rows, :] = high
                near_ref[spot, later, :] = low
            lowest = prep_row(0, spot) - base
            charge = prep_row(27, spot)
            terms = [term * charge for term in kinds(1, spot)]
            weights = [
                looked_up(row_index + float(tile * 8), lowest, [terms])[0]
                for tile in range(steps_x)
            ]
            modes = [
                deep_ref[pl.ds(spot * depth + k, 8, stride=0), :] for k in range(depth)
            ]
            blocks = [weight * mode for mode in modes for weight in weights]
            for pair in range(len(blocks) // 2):
                high, low = halves(jnp.concatenate(blocks[2 * pair : 2 * pair + 2], axis=0))
                rows = slice(pair * 16, pair * 16 + 16)
                side_ref[place, rows, :lanes] = high
                side_ref[place, rows, lanes:] = low
        for place, (_, _, _, j, rows, _) in enumerate(tasks):
            product = lax.dot_general(
                side_ref[place],
                wy_ref[place],
                (((1,), (1,)), ((), ())),
                preferred_element_type=jnp.float32,
            )
            product = product[:, :window] + product[:, window:]
            m = lax.div(j, 2)
            here = pl.ds(pl.multiple_of(m * window, lanes), window)
            mesh_ref[j - 2 * m, :, rows, here] += product.reshape(depth, window_rows, window)

    def across(value):
        high, low = halves(value)
        return dot(xh_ref[...], high) + dot(xl_ref[...], high) + dot(xh_ref[...], low)

    def along(value):
        high, low = halves(value)
        return dot(high, yh_ref[...]) + dot(high, yl_ref[...]) + dot(low, yh_ref[...])

    plane_lane = lax.broadcasted_iota(jnp.int32, (GRID_X, window), 1)
    for copy in copies[:-2]:
        copy.wait()
    shape = (GRID_X, GRID_Y)
    square_ref[...] = jnp.broadcast_to(column_ref[:, 0:1], shape) + row_ref[0:1, :]
    scale_ref[...] = jnp.broadcast_to(column_ref[:, 1:2], shape) * row_ref[1:2, :]

    def charge_of(k):
        charge = mesh_ref[0, k, :GRID_X, :] + pltpu.roll(mesh_ref[1, k, :GRID_X, :], cells_y, 1)
        over = slice(GRID_X, GRID_X + extra)
        beyond = mesh_ref[0, k, over, :] + pltpu.roll(mesh_ref[1, k, over, :], cells_y, 1)
        return jnp.concatenate([charge[:extra] + beyond, charge[extra:]], axis=0)

    def green_of(k):
        mode = pl.ds(place * depth + k, 1)
        square = square_ref[...] + table_ref[mode, 9:10]
        scale = scale_ref[...] * table_ref[mode, 10:11]
        return jnp.where(square > 0.0, scale / square, 0.0)

    def place_plane(k, plane):
        for odd in range(2):
            if odd:
                plane = pltpu.roll(plane, GRID_Y - cells_y, 1)
            for j_half in range(windows):
                j = 2 * j_half + odd
                block = plane[:, j_half * window : (j_half + 1) * window]
                high = block.astype(jnp.bfloat16).astype(jnp.float32)
                low = block - high
                shifted = pltpu.roll(high, stride, 1)
                left = jnp.where(plane_lane < stride, high, shifted)
                right = jnp.where(
                    plane_lane < 2 * stride - window,
                    shifted,
                    pltpu.roll(low, 2 * stride - window, 1),
                )
                for side, value in enumerate((left, right)):
                    span = slice((2 * j + side) * window, (2 * j + side + 1) * window)
                    stack_ref[k, :GRID_X, span] = value
                    stack_ref[k, GRID_X : GRID_X + extra, span] = value[:extra]

    @pl.loop(0, depth // plane_group)
    def _(pair):
        spots = [pair * plane_group + inner for inner in range(plane_group)]
        stages = [
            lambda k, _: across(charge_of(k)),
            lambda k, value: along(value),
            lambda k, value: along(value * green_of(k)),
            lambda k, value: across(value),
            lambda k, value: place_plane(k, value),
        ]
        values = [None] * plane_group
        for wave in range(plane_group + len(stages) - 1):
            for inner in range(plane_group):
                if 0 <= wave - inner < len(stages):
                    values[inner] = stages[wave - inner](spots[inner], values[inner])

    @pl.loop(0, lax.div(total + gather_size - 1, gather_size))
    def _(turn):
        tasks = [task(turn * gather_size + place) for place in range(gather_size)]
        blank = jnp.zeros((2 * window - 3 * stride, lanes), jnp.bfloat16)
        for place, (spot, _, _, j, rows, _) in enumerate(tasks):
            near = near_ref[spot]
            highs, lows = [], []
            for _, high, low in y_table(spot, 14, 32):
                highs.append(high)
                lows.append(low)
            columns = jnp.concatenate(
                [
                    jnp.concatenate([near, near[:stride], blank], axis=0),
                    jnp.concatenate([*highs, *lows, *highs, blank], axis=0),
                ],
                axis=1,
            )
            span = pl.ds(pl.multiple_of(j * 2 * window, lanes), 2 * window)
            block = stack_ref[:, rows, span].reshape(depth * window_rows, 2 * window)
            level_ref[place] = dot(block.astype(jnp.bfloat16), columns)
        for place, (spot, cell, chunk, _, _, base) in enumerate(tasks):
            lowest = prep_row(0, spot) - base
            values = kinds(1, spot)
            slopes = kinds(5, spot)
            modes = [pl.ds(spot * depth + k, 8, stride=0) for k in range(depth)]
            deep = [deep_ref[mode, :] for mode in modes]
            steep = [steep_ref[mode, :] for mode in modes]
            zero = jnp.zeros((8, lanes), jnp.float32)
            sums = [zero, zero, zero]
            for tile in range(steps_x):
                weight, slope = looked_up(row_index + float(tile * 8), lowest, [values, slopes])
                parts = [zero, zero, zero]
                for k in range(depth):
                    at = slice(k * window_rows + tile * 8, k * window_rows + tile * 8 + 8)
                    flat = level_ref[place, at, :lanes]
                    tilt = level_ref[place, at, lanes:]
                    parts = [
                        parts[0] + deep[k] * flat,
                        parts[1] + deep[k] * tilt,
                        parts[2] + steep[k] * flat,
                    ]
                sums = [
                    sums[0] + slope * parts[0],
                    sums[1] + weight * parts[1],
                    sums[2] + weight * parts[2],
                ]
            for axis in range(3):
                out_ref[cell, axis, pl.ds(chunk, 1), :] += jnp.sum(
                    sums[axis], axis=0, keepdims=True
                )


def finish_kernel(sizes, cells, pairs_ref, partial_ref, atoms_ref, rank_ref, column_ref, before_ref, short_ref, long_ref, land_ref, partner_ref, sum_ref, order_ref, force_ref, send_sem, recv_sem):
    count_x, count_y = sizes
    place_x, place_y = (lax.axis_index("gx"), lax.axis_index("gy"))
    me = place_x * count_y + place_y
    peers = peers_of(count_x, count_y)
    barrier = pltpu.get_barrier_semaphore()
    for peer_x, peer_y in peers:
        pl.semaphore_signal(
            barrier,
            inc=1,
            device_id={"gx": peer_x, "gy": peer_y},
            device_id_type=pl.DeviceIdType.MESH,
        )
    clusters = pairs_ref.shape[2]
    atom_total = atoms_ref.shape[2]
    size = atom_total // clusters
    place_partners(sizes, cells, pairs_ref, atoms_ref, partner_ref)
    pl.semaphore_wait(barrier, len(peers))
    copies = []
    for order, (peer_x, peer_y) in enumerate(peers):
        copy = pltpu.make_async_remote_copy(
            src_ref=partial_ref.at[peer_x * count_y + peer_y],
            dst_ref=land_ref.at[order],
            send_sem=send_sem.at[order],
            recv_sem=recv_sem.at[order],
            device_id={"gx": peer_x, "gy": peer_y},
            device_id_type=pl.DeviceIdType.MESH,
        )
        copy.start()
        copies.append(copy)
    pair_sums(clusters, size, 32, column_ref, partner_ref, before_ref, sum_ref)
    for axis in range(3):
        for c in range(clusters):
            span = slice(c * size, (c + 1) * size)
            summed = row_sums(sum_ref[axis, span, :])
            short_ref[axis, 0, :, span] = summed
    rank = rank_ref[...]

    @pl.loop(0, atom_total // size)
    def _(block):
        place = lax.broadcasted_iota(jnp.int32, (size, atom_total), 0) + block * size
        order_ref[pl.ds(pl.multiple_of(block * size, size), size), :] = jnp.where(
            place.astype(jnp.float32) == rank, 1.0, 0.0
        ).astype(jnp.bfloat16)

    force_ref[...] = jnp.zeros_like(force_ref)
    for copy in copies:
        copy.wait()
    total = partial_ref[me]
    for order in range(len(peers)):
        total = total + land_ref[order]
    for part in range(3):
        piece = total.astype(jnp.bfloat16).astype(jnp.float32)
        total = total - piece
        for axis in range(3):
            for tile in range(atom_total // lanes):
                span = slice(tile * lanes, (tile + 1) * lanes)
                row = 4 * part + axis
                force_ref[row : row + 1, span] = piece[axis, tile : tile + 1, :]
    placed = dot(force_ref[...].astype(jnp.bfloat16), order_ref[...])
    placed = (placed[0:4] + placed[4:8]) + placed[8:12]
    for axis in range(3):
        long_ref[axis, 0, :, :] = placed[axis : axis + 1, :]


def finished(pair_lists, partial, raw, rank, columns, before, count_x, count_y, cells_x, cells_y):
    devices, _, atom_total = raw.shape
    clusters, listed = pair_lists.shape[2:]
    size = atom_total // clusters
    vmem = pl.BlockSpec(memory_space=pltpu.VMEM)
    flags = pltpu.SemaphoreType.DMA((devices - 1,))
    return pl.pallas_call(
        functools.partial(finish_kernel, (count_x, count_y), (cells_x, cells_y)),
        in_specs=[pl.BlockSpec(memory_space=pltpu.SMEM)] + [vmem] * 5,
        out_specs=[vmem, vmem],
        out_shape=[jax.ShapeDtypeStruct((3, 1, 1, atom_total), jnp.float32)] * 2,
        scratch_shapes=[
            pltpu.VMEM((devices - 1, *partial.shape[1:]), jnp.float32),
            pltpu.VMEM((clusters, 4, 8, (listed - 1) * size), jnp.float32),
            pltpu.VMEM((3, atom_total, lanes), jnp.float32),
            pltpu.VMEM((atom_total, atom_total), jnp.bfloat16),
            pltpu.VMEM((16, atom_total), jnp.float32),
            flags,
            flags,
        ],
        compiler_params=pltpu.CompilerParams(
            collective_id=1, has_side_effects=True, vmem_limit_bytes=16 << 20
        ),
        name="finish",
    )(
        pltpu.with_memory_space_constraint(pair_lists, pltpu.HBM),
        partial,
        raw,
        rank,
        columns,
        before,
    )


def green_table(period):
    index = np.arange(period)
    signed = np.where(index <= period // 2, index, index - period) / (period * spacing)
    modulus = ((2.0 + np.cos(index * (2.0 * np.pi / period))) / 3.0) ** 2
    square = signed * signed
    return np.stack([square, np.exp(-((np.pi / ewald_split) ** 2) * square) / modulus]).astype(
        np.float32
    )


def green_factors(index, period):
    signed = jnp.where(index <= period // 2, index, index - period).astype(jnp.float32) / (
        period * spacing
    )
    modulus = ((2.0 + jnp.cos(index.astype(jnp.float32) * (2.0 * jnp.pi / period))) / 3.0) ** 2
    square = signed * signed
    return jnp.stack([square, jnp.exp(-((jnp.pi / ewald_split) ** 2) * square) / modulus])


def one_cluster(own_rows, partner):
    offsets = (own_rows[:3, :, None] - partner[:3, None, :]) * spacing
    dist_square = jnp.sum(offsets * offsets, axis=0)
    soft_square = dist_square + soft_core
    soft_dist = jnp.sqrt(soft_square)
    scaled = ewald_split * soft_dist
    strength = (
        jax.scipy.special.erfc(scaled) / soft_dist
        + ewald_split * root_factor * jnp.exp(-scaled * scaled)
    ) / soft_square
    cutoff_taper = jnp.where(
        dist_square < cutoff * cutoff, (1.0 - dist_square / (cutoff * cutoff)) ** 2, 0.0
    )
    weight = partner[3][None, :] * strength * cutoff_taper
    return own_rows[3] * jnp.sum(weight[None] * offsets, axis=2)


def far_by_planes(bounds, atoms, count_x, count_y, cells_x, cells_y):
    devices = count_x * count_y
    depth = GRID_Z // devices
    tiles = atoms.shape[2]
    pad_y = round_up(cells_y + 3, 8)
    stride = round_up(pad_y, 16)
    window = 2 * cells_y
    turn_x = halves(jnp.asarray(hartley(GRID_X)))
    turn_y = halves(jnp.asarray(hartley(GRID_Y)))
    volume = GRID_X * GRID_Y * GRID_Z * spacing**3
    column = jnp.asarray(green_table(GRID_X).T)
    row = jnp.asarray(green_table(GRID_Y))
    every_k = np.arange(GRID_Z)
    taps = np.outer(every_k, np.arange(4)) * (2.0 * np.pi / GRID_Z)
    square, scale = green_table(GRID_Z)
    table = np.concatenate(
        [
            every_k[:, None],
            np.cos(taps) + np.sin(taps),
            np.cos(taps) - np.sin(taps),
            square[:, None],
            scale[:, None] / (np.pi * volume),
        ],
        axis=1,
    ).astype(np.float32)
    vmem = pl.BlockSpec(memory_space=pltpu.VMEM)
    rows = GRID_X + window_rows
    batch = depth * window_rows
    angle = every_k * (2.0 * np.pi / GRID_Z)
    circle = np.repeat(np.stack([np.cos(angle), np.sin(angle)]), 8, axis=0).astype(np.float32)
    constants = (*turn_x, *turn_y, column, row, jnp.asarray(circle), jnp.asarray(table))
    fixed = pl.BlockSpec(memory_space=pltpu.HBM)
    return pl.pallas_call(
        functools.partial(mesh_kernel, (count_x, count_y), (cells_x, cells_y), pad_y),
        in_specs=[pl.BlockSpec(memory_space=pltpu.SMEM)] + [vmem] + [fixed] * fixed_arrays,
        out_specs=vmem,
        out_shape=jax.ShapeDtypeStruct((devices, 3, tiles, lanes), jnp.float32),
        scratch_shapes=[
            pltpu.VMEM((2, depth, rows, GRID_Y), jnp.float32),
            pltpu.VMEM((depth, rows, 4 * GRID_Y), jnp.float32),
            pltpu.VMEM((36 * devices * tiles + 8, lanes), jnp.float32),
            pltpu.VMEM((devices * tiles * depth + 8, lanes), jnp.float32),
            pltpu.VMEM((devices * tiles * depth + 8, lanes), jnp.float32),
            pltpu.VMEM((devices * tiles, 2 * stride, lanes), jnp.bfloat16),
            pltpu.VMEM((group_size, 2 * window, 2 * lanes), jnp.bfloat16),
            pltpu.VMEM((group_size, batch, 2 * lanes), jnp.bfloat16),
            pltpu.VMEM((gather_size, batch, 2 * lanes), jnp.float32),
            pltpu.VMEM((GRID_X, GRID_Y), jnp.float32),
            pltpu.VMEM((GRID_X, GRID_Y), jnp.float32),
            pltpu.SMEM((4 * devices * tiles,), jnp.int32),
            *[pltpu.VMEM(value.shape, value.dtype) for value in constants],
            pltpu.SemaphoreType.DMA((fixed_arrays,)),
        ],
        compiler_params=pltpu.CompilerParams(vmem_limit_bytes=36 << 20),
        name="mesh",
    )(
        bounds, atoms, *[pltpu.with_memory_space_constraint(value, pltpu.HBM) for value in constants]
    )


def convolved_by_lines(charge_mesh, count_x, count_y):
    turn_x = jnp.asarray(hartley(GRID_X))
    turn_y = jnp.asarray(hartley(GRID_Y))
    product = functools.partial(
        jnp.einsum, precision=lax.Precision.HIGHEST, preferred_element_type=jnp.float32
    )
    exchange = functools.partial(lax.all_to_all, tiled=True)
    lines = exchange(charge_mesh, "gx", split_axis=2, concat_axis=0)
    lines = product("xyk,xu->uyk", lines, turn_x)
    lines = exchange(lines, "gy", split_axis=0, concat_axis=1)
    lines = product("uyk,yv->uvk", lines, turn_y)
    wide, _, depth = lines.shape
    start_x = lax.axis_index("gy") * wide
    start_z = lax.axis_index("gx") * depth
    volume = GRID_X * GRID_Y * GRID_Z * spacing**3
    fx = green_factors(start_x + jnp.arange(wide, dtype=jnp.int32), GRID_X)
    fy = green_factors(jnp.arange(GRID_Y, dtype=jnp.int32), GRID_Y)
    fz = green_factors(start_z + jnp.arange(depth, dtype=jnp.int32), GRID_Z)
    square = fx[0][:, None, None] + fy[0][:, None] + fz[0]
    scale = fx[1][:, None, None] * fy[1][:, None] * fz[1] / (math.pi * volume)
    lines = lines * jnp.where(square > 0.0, scale / jnp.where(square > 0.0, square, 1.0), 0.0)
    lines = product("uvk,vy->uyk", lines, turn_y)
    lines = exchange(lines, "gy", split_axis=1, concat_axis=0)
    lines = product("uyk,ux->xyk", lines, turn_x)
    return exchange(lines, "gx", split_axis=0, concat_axis=2)


def far_by_lines(atoms, base, count_x, count_y, cells_x, cells_y, cells_z):
    atom_total = atoms.shape[1]
    cells = (cells_x, cells_y, cells_z)
    pad = (round_up(cells_x + 3, rows_group), round_up(cells_y + 3, 8))
    pad_x, pad_y = pad
    turn_z = jnp.asarray(hartley(GRID_Z))
    spread = pl.pallas_call(
        functools.partial(spread_kernel, cells, pad),
        out_shape=jax.ShapeDtypeStruct((pad_x, pad_y, GRID_Z), jnp.float32),
        scratch_shapes=[
            pltpu.VMEM((pad_x, atom_total), jnp.float32),
            pltpu.VMEM((pad_y, atom_total), jnp.float32),
            pltpu.VMEM((atom_total, 2 * GRID_Z), jnp.bfloat16),
            pltpu.VMEM((rows_group * pad_y, atom_total), jnp.bfloat16),
            pltpu.VMEM((rows_group * pad_y, atom_total), jnp.bfloat16),
        ],
        name="spread",
    )(atoms, base, turn_z)

    from_x = moved(spread[cells_x : cells_x + 3, :cells_y], 1, 0)
    from_y = moved(spread[:cells_x, cells_y : cells_y + 3], 0, 1)
    from_both = moved(spread[cells_x : cells_x + 3, cells_y : cells_y + 3], 1, 1)
    charge_mesh = (
        spread[:cells_x, :cells_y]
        .at[:3]
        .add(from_x)
        .at[:, :3]
        .add(from_y)
        .at[:3, :3]
        .add(from_both)
    )
    potential = convolved_by_lines(charge_mesh, count_x, count_y)
    upper_x = moved(potential[:3], -1, 0)
    upper_y = moved(potential[:, :3], 0, -1)
    upper_both = moved(potential[:3, :3], -1, -1)
    wider = jnp.concatenate(
        [
            jnp.concatenate([potential, upper_x], axis=0),
            jnp.concatenate([upper_y, upper_both], axis=0),
        ],
        axis=1,
    )
    wider = jnp.pad(wider, ((0, pad_x - cells_x - 3), (0, pad_y - cells_y - 3), (0, 0)))
    return pl.pallas_call(
        functools.partial(gather_kernel, cells, pad),
        out_shape=jax.ShapeDtypeStruct((3, atom_total), jnp.float32),
        scratch_shapes=[
            pltpu.VMEM((pad_x, atom_total), jnp.float32),
            pltpu.VMEM((pad_x, atom_total), jnp.float32),
            pltpu.VMEM((pad_y, atom_total), jnp.float32),
            pltpu.VMEM((pad_y, atom_total), jnp.float32),
            pltpu.VMEM((2 * GRID_Z, 2 * atom_total), jnp.bfloat16),
            pltpu.VMEM((rows_group * pad_y, 2 * atom_total), jnp.float32),
        ],
        name="gather",
    )(atoms, base, turn_z, wider)


def local(positions, charges, pair_lists, slab_dest, atom_counts):
    count_x = lax.axis_size("gx")
    count_y = lax.axis_size("gy")
    devices = count_x * count_y
    atom_total = positions.shape[3]
    clusters = pair_lists.shape[2]
    cluster_size = atom_total // clusters
    blocks = slab_dest.shape[2]
    block_size = atom_total // blocks
    cells_x = GRID_X // count_x
    cells_y = GRID_Y // count_y
    cells_z = GRID_Z // count_y
    by_planes = (
        GRID_Z == 8 * devices
        and GRID_Z == lanes
        and cells_y == 64
        and cells_x % 8 == 0
        and cells_x <= 64
        and count_y % 2 == 0
        and atom_total == 8 * lanes
        and cluster_size % lanes == 0
    )
    if by_planes:
        sizes = (count_x, count_y, cells_x, cells_y)
        raw, atoms, bounds, rank, columns, before = shared(
            positions, charges, atom_counts, clusters, *sizes
        )
        partial = far_by_planes(bounds, atoms, *sizes)
        short_sums, long_sums = finished(
            pair_lists, partial, raw, rank, columns, before, *sizes
        )
        living = jnp.arange(atom_total, dtype=jnp.int32) < atom_counts[0, 0]
        charge = jnp.where(living, charges[0, 0], 0.0)
        return (short_sums * (charge * spacing), long_sums * (charge * (-1.0 / spacing)))
    living = jnp.arange(atom_total, dtype=jnp.int32) < atom_counts[0, 0]
    charge = jnp.where(living, charges[0, 0], 0.0)
    packed = jnp.concatenate([positions, charge[None, None, None, :]], axis=0)
    atoms = packed.reshape(4, atom_total)
    base = jnp.broadcast_to(
        (slab_dest[0, 0] * cells_z)[:, None], (blocks, block_size)
    ).reshape(1, atom_total)
    gathered = lax.all_gather(atoms, ("gx", "gy"), axis=0, tiled=False)
    far_part = far_by_lines(atoms, base, count_x, count_y, cells_x, cells_y, cells_z)

    chosen = pair_lists[0, 0]
    beside = chosen // clusters
    step_x, step_y = (beside // 3 - 1, beside % 3 - 1)
    at_x = (lax.axis_index("gx") + step_x + count_x) % count_x
    at_y = (lax.axis_index("gy") + step_y + count_y) % count_y
    number = (at_x * count_y + at_y) * clusters + chosen % clusters
    pick = (number[:, :, None] == jnp.arange(devices * clusters, dtype=jnp.int32)).astype(
        jnp.float32
    )
    pool = gathered[:, :4].reshape(devices, 4, clusters, cluster_size)
    pool = jnp.transpose(pool, (1, 0, 2, 3)).reshape(4, devices * clusters, cluster_size)
    partners = jnp.einsum(
        "cln,fnk->cflk",
        pick,
        pool,
        precision=lax.Precision.HIGHEST,
        preferred_element_type=jnp.float32,
    )
    shift_x = (step_x * cells_x).astype(jnp.float32)
    shift_y = (step_y * cells_y).astype(jnp.float32)
    flat = jnp.zeros_like(shift_x)
    shift = jnp.stack([shift_x, shift_y, flat, flat], axis=1)
    partners = (partners + shift[:, :, :, None]).reshape(clusters, 4, -1)
    own = packed.reshape(4, clusters, cluster_size)
    pair_part = jnp.stack(
        [one_cluster(own[:, c], partners[c]) for c in range(clusters)], axis=1
    )
    short_forces = pair_part.reshape(3, 1, 1, atom_total)
    return (short_forces, far_part.reshape(3, 1, 1, atom_total))


def solution(mesh):
    return jax.shard_map(
        local,
        mesh=mesh,
        in_specs=(
            P(None, ("rep", "gx"), "gy", None),
            P(("rep", "gx"), "gy", None),
            P(("rep", "gx"), "gy", None, None),
            P(("rep", "gx"), "gy", None),
            P(("rep", "gx"), "gy"),
        ),
        out_specs=(P(None, ("rep", "gx"), "gy", None), P(None, ("rep", "gx"), "gy", None)),
        check_vma=False,
    )
```

```python
import functools
import math

import jax
import jax.numpy as jnp
import numpy as np
from jax import lax
from jax.experimental import pallas as pl
from jax.experimental.pallas import tpu as pltpu
from jax.sharding import PartitionSpec as P

GRID_X = 256
GRID_Y = 256
GRID_Z = 128


spacing = 0.16
ewald_split = 3.47
cutoff = 0.9
soft_core = 0.09
root_factor = 1.1283791670955126
rows_group = 8
lanes = 128
window_rows = 24
group_size = 12
gather_size = 8
cell_group = 4
plane_group = 8
fixed_arrays = 8


def moved(value, step_x, step_y):
    count_x = lax.axis_size("gx")
    count_y = lax.axis_size("gy")
    pairs = [
        (i * count_y + j, (i + step_x) % count_x * count_y + (j + step_y) % count_y)
        for i in range(count_x)
        for j in range(count_y)
    ]
    return lax.ppermute(value, ("gx", "gy"), pairs)


def round_up(value, multiple):
    return -(-value // multiple) * multiple


def hartley(period):
    turns = np.outer(np.arange(period), np.arange(period)) % period
    phases = turns * (2.0 * np.pi / period)
    return (np.cos(phases) + np.sin(phases)).astype(np.float32)


def halves(value):
    high = value.astype(jnp.bfloat16)
    low = (value - high.astype(jnp.float32)).astype(jnp.bfloat16)
    return (high, low)


def dot(left_side, right_side):
    return jnp.dot(left_side, right_side, preferred_element_type=jnp.float32)


def spline_weights(fraction):
    remain = 1.0 - fraction
    square = fraction * fraction
    cube_part = square * fraction
    values = [
        remain * remain * remain / 6.0,
        (3.0 * cube_part - 6.0 * square + 4.0) / 6.0,
        (-3.0 * cube_part + 3.0 * square + 3.0 * fraction + 1.0) / 6.0,
        cube_part / 6.0,
    ]
    slopes = [
        -0.5 * remain * remain,
        0.5 * (3.0 * square - 4.0 * fraction),
        0.5 * (-3.0 * square + 2.0 * fraction + 1.0),
        0.5 * square,
    ]
    return (values, slopes)


def split_cells(coordinate, offset, cell_count):
    inside = coordinate - offset
    lowest = jnp.clip(jnp.floor(inside).astype(jnp.int32), 0, cell_count - 1)
    return (lowest, inside - lowest.astype(inside.dtype))


def spline_table(lowest, values, table_size, period=None):
    points = lax.broadcasted_iota(jnp.int32, (table_size, lowest.shape[1]), 0)
    lookup = jnp.zeros(points.shape, jnp.float32)
    for spline_term in range(4):
        at = lowest + spline_term
        if period is not None:
            at = jnp.where(at >= period, at - period, at)
        lookup = jnp.where(points == at, values[spline_term], lookup)
    return lookup


def spread_kernel(cells, pad, atoms_ref, base_ref, turn_ref, out_ref, wx_ref, wy_ref, wz_ref, hi_ref, lo_ref):
    cells_x, cells_y, cells_z = cells
    pad_x, pad_y = pad
    atom_total = atoms_ref.shape[1]
    low_x, frac_x = split_cells(atoms_ref[0:1, :], 0.0, cells_x)
    low_y, frac_y = split_cells(atoms_ref[1:2, :], 0.0, cells_y)
    base = base_ref[...]
    low_z, frac_z = split_cells(atoms_ref[2:3, :], base.astype(jnp.float32), cells_z)
    wx_ref[...] = spline_table(low_x, spline_weights(frac_x)[0], pad_x) * atoms_ref[3:4, :]
    wy_ref[...] = spline_table(low_y, spline_weights(frac_y)[0], pad_y)
    turn = turn_ref[...]
    size_z = turn.shape[0]
    table_z = spline_table(base + low_z, spline_weights(frac_z)[0], size_z, size_z)
    waves = jnp.dot(
        turn, table_z, precision=lax.Precision.HIGHEST, preferred_element_type=jnp.float32
    ).T
    high, low = halves(waves)
    wz_ref[:, :size_z] = high
    wz_ref[:, size_z:] = low

    @pl.loop(0, pad_x // rows_group)
    def _(chunk):
        for inner in range(rows_group):
            row = wx_ref[pl.ds(chunk * rows_group + inner, 1), :]
            high, low = halves(row * wy_ref[...])
            hi_ref[pl.ds(inner * pad_y, pad_y), :] = high
            lo_ref[pl.ds(inner * pad_y, pad_y), :] = low
        both = dot(hi_ref[...], wz_ref[...])
        rest = dot(lo_ref[...], wz_ref[:, :size_z])
        total = both[:, :size_z] + both[:, size_z:] + rest
        out_ref[pl.ds(chunk * rows_group, rows_group)] = total.reshape(rows_group, pad_y, size_z)


def gather_kernel(cells, pad, atoms_ref, base_ref, turn_ref, mesh_ref, out_ref, wx_ref, vx_ref, wy_ref, vy_ref, wz_ref, level_ref):
    cells_x, cells_y, cells_z = cells
    pad_x, pad_y = pad
    atom_total = atoms_ref.shape[1]
    low_x, frac_x = split_cells(atoms_ref[0:1, :], 0.0, cells_x)
    low_y, frac_y = split_cells(atoms_ref[1:2, :], 0.0, cells_y)
    base = base_ref[...]
    low_z, frac_z = split_cells(atoms_ref[2:3, :], base.astype(jnp.float32), cells_z)
    values, slopes = spline_weights(frac_x)
    wx_ref[...] = spline_table(low_x, values, pad_x)
    vx_ref[...] = spline_table(low_x, slopes, pad_x)
    values, slopes = spline_weights(frac_y)
    wy_ref[...] = spline_table(low_y, values, pad_y)
    vy_ref[...] = spline_table(low_y, slopes, pad_y)
    values, slopes = spline_weights(frac_z)
    turn = turn_ref[...]
    size_z = turn.shape[0]
    for place, terms in enumerate((values, slopes)):
        table_z = spline_table(base + low_z, terms, size_z, size_z)
        waves = jnp.dot(
            turn, table_z, precision=lax.Precision.HIGHEST, preferred_element_type=jnp.float32
        )
        high, low = halves(waves)
        wz_ref[:size_z, pl.ds(place * atom_total, atom_total)] = high
        wz_ref[size_z:, pl.ds(place * atom_total, atom_total)] = low
    groups = pad_y // 8

    def one_chunk(chunk, sums):
        rows = mesh_ref[pl.ds(chunk * rows_group, rows_group)].reshape(rows_group * pad_y, size_z)
        high, low = halves(rows)
        level_ref[...] = dot(jnp.concatenate([high, high], axis=1), wz_ref[...]) + dot(
            low, wz_ref[:size_z, :]
        )
        first, second, third = sums
        for inner in range(rows_group):
            flat = level_ref[pl.ds(inner * pad_y, pad_y), :atom_total]
            tilt = level_ref[pl.ds(inner * pad_y, pad_y), atom_total:]
            across = wy_ref[...]
            part_x = jnp.sum((across * flat).reshape(groups, 8, atom_total), axis=0)
            part_y = jnp.sum((vy_ref[...] * flat).reshape(groups, 8, atom_total), axis=0)
            part_z = jnp.sum((across * tilt).reshape(groups, 8, atom_total), axis=0)
            weight = wx_ref[pl.ds(chunk * rows_group + inner, 1), :]
            slope = vx_ref[pl.ds(chunk * rows_group + inner, 1), :]
            first = first + slope * part_x
            second = second + weight * part_y
            third = third + weight * part_z
        return (first, second, third)

    zero = jnp.zeros((8, atom_total), jnp.float32)
    sums = lax.fori_loop(0, pad_x // rows_group, one_chunk, (zero, zero, zero))
    factor = -atoms_ref[3:4, :] / spacing
    for place in range(3):
        out_ref[pl.ds(place, 1), :] = factor * jnp.sum(sums[place], axis=0, keepdims=True)


def peers_of(count_x, count_y):
    place_x, place_y = (lax.axis_index("gx"), lax.axis_index("gy"))
    peers = []
    for order in range(1, count_x * count_y):
        peer_x = lax.rem(place_x + order // count_y, count_x)
        peer_y = lax.rem(place_y + order % count_y, count_y)
        peers.append((peer_x, peer_y))
    return peers


root_terms = (
    3.9164407301418542,
    -0.0037127819564810594,
    0.16802528315459195,
    -0.003061234121505335,
    -0.0076524954798020545,
    0.002268454833542123,
    -0.0003056487922112269,
    1.686888935413571e-05,
)


def pair_weight(square):
    soft_square = square * (spacing * spacing) + soft_core
    inverse = lax.rsqrt(soft_square)
    series = jnp.full_like(inverse, root_terms[-1])
    for term in root_terms[-2::-1]:
        series = series * inverse + term
    decay = jnp.exp(soft_square * (-ewald_split * ewald_split))
    taper = jnp.maximum(1.0 - square * (spacing * spacing / (cutoff * cutoff)), 0.0)
    return (decay * series) * (inverse * taper) ** 2


def row_sums(values):
    total = None
    ones = jnp.ones((16, values.shape[1]), jnp.bfloat16)
    for _ in range(3):
        part = values.astype(jnp.bfloat16)
        values = values - part.astype(jnp.float32)
        summed = lax.dot_general(
            ones, part, (((1,), (1,)), ((), ())), preferred_element_type=jnp.float32
        )
        total = summed if total is None else total + summed
    return total[0:1, :]


def place_partners(sizes, cells, pairs_ref, atoms_ref, partner_ref):
    count_x, count_y = sizes
    cells_x, cells_y = cells
    place_x, place_y = (lax.axis_index("gx"), lax.axis_index("gy"))
    clusters, listed = pairs_ref.shape[2:]
    size = atoms_ref.shape[2] // clusters
    for c in range(clusters):
        for n in range(1, listed):
            chosen = pairs_ref[0, 0, c, n]
            beside = lax.div(chosen, clusters)
            which = chosen - beside * clusters
            row_x = lax.div(beside, 3)
            step_x = row_x - 1
            step_y = beside - row_x * 3 - 1
            from_x = lax.rem(place_x + step_x + count_x, count_x)
            from_y = lax.rem(place_y + step_y + count_y, count_y)
            block = atoms_ref[from_x * count_y + from_y]
            part = block[:, :size]
            for k in range(1, clusters):
                part = jnp.where(which == k, block[:, k * size : (k + 1) * size], part)
            shifts = (
                (step_x * cells_x).astype(jnp.float32),
                (step_y * cells_y).astype(jnp.float32),
            )
            for axis in range(4):
                row = part[axis : axis + 1, :]
                if axis < 2:
                    row = row + shifts[axis]
                partner_ref[c, axis, :, (n - 1) * size : n * size] = jnp.broadcast_to(
                    row, (8, size)
                )


def pair_sums(clusters, size, height, column_ref, partner_ref, before_ref, sum_ref):
    @pl.loop(0, clusters)
    def _(c):
        @pl.loop(0, size // height)
        def _(step):
            for part in range(height // 8):
                start = c * size + step * height + part * 8
                rows = pl.ds(pl.multiple_of(start, 8), 8)
                own = [column_ref[axis, rows, :] for axis in range(3)]
                sums = [
                    jnp.zeros((8, lanes), jnp.float32)
                    if before_ref is None
                    else before_ref[axis, rows, :]
                    for axis in range(3)
                ]
                for tile in range(partner_ref.shape[3] // lanes):
                    span = slice(tile * lanes, (tile + 1) * lanes)
                    offsets = [own[axis] - partner_ref[c, axis, :, span] for axis in range(3)]
                    square = sum(offset * offset for offset in offsets)
                    weight = pair_weight(square) * partner_ref[c, 3, :, span]
                    sums = [total + weight * offset for total, offset in zip(sums, offsets)]
                for axis in range(3):
                    sum_ref[axis, rows, :] = sums[axis]


def share_kernel(sizes, cells, clusters, count_ref, position_ref, charge_ref, raw_ref, sorted_ref, bounds_ref, rank_ref, column_ref, sum_ref, key_ref, split_ref, partner_ref, raw_send, raw_recv, sort_send, sort_recv, mark_send, mark_recv):
    count_x, count_y = sizes
    cells_x, _ = cells
    place_x, place_y = (lax.axis_index("gx"), lax.axis_index("gy"))
    me = place_x * count_y + place_y
    place_chip, place_core = (place_y // 2, lax.rem(place_y, 2))
    chips = count_y // 2

    def at(step_x, step_chip, flip):
        peer_x = lax.rem(place_x + step_x, count_x)
        peer_chip = lax.rem(place_chip + step_chip, chips)
        peer_core = 1 - place_core if flip else place_core
        return (peer_x, peer_chip * 2 + peer_core)

    peers = peers_of(count_x, count_y)
    barrier = pltpu.get_barrier_semaphore()
    for peer_x, peer_y in peers:
        pl.semaphore_signal(
            barrier,
            inc=1,
            device_id={"gx": peer_x, "gy": peer_y},
            device_id_type=pl.DeviceIdType.MESH,
        )

    def sent(ref, owner, peer, send_sem, recv_sem, order, slot):
        return pltpu.make_async_remote_copy(
            src_ref=ref.at[owner],
            dst_ref=ref.at[owner],
            send_sem=send_sem.at[order],
            recv_sem=recv_sem.at[slot],
            device_id={"gx": peer[0], "gy": peer[1]},
            device_id_type=pl.DeviceIdType.MESH,
        )

    passed = []

    def passes(owner, peer):
        order = len(passed)
        copies = [
            sent(sorted_ref, owner, peer, sort_send, sort_recv, order, owner),
            sent(bounds_ref, owner, peer, mark_send, mark_recv, order, owner),
        ]
        for copy in copies:
            copy.start()
        passed.append(copies)

    def arrives(owner, peer):
        sent(sorted_ref, owner, peer, sort_send, sort_recv, 0, owner).wait_recv()
        sent(bounds_ref, owner, peer, mark_send, mark_recv, 0, owner).wait_recv()

    atom_total = charge_ref.shape[2]
    tiles = atom_total // lanes
    slot = lax.broadcasted_iota(jnp.int32, (1, atom_total), 1)
    living = slot < count_ref[0, 0]
    charge = jnp.where(living, charge_ref[0], 0.0)
    rows = [position_ref[axis, 0] for axis in range(3)] + [charge]
    for axis in range(4):
        raw_ref[me, pl.ds(axis, 1), :] = rows[axis]
    column = jnp.clip(jnp.floor(rows[0]), 0.0, cells_x - 1.0)
    key = jnp.where(living, column, float(cells_x)) * float(atom_total) + slot.astype(jnp.float32)
    for tile in range(tiles):
        span = slice(tile * lanes, (tile + 1) * lanes)
        key_ref[span, :] = jnp.broadcast_to(key[:, span], (lanes, lanes)).T
    wide = [
        jnp.broadcast_to(key[:, tile * lanes : (tile + 1) * lanes], (8, lanes))
        for tile in range(tiles)
    ]

    def count_group(group, totals):
        for inner in range(8):
            others = key_ref[pl.ds(pl.multiple_of(group * 64 + inner * 8, 8), 8), :]
            totals = tuple(
                total + jnp.where(others < own, 1.0, 0.0) for total, own in zip(totals, wide)
            )
        return totals

    zero = jnp.zeros((8, lanes), jnp.float32)
    totals = lax.fori_loop(0, atom_total // 64, count_group, (zero,) * tiles)
    for tile, total in enumerate(totals):
        rank_ref[:, tile * lanes : (tile + 1) * lanes] = jnp.sum(total, axis=0, keepdims=True)

    split_ref[...] = jnp.zeros_like(split_ref)
    rest = raw_ref[me]
    for part in range(3):
        piece = rest.astype(jnp.bfloat16).astype(jnp.float32)
        split_ref[4 * part : 4 * part + 4, :] = piece
        rest = rest - piece
    split = split_ref[...].astype(jnp.bfloat16)
    rank = rank_ref[...]
    block = 2 * lanes
    for part in range(atom_total // block):
        place = lax.broadcasted_iota(jnp.int32, (block, atom_total), 0) + part * block
        chosen = jnp.where(place.astype(jnp.float32) == rank, 1.0, 0.0).astype(jnp.bfloat16)
        found = lax.dot_general(
            split, chosen, (((1,), (1,)), ((), ())), preferred_element_type=jnp.float32
        )
        found = (found[0:4] + found[4:8]) + found[8:12]
        for tile in range(block // lanes):
            row = part * (block // lanes) + tile
            for axis in range(4):
                sorted_ref[me, axis, row : row + 1, :] = found[
                    axis : axis + 1, tile * lanes : (tile + 1) * lanes
                ]
    spot = lax.broadcasted_iota(jnp.int32, (tiles, lanes), 0) * lanes
    spot = spot + lax.broadcasted_iota(jnp.int32, (tiles, lanes), 1)
    inside = spot < count_ref[0, 0]
    column = jnp.clip(jnp.floor(sorted_ref[me, 0]), 0.0, cells_x - 1.0)
    lowest = jnp.min(jnp.where(inside, column, float(cells_x)), axis=1, keepdims=True)
    highest = jnp.max(jnp.where(inside, column, -1.0), axis=1, keepdims=True)
    first = jnp.floor(lowest * 0.125)
    last = jnp.floor((highest + 3.0) * 0.125)
    windows = jnp.where(
        highest >= 0.0, jnp.floor((last - first) * (8.0 / window_rows) + 0.01) + 1.0, 0.0
    )
    lane = lax.broadcasted_iota(jnp.int32, (tiles, lanes), 1)
    row = lax.broadcasted_iota(jnp.int32, (tiles, lanes), 0)
    marks = jnp.where(lane == row, first, jnp.where(lane == row + tiles, windows, 0.0))
    marks = jnp.sum(marks, axis=0, keepdims=True)
    bounds_ref[me] = marks.astype(jnp.int32)

    near = sorted(
        (min(step, count_x - step) + min(chip, chips - chip), step, chip)
        for step in range(count_x)
        for chip in range(chips)
    )[1:]
    mate = at(0, 0, True)
    pl.semaphore_wait(barrier, len(peers))
    for _, step, chip in reversed(near):
        passes(me, at(step, chip, False))
    passes(me, mate)
    beside = sorted(
        {
            step_x % count_x * count_y + step_y % count_y
            for step_x in (-1, 0, 1)
            for step_y in (-1, 0, 1)
        }
        - {0}
    )
    copies = [
        sent(raw_ref, me, peers[order - 1], raw_send, raw_recv, order - 1, order - 1)
        for order in beside
    ]
    for copy in copies:
        copy.start()

    for axis in range(3):
        for tile in range(tiles):
            span = slice(tile * lanes, (tile + 1) * lanes)
            column_ref[axis, span, :] = jnp.broadcast_to(rows[axis][:, span], (lanes, lanes)).T
    size = atom_total // clusters
    for c in range(clusters):
        for axis in range(4):
            row = rows[axis][:, c * size : (c + 1) * size]
            partner_ref[c, axis] = jnp.broadcast_to(row, (8, size))
    pair_sums(clusters, size, 64, column_ref, partner_ref, None, sum_ref)
    for _, step, chip in near:
        owner_x, owner_y = at(step, chip, False)
        arrives(owner_x * count_y + owner_y, (owner_x, owner_y))
        passes(owner_x * count_y + owner_y, mate)
    for _, step, chip in [(0, 0, 0), *near]:
        owner_x, owner_y = at(step, chip, True)
        arrives(owner_x * count_y + owner_y, mate)
    for copy in copies:
        copy.wait()
    for pair in passed:
        for copy in pair:
            copy.wait_send()


def shared(positions, charges, atom_counts, clusters, count_x, count_y, cells_x, cells_y):
    devices = count_x * count_y
    atom_total = charges.shape[2]
    vmem = pl.BlockSpec(memory_space=pltpu.VMEM)
    smem = pl.BlockSpec(memory_space=pltpu.SMEM)
    fewer = pltpu.SemaphoreType.DMA((devices - 1,))
    flags = pltpu.SemaphoreType.DMA((devices,))
    return pl.pallas_call(
        functools.partial(share_kernel, (count_x, count_y), (cells_x, cells_y), clusters),
        in_specs=[smem, vmem, vmem],
        out_specs=[vmem] * 6,
        out_shape=[
            jax.ShapeDtypeStruct((devices, 4, atom_total), jnp.float32),
            jax.ShapeDtypeStruct((devices, 4, atom_total // lanes, lanes), jnp.float32),
            jax.ShapeDtypeStruct((devices, 1, lanes), jnp.int32),
            jax.ShapeDtypeStruct((1, atom_total), jnp.float32),
            jax.ShapeDtypeStruct((3, atom_total, lanes), jnp.float32),
            jax.ShapeDtypeStruct((3, atom_total, lanes), jnp.float32),
        ],
        scratch_shapes=[
            pltpu.VMEM((atom_total, lanes), jnp.float32),
            pltpu.VMEM((16, atom_total), jnp.float32),
            pltpu.VMEM((clusters, 4, 8, atom_total // clusters), jnp.float32),
            fewer,
            fewer,
        ]
        + [flags] * 4,
        compiler_params=pltpu.CompilerParams(
            collective_id=0, has_side_effects=True, vmem_limit_bytes=12 << 20
        ),
        name="share",
    )(
        atom_counts,
        *[pltpu.with_memory_space_constraint(value, pltpu.HBM) for value in (positions, charges)],
    )


def depth_rows(table, circle, height, terms):
    turns = height * table[:, 0:1]
    turns = turns - GRID_Z * jnp.floor(turns * (1.0 / GRID_Z))
    index = turns.astype(jnp.int32)
    cosine, sine = [jnp.take_along_axis(part, index, axis=1) for part in circle]
    results = []
    for weights in terms:
        even = sum(table[:, 1 + t : 2 + t] * weights[t] for t in range(4))
        odd = sum(table[:, 5 + t : 6 + t] * weights[t] for t in range(4))
        results.append(cosine * even + sine * odd)
    return results


def mesh_kernel(sizes, cells, pad_y, bounds_ref, atoms_ref, *refs):
    constants, (out_ref, *scratch) = refs[:fixed_arrays], refs[fixed_arrays:]
    held, copy_sem = scratch[-fixed_arrays - 1 : -1], scratch[-1]
    copies = [
        pltpu.make_async_copy(source, target, copy_sem.at[place])
        for place, (source, target) in enumerate(zip(constants, held))
    ]
    for copy in copies:
        copy.start()
    xh_ref, xl_ref, yh_ref, yl_ref, column_ref, row_ref, circle_ref, table_ref = held
    mesh_ref, stack_ref, prep_ref, deep_ref, steep_ref, near_ref, wy_ref, side_ref, level_ref, square_ref, scale_ref, work_ref = scratch[: -fixed_arrays - 1]
    count_x, count_y = sizes
    cells_x, cells_y = cells
    devices = count_x * count_y
    place = lax.axis_index("gx") * count_y + lax.axis_index("gy")
    tiles = atoms_ref.shape[2]
    depth = stack_ref.shape[0]
    window = 2 * cells_y
    windows = GRID_Y // window
    extra = 8
    share = -(-group_size * cell_group // devices)
    stack_ref[:, GRID_X:, :] = jnp.zeros_like(stack_ref[:, GRID_X:, :])
    out_ref[...] = jnp.zeros_like(out_ref)

    steps_x = window_rows // 8
    most = (cells_x + 2) // 8 // steps_x + 1

    def prep_row(kind, spot):
        return prep_ref[pl.ds(kind * devices * tiles + spot, 8, stride=0), :]

    def listed_work(cell, total):
        for tile in range(tiles):
            for step in range(most):
                work_ref[total + step] = (cell * tiles + tile) * most + step
            total = total + bounds_ref[cell, 0, tiles + tile]

        return total

    def keep_splines(cell):
        def keep(kind, value):
            rows = pl.ds(pl.multiple_of((kind * devices + cell) * tiles, 8), tiles)
            prep_ref[rows, :] = value

        for axis, count in enumerate((cells_x, cells_y)):
            value = atoms_ref[cell, axis]
            lowest = jnp.clip(jnp.floor(value), 0.0, count - 1.0)
            values, slopes = spline_weights(value - lowest)
            keep(9 * axis, lowest)
            for term in range(4):
                keep(9 * axis + 1 + term, values[term])
                keep(9 * axis + 5 + term, slopes[term])
                if axis == 1:
                    for kind, whole in ((28, values[term]), (32, slopes[term])):
                        keep(kind + term, whole - whole.astype(jnp.bfloat16).astype(jnp.float32))
        value = atoms_ref[cell, 2]
        height = jnp.floor(value)
        values, slopes = spline_weights(value - height)
        keep(18, height)
        for term in range(4):
            keep(19 + term, values[term])
            keep(23 + term, slopes[term])
        keep(27, atoms_ref[cell, 3])

    def keep_modes(cell):
        for tile in range(tiles):
            spot = cell * tiles + tile
            height = prep_row(18, spot)
            terms = [[prep_row(19 + 4 * s + term, spot) for term in range(4)] for s in range(2)]
            deep, steep = depth_rows(table, circle, height, terms)
            rows = pl.ds(pl.multiple_of(spot * depth, 8), depth)
            deep_ref[rows, :] = deep
            steep_ref[rows, :] = steep

    def prepare_some(turn, total):
        for inner in range(cell_group):
            cell = turn * cell_group + inner
            mesh_ref[lax.div(cell, depth), lax.rem(cell, depth)] = jnp.zeros(
                mesh_ref.shape[2:], jnp.float32
            )
            total = listed_work(cell, total)
        for inner in range(cell_group):
            keep_splines(turn * cell_group + inner)
        for inner in range(share):
            place = jnp.minimum(turn * share + inner, group_size - 1)
            wy_ref[place] = jnp.zeros(wy_ref.shape[1:], wy_ref.dtype)
        return total

    total = lax.fori_loop(0, devices // cell_group, prepare_some, jnp.int32(0))
    copies[-2].wait()
    copies[-1].wait()
    circle = [circle_ref[:8, :], circle_ref[8:, :]]
    table = table_ref[pl.ds(pl.multiple_of(place * depth, 8), depth), :]

    @pl.loop(0, devices // cell_group)
    def _(turn):
        for inner in range(cell_group):
            keep_modes(turn * cell_group + inner)

    rounds = lax.div(total + group_size - 1, group_size)

    row_index = lax.broadcasted_iota(jnp.int32, (8, lanes), 0).astype(jnp.float32)

    def looked_up(points, lowest, term_lists):
        results = [jnp.zeros_like(points) for _ in term_lists]
        for term in range(4):
            hit = points == lowest + float(term)
            results = [
                jnp.where(hit, terms[term], result)
                for terms, result in zip(term_lists, results)
            ]
        return results

    def kinds(first, spot):
        return [prep_row(first + term, spot) for term in range(4)]

    stride = round_up(pad_y, 16)
    far_away = 1.0e6

    def task(index):
        entry = jnp.where(index < total, work_ref[index], 0)
        spot = lax.div(entry, most)
        cell = lax.div(spot, tiles)
        chunk = spot - cell * tiles
        begin = bounds_ref[cell, 0, chunk] * 8 + (entry - spot * most) * window_rows
        base = jnp.where(index < total, begin.astype(jnp.float32), far_away)
        i = lax.div(cell, count_y)
        rows = pl.ds(pl.multiple_of(i * cells_x + begin, 8), window_rows)
        return (spot, cell, chunk, cell - i * count_y, rows, base)

    packed_index = jnp.concatenate([row_index, row_index + 8.0], axis=0).astype(jnp.bfloat16)

    def packed_row(kind, spot):
        row = prep_row(kind, spot)
        return jnp.concatenate([row, row], axis=0).astype(jnp.bfloat16)

    def y_table(spot, kind, low_kind):
        lowest = packed_row(9, spot)
        highs = [packed_row(kind + term, spot) for term in range(4)]
        lows = [packed_row(low_kind + term, spot) for term in range(4)]
        starts = [lowest + jnp.bfloat16(term) for term in range(4)]
        for group in range(stride // 16):
            points = packed_index + jnp.bfloat16(group * 16)
            high = low = jnp.zeros_like(points)
            for term in range(4):
                hit = points == starts[term]
                high = jnp.where(hit, highs[term], high)
                low = jnp.where(hit, lows[term], low)
            yield (slice(group * 16, group * 16 + 16), high, low)

    @pl.loop(0, rounds)
    def _(turn):
        tasks = [task(turn * group_size + place) for place in range(group_size)]
        for place, (spot, _, _, _, _, base) in enumerate(tasks):
            for rows, high, low in y_table(spot, 10, 28):
                after = slice(window + rows.start, window + rows.stop)
                later = slice(stride + rows.start, stride + rows.stop)
                wy_ref[place, rows, :lanes] = high
                wy_ref[place, rows, lanes:] = high
                wy_ref[place, after, :lanes] = low
                near_ref[spot, rows, :] = high
                near_ref[spot, later, :] = low
            lowest = prep_row(0, spot) - base
            charge = prep_row(27, spot)
            terms = [term * charge for term in kinds(1, spot)]
            weights = [
                looked_up(row_index + float(tile * 8), lowest, [terms])[0]
                for tile in range(steps_x)
            ]
            modes = [
                deep_ref[pl.ds(spot * depth + k, 8, stride=0), :] for k in range(depth)
            ]
            blocks = [weight * mode for mode in modes for weight in weights]
            for pair in range(len(blocks) // 2):
                high, low = halves(jnp.concatenate(blocks[2 * pair : 2 * pair + 2], axis=0))
                rows = slice(pair * 16, pair * 16 + 16)
                side_ref[place, rows, :lanes] = high
                side_ref[place, rows, lanes:] = low
        for place, (_, _, _, j, rows, _) in enumerate(tasks):
            product = lax.dot_general(
                side_ref[place],
                wy_ref[place],
                (((1,), (1,)), ((), ())),
                preferred_element_type=jnp.float32,
            )
            product = product[:, :window] + product[:, window:]
            m = lax.div(j, 2)
            here = pl.ds(pl.multiple_of(m * window, lanes), window)
            mesh_ref[j - 2 * m, :, rows, here] += product.reshape(depth, window_rows, window)

    def across(value):
        high, low = halves(value)
        return dot(xh_ref[...], high) + dot(xl_ref[...], high) + dot(xh_ref[...], low)

    def along(value):
        high, low = halves(value)
        return dot(high, yh_ref[...]) + dot(high, yl_ref[...]) + dot(low, yh_ref[...])

    plane_lane = lax.broadcasted_iota(jnp.int32, (GRID_X, window), 1)
    for copy in copies[:-2]:
        copy.wait()
    shape = (GRID_X, GRID_Y)
    square_ref[...] = jnp.broadcast_to(column_ref[:, 0:1], shape) + row_ref[0:1, :]
    scale_ref[...] = jnp.broadcast_to(column_ref[:, 1:2], shape) * row_ref[1:2, :]

    def charge_of(k):
        charge = mesh_ref[0, k, :GRID_X, :] + pltpu.roll(mesh_ref[1, k, :GRID_X, :], cells_y, 1)
        over = slice(GRID_X, GRID_X + extra)
        beyond = mesh_ref[0, k, over, :] + pltpu.roll(mesh_ref[1, k, over, :], cells_y, 1)
        return jnp.concatenate([charge[:extra] + beyond, charge[extra:]], axis=0)

    def green_of(k):
        mode = pl.ds(place * depth + k, 1)
        square = square_ref[...] + table_ref[mode, 9:10]
        scale = scale_ref[...] * table_ref[mode, 10:11]
        return jnp.where(square > 0.0, scale / square, 0.0)

    def place_plane(k, plane):
        for odd in range(2):
            if odd:
                plane = pltpu.roll(plane, GRID_Y - cells_y, 1)
            for j_half in range(windows):
                j = 2 * j_half + odd
                block = plane[:, j_half * window : (j_half + 1) * window]
                high = block.astype(jnp.bfloat16).astype(jnp.float32)
                low = block - high
                shifted = pltpu.roll(high, stride, 1)
                left = jnp.where(plane_lane < stride, high, shifted)
                right = jnp.where(
                    plane_lane < 2 * stride - window,
                    shifted,
                    pltpu.roll(low, 2 * stride - window, 1),
                )
                for side, value in enumerate((left, right)):
                    span = slice((2 * j + side) * window, (2 * j + side + 1) * window)
                    stack_ref[k, :GRID_X, span] = value
                    stack_ref[k, GRID_X : GRID_X + extra, span] = value[:extra]

    @pl.loop(0, depth // plane_group)
    def _(pair):
        spots = [pair * plane_group + inner for inner in range(plane_group)]
        stages = [
            lambda k, _: across(charge_of(k)),
            lambda k, value: along(value),
            lambda k, value: along(value * green_of(k)),
            lambda k, value: across(value),
            lambda k, value: place_plane(k, value),
        ]
        values = [None] * plane_group
        for wave in range(plane_group + len(stages) - 1):
            for inner in range(plane_group):
                if 0 <= wave - inner < len(stages):
                    values[inner] = stages[wave - inner](spots[inner], values[inner])

    @pl.loop(0, lax.div(total + gather_size - 1, gather_size))
    def _(turn):
        tasks = [task(turn * gather_size + place) for place in range(gather_size)]
        blank = jnp.zeros((2 * window - 3 * stride, lanes), jnp.bfloat16)
        for place, (spot, _, _, j, rows, _) in enumerate(tasks):
            near = near_ref[spot]
            highs, lows = [], []
            for _, high, low in y_table(spot, 14, 32):
                highs.append(high)
                lows.append(low)
            columns = jnp.concatenate(
                [
                    jnp.concatenate([near, near[:stride], blank], axis=0),
                    jnp.concatenate([*highs, *lows, *highs, blank], axis=0),
                ],
                axis=1,
            )
            span = pl.ds(pl.multiple_of(j * 2 * window, lanes), 2 * window)
            block = stack_ref[:, rows, span].reshape(depth * window_rows, 2 * window)
            level_ref[place] = dot(block.astype(jnp.bfloat16), columns)
        for place, (spot, cell, chunk, _, _, base) in enumerate(tasks):
            lowest = prep_row(0, spot) - base
            values = kinds(1, spot)
            slopes = kinds(5, spot)
            modes = [pl.ds(spot * depth + k, 8, stride=0) for k in range(depth)]
            deep = [deep_ref[mode, :] for mode in modes]
            steep = [steep_ref[mode, :] for mode in modes]
            zero = jnp.zeros((8, lanes), jnp.float32)
            sums = [zero, zero, zero]
            for tile in range(steps_x):
                weight, slope = looked_up(row_index + float(tile * 8), lowest, [values, slopes])
                parts = [zero, zero, zero]
                for k in range(depth):
                    at = slice(k * window_rows + tile * 8, k * window_rows + tile * 8 + 8)
                    flat = level_ref[place, at, :lanes]
                    tilt = level_ref[place, at, lanes:]
                    parts = [
                        parts[0] + deep[k] * flat,
                        parts[1] + deep[k] * tilt,
                        parts[2] + steep[k] * flat,
                    ]
                sums = [
                    sums[0] + slope * parts[0],
                    sums[1] + weight * parts[1],
                    sums[2] + weight * parts[2],
                ]
            for axis in range(3):
                out_ref[cell, axis, pl.ds(chunk, 1), :] += jnp.sum(
                    sums[axis], axis=0, keepdims=True
                )


def finish_kernel(sizes, cells, pairs_ref, partial_ref, atoms_ref, rank_ref, column_ref, before_ref, short_ref, long_ref, land_ref, partner_ref, sum_ref, order_ref, force_ref, send_sem, recv_sem):
    count_x, count_y = sizes
    place_x, place_y = (lax.axis_index("gx"), lax.axis_index("gy"))
    me = place_x * count_y + place_y
    peers = peers_of(count_x, count_y)
    barrier = pltpu.get_barrier_semaphore()
    for peer_x, peer_y in peers:
        pl.semaphore_signal(
            barrier,
            inc=1,
            device_id={"gx": peer_x, "gy": peer_y},
            device_id_type=pl.DeviceIdType.MESH,
        )
    clusters = pairs_ref.shape[2]
    atom_total = atoms_ref.shape[2]
    size = atom_total // clusters
    place_partners(sizes, cells, pairs_ref, atoms_ref, partner_ref)
    pl.semaphore_wait(barrier, len(peers))
    copies = []
    for order, (peer_x, peer_y) in enumerate(peers):
        copy = pltpu.make_async_remote_copy(
            src_ref=partial_ref.at[peer_x * count_y + peer_y],
            dst_ref=land_ref.at[order],
            send_sem=send_sem.at[order],
            recv_sem=recv_sem.at[order],
            device_id={"gx": peer_x, "gy": peer_y},
            device_id_type=pl.DeviceIdType.MESH,
        )
        copy.start()
        copies.append(copy)
    pair_sums(clusters, size, 32, column_ref, partner_ref, before_ref, sum_ref)
    for axis in range(3):
        for c in range(clusters):
            span = slice(c * size, (c + 1) * size)
            summed = row_sums(sum_ref[axis, span, :])
            short_ref[axis, 0, :, span] = summed
    rank = rank_ref[...]

    @pl.loop(0, atom_total // size)
    def _(block):
        place = lax.broadcasted_iota(jnp.int32, (size, atom_total), 0) + block * size
        order_ref[pl.ds(pl.multiple_of(block * size, size), size), :] = jnp.where(
            place.astype(jnp.float32) == rank, 1.0, 0.0
        ).astype(jnp.bfloat16)

    force_ref[...] = jnp.zeros_like(force_ref)
    for copy in copies:
        copy.wait()
    total = partial_ref[me]
    for order in range(len(peers)):
        total = total + land_ref[order]
    for part in range(3):
        piece = total.astype(jnp.bfloat16).astype(jnp.float32)
        total = total - piece
        for axis in range(3):
            for tile in range(atom_total // lanes):
                span = slice(tile * lanes, (tile + 1) * lanes)
                row = 4 * part + axis
                force_ref[row : row + 1, span] = piece[axis, tile : tile + 1, :]
    placed = dot(force_ref[...].astype(jnp.bfloat16), order_ref[...])
    placed = (placed[0:4] + placed[4:8]) + placed[8:12]
    for axis in range(3):
        long_ref[axis, 0, :, :] = placed[axis : axis + 1, :]


def finished(pair_lists, partial, raw, rank, columns, before, count_x, count_y, cells_x, cells_y):
    devices, _, atom_total = raw.shape
    clusters, listed = pair_lists.shape[2:]
    size = atom_total // clusters
    vmem = pl.BlockSpec(memory_space=pltpu.VMEM)
    flags = pltpu.SemaphoreType.DMA((devices - 1,))
    return pl.pallas_call(
        functools.partial(finish_kernel, (count_x, count_y), (cells_x, cells_y)),
        in_specs=[pl.BlockSpec(memory_space=pltpu.SMEM)] + [vmem] * 5,
        out_specs=[vmem, vmem],
        out_shape=[jax.ShapeDtypeStruct((3, 1, 1, atom_total), jnp.float32)] * 2,
        scratch_shapes=[
            pltpu.VMEM((devices - 1, *partial.shape[1:]), jnp.float32),
            pltpu.VMEM((clusters, 4, 8, (listed - 1) * size), jnp.float32),
            pltpu.VMEM((3, atom_total, lanes), jnp.float32),
            pltpu.VMEM((atom_total, atom_total), jnp.bfloat16),
            pltpu.VMEM((16, atom_total), jnp.float32),
            flags,
            flags,
        ],
        compiler_params=pltpu.CompilerParams(
            collective_id=1, has_side_effects=True, vmem_limit_bytes=16 << 20
        ),
        name="finish",
    )(
        pltpu.with_memory_space_constraint(pair_lists, pltpu.HBM),
        partial,
        raw,
        rank,
        columns,
        before,
    )


def green_table(period):
    index = np.arange(period)
    signed = np.where(index <= period // 2, index, index - period) / (period * spacing)
    modulus = ((2.0 + np.cos(index * (2.0 * np.pi / period))) / 3.0) ** 2
    square = signed * signed
    return np.stack([square, np.exp(-((np.pi / ewald_split) ** 2) * square) / modulus]).astype(
        np.float32
    )


def green_factors(index, period):
    signed = jnp.where(index <= period // 2, index, index - period).astype(jnp.float32) / (
        period * spacing
    )
    modulus = ((2.0 + jnp.cos(index.astype(jnp.float32) * (2.0 * jnp.pi / period))) / 3.0) ** 2
    square = signed * signed
    return jnp.stack([square, jnp.exp(-((jnp.pi / ewald_split) ** 2) * square) / modulus])


def one_cluster(own_rows, partner):
    offsets = (own_rows[:3, :, None] - partner[:3, None, :]) * spacing
    dist_square = jnp.sum(offsets * offsets, axis=0)
    soft_square = dist_square + soft_core
    soft_dist = jnp.sqrt(soft_square)
    scaled = ewald_split * soft_dist
    strength = (
        jax.scipy.special.erfc(scaled) / soft_dist
        + ewald_split * root_factor * jnp.exp(-scaled * scaled)
    ) / soft_square
    cutoff_taper = jnp.where(
        dist_square < cutoff * cutoff, (1.0 - dist_square / (cutoff * cutoff)) ** 2, 0.0
    )
    weight = partner[3][None, :] * strength * cutoff_taper
    return own_rows[3] * jnp.sum(weight[None] * offsets, axis=2)


def far_by_planes(bounds, atoms, count_x, count_y, cells_x, cells_y):
    devices = count_x * count_y
    depth = GRID_Z // devices
    tiles = atoms.shape[2]
    pad_y = round_up(cells_y + 3, 8)
    stride = round_up(pad_y, 16)
    window = 2 * cells_y
    turn_x = halves(jnp.asarray(hartley(GRID_X)))
    turn_y = halves(jnp.asarray(hartley(GRID_Y)))
    volume = GRID_X * GRID_Y * GRID_Z * spacing**3
    column = jnp.asarray(green_table(GRID_X).T)
    row = jnp.asarray(green_table(GRID_Y))
    every_k = np.arange(GRID_Z)
    taps = np.outer(every_k, np.arange(4)) * (2.0 * np.pi / GRID_Z)
    square, scale = green_table(GRID_Z)
    table = np.concatenate(
        [
            every_k[:, None],
            np.cos(taps) + np.sin(taps),
            np.cos(taps) - np.sin(taps),
            square[:, None],
            scale[:, None] / (np.pi * volume),
        ],
        axis=1,
    ).astype(np.float32)
    vmem = pl.BlockSpec(memory_space=pltpu.VMEM)
    rows = GRID_X + window_rows
    batch = depth * window_rows
    angle = every_k * (2.0 * np.pi / GRID_Z)
    circle = np.repeat(np.stack([np.cos(angle), np.sin(angle)]), 8, axis=0).astype(np.float32)
    constants = (*turn_x, *turn_y, column, row, jnp.asarray(circle), jnp.asarray(table))
    fixed = pl.BlockSpec(memory_space=pltpu.HBM)
    return pl.pallas_call(
        functools.partial(mesh_kernel, (count_x, count_y), (cells_x, cells_y), pad_y),
        in_specs=[pl.BlockSpec(memory_space=pltpu.SMEM)] + [vmem] + [fixed] * fixed_arrays,
        out_specs=vmem,
        out_shape=jax.ShapeDtypeStruct((devices, 3, tiles, lanes), jnp.float32),
        scratch_shapes=[
            pltpu.VMEM((2, depth, rows, GRID_Y), jnp.float32),
            pltpu.VMEM((depth, rows, 4 * GRID_Y), jnp.float32),
            pltpu.VMEM((36 * devices * tiles + 8, lanes), jnp.float32),
            pltpu.VMEM((devices * tiles * depth + 8, lanes), jnp.float32),
            pltpu.VMEM((devices * tiles * depth + 8, lanes), jnp.float32),
            pltpu.VMEM((devices * tiles, 2 * stride, lanes), jnp.bfloat16),
            pltpu.VMEM((group_size, 2 * window, 2 * lanes), jnp.bfloat16),
            pltpu.VMEM((group_size, batch, 2 * lanes), jnp.bfloat16),
            pltpu.VMEM((gather_size, batch, 2 * lanes), jnp.float32),
            pltpu.VMEM((GRID_X, GRID_Y), jnp.float32),
            pltpu.VMEM((GRID_X, GRID_Y), jnp.float32),
            pltpu.SMEM((4 * devices * tiles,), jnp.int32),
            *[pltpu.VMEM(value.shape, value.dtype) for value in constants],
            pltpu.SemaphoreType.DMA((fixed_arrays,)),
        ],
        compiler_params=pltpu.CompilerParams(vmem_limit_bytes=36 << 20),
        name="mesh",
    )(
        bounds, atoms, *[pltpu.with_memory_space_constraint(value, pltpu.HBM) for value in constants]
    )


def convolved_by_lines(charge_mesh, count_x, count_y):
    turn_x = jnp.asarray(hartley(GRID_X))
    turn_y = jnp.asarray(hartley(GRID_Y))
    product = functools.partial(
        jnp.einsum, precision=lax.Precision.HIGHEST, preferred_element_type=jnp.float32
    )
    exchange = functools.partial(lax.all_to_all, tiled=True)
    lines = exchange(charge_mesh, "gx", split_axis=2, concat_axis=0)
    lines = product("xyk,xu->uyk", lines, turn_x)
    lines = exchange(lines, "gy", split_axis=0, concat_axis=1)
    lines = product("uyk,yv->uvk", lines, turn_y)
    wide, _, depth = lines.shape
    start_x = lax.axis_index("gy") * wide
    start_z = lax.axis_index("gx") * depth
    volume = GRID_X * GRID_Y * GRID_Z * spacing**3
    fx = green_factors(start_x + jnp.arange(wide, dtype=jnp.int32), GRID_X)
    fy = green_factors(jnp.arange(GRID_Y, dtype=jnp.int32), GRID_Y)
    fz = green_factors(start_z + jnp.arange(depth, dtype=jnp.int32), GRID_Z)
    square = fx[0][:, None, None] + fy[0][:, None] + fz[0]
    scale = fx[1][:, None, None] * fy[1][:, None] * fz[1] / (math.pi * volume)
    lines = lines * jnp.where(square > 0.0, scale / jnp.where(square > 0.0, square, 1.0), 0.0)
    lines = product("uvk,vy->uyk", lines, turn_y)
    lines = exchange(lines, "gy", split_axis=1, concat_axis=0)
    lines = product("uyk,ux->xyk", lines, turn_x)
    return exchange(lines, "gx", split_axis=0, concat_axis=2)


def far_by_lines(atoms, base, count_x, count_y, cells_x, cells_y, cells_z):
    atom_total = atoms.shape[1]
    cells = (cells_x, cells_y, cells_z)
    pad = (round_up(cells_x + 3, rows_group), round_up(cells_y + 3, 8))
    pad_x, pad_y = pad
    turn_z = jnp.asarray(hartley(GRID_Z))
    spread = pl.pallas_call(
        functools.partial(spread_kernel, cells, pad),
        out_shape=jax.ShapeDtypeStruct((pad_x, pad_y, GRID_Z), jnp.float32),
        scratch_shapes=[
            pltpu.VMEM((pad_x, atom_total), jnp.float32),
            pltpu.VMEM((pad_y, atom_total), jnp.float32),
            pltpu.VMEM((atom_total, 2 * GRID_Z), jnp.bfloat16),
            pltpu.VMEM((rows_group * pad_y, atom_total), jnp.bfloat16),
            pltpu.VMEM((rows_group * pad_y, atom_total), jnp.bfloat16),
        ],
        name="spread",
    )(atoms, base, turn_z)

    from_x = moved(spread[cells_x : cells_x + 3, :cells_y], 1, 0)
    from_y = moved(spread[:cells_x, cells_y : cells_y + 3], 0, 1)
    from_both = moved(spread[cells_x : cells_x + 3, cells_y : cells_y + 3], 1, 1)
    charge_mesh = (
        spread[:cells_x, :cells_y]
        .at[:3]
        .add(from_x)
        .at[:, :3]
        .add(from_y)
        .at[:3, :3]
        .add(from_both)
    )
    potential = convolved_by_lines(charge_mesh, count_x, count_y)
    upper_x = moved(potential[:3], -1, 0)
    upper_y = moved(potential[:, :3], 0, -1)
    upper_both = moved(potential[:3, :3], -1, -1)
    wider = jnp.concatenate(
        [
            jnp.concatenate([potential, upper_x], axis=0),
            jnp.concatenate([upper_y, upper_both], axis=0),
        ],
        axis=1,
    )
    wider = jnp.pad(wider, ((0, pad_x - cells_x - 3), (0, pad_y - cells_y - 3), (0, 0)))
    return pl.pallas_call(
        functools.partial(gather_kernel, cells, pad),
        out_shape=jax.ShapeDtypeStruct((3, atom_total), jnp.float32),
        scratch_shapes=[
            pltpu.VMEM((pad_x, atom_total), jnp.float32),
            pltpu.VMEM((pad_x, atom_total), jnp.float32),
            pltpu.VMEM((pad_y, atom_total), jnp.float32),
            pltpu.VMEM((pad_y, atom_total), jnp.float32),
            pltpu.VMEM((2 * GRID_Z, 2 * atom_total), jnp.bfloat16),
            pltpu.VMEM((rows_group * pad_y, 2 * atom_total), jnp.float32),
        ],
        name="gather",
    )(atoms, base, turn_z, wider)


def local(positions, charges, pair_lists, slab_dest, atom_counts):
    count_x = lax.axis_size("gx")
    count_y = lax.axis_size("gy")
    devices = count_x * count_y
    atom_total = positions.shape[3]
    clusters = pair_lists.shape[2]
    cluster_size = atom_total // clusters
    blocks = slab_dest.shape[2]
    block_size = atom_total // blocks
    cells_x = GRID_X // count_x
    cells_y = GRID_Y // count_y
    cells_z = GRID_Z // count_y
    by_planes = (
        GRID_Z == 8 * devices
        and GRID_Z == lanes
        and cells_y == 64
        and cells_x % 8 == 0
        and cells_x <= 64
        and count_y % 2 == 0
        and atom_total == 8 * lanes
        and cluster_size % lanes == 0
    )
    if by_planes:
        sizes = (count_x, count_y, cells_x, cells_y)
        raw, atoms, bounds, rank, columns, before = shared(
            positions, charges, atom_counts, clusters, *sizes
        )
        partial = far_by_planes(bounds, atoms, *sizes)
        short_sums, long_sums = finished(
            pair_lists, partial, raw, rank, columns, before, *sizes
        )
        living = jnp.arange(atom_total, dtype=jnp.int32) < atom_counts[0, 0]
        charge = jnp.where(living, charges[0, 0], 0.0)
        return (short_sums * (charge * spacing), long_sums * (charge * (-1.0 / spacing)))
    living = jnp.arange(atom_total, dtype=jnp.int32) < atom_counts[0, 0]
    charge = jnp.where(living, charges[0, 0], 0.0)
    packed = jnp.concatenate([positions, charge[None, None, None, :]], axis=0)
    atoms = packed.reshape(4, atom_total)
    base = jnp.broadcast_to(
        (slab_dest[0, 0] * cells_z)[:, None], (blocks, block_size)
    ).reshape(1, atom_total)
    gathered = lax.all_gather(atoms, ("gx", "gy"), axis=0, tiled=False)
    far_part = far_by_lines(atoms, base, count_x, count_y, cells_x, cells_y, cells_z)

    chosen = pair_lists[0, 0]
    beside = chosen // clusters
    step_x, step_y = (beside // 3 - 1, beside % 3 - 1)
    at_x = (lax.axis_index("gx") + step_x + count_x) % count_x
    at_y = (lax.axis_index("gy") + step_y + count_y) % count_y
    number = (at_x * count_y + at_y) * clusters + chosen % clusters
    pick = (number[:, :, None] == jnp.arange(devices * clusters, dtype=jnp.int32)).astype(
        jnp.float32
    )
    pool = gathered[:, :4].reshape(devices, 4, clusters, cluster_size)
    pool = jnp.transpose(pool, (1, 0, 2, 3)).reshape(4, devices * clusters, cluster_size)
    partners = jnp.einsum(
        "cln,fnk->cflk",
        pick,
        pool,
        precision=lax.Precision.HIGHEST,
        preferred_element_type=jnp.float32,
    )
    shift_x = (step_x * cells_x).astype(jnp.float32)
    shift_y = (step_y * cells_y).astype(jnp.float32)
    flat = jnp.zeros_like(shift_x)
    shift = jnp.stack([shift_x, shift_y, flat, flat], axis=1)
    partners = (partners + shift[:, :, :, None]).reshape(clusters, 4, -1)
    own = packed.reshape(4, clusters, cluster_size)
    pair_part = jnp.stack(
        [one_cluster(own[:, c], partners[c]) for c in range(clusters)], axis=1
    )
    short_forces = pair_part.reshape(3, 1, 1, atom_total)
    return (short_forces, far_part.reshape(3, 1, 1, atom_total))


def solution(mesh):
    return jax.shard_map(
        local,
        mesh=mesh,
        in_specs=(
            P(None, ("rep", "gx"), "gy", None),
            P(("rep", "gx"), "gy", None),
            P(("rep", "gx"), "gy", None, None),
            P(("rep", "gx"), "gy", None),
            P(("rep", "gx"), "gy"),
        ),
        out_specs=(P(None, ("rep", "gx"), "gy", None), P(None, ("rep", "gx"), "gy", None)),
        check_vma=False,
    )
```
